32 devices in a mesh: dp: 8 (over z, x), expert: 4 (over y, core).
Axes of the slice: x: 2, y: 2, z: 4, core: 2. Of those that a mesh axis runs over, the one named last changes fastest.
Arguments:
- tokens: bfloat16 [20480, 1536], P(('dp', 'expert')), may hold values from -6 to 6
- attn_gain: bfloat16 [1536], P(('dp', 'expert')), may hold values from 0.5 to 1.5
- w_query: bfloat16 [1536, 1536], P(('dp', 'expert')), may hold values from -0.21875 to 0.21875
- w_key: bfloat16 [1536, 512], P(('dp', 'expert')), may hold values from -0.21875 to 0.21875
- w_value: bfloat16 [1536, 512], P(('dp', 'expert')), may hold values from -0.15625 to 0.15625
- w_out: bfloat16 [1536, 1536], P(('dp', 'expert')), may hold values from -0.625 to 0.625
- w_router: bfloat16 [1536, 40], P(('dp', 'expert')), may hold values from -0.078125 to 0.078125
- ffn_gain: bfloat16 [1536], P(('dp', 'expert')), may hold values from 0.5 to 1.5
- w_gate: bfloat16 [40, 1536, 512], P('expert', 'dp'), may hold values from -0.15625 to 0.15625
- w_up: bfloat16 [40, 1536, 512], P('expert', 'dp'), may hold values from -0.15625 to 0.15625
- w_down: bfloat16 [40, 512, 1536], P('expert', None, 'dp'), may hold values from -1 to 1
- routes: int32 [20480, 8], P(('dp', 'expert')), may hold values from 0 to 39, all different within a row; in each aligned block of 640 rows (0 to 639, 640 to 1279, ...) at most 136 rows name the same one
- cotangent: bfloat16 [20480, 1536], P(('dp', 'expert')), may hold values from -6 to 6
Outputs:
- output: bfloat16 [20480, 1536], P(('dp', 'expert'))
- input_grad: bfloat16 [20480, 1536], P(('dp', 'expert'))
- attn_gain_grad: float32 [1536], P(('dp', 'expert'))
- query_grad: float32 [1536, 1536], P(('dp', 'expert'))
- key_grad: float32 [1536, 512], P(('dp', 'expert'))
- value_grad: float32 [1536, 512], P(('dp', 'expert'))
- out_grad: float32 [1536, 1536], P(('dp', 'expert'))
- router_grad: float32 [1536, 40], P(('dp', 'expert'))
- ffn_gain_grad: float32 [1536], P(('dp', 'expert'))
- gate_grad: float32 [40, 1536, 512], P('expert', 'dp')
- up_grad: float32 [40, 1536, 512], P('expert', 'dp')
- down_grad: float32 [40, 512, 1536], P('expert', None, 'dp')
The draws below stay inside these ranges and needn't reach their ends.
Inputs may be any that keep to these rules, and one draw needn't show every extreme that they name: `routes`: each row names 8 different experts. Among the rows of one device no expert is named more than 136 times, and in some device's rows some expert is named exactly 136 times.
All inputs are finite; a program needn't handle non-finite values.
Results may differ from the reference program's by a relative error of at most 0.02.
Values may be sent and summed in bfloat16 or wider, within the bound.
A program may use at most 320 MiB of HBM per device.

```python
import math
import jax
import jax.numpy as jnp
import numpy as np
from jax import lax

D = 1536
HQ = 24
KVH = 8
HD = 64
FF = 512
TOP = 8
P_DEV = 128
CONT = 512
EXPERTS = 40
TOK_DEV = 640
GROUP_DEVS = 8
PROMPT = 1024
GROUPS = 4
TOKENS = 20480
KVW = 512
RATIO = 3
CAP = 136
DEVICES = 32


def block_levels(key, dims, cuts, smallest, largest):
    def one(axis_at, parts):
        draws = jax.random.uniform(jax.random.fold_in(jax.random.fold_in(key, 6), axis_at), (parts,), jnp.float32, smallest / len(cuts), largest / len(cuts))
        return jnp.repeat(jnp.exp(draws), dims[axis_at] // parts).reshape((-1,) + (1,) * (len(dims) - axis_at - 1))

    factor_of = one(*cuts[0])
    for cut in cuts[1:]:
        factor_of = factor_of * one(*cut)
    return factor_of


def routed_block(own_key, own, number, rows, count, top, most, slope):
    ranking = jax.random.permutation(own_key, count)
    heavy_load, ordinary = shares(count, rows * top, most, slope, True), shares(count, rows * top, most, slope, False)
    places = jnp.arange(count)

    def named(lengths, turn):
        used = int((lengths > 0).sum())
        fixed = max(1, used // 4)
        shifted = fixed + (places - fixed + turn * (used - fixed)) % max(1, count - fixed)
        return jnp.zeros((count,), jnp.int32).at[ranking[jnp.where(places < fixed, places, shifted)]].set(jnp.asarray(lengths, jnp.int32))

    lengths = jnp.where(number % 4 == 0, named(heavy_load, number // 4), named(ordinary, number - number // 4 - 1))
    mixed = jax.random.permutation(jax.random.fold_in(own, 3), count)
    source_of, receiver = mixed[0:count // 2 * 2:2], mixed[1:count // 2 * 2:2]
    slack = jnp.minimum(lengths[source_of] - 1, most - lengths[receiver]) // 2
    slack = jnp.where((source_of == ranking[0]) | (receiver == ranking[0]) | (lengths[receiver] == 0), 0, jnp.maximum(slack, 0))
    shifted = jax.random.randint(jax.random.fold_in(own, 4), (count // 2,), 0, 1 << 20) % (slack + 1)
    lengths = lengths.at[source_of].add(-shifted).at[receiver].add(shifted)
    members = jnp.searchsorted(jnp.cumsum(lengths), jnp.arange(rows * top), side="right").astype(jnp.int32)
    grid = members.reshape(top, rows).T
    grid = grid[jax.random.permutation(jax.random.fold_in(own, 1), rows)]
    turn = jax.random.randint(jax.random.fold_in(own, 2), (rows, 1), 0, top)
    return jnp.take_along_axis(grid, (jnp.arange(top)[None, :] + turn) % top, axis=1)


def shares(count, total, limit, lean, full):
    loads = [(1 << 20) // math.isqrt(standing ** lean) + 1 for standing in range(1, count + 1)]
    largest = limit if full else min(limit, max(-(-total // count), total * loads[0] // sum(loads)))
    least = 1 if total - largest >= count - 1 else 0
    counts, surplus = [largest] + [least] * (count - 1), total - largest - least * (count - 1)
    while surplus > 0:
        candidates = [i for i in range(1, count) if counts[i] < largest] or [i for i in range(1, count) if counts[i] < limit]
        mass, remaining = sum([loads[i] for i in candidates]), surplus
        for i in candidates:
            extra = min(limit - counts[i], max(1, remaining * loads[i] // mass), surplus)
            counts[i] = counts[i] + extra
            surplus = surplus - extra
    return np.array(counts)


def noise(stream_key, extent, scale, reach, cuts=(), held_as=jnp.bfloat16):
    values = scale * jax.random.normal(stream_key, extent, jnp.float32)
    if cuts:
        values = values * block_levels(stream_key, extent, cuts, -0.22, 0.18)
    return jnp.clip(values, -reach, reach).astype(held_as)


def setup_inputs(seed: int = 0) -> dict:
    splits = jax.random.split(jax.random.key(seed), 14)
    tokens = noise(splits[0], (TOKENS, D), 1.0, 6.0, ((0, 32),))
    attn_gain = jnp.clip(1.0 + 0.1 * jax.random.normal(splits[1], (D,), jnp.float32), 0.5, 1.5).astype(jnp.bfloat16)
    w_query = noise(splits[2], (D, D), (D // 2) ** -0.5, 0.21875, ((0, 32),))
    w_key = noise(splits[3], (D, KVW), (D // 2) ** -0.5, 0.21875, ((0, 32),))
    w_value = noise(splits[4], (D, KVW), D ** -0.5, 0.15625, ((0, 32),))
    w_out = noise(splits[5], (D, D), (D // 16) ** -0.5, 0.625, ((0, 32),))
    w_router = noise(splits[6], (D, EXPERTS), (4 * D) ** -0.5, 0.078125, ((0, 32),))
    ffn_gain = jnp.clip(1.0 + 0.1 * jax.random.normal(splits[7], (D,), jnp.float32), 0.5, 1.5).astype(jnp.bfloat16)
    w_gate = noise(splits[8], (EXPERTS, D, FF), D ** -0.5, 0.15625, ((0, 4), (1, 8)))
    w_up = noise(splits[9], (EXPERTS, D, FF), D ** -0.5, 0.15625, ((0, 4), (1, 8)))
    w_down = noise(splits[10], (EXPERTS, FF, D), (FF // 16) ** -0.5, 1.0, ((0, 4), (2, 8)))
    routes_keys = jax.random.split(jax.random.fold_in(splits[11], 1), TOKENS // TOK_DEV)
    routes_turns = jax.random.permutation(jax.random.fold_in(splits[11], 3), TOKENS // TOK_DEV)
    routes = jax.vmap(lambda own, number: routed_block(jax.random.fold_in(splits[11], 2), own, number, TOK_DEV, EXPERTS, TOP, CAP, 1))(routes_keys, routes_turns).reshape((TOKENS, TOP))
    cotangent = noise(splits[12], (TOKENS, D), 1.0, 6.0, ((0, 32),))
    return {"tokens": tokens, "attn_gain": attn_gain, "w_query": w_query, "w_key": w_key, "w_value": w_value, "w_out": w_out, "w_router": w_router, "ffn_gain": ffn_gain, "w_gate": w_gate, "w_up": w_up, "w_down": w_down, "routes": routes, "cotangent": cotangent}


@jax.custom_vjp
def low(v):
    return lax.optimization_barrier(v.astype(jnp.bfloat16)).astype(jnp.float32)

@jax.custom_vjp
def low_back(v):
    return v

def low_keep(v):
    return (low(v), None)

def low_pass(kept, grad):
    return (grad,)

def back_keep(v):
    return (v, None)

def back_low(kept, grad):
    return (low(grad),)
low.defvjp(low_keep, low_pass)
low_back.defvjp(back_keep, back_low)
EPSILON = 1e-06
NEGATIVE = -1e+30
HIGHEST = lax.Precision.HIGHEST

def rms_scale(values):
    return lax.rsqrt(lax.optimization_barrier(jnp.mean(values * values, axis=-1, keepdims=True)) + EPSILON)

def matmul(left_side, right_side):
    return jnp.dot(left_side, right_side, precision=HIGHEST, preferred_element_type=jnp.float32)

def visible_mask(place_index):
    row_ids = jnp.arange(TOK_DEV, dtype=jnp.int32)[:, None]
    col_ids = jnp.arange(PROMPT + CONT, dtype=jnp.int32)[None, :]
    in_prompt = col_ids < PROMPT
    causal_prompt = in_prompt & (col_ids <= place_index * P_DEV + row_ids)
    own_causal = in_prompt | (col_ids - PROMPT <= row_ids - P_DEV)
    return jnp.where(row_ids < P_DEV, causal_prompt, own_causal)

@jax.checkpoint
def attend(queries, key_rows, value_rows, place_index):
    heads_q = queries.reshape(TOK_DEV, KVH, RATIO, HD)
    heads_k = key_rows.reshape(PROMPT + CONT, KVH, HD)
    heads_v = value_rows.reshape(PROMPT + CONT, KVH, HD)
    scores = jnp.einsum('qgrd,kgd->grqk', heads_q, heads_k, precision=HIGHEST) * HD ** (-0.5)
    scores = low_back(scores)
    scores = jnp.where(visible_mask(place_index)[None, None], scores, NEGATIVE)
    attention = low(jax.nn.softmax(scores, axis=-1))
    mixed_rows = jnp.einsum('grqk,kgd->qgrd', attention, heads_v, precision=HIGHEST)
    return mixed_rows.reshape(TOK_DEV, HQ * HD)

@jax.checkpoint
def expert_rows(gate_mat, up_mat, down_mat, block_rows):
    block_rows = low_back(block_rows)
    gate_val = low_back(matmul(block_rows, gate_mat))
    up_val = low_back(matmul(block_rows, up_mat))
    active = low(jax.nn.silu(gate_val) * up_val)
    return low_back(low(matmul(active, down_mat)))

def per_device(flat_rows):
    width = flat_rows.shape[1]
    grouped = flat_rows.reshape(GROUPS, GROUP_DEVS, TOK_DEV, width)
    prompt_part = grouped[:, :, :P_DEV].reshape(GROUPS, 1, PROMPT, width)
    prompt_part = jnp.broadcast_to(prompt_part, (GROUPS, GROUP_DEVS, PROMPT, width))
    joined = jnp.concatenate([prompt_part, grouped[:, :, P_DEV:]], axis=2)
    return joined.reshape(DEVICES, PROMPT + CONT, width)

def expert_layer(hidden_two, logits, routes, w_gate, w_up, w_down):
    flat_ids = routes.reshape(DEVICES, TOK_DEV * TOP)
    expert_hits = (flat_ids[:, :, None] == jnp.arange(EXPERTS, dtype=jnp.int32)).astype(jnp.int32)
    earlier = jnp.cumsum(expert_hits, axis=1) - expert_hits
    slot_index = lax.optimization_barrier(jnp.sum(earlier * expert_hits, axis=2)).astype(jnp.int32)
    device_ids = jnp.arange(DEVICES, dtype=jnp.int32)[:, None]
    position = (device_ids * CAP + slot_index).astype(jnp.int32)
    source_rows = (device_ids * TOK_DEV + jnp.arange(TOK_DEV * TOP, dtype=jnp.int32)[None, :] // TOP).astype(jnp.int32)
    row_table = jnp.full((EXPERTS, DEVICES * CAP), TOKENS, jnp.int32).at[flat_ids, position].set(source_rows)
    gate_weights = jax.nn.softmax(jnp.take_along_axis(logits, routes, axis=1), axis=-1)
    weight_table = jnp.zeros((EXPERTS, DEVICES * CAP), jnp.float32).at[flat_ids, position].set(gate_weights.reshape(DEVICES, TOK_DEV * TOP))
    padded = jnp.concatenate([hidden_two, jnp.zeros((1, D), jnp.float32)], axis=0)

    def expert_step(summed, pieces):
        gate_mat, up_mat, down_mat, index_row, weight_row = pieces
        result = expert_rows(gate_mat, up_mat, down_mat, padded[index_row])
        return (summed.at[index_row].add(result * weight_row[:, None]), None)
    summed, unused = lax.scan(expert_step, jnp.zeros((TOKENS + 1, D), jnp.float32), (w_gate, w_up, w_down, row_table, weight_table))
    return summed[:TOKENS]

def layer(tokens, attn_gain, w_query, w_key, w_value, w_out, w_router, ffn_gain, w_gate, w_up, w_down, routes):
    hidden_one = low(tokens * rms_scale(tokens) * attn_gain)
    queries = low_back(low(matmul(hidden_one, w_query)))
    key_rows = low_back(low(matmul(hidden_one, w_key)))
    value_rows = low_back(low(matmul(hidden_one, w_value)))
    places = (jnp.arange(DEVICES, dtype=jnp.int32) % GROUP_DEVS).astype(jnp.int32)
    mixed_rows = lax.map(lambda pieces: attend(pieces[0], pieces[1], pieces[2], pieces[3]), (queries.reshape(DEVICES, TOK_DEV, D), per_device(key_rows), per_device(value_rows), places))
    mixed_rows = low_back(low(mixed_rows.reshape(TOKENS, D)))
    second = tokens + low_back(matmul(mixed_rows, w_out))
    hidden_two = low(second * rms_scale(second) * ffn_gain)
    logits = low_back(matmul(hidden_two, w_router))
    return second + expert_layer(hidden_two, logits, routes, w_gate, w_up, w_down)

def reference(tokens, attn_gain, w_query, w_key, w_value, w_out, w_router, ffn_gain, w_gate, w_up, w_down, routes, cotangent):
    floats = tuple((array_item.astype(jnp.float32) for array_item in (tokens, attn_gain, w_query, w_key, w_value, w_out, w_router, ffn_gain, w_gate, w_up, w_down)))

    def forward(*weights):
        return layer(*weights, routes)
    output, pull_back = jax.vjp(forward, *floats)
    gradients = pull_back(cotangent.astype(jnp.float32))
    return (output.astype(jnp.bfloat16), gradients[0].astype(jnp.bfloat16), gradients[1], gradients[2], gradients[3], gradients[4], gradients[5], gradients[6], gradients[7], gradients[8], gradients[9], gradients[10])
```

```python
import functools
import jax
import jax.numpy as jnp
from jax import lax
from jax.sharding import PartitionSpec as P
from jax.experimental import pallas as pl
from jax.experimental.pallas import tpu as pltpu

HD = 64
P_DEV = 128
NEGATIVE = -1e30
F32 = jnp.float32
BF = jnp.bfloat16


def dot_nt(a, b):
    return lax.dot_general(a, b, (((1,), (1,)), ((), ())), preferred_element_type=F32)


def dot_nn(a, b):
    return lax.dot_general(a, b, (((1,), (0,)), ((), ())), preferred_element_type=F32)


def dot_tn(a, b):
    return lax.dot_general(a, b, (((0,), (0,)), ((), ())), preferred_element_type=F32)


def halves(pair):
    lane = lax.broadcasted_iota(jnp.int32, pair.shape, 1)
    zero = jnp.zeros_like(pair)
    return jnp.where(lane < HD, pair, zero), jnp.where(lane < HD, zero, pair)


def placed_halves(pair_f32):
    low0, high1 = halves(pair_f32)
    high0 = pltpu.roll(low0, HD, 1)
    low1 = pltpu.roll(high1, HD, 1)
    return ((low0.astype(BF), high0.astype(BF)), (low1.astype(BF), high1.astype(BF)))


def attend_kernel(place_ref, q_ref, kp_ref, vp_ref, ko_ref, vo_ref, o_ref, lse_ref, kpad, vpad, s_scr, p_scr):
    rows = q_ref.shape[0]
    prompt = kp_ref.shape[0]
    cont = ko_ref.shape[0]
    place = place_ref[0]
    for src, dst in ((kp_ref, kpad), (vp_ref, vpad)):
        for head, pair in enumerate(placed_halves(src[...].astype(F32))):
            for half in range(2):
                dst[head, half, 0:prompt, :] = pair[half]
    for src, dst in ((ko_ref, kpad), (vo_ref, vpad)):
        for head, pair in enumerate(placed_halves(src[...].astype(F32))):
            for half in range(2):
                dst[head, half, prompt:prompt + cont, :] = pair[half]
    key_id = lax.broadcasted_iota(jnp.int32, (prompt, P_DEV), 0)
    row_id = lax.broadcasted_iota(jnp.int32, (prompt, P_DEV), 1)
    seen_prompt = key_id <= place * P_DEV + row_id
    diag = lax.broadcasted_iota(jnp.int32, (P_DEV, P_DEV), 0) <= lax.broadcasted_iota(jnp.int32, (P_DEV, P_DEV), 1)
    blocks = cont // P_DEV
    stats = []
    for chunk in range(3):
        queries = (q_ref[:, chunk * 128:(chunk + 1) * 128].astype(F32) * HD ** (-0.5)).astype(BF)
        total = None
        for half in range(2):
            position = chunk * 2 + half
            head = position // 3
            keys = kpad.at[head, half]
            scores = dot_nt(keys[0:prompt, :], queries)
            first = jnp.where(seen_prompt, scores[:, 0:P_DEV], NEGATIVE)
            rest = scores[:, P_DEV:]
            s_scr[0:prompt, 0:P_DEV] = first
            s_scr[0:prompt, P_DEV:] = rest
            top = jnp.concatenate([jnp.max(first, 0, keepdims=True), jnp.max(rest, 0, keepdims=True)], 1)
            tops = [top[:, i * P_DEV:(i + 1) * P_DEV] for i in range(1 + blocks)]
            for block in range(blocks):
                start = (1 + block) * P_DEV
                at = prompt + block * P_DEV
                own = dot_nt(keys[at:at + P_DEV, :], queries[start:, :])
                edge = jnp.where(diag, own[:, 0:P_DEV], NEGATIVE)
                s_scr[at:at + P_DEV, start:start + P_DEV] = edge
                tops[1 + block] = jnp.maximum(tops[1 + block], jnp.max(edge, 0, keepdims=True))
                if block + 1 < blocks:
                    later = own[:, P_DEV:]
                    s_scr[at:at + P_DEV, start + P_DEV:] = later
                    best = jnp.max(later, 0, keepdims=True)
                    for i in range(block + 1, blocks):
                        at_i = (i - block - 1) * P_DEV
                        tops[1 + i] = jnp.maximum(tops[1 + i], best[:, at_i:at_i + P_DEV])
            top = jnp.concatenate(tops, 1)
            weights = jnp.exp(s_scr[0:prompt, :] - top)
            mass = jnp.sum(weights, 0, keepdims=True)
            masses = [mass[:, i * P_DEV:(i + 1) * P_DEV] for i in range(1 + blocks)]
            values = vpad.at[head, half]
            mixed = dot_tn(values[0:prompt, :], weights.astype(BF))
            for block in range(blocks):
                start = (1 + block) * P_DEV
                at = prompt + block * P_DEV
                part = jnp.exp(s_scr[at:at + P_DEV, start:] - top[:, start:])
                p_scr[block * P_DEV:(block + 1) * P_DEV, start:] = part.astype(BF)
                if block:
                    p_scr[block * P_DEV:(block + 1) * P_DEV, P_DEV:start] = jnp.zeros((P_DEV, block * P_DEV), BF)
                part_mass = jnp.sum(part, 0, keepdims=True)
                for i in range(block, blocks):
                    at_i = (i - block) * P_DEV
                    masses[1 + i] = masses[1 + i] + part_mass[:, at_i:at_i + P_DEV]
            own_mixed = dot_tn(values[prompt:prompt + cont, :], p_scr[:, P_DEV:])
            mass = jnp.concatenate(masses, 1)
            scale = 1.0 / mass
            mixed = jnp.concatenate([mixed[:, 0:P_DEV], mixed[:, P_DEV:] + own_mixed], 1) * scale
            total = mixed if total is None else total + mixed
            stats.append(top + jnp.log(mass))
        o_ref[:, chunk * 128:(chunk + 1) * 128] = jnp.transpose(total).astype(BF)
    lse_ref[0] = jnp.concatenate(stats + [jnp.zeros((2, rows), F32)], 0)


def attend(place, query, prompt_key, prompt_value, own_key, own_value):
    rows = query.shape[0]
    prompt = prompt_key.shape[0]
    cont = own_key.shape[0]
    pairs = prompt_key.shape[1] // 128
    col = lambda i: (0, i)
    return pl.pallas_call(
        attend_kernel,
        grid=(pairs,),
        in_specs=[
            pl.BlockSpec(memory_space=pltpu.SMEM),
            pl.BlockSpec((rows, 384), col),
            pl.BlockSpec((prompt, 128), col),
            pl.BlockSpec((prompt, 128), col),
            pl.BlockSpec((cont, 128), col),
            pl.BlockSpec((cont, 128), col),
        ],
        out_specs=[pl.BlockSpec((rows, 384), col), pl.BlockSpec((1, 8, rows), lambda i: (i, 0, 0))],
        out_shape=[
            jax.ShapeDtypeStruct(query.shape, BF),
            jax.ShapeDtypeStruct((pairs, 8, rows), F32),
        ],
        scratch_shapes=[
            pltpu.VMEM((2, 2, prompt + cont, 128), BF),
            pltpu.VMEM((2, 2, prompt + cont, 128), BF),
            pltpu.VMEM((prompt + cont, rows), F32),
            pltpu.VMEM((cont, rows), BF),
        ],
        cost_estimate=pl.CostEstimate(flops=10**6, bytes_accessed=10**6, transcendentals=0),
        name="attend",
    )(place, query, prompt_key, prompt_value, own_key, own_value)


def attend_back_kernel(place_ref, q_ref, kp_ref, vp_ref, ko_ref, vo_ref, o_ref, do_ref, lse_ref,
                       dq_ref, dkp_ref, dvp_ref, dko_ref, dvo_ref, kpad, vpad, dk_acc, dv_acc):
    rows = q_ref.shape[0]
    prompt = kp_ref.shape[0]
    cont = ko_ref.shape[0]
    step = 2 * P_DEV
    place = place_ref[0]
    for src, dst, at, size in ((kp_ref, kpad, 0, prompt), (vp_ref, vpad, 0, prompt),
                               (ko_ref, kpad, prompt, cont), (vo_ref, vpad, prompt, cont)):
        for head, pair in enumerate(placed_halves(src[...].astype(F32))):
            for half in range(2):
                dst[head, half, at:at + size, :] = pair[half]
    dk_acc[...] = jnp.zeros_like(dk_acc)
    dv_acc[...] = jnp.zeros_like(dv_acc)
    for chunk in range(3):
        lanes = slice(chunk * 128, (chunk + 1) * 128)
        scaled = q_ref[:, lanes].astype(F32) * HD ** (-0.5)
        queries = scaled.astype(BF)
        query_halves = [part.astype(BF) for part in halves(scaled)]
        outs = o_ref[:, lanes].astype(F32)
        grads_f32 = do_ref[:, lanes].astype(F32)
        grads = do_ref[:, lanes]
        grad_halves = [part.astype(BF) for part in halves(grads_f32)]
        inner = jnp.transpose(outs * grads_f32)
        total = jnp.zeros((128, rows), F32)
        for half in range(2):
            position = chunk * 2 + half
            head = position // 3
            level = lse_ref[0, position:position + 1, :]
            delta = jnp.sum(inner[half * HD:(half + 1) * HD, :], 0, keepdims=True)

            def block(at, cols, mask, queries=queries, grads=grads, query_half=query_halves[half],
                      grad_half=grad_halves[half], level=level, delta=delta, head=head, half=half):
                keys = kpad[head, half, pl.ds(at, step), :]
                values = vpad[head, half, pl.ds(at, step), :]
                scores = dot_nt(keys, queries[cols, :])
                weights = jnp.exp(mask(scores) - level[:, cols])
                grad_weights = dot_nt(values, grads[cols, :])
                grad_scores = weights * (grad_weights - delta[:, cols])
                low_weights = weights.astype(BF)
                low_scores = grad_scores.astype(BF)
                dv_acc[head, pl.ds(at, step), :] += dot_nn(low_weights, grad_half[cols, :])
                dk_acc[head, pl.ds(at, step), :] += dot_nn(low_scores, query_half[cols, :])
                return dot_tn(keys, low_scores)

            def prompt_step(i, carry):
                at = pl.multiple_of(i * step, step)

                def mask(scores):
                    key_id = at + lax.broadcasted_iota(jnp.int32, (step, P_DEV), 0)
                    row_id = lax.broadcasted_iota(jnp.int32, (step, P_DEV), 1)
                    first = jnp.where(key_id <= place * P_DEV + row_id, scores[:, 0:P_DEV], NEGATIVE)
                    return jnp.concatenate([first, scores[:, P_DEV:]], 1)

                return carry + block(at, slice(0, rows), mask)

            total = lax.fori_loop(0, prompt // step, prompt_step, total)
            for own in range(cont // step):
                start = P_DEV + own * step

                def mask(scores):
                    key_id = lax.broadcasted_iota(jnp.int32, (step, step), 0)
                    row_id = lax.broadcasted_iota(jnp.int32, (step, step), 1)
                    edge = jnp.where(key_id <= row_id, scores[:, 0:step], NEGATIVE)
                    if scores.shape[1] == step:
                        return edge
                    return jnp.concatenate([edge, scores[:, step:]], 1)

                part = block(prompt + own * step, slice(start, rows), mask)
                total = jnp.concatenate([total[:, 0:start], total[:, start:] + part], 1)
        dq_ref[:, lanes] = (jnp.transpose(total) * HD ** (-0.5)).astype(BF)
    for acc, out_prompt, out_own in ((dk_acc, dkp_ref, dko_ref), (dv_acc, dvp_ref, dvo_ref)):
        low0, high0 = halves(acc[0])
        low1, high1 = halves(acc[1])
        merged = low0 + pltpu.roll(high0, HD, 1) + high1 + pltpu.roll(low1, HD, 1)
        out_prompt[...] = merged[0:prompt].astype(BF)
        out_own[...] = merged[prompt:].astype(BF)


def attend_back(place, query, prompt_key, prompt_value, own_key, own_value, mixed, grad, lse):
    rows = query.shape[0]
    prompt = prompt_key.shape[0]
    cont = own_key.shape[0]
    pairs = prompt_key.shape[1] // 128
    col = lambda i: (0, i)
    wide = pl.BlockSpec((rows, 384), col)
    keys_p = pl.BlockSpec((prompt, 128), col)
    keys_o = pl.BlockSpec((cont, 128), col)
    return pl.pallas_call(
        attend_back_kernel,
        grid=(pairs,),
        in_specs=[
            pl.BlockSpec(memory_space=pltpu.SMEM),
            wide, keys_p, keys_p, keys_o, keys_o, wide, wide,
            pl.BlockSpec((1, 8, rows), lambda i: (i, 0, 0)),
        ],
        out_specs=[wide, keys_p, keys_p, keys_o, keys_o],
        out_shape=[
            jax.ShapeDtypeStruct(query.shape, BF),
            jax.ShapeDtypeStruct(prompt_key.shape, BF),
            jax.ShapeDtypeStruct(prompt_key.shape, BF),
            jax.ShapeDtypeStruct(own_key.shape, BF),
            jax.ShapeDtypeStruct(own_key.shape, BF),
        ],
        scratch_shapes=[
            pltpu.VMEM((2, 2, prompt + cont, 128), BF),
            pltpu.VMEM((2, 2, prompt + cont, 128), BF),
            pltpu.VMEM((2, prompt + cont, 128), F32),
            pltpu.VMEM((2, prompt + cont, 128), F32),
        ],
        cost_estimate=pl.CostEstimate(flops=10**6, bytes_accessed=10**6, transcendentals=0),
        name="attend_back",
    )(place, query, prompt_key, prompt_value, own_key, own_value, mixed, grad, lse)


SLOTS_ALIGN = 16


def gather_kernel(count, with_gates, pos_ref, *refs):
    if with_gates:
        gate_ref, rows_ref, x_ref, g_ref, pick = refs
    else:
        rows_ref, x_ref, pick = refs
    tokens = rows_ref.shape[1]
    slots = x_ref.shape[1] // count
    half = rows_ref.shape[2] // 2
    slot_id = lax.broadcasted_iota(jnp.int32, (slots, tokens), 0)
    for k in range(count):
        hit = slot_id == pos_ref[0, k:k + 1, :]
        pick[k * slots:(k + 1) * slots, :] = jnp.where(hit, 1.0, 0.0).astype(BF)
        if with_gates:
            gate = jnp.sum(jnp.where(hit, gate_ref[0, k:k + 1, :], 0.0), 1, keepdims=True)
            g_ref[0, k * slots:(k + 1) * slots, :] = jnp.broadcast_to(gate, (slots, 128))
    x_ref[0, :, 0:half] = dot_nn(pick[...], rows_ref[0, :, 0:half]).astype(BF)
    x_ref[0, :, half:] = dot_nn(pick[...], rows_ref[0, :, half:]).astype(BF)


def gather_rows(positions, gates, rows, count, slots):
    sources, tokens, width = rows.shape
    size = count * slots
    table = pl.BlockSpec((1, 8, tokens), lambda s: (s, 0, 0))
    block = lambda shape: pl.BlockSpec((1,) + shape, lambda s: (s, 0, 0))
    tables = [positions] if gates is None else [positions, gates]
    outs = [((size, width), BF)] if gates is None else [((size, width), BF), ((size, 128), F32)]
    return pl.pallas_call(
        functools.partial(gather_kernel, count, gates is not None),
        grid=(sources,),
        in_specs=[table] * len(tables) + [block((tokens, width))],
        out_specs=[block(shape) for shape, _ in outs],
        out_shape=[jax.ShapeDtypeStruct((sources,) + shape, dtype) for shape, dtype in outs],
        scratch_shapes=[pltpu.VMEM((size, tokens), BF)],
        cost_estimate=pl.CostEstimate(flops=10**6, bytes_accessed=10**6, transcendentals=0),
        name="gather_rows",
    )(*tables, rows)


def expert_kernel(k, shards, slots, dp_ref, x_ref, g_ref, gate_ref, *refs):
    w_refs = refs[0:shards // 2]
    (y_out, dx_out, dg_out, keep_out, send_out,
     xs, gs, gates, ws, ys, dxs, dgs, dab, actg, stage,
     in_sem, w_sem, out_sem, grad_sem) = refs[shards // 2:]
    dp = dp_ref[0]
    sources = x_ref.shape[0]
    width = xs.shape[1]
    piece = width // shards
    hidden = ws.shape[2]
    mine = pl.ds(k * slots, slots)

    def row_copies(s):
        at = pl.ds(pl.multiple_of(s * slots, 16), slots)
        return (
            pltpu.make_async_copy(x_ref.at[s, mine, :], xs.at[at, :], in_sem.at[0, s]),
            pltpu.make_async_copy(g_ref.at[s, mine, :], gs.at[at, :], in_sem.at[1, s]),
            pltpu.make_async_copy(gate_ref.at[s, mine, :], gates.at[at, :], in_sem.at[2, s]),
        )

    weight_copies = [
        pltpu.make_async_copy(
            w_refs[(r & 1) + 2 * (r >> 2)].at[(r >> 1) & 1], ws.at[:, pl.ds(pl.multiple_of((dp ^ r) * piece, 16), piece), :], w_sem.at[r]
        )
        for r in range(shards)
    ]
    for s in range(sources):
        for copy in row_copies(s):
            copy.start()
        if s == 1:
            for copy in weight_copies:
                copy.start()
    for copy in weight_copies:
        copy.wait()
    chunk = 2 * slots

    def out_copies(c):
        at = pl.ds(pl.multiple_of(c * chunk, 32), chunk)
        return [
            pltpu.make_async_copy(src.at[at, :], dst.at[at, :], out_sem.at[i, c])
            for i, (src, dst) in enumerate(((ys, y_out), (dxs, dx_out), (dgs, dg_out)))
        ]

    def forward_chunk(c, carry):
        for copy in row_copies(2 * c) + row_copies(2 * c + 1):
            copy.wait()
        rows = pl.ds(pl.multiple_of(c * chunk, 32), chunk)
        x = xs[rows, :]
        a = dot_nn(x, ws[0])
        b = dot_nn(x, ws[1])
        pulled = dot_nn(gs[rows, :], ws[2])
        gate = gates[rows, 0:1]
        sig = jax.nn.sigmoid(a)
        silu = a * sig
        act = silu * b
        dgs[rows, :] = jnp.broadcast_to(jnp.sum(act * pulled, 1, keepdims=True), (chunk, 128))
        weighted = (gate * act).astype(BF)
        actg[rows, :] = weighted
        dact = gate * pulled
        da = (dact * b * sig * (1.0 + a * (1.0 - sig))).astype(BF)
        db = (dact * silu).astype(BF)
        dab[rows, 0:hidden] = da
        dab[rows, hidden:] = db
        ys[rows, :] = dot_nt(weighted, ws[2]).astype(BF)
        dxs[rows, :] = (dot_nt(da, ws[0]) + dot_nt(db, ws[1])).astype(BF)
        for copy in out_copies(c):
            copy.start()
        return carry

    lax.fori_loop(0, sources // 2, forward_chunk, 0)
    block = 384
    inner = block // piece
    high = dp // inner
    low = dp % inner

    def grad_copies(jr):
        slot = lax.rem(jr, 2)
        copies = []
        for ri in range(inner):
            dst = (send_out if ri % 2 else keep_out).at[jr * (inner // 2) + ri // 2]
            src = stage.at[slot, :, pl.ds(pl.multiple_of((low ^ ri) * piece, 16), piece), :]
            copies.append(pltpu.make_async_copy(src, dst, grad_sem.at[slot, ri]))
        return copies

    def grad_block(jr, carry):
        slot = lax.rem(jr, 2)

        @pl.when(jr >= 2)
        def _():
            for copy in grad_copies(jr - 2):
                copy.wait()

        cols = pl.ds(pl.multiple_of((high ^ jr) * block, 128), block)
        left = dot_tn(xs[:, cols], dab[...])
        stage[slot, 0] = left[:, 0:hidden].astype(BF)
        stage[slot, 1] = left[:, hidden:].astype(BF)
        stage[slot, 2] = dot_tn(gs[:, cols], actg[...]).astype(BF)
        for copy in grad_copies(jr):
            copy.start()
        return carry

    blocks = width // block
    lax.fori_loop(0, blocks, grad_block, 0)
    for jr in range(blocks - 2, blocks):
        for copy in grad_copies(jr):
            copy.wait()
    for c in range(sources // 2):
        for copy in out_copies(c):
            copy.wait()


def run_expert(k, dp_index, xs, gs, gates, weights, slots):
    sources, shards = xs.shape[0], 2 * len(weights)
    rows = sources * slots
    width = xs.shape[2]
    piece, hidden = weights[0].shape[2:]
    inner = 384 // piece
    anywhere = pl.BlockSpec(memory_space=pl.ANY)
    return pl.pallas_call(
        functools.partial(expert_kernel, k, shards, slots),
        in_specs=[pl.BlockSpec(memory_space=pltpu.SMEM)] + [anywhere] * (3 + shards // 2),
        out_specs=[anywhere] * 5,
        out_shape=[
            jax.ShapeDtypeStruct((rows, width), BF),
            jax.ShapeDtypeStruct((rows, width), BF),
            jax.ShapeDtypeStruct((rows, 128), F32),
            jax.ShapeDtypeStruct((shards // 2, 3, piece, hidden), BF),
            jax.ShapeDtypeStruct((shards // 2, 3, piece, hidden), BF),
        ],
        scratch_shapes=[
            pltpu.VMEM((rows, width), BF),
            pltpu.VMEM((rows, width), BF),
            pltpu.VMEM((rows, 128), F32),
            pltpu.VMEM((3, width, hidden), BF),
            pltpu.VMEM((rows, width), BF),
            pltpu.VMEM((rows, width), BF),
            pltpu.VMEM((rows, 128), F32),
            pltpu.VMEM((rows, 2 * hidden), BF),
            pltpu.VMEM((rows, hidden), BF),
            pltpu.VMEM((2, 3, 384, hidden), BF),
            pltpu.SemaphoreType.DMA((3, sources)),
            pltpu.SemaphoreType.DMA((shards,)),
            pltpu.SemaphoreType.DMA((3, sources // 2)),
            pltpu.SemaphoreType.DMA((2, inner)),
        ],
        compiler_params=pltpu.CompilerParams(vmem_limit_bytes=60 * 2**20),
        cost_estimate=pl.CostEstimate(flops=10**6, bytes_accessed=10**6, transcendentals=0),
        name="expert",
    )(dp_index, xs, gs, gates, *weights)


def combine_kernel(count, slots, pos_ref, *refs):
    y_refs = refs[0:count]
    keep, send, ys, pick = refs[count:]
    tokens = pos_ref.shape[2]
    half = keep.shape[2] // 2
    slot_id = lax.broadcasted_iota(jnp.int32, (slots, tokens), 0)
    for j, out in enumerate((keep, send)):
        for k in range(count):
            rows = slice(k * slots, (k + 1) * slots)
            ys[rows, :] = y_refs[k][j * slots:(j + 1) * slots, :]
            pick[rows, :] = jnp.where(slot_id == pos_ref[j, k:k + 1, :], 1.0, 0.0).astype(BF)
        out[0, :, 0:half] = dot_tn(pick[...], ys[:, 0:half]).astype(BF)
        out[0, :, half:] = dot_tn(pick[...], ys[:, half:]).astype(BF)


def combine_rows(positions, results, slots):
    sources, _, tokens = positions.shape
    count = len(results)
    width = results[0].shape[1]
    out = pl.BlockSpec((1, tokens, width), lambda i: (i, 0, 0))
    return pl.pallas_call(
        functools.partial(combine_kernel, count, slots),
        grid=(sources // 2,),
        in_specs=[pl.BlockSpec((2, 8, tokens), lambda i: (i, 0, 0))]
        + [pl.BlockSpec((2 * slots, width), lambda i: (i, 0))] * count,
        out_specs=[out] * 2,
        out_shape=[jax.ShapeDtypeStruct((sources // 2, tokens, width), BF)] * 2,
        scratch_shapes=[pltpu.VMEM((count * slots, width), BF), pltpu.VMEM((count * slots, tokens), BF)],
        cost_estimate=pl.CostEstimate(flops=10**6, bytes_accessed=10**6, transcendentals=0),
        name="combine_rows",
    )(positions, *results)


def barrier_with(partners):
    sem = pltpu.get_barrier_semaphore()
    for partner in partners:
        pl.semaphore_signal(sem, inc=1, device_id=partner, device_id_type=pl.DeviceIdType.MESH)
    pl.semaphore_wait(sem, len(partners))


def flipped(axis, mask):
    at = lax.axis_index(axis)
    bit = lax.rem(lax.div(at, mask), 2)
    return {axis: at + mask * (1 - 2 * bit)}


def own_bit(axis, mask):
    return lax.rem(lax.div(lax.axis_index(axis), mask), 2)


CUBE = (("dp", 4), ("dp", 2), ("dp", 1), ("expert", 2), ("expert", 1))
ROTATIONS = ((0, 1, 2, 3), (0, 2, 3, 1), (0, 3, 1, 2))


def part_of(gathered, bits, cols):
    index = tuple(pl.ds(0, 2) if dim in gathered else pl.ds(bits[dim], 1) for dim in range(5))
    return index + (slice(None), cols)


def gather_all_kernel(pieces, shard_ref, give_ref, full_ref, take_ref, own_sem, send_sem, recv_sem, piece_sem):
    barrier_with([flipped(*dim) for dim in CUBE])
    bits = [own_bit(*dim) for dim in CUBE]
    width = full_ref.shape[6] // 3
    cols = [pl.ds(c * width, width) for c in range(3)]
    here = tuple(pl.ds(bit, 1) for bit in bits)
    own = pltpu.make_async_copy(shard_ref, full_ref.at[here], own_sem)
    own.start()
    own.wait()

    def spread(step, c, gathered, dim, cols):
        at = part_of(gathered, bits, cols)
        return pltpu.make_async_remote_copy(
            src_ref=full_ref.at[at], dst_ref=full_ref.at[at], send_sem=send_sem.at[step, c],
            recv_sem=recv_sem.at[step, c], device_id=flipped(*CUBE[dim]), device_id_type=pl.DeviceIdType.MESH,
        )

    def hand(k):
        return pltpu.make_async_remote_copy(
            src_ref=give_ref.at[k], dst_ref=take_ref.at[k], send_sem=piece_sem.at[0, k],
            recv_sem=piece_sem.at[1, k], device_id=flipped("dp", 2), device_id_type=pl.DeviceIdType.MESH,
        )

    copies, passed = [], []
    running = [None] * 3
    for step in range(4):
        for c in range(3):
            if running[c] is not None:
                running[c].wait_recv()
            copy = spread(step, c, ROTATIONS[c][:step], ROTATIONS[c][step], cols[c])
            copy.start()
            copies.append(copy)
            running[c] = copy
        if step < pieces:
            passed.append(hand(step))
            passed[-1].start()
    for c in range(3):
        running[c].wait_recv()
        copy = spread(4, c, (0, 1, 2, 3), 4, cols[c])
        copy.start()
        copies.append(copy)
        running[c] = copy
    for k in range(4, pieces):
        passed.append(hand(k))
        passed[-1].start()
    for c in range(3):
        running[c].wait_recv()
    for copy in copies:
        copy.wait_send()
    for copy in passed:
        copy.wait()


def gather_all(shard, give):
    rows, width = shard.shape
    pieces = give.shape[0]
    anywhere = pl.BlockSpec(memory_space=pl.ANY)
    full, take = pl.pallas_call(
        functools.partial(gather_all_kernel, pieces),
        in_specs=[pl.BlockSpec(memory_space=pltpu.VMEM), anywhere],
        out_specs=[anywhere, anywhere],
        out_shape=[
            jax.ShapeDtypeStruct((2,) * 5 + (rows, width), BF),
            jax.ShapeDtypeStruct(give.shape, BF),
        ],
        scratch_shapes=[
            pltpu.SemaphoreType.DMA,
            pltpu.SemaphoreType.DMA((5, 3)),
            pltpu.SemaphoreType.DMA((5, 3)),
            pltpu.SemaphoreType.DMA((2, pieces)),
        ],
        compiler_params=pltpu.CompilerParams(collective_id=1, has_side_effects=True),
        name="gather_all",
    )(shard.reshape((1,) * 5 + (rows, width)), give)
    return full.reshape(32 * rows, width), take


TEAM = (("dp", 2), ("expert", 2), ("expert", 1))


def job_copies(jobs, gives, takes, sems):
    return [
        pltpu.make_async_remote_copy(
            src_ref=gives[j], dst_ref=takes[j], send_sem=sems.at[0, j], recv_sem=sems.at[1, j],
            device_id=flipped(*jobs[j]), device_id_type=pl.DeviceIdType.MESH,
        )
        for j in range(len(jobs))
    ]


def partners_of(dims, jobs):
    return [flipped(*dim) for dim in dict.fromkeys(tuple(dims) + tuple(jobs))]


def team_rows_kernel(jobs, rows_ref, gates_ref, *refs):
    count = len(jobs)
    gives, takes = refs[0:count], refs[count + 2:2 * count + 2]
    all_ref, table_ref = refs[count:count + 2]
    own_sem, send_sem, recv_sem, job_sem = refs[2 * count + 2:]
    barrier_with(partners_of(TEAM, jobs))
    half = all_ref.shape[4] // 2
    own = [
        pltpu.make_async_copy(rows_ref, all_ref.at[0:1, 0:1, 0:1], own_sem.at[0]),
        pltpu.make_async_copy(gates_ref, table_ref.at[0:1, 0:1, 0:1], own_sem.at[1]),
    ]
    for copy in own:
        copy.start()
    for copy in own:
        copy.wait()
    flows = (
        (all_ref, (0, 1, 2), (slice(None), pl.ds(0, half))),
        (all_ref, (1, 0, 2), (slice(None), pl.ds(half, half))),
        (table_ref, (0, 1, 2), (slice(None), slice(None))),
    )
    copies = []
    running = [None] * 3
    for step in range(3):
        for f, (ref, order, tail) in enumerate(flows):
            if running[f] is not None:
                running[f].wait_recv()
            dim = order[step]
            index = [pl.ds(0, 2) if d in order[:step] else pl.ds(0, 1) for d in range(3)]
            src = ref.at[tuple(index) + tail]
            index[dim] = pl.ds(1, 1)
            copy = pltpu.make_async_remote_copy(
                src_ref=src, dst_ref=ref.at[tuple(index) + tail], send_sem=send_sem.at[step, f],
                recv_sem=recv_sem.at[step, f], device_id=flipped(*TEAM[dim]), device_id_type=pl.DeviceIdType.MESH,
            )
            copy.start()
            copies.append(copy)
            running[f] = copy
        if step == 0:
            background = job_copies(jobs, gives, takes, job_sem)
            for copy in background:
                copy.start()
    for copy in running:
        copy.wait_recv()
    for copy in copies:
        copy.wait_send()
    for copy in background:
        copy.wait()


def team_rows(rows, gates, jobs=(), gives=()):
    tokens, width = rows.shape
    table = gates.shape
    anywhere = pl.BlockSpec(memory_space=pl.ANY)
    full, tables, *takes = pl.pallas_call(
        functools.partial(team_rows_kernel, tuple(jobs)),
        in_specs=[pl.BlockSpec(memory_space=pltpu.VMEM)] * 2 + [anywhere] * len(jobs),
        out_specs=[anywhere] * (2 + len(jobs)),
        out_shape=[
            jax.ShapeDtypeStruct((2, 2, 2, tokens, width), BF),
            jax.ShapeDtypeStruct((2, 2, 2) + table, F32),
        ] + [jax.ShapeDtypeStruct(give.shape, give.dtype) for give in gives],
        scratch_shapes=[
            pltpu.SemaphoreType.DMA((2,)),
            pltpu.SemaphoreType.DMA((3, 3)),
            pltpu.SemaphoreType.DMA((3, 3)),
            pltpu.SemaphoreType.DMA((2, max(1, len(jobs)))),
        ],
        compiler_params=pltpu.CompilerParams(collective_id=2, has_side_effects=True),
        name="team_rows",
    )(rows.reshape(1, 1, 1, tokens, width), gates.reshape((1, 1, 1) + table), *gives)
    return full.reshape(8, tokens, width), tables.reshape((8,) + table), takes


def add_into(acc, at, other):
    acc[at] = (acc[at].astype(F32) + other.astype(F32)).astype(BF)


def return_kernel(count, slots, early, late, pos_ref, *refs):
    jobs = early + late
    y_refs, dg_refs = refs[0:count], refs[count:2 * count]
    refs = refs[2 * count:]
    gives, takes = refs[0:len(jobs)], refs[len(jobs) + 2:2 * len(jobs) + 2]
    out_ref, gate_ref = refs[len(jobs):len(jobs) + 2]
    (acc, core_in, row_in, pair_in, last_in, ys, pick, table, table_core, table_row, table_pair,
     load_sem, send_sem, recv_sem, job_sem) = refs[2 * len(jobs) + 2:]
    tokens, width = out_ref.shape
    half = width // 2
    barrier_with(partners_of(TEAM, jobs))
    background = job_copies(jobs, gives, takes, job_sem)
    for copy in background[:len(early)]:
        copy.start()
    first = (lax.axis_index("expert") * 2 + own_bit("dp", 2)) * count
    slot_id = lax.broadcasted_iota(jnp.int32, (slots, tokens), 0)

    def remote(src, dst, n, dim):
        return pltpu.make_async_remote_copy(
            src_ref=src, dst_ref=dst, send_sem=send_sem.at[n], recv_sem=recv_sem.at[n],
            device_id=flipped(*TEAM[dim]), device_id_type=pl.DeviceIdType.MESH,
        )

    def loads(r, slot):
        return [
            pltpu.make_async_copy(
                y_refs[k].at[pl.ds(pl.multiple_of(r * slots, 16), slots), :],
                ys.at[slot, pl.ds(k * slots, slots), :], load_sem.at[slot, k],
            )
            for k in range(count)
        ]

    table[...] = jnp.zeros_like(table)

    def build(step, r, following):
        slot = lax.rem(step, 2)
        for copy in loads(r, slot):
            copy.wait()

        @pl.when(step < 7)
        def _():
            for copy in loads(following, 1 - slot):
                copy.start()

        for k in range(count):
            hit = slot_id == pos_ref[r, k:k + 1, :]
            pick[k * slots:(k + 1) * slots, :] = jnp.where(hit, 1.0, 0.0).astype(BF)
            pulled = dg_refs[k][pl.ds(pl.multiple_of(r * slots, 16), slots), 0:1]
            table[r, pl.ds(first + k, 1), :] = jnp.sum(jnp.where(hit, pulled, 0.0), 0, keepdims=True)
        acc[r, :, 0:half] = dot_tn(pick[...], ys[slot, :, 0:half]).astype(BF)
        acc[r, :, half:] = dot_tn(pick[...], ys[slot, :, half:]).astype(BF)

    for copy in loads(1, 0):
        copy.start()

    def odd(i, carry):
        r = 2 * i + 1
        build(i, r, jnp.where(i < 3, r + 2, 0))
        remote(acc.at[r], core_in.at[i], i, 2).start()
        return carry

    def even(i, carry):
        build(i + 4, 2 * i, 2 * i + 2)
        return carry

    lax.fori_loop(0, 4, odd, 0)
    tables = [remote(table.at[2 * i + 1], table_core.at[i], 4 + i, 2) for i in range(4)]
    for copy in tables:
        copy.start()
    lax.fori_loop(0, 4, even, 0)

    def settle(i):
        remote(acc.at[2 * i + 1], core_in.at[i], i, 2).wait()
        add_into(acc, 2 * i, core_in[i])

    left, right = slice(0, half), slice(half, width)
    settle(3)
    a = [remote(acc.at[6, :, pl.ds(0, half)], row_in.at[1], 8, 1), remote(acc.at[6, :, pl.ds(half, half)], pair_in.at[1], 9, 0)]
    for copy in a:
        copy.start()
    settle(1)
    a.append(remote(acc.at[2, :, pl.ds(0, half)], row_in.at[0], 10, 1))
    a[-1].start()
    settle(2)
    a.append(remote(acc.at[4, :, pl.ds(half, half)], pair_in.at[0], 11, 0))
    a[-1].start()
    for i, copy in enumerate(tables):
        copy.wait()
        table[2 * i] = table[2 * i] + table_core[i]
    t = [remote(table.at[2], table_row.at[0], 12, 1), remote(table.at[6], table_row.at[1], 13, 1)]
    for copy in t:
        copy.start()
    settle(0)
    a[0].wait()
    add_into(acc, (4, slice(None), left), row_in[1])
    b = [remote(acc.at[4, :, pl.ds(0, half)], last_in.at[0], 14, 0)]
    b[0].start()
    a[1].wait()
    add_into(acc, (2, slice(None), right), pair_in[1])
    b.append(remote(acc.at[2, :, pl.ds(half, half)], last_in.at[1], 15, 1))
    b[1].start()
    for copy in background[len(early):]:
        copy.start()
    for i, copy in enumerate(t):
        copy.wait()
        table[4 * i] = table[4 * i] + table_row[i]
    t = remote(table.at[4], table_pair, 16, 0)
    t.start()
    a[2].wait()
    add_into(acc, (0, slice(None), left), row_in[0])
    a[3].wait()
    add_into(acc, (0, slice(None), right), pair_in[0])
    b[0].wait()
    out_ref[:, left] = (acc[0, :, left].astype(F32) + last_in[0].astype(F32)).astype(BF)
    b[1].wait()
    out_ref[:, right] = (acc[0, :, right].astype(F32) + last_in[1].astype(F32)).astype(BF)
    t.wait()
    gate_ref[...] = table[0] + table_pair[...]
    for copy in background:
        copy.wait()


def return_rows(positions, results, gate_rows, experts, slots, early=(), late=(), gives=()):
    sources, _, tokens = positions.shape
    count = len(results)
    width = results[0].shape[1]
    half = width // 2
    vmem, anywhere = pl.BlockSpec(memory_space=pltpu.VMEM), pl.BlockSpec(memory_space=pl.ANY)
    jobs = tuple(early) + tuple(late)
    rows, gates, *takes = pl.pallas_call(
        functools.partial(return_kernel, count, slots, tuple(early), tuple(late)),
        in_specs=[vmem] + [anywhere] * count + [vmem] * count + [anywhere] * len(jobs),
        out_specs=[vmem, vmem] + [anywhere] * len(jobs),
        out_shape=[jax.ShapeDtypeStruct((tokens, width), BF), jax.ShapeDtypeStruct((experts, tokens), F32)]
        + [jax.ShapeDtypeStruct(give.shape, give.dtype) for give in gives],
        scratch_shapes=[
            pltpu.VMEM((8, tokens, width), BF),
            pltpu.VMEM((4, tokens, width), BF),
            pltpu.VMEM((2, tokens, half), BF),
            pltpu.VMEM((2, tokens, half), BF),
            pltpu.VMEM((2, tokens, half), BF),
            pltpu.VMEM((2, count * slots, width), BF),
            pltpu.VMEM((count * slots, tokens), BF),
            pltpu.VMEM((8, experts, tokens), F32),
            pltpu.VMEM((4, experts, tokens), F32),
            pltpu.VMEM((2, experts, tokens), F32),
            pltpu.VMEM((experts, tokens), F32),
            pltpu.SemaphoreType.DMA((2, count)),
            pltpu.SemaphoreType.DMA((17,)),
            pltpu.SemaphoreType.DMA((17,)),
            pltpu.SemaphoreType.DMA((2, max(1, len(jobs)))),
        ],
        compiler_params=pltpu.CompilerParams(collective_id=3, has_side_effects=True, vmem_limit_bytes=60 * 2**20),
        name="return_rows",
    )(positions, *results, *gate_rows, *gives)
    return rows, gates, takes


def scatter_all_kernel(grads_ref, out_ref, acc, core_in, in_1, in_2, in_3, in_4, load_sem, send_sem, recv_sem):
    barrier_with([flipped(*dim) for dim in CUBE])
    bits = [own_bit(*dim) for dim in CUBE]
    width = out_ref.shape[1] // 3
    inboxes = (in_1, in_2, in_3, in_4)

    def remote(src, dst, n, dim):
        return pltpu.make_async_remote_copy(
            src_ref=src, dst_ref=dst, send_sem=send_sem.at[n], recv_sem=recv_sem.at[n],
            device_id=flipped(*CUBE[dim]), device_id_type=pl.DeviceIdType.MESH,
        )

    first = []
    for c in range(3):
        cols = pl.ds(c * width, width)
        at = tuple(pl.ds(0, 2) for _ in range(4)) + (pl.ds(1 - bits[4], 1), slice(None), cols)
        copy = remote(grads_ref.at[at], core_in.at[:, :, :, :, :, :, cols], 12 + c, 4)
        copy.start()
        first.append(copy)
    load = pltpu.make_async_copy(
        grads_ref.at[tuple(pl.ds(0, 2) for _ in range(4)) + (pl.ds(bits[4], 1),)], acc, load_sem
    )
    load.start()
    load.wait()
    sends = [None] * 3
    for step in range(5):
        for c in range(3):
            cols = pl.ds(c * width, width)
            rest = ROTATIONS[c][:4 - step]
            if step == 0:
                first[c].wait()
            else:
                sends[c].wait()
            for n in range(2 ** len(rest)):
                spread = [(n >> (len(rest) - 1 - i)) & 1 for i in range(len(rest))]
                index = [bits[d] if d not in rest else spread[rest.index(d)] for d in range(5)]
                at = tuple(index[:4]) + (0, slice(None), cols)
                if step == 0:
                    other = core_in[index[0], index[1], index[2], index[3], 0, :, cols]
                else:
                    other = inboxes[step - 1][n, :, cols]
                if step < 4:
                    add_into(acc, at, other)
                else:
                    out_ref[:, cols] = acc[at].astype(F32) + other.astype(F32)
            if step < 4:
                dim = rest[-1]
                spread_dims = rest[:-1]
                group = []
                for n in range(2 ** len(spread_dims)):
                    spread = [(n >> (len(spread_dims) - 1 - i)) & 1 for i in range(len(spread_dims))]
                    index = [
                        1 - bits[d] if d == dim else (spread[spread_dims.index(d)] if d in spread_dims else bits[d])
                        for d in range(5)
                    ]
                    base = (0, 24, 36, 42)[step] + c * 2 ** len(spread_dims) + n
                    copy = remote(
                        acc.at[tuple(index[:4]) + (0, slice(None), cols)], inboxes[step].at[n, :, cols], 15 + base, dim
                    )
                    copy.start()
                    group.append(copy)
                sends[c] = Group(group)


class Group:
    def __init__(self, copies):
        self.copies = copies

    def wait(self):
        for copy in self.copies:
            copy.wait()


def scatter_all(grads):
    rows, width = grads.shape[0] // 32, grads.shape[1]
    vmem = pl.BlockSpec(memory_space=pltpu.VMEM)
    return pl.pallas_call(
        scatter_all_kernel,
        in_specs=[pl.BlockSpec(memory_space=pl.ANY)],
        out_specs=vmem,
        out_shape=jax.ShapeDtypeStruct((rows, width), F32),
        scratch_shapes=[pltpu.VMEM((2, 2, 2, 2, 1, rows, width), BF)] * 2
        + [pltpu.VMEM((n, rows, width), BF) for n in (8, 4, 2, 1)]
        + [pltpu.SemaphoreType.DMA, pltpu.SemaphoreType.DMA((60,)), pltpu.SemaphoreType.DMA((60,))],
        compiler_params=pltpu.CompilerParams(collective_id=4, has_side_effects=True, vmem_limit_bytes=60 * 2**20),
        name="scatter_all",
    )(grads.reshape((2,) * 5 + (rows, width)))


D = 1536
EPSILON = 1e-06
EVERYWHERE = ("dp", "expert")


def exchange(value, axis, mask):
    return lax.ppermute(value, axis, [(i, i ^ mask) for i in range(lax.axis_size(axis))])


def tie(first, *others):
    return lax.optimization_barrier((first, *others))[0]


def rms_scale(values):
    return lax.rsqrt(jnp.mean(values * values, axis=-1, keepdims=True) + EPSILON)


def product(left, right):
    return jnp.dot(left, right, preferred_element_type=F32)


def contract_rows(left, right):
    return jnp.einsum("ta,tb->ab", left, right, preferred_element_type=F32)


def times_transposed(left, right):
    return jnp.einsum("ta,ba->tb", left, right, preferred_element_type=F32)


def added(left, right):
    return (left.astype(F32) + right.astype(F32)).astype(BF)


def team_gather(value, order):
    pieces = {0: value}
    for axis, mask, bit in order:
        pieces.update({r | bit: exchange(v, axis, mask) for r, v in list(pieces.items())})
    return jnp.stack([pieces[r] for r in sorted(pieces)])


TEAM_BITS = (("dp", 2, 4), ("expert", 2, 2), ("expert", 1, 1))


def group_gather(value):
    for axis, name, mask in ((0, "dp", 1), (1, "expert", 2), (2, "expert", 1)):
        other = exchange(value, name, mask)
        mine = lax.axis_index(name) & mask
        value = jnp.where(
            mine == 0, jnp.concatenate([value, other], axis), jnp.concatenate([other, value], axis)
        )
    return value


def group_scatter(value):
    for axis, name, mask in ((2, "expert", 1), (1, "expert", 2), (0, "dp", 1)):
        mine = jnp.minimum(lax.axis_index(name) & mask, 1)
        kept = lax.dynamic_slice_in_dim(value, mine, 1, axis)
        sent = lax.dynamic_slice_in_dim(value, 1 - mine, 1, axis)
        value = added(kept, exchange(sent, name, mask))
    return value


def local(tokens, attn_gain, w_query, w_key, w_value, w_out, w_router, ffn_gain, w_gate, w_up, w_down, routes, cotangent):
    dp, expert_at = lax.axis_index("dp"), lax.axis_index("expert")
    shards, owners = lax.axis_size("dp"), lax.axis_size("expert")
    cube = shards == 8 and owners == 4
    turn = (dp >> 1) & 1
    tok_rows = tokens.shape[0]
    per_owner, piece, hidden = w_gate.shape
    count = per_owner // 2
    expert_count = per_owner * owners
    top_count = routes.shape[1]
    kvw = w_key.shape[1]
    capacity = 8 * ((17 * top_count * tok_rows + 128 * expert_count - 1) // (128 * expert_count))
    slots = SLOTS_ALIGN * (-(-capacity // SLOTS_ALIGN))
    dp_index = dp.astype(jnp.int32).reshape(1)
    wide = D + 2 * kvw

    stacked = jnp.stack([w_gate, w_up, w_down.transpose(0, 2, 1)], 1)
    own = lax.dynamic_slice_in_dim(stacked, turn * count, count, 0)
    other = lax.dynamic_slice_in_dim(stacked, (1 - turn) * count, count, 0)
    gains = jnp.stack([attn_gain, ffn_gain], 1)
    first_shard = jnp.concatenate([w_query, w_key, w_value, jnp.pad(gains, ((0, 0), (0, 126)))], 1)
    ahead = 2
    if cube:
        first_full, taken = gather_all(first_shard, other[:ahead])
    else:
        first_full = lax.all_gather(first_shard, EVERYWHERE, axis=0, tiled=True)
        taken = exchange(other[:ahead], "dp", 2)
    qkv_full = first_full[:, :wide]
    gains_full = first_full[:, wide:].astype(F32).T
    gain_first, gain_second = gains_full[0], gains_full[1]
    second_shard = jnp.concatenate([w_out, jnp.pad(w_router, ((0, 0), (0, 128 - expert_count)))], 1)
    second_full = lax.all_gather(tie(second_shard, first_full), EVERYWHERE, axis=0, tiled=True)
    out_full = second_full[:, :D]
    router_full = second_full[:, D:D + expert_count]

    relay_bits = [1 << b for b in range(2, shards.bit_length() - 1)]
    taken_late = exchange(tie(other[ahead:], first_full), "dp", 2)
    pairs = [
        jnp.stack([own[k], taken[k] if k < ahead else taken_late[k - ahead]]) for k in range(count)
    ]

    def crossed(relayed):
        return [w for v in relayed for w in (v, exchange(v, "dp", 1))]

    def relays(pair):
        pieces = [pair]
        for bit in relay_bits:
            pieces += [exchange(v, "dp", bit) for v in pieces]
        return pieces

    routes_t = team_gather(routes.T, TEAM_BITS)
    first_expert = expert_at * per_owner + turn * count
    local_ids = first_expert + jnp.arange(count, dtype=jnp.int32)
    hits = jnp.any(routes_t[:, None] == local_ids[None, :, None, None], axis=2)
    row_id = lax.broadcasted_iota(jnp.int32, (tok_rows, tok_rows), 0)
    col_id = lax.broadcasted_iota(jnp.int32, (tok_rows, tok_rows), 1)
    before = jnp.where(row_id < col_id, 1.0, 0.0).astype(BF)
    ranks = product(hits.astype(BF).reshape(-1, tok_rows), before).reshape(hits.shape)
    positions = jnp.where(hits, ranks.astype(jnp.int32), -1)
    positions = jnp.pad(positions, ((0, 0), (0, 8 - count), (0, 0)), constant_values=-1)

    inputs = tokens.astype(F32)
    scale_one = rms_scale(inputs)
    normed_one = inputs * scale_one
    hidden_one = (normed_one * gain_first).astype(BF)
    qkv = product(hidden_one, qkv_full).astype(BF)
    query, key_value = qkv[:, :D], qkv[:, D:]
    place = ((dp & 1) * owners + expert_at).astype(jnp.int32).reshape(1)
    prompt = group_gather(key_value[:P_DEV].reshape(1, 1, 1, P_DEV, 2 * kvw)).reshape(-1, 2 * kvw)
    prompt_key, prompt_value = prompt[:, :kvw], prompt[:, kvw:]
    own_key, own_value = key_value[P_DEV:, :kvw], key_value[P_DEV:, kvw:]
    mixed, levels = attend(place, query, prompt_key, prompt_value, own_key, own_value)
    grad_rows = team_gather(tie(cotangent, first_full), TEAM_BITS)
    second = inputs + product(mixed, out_full)
    scale_two = rms_scale(second)
    normed_two = second * scale_two
    hidden_two = (normed_two * gain_second).astype(BF)
    logits = product(hidden_two, router_full)
    expert_ids = jnp.arange(expert_count, dtype=jnp.int32)
    chosen = jnp.any(routes[:, :, None] == expert_ids, axis=1)
    peak = jnp.max(jnp.where(chosen, logits, NEGATIVE), axis=-1, keepdims=True)
    raised = jnp.where(chosen, jnp.exp(jnp.where(chosen, logits - peak, 0.0)), 0.0)
    gates = raised / jnp.sum(raised, axis=-1, keepdims=True)

    weights = [None] * count
    early = relays(pairs[0])
    weights[0] = crossed(early)
    sent_rows = tie(hidden_two, early)
    if cube:
        jobs = (("dp", 4), ("dp", 4), ("dp", 1), ("dp", 1))
        rows, gates_t, takes = team_rows(
            sent_rows, gates.T, jobs, (pairs[1], pairs[2], pairs[1], pairs[2])
        )
        weights[1] = [pairs[1], takes[2], takes[0], exchange(takes[0], "dp", 1)]
        weights[2] = [pairs[2], takes[3], takes[1], exchange(takes[1], "dp", 1)]
        rest = (3, 4)
    else:
        rows, gates_t, _ = team_rows(sent_rows, gates.T)
        rest = (1, 2, 3, 4)
    for k in rest:
        weights[k] = crossed(relays(tie(pairs[k], rows)))
    gates_t = lax.dynamic_slice_in_dim(gates_t, first_expert, count, 1)
    gates_t = jnp.pad(gates_t, ((0, 0), (0, 8 - count), (0, 0)))
    grad_slots, = gather_rows(positions, None, tie(grad_rows, rows), count, slots)
    row_slots, gate_slots = gather_rows(positions, gates_t, rows, count, slots)

    results, backs, gate_rows, sums = [], [], [], []
    expert_index = dp_index
    for k in range(count):
        y, dx, dg, keep, send = run_expert(k, expert_index, row_slots, grad_slots, gate_slots, weights[k], slots)
        results.append(y)
        backs.append(dx)
        gate_rows.append(dg)
        sums.append((keep, exchange(send, "dp", 1)))
        expert_index = tie(dp_index, dx, [s[1] for s in sums[:max(0, k - 1)]])

    def relay(k, keep):
        for bit in reversed(relay_bits):
            middle = keep.shape[0] // 2
            keep = added(keep[:middle], exchange(keep[middle:], "dp", bit))
        return keep

    halved = [added(*sums[k]) for k in range(2)]
    if cube:
        routed_back, gate_grad, takes = return_rows(
            positions, backs, gate_rows, expert_count, slots,
            (("dp", 4),), (("dp", 4),), (halved[0][2:], halved[1][2:]),
        )
        relayed = [added(halved[k][:2], takes[k]) for k in range(2)]
    else:
        routed_back, gate_grad, _ = return_rows(positions, backs, gate_rows, expert_count, slots)
        relayed = [relay(k, halved[k]) for k in range(2)]
    for k in range(2, count):
        kept, came = lax.optimization_barrier((sums[k], routed_back))[0]
        relayed.append(relay(k, added(kept, came)))
    gate_grad = gate_grad.T
    routed_back = routed_back.astype(F32)

    grad_output = cotangent.astype(F32)
    picked = jnp.where(chosen, gate_grad, 0.0)
    grad_logits = (gates * (picked - jnp.sum(gates * picked, axis=-1, keepdims=True))).astype(BF)
    grad_hidden_two = times_transposed(grad_logits, router_full) + routed_back
    grad_normed_two = grad_hidden_two * gain_second
    grad_second = grad_output + scale_two * (
        grad_normed_two - normed_two * jnp.mean(grad_normed_two * normed_two, axis=-1, keepdims=True)
    )
    grad_branch = grad_second.astype(BF)
    ones = jnp.ones((tok_rows, 128), BF)
    lane = lax.broadcasted_iota(jnp.int32, (tok_rows, 128), 1)
    wide_logits = jnp.pad(grad_logits, ((0, 0), (0, 128 - expert_count)))
    small = contract_rows(hidden_two, wide_logits) + contract_rows(
        (grad_hidden_two * normed_two).astype(BF), jnp.where(lane == expert_count, ones, jnp.zeros_like(ones))
    )
    second_grads = jnp.concatenate([contract_rows(mixed, grad_branch).astype(BF), small.astype(BF)], 1)
    second_share = lax.psum_scatter(second_grads, EVERYWHERE, scatter_dimension=0, tiled=True).astype(F32)
    grad_mixed = times_transposed(grad_branch, out_full).astype(BF)

    out_keep, out_send = combine_rows(tie(positions, grad_mixed), results, slots)
    total = added(out_keep, exchange(out_send, "expert", 1)).reshape(2, 2, tok_rows, D)
    total = added(total[:, 0], exchange(total[:, 1], "expert", 2))
    total = added(total[0], exchange(total[1], "dp", 2))
    output = (second + total.astype(F32)).astype(BF)

    grad_mixed = tie(grad_mixed, [sums[k][1] for k in range(2, count)], out_keep)
    grad_query, dkp, dvp, dko, dvo = attend_back(
        place, query, prompt_key, prompt_value, own_key, own_value, mixed, grad_mixed, levels
    )
    grad_prompt = jnp.concatenate([dkp, dvp], 1).reshape(2, 2, 2, P_DEV, 2 * kvw)
    grad_prompt = group_scatter(grad_prompt).reshape(P_DEV, 2 * kvw)
    grad_qkv = jnp.concatenate([
        grad_query, jnp.concatenate([grad_prompt, jnp.concatenate([dko, dvo], 1)], 0)
    ], 1)
    grad_hidden_one = times_transposed(grad_qkv, qkv_full)
    first_grads = jnp.concatenate([
        contract_rows(hidden_one, grad_qkv).astype(BF),
        contract_rows((grad_hidden_one * normed_one).astype(BF), ones).astype(BF),
    ], 1)
    if cube:
        first_share = scatter_all(first_grads)
    else:
        first_share = lax.psum_scatter(first_grads, EVERYWHERE, scatter_dimension=0, tiled=True).astype(F32)
    grad_normed_one = grad_hidden_one * gain_first
    grad_input = grad_second + scale_one * (
        grad_normed_one - normed_one * jnp.mean(grad_normed_one * normed_one, axis=-1, keepdims=True)
    )

    mine = jnp.stack([keep[0] for keep in relayed])
    theirs = exchange(jnp.stack([keep[1] for keep in relayed]), "dp", 2)
    lower = jnp.where(turn == 0, mine, theirs)
    upper = jnp.where(turn == 0, theirs, mine)
    expert_grads = jnp.concatenate([lower, upper]).astype(F32)
    return (
        output,
        grad_input.astype(BF),
        first_share[:, wide],
        first_share[:, :D],
        first_share[:, D:D + kvw],
        first_share[:, D + kvw:wide],
        second_share[:, :D],
        second_share[:, D:D + expert_count],
        second_share[:, D + expert_count],
        expert_grads[:, 0],
        expert_grads[:, 1],
        expert_grads[:, 2].transpose(0, 2, 1),
    )


def solution(mesh):
    rows, line = P(("dp", "expert"), None), P(("dp", "expert"))
    gate, down = P("expert", "dp", None), P("expert", None, "dp")
    return jax.shard_map(
        local,
        mesh=mesh,
        in_specs=(rows, line, rows, rows, rows, rows, rows, line, gate, gate, down, rows, rows),
        out_specs=(rows, rows, line, rows, rows, rows, rows, rows, line, gate, gate, down),
        check_vma=False,
    )
```

```python
import functools
import jax
import jax.numpy as jnp
from jax import lax
from jax.sharding import PartitionSpec as P
from jax.experimental import pallas as pl
from jax.experimental.pallas import tpu as pltpu

HD = 64
P_DEV = 128
NEGATIVE = -1e30
F32 = jnp.float32
BF = jnp.bfloat16


def dot_nt(a, b):
    return lax.dot_general(a, b, (((1,), (1,)), ((), ())), preferred_element_type=F32)


def dot_nn(a, b):
    return lax.dot_general(a, b, (((1,), (0,)), ((), ())), preferred_element_type=F32)


def dot_tn(a, b):
    return lax.dot_general(a, b, (((0,), (0,)), ((), ())), preferred_element_type=F32)


def halves(pair):
    lane = lax.broadcasted_iota(jnp.int32, pair.shape, 1)
    zero = jnp.zeros_like(pair)
    return jnp.where(lane < HD, pair, zero), jnp.where(lane < HD, zero, pair)


def placed_halves(pair_f32):
    low0, high1 = halves(pair_f32)
    high0 = pltpu.roll(low0, HD, 1)
    low1 = pltpu.roll(high1, HD, 1)
    return ((low0.astype(BF), high0.astype(BF)), (low1.astype(BF), high1.astype(BF)))


def attend_kernel(place_ref, q_ref, kp_ref, vp_ref, ko_ref, vo_ref, o_ref, lse_ref, kpad, vpad, s_scr, p_scr):
    rows = q_ref.shape[0]
    prompt = kp_ref.shape[0]
    cont = ko_ref.shape[0]
    place = place_ref[0]
    for src, dst in ((kp_ref, kpad), (vp_ref, vpad)):
        for head, pair in enumerate(placed_halves(src[...].astype(F32))):
            for half in range(2):
                dst[head, half, 0:prompt, :] = pair[half]
    for src, dst in ((ko_ref, kpad), (vo_ref, vpad)):
        for head, pair in enumerate(placed_halves(src[...].astype(F32))):
            for half in range(2):
                dst[head, half, prompt:prompt + cont, :] = pair[half]
    key_id = lax.broadcasted_iota(jnp.int32, (prompt, P_DEV), 0)
    row_id = lax.broadcasted_iota(jnp.int32, (prompt, P_DEV), 1)
    seen_prompt = key_id <= place * P_DEV + row_id
    diag = lax.broadcasted_iota(jnp.int32, (P_DEV, P_DEV), 0) <= lax.broadcasted_iota(jnp.int32, (P_DEV, P_DEV), 1)
    blocks = cont // P_DEV
    stats = []
    for chunk in range(3):
        queries = (q_ref[:, chunk * 128:(chunk + 1) * 128].astype(F32) * HD ** (-0.5)).astype(BF)
        total = None
        for half in range(2):
            position = chunk * 2 + half
            head = position // 3
            keys = kpad.at[head, half]
            scores = dot_nt(keys[0:prompt, :], queries)
            first = jnp.where(seen_prompt, scores[:, 0:P_DEV], NEGATIVE)
            rest = scores[:, P_DEV:]
            s_scr[0:prompt, 0:P_DEV] = first
            s_scr[0:prompt, P_DEV:] = rest
            top = jnp.concatenate([jnp.max(first, 0, keepdims=True), jnp.max(rest, 0, keepdims=True)], 1)
            tops = [top[:, i * P_DEV:(i + 1) * P_DEV] for i in range(1 + blocks)]
            for block in range(blocks):
                start = (1 + block) * P_DEV
                at = prompt + block * P_DEV
                own = dot_nt(keys[at:at + P_DEV, :], queries[start:, :])
                edge = jnp.where(diag, own[:, 0:P_DEV], NEGATIVE)
                s_scr[at:at + P_DEV, start:start + P_DEV] = edge
                tops[1 + block] = jnp.maximum(tops[1 + block], jnp.max(edge, 0, keepdims=True))
                if block + 1 < blocks:
                    later = own[:, P_DEV:]
                    s_scr[at:at + P_DEV, start + P_DEV:] = later
                    best = jnp.max(later, 0, keepdims=True)
                    for i in range(block + 1, blocks):
                        at_i = (i - block - 1) * P_DEV
                        tops[1 + i] = jnp.maximum(tops[1 + i], best[:, at_i:at_i + P_DEV])
            top = jnp.concatenate(tops, 1)
            weights = jnp.exp(s_scr[0:prompt, :] - top)
            mass = jnp.sum(weights, 0, keepdims=True)
            masses = [mass[:, i * P_DEV:(i + 1) * P_DEV] for i in range(1 + blocks)]
            values = vpad.at[head, half]
            mixed = dot_tn(values[0:prompt, :], weights.astype(BF))
            for block in range(blocks):
                start = (1 + block) * P_DEV
                at = prompt + block * P_DEV
                part = jnp.exp(s_scr[at:at + P_DEV, start:] - top[:, start:])
                p_scr[block * P_DEV:(block + 1) * P_DEV, start:] = part.astype(BF)
                if block:
                    p_scr[block * P_DEV:(block + 1) * P_DEV, P_DEV:start] = jnp.zeros((P_DEV, block * P_DEV), BF)
                part_mass = jnp.sum(part, 0, keepdims=True)
                for i in range(block, blocks):
                    at_i = (i - block) * P_DEV
                    masses[1 + i] = masses[1 + i] + part_mass[:, at_i:at_i + P_DEV]
            own_mixed = dot_tn(values[prompt:prompt + cont, :], p_scr[:, P_DEV:])
            mass = jnp.concatenate(masses, 1)
            scale = 1.0 / mass
            mixed = jnp.concatenate([mixed[:, 0:P_DEV], mixed[:, P_DEV:] + own_mixed], 1) * scale
            total = mixed if total is None else total + mixed
            stats.append(top + jnp.log(mass))
        o_ref[:, chunk * 128:(chunk + 1) * 128] = jnp.transpose(total).astype(BF)
    lse_ref[0] = jnp.concatenate(stats + [jnp.zeros((2, rows), F32)], 0)


def attend(place, query, prompt_key, prompt_value, own_key, own_value):
    rows = query.shape[0]
    prompt = prompt_key.shape[0]
    cont = own_key.shape[0]
    pairs = prompt_key.shape[1] // 128
    col = lambda i: (0, i)
    return pl.pallas_call(
        attend_kernel,
        grid=(pairs,),
        in_specs=[
            pl.BlockSpec(memory_space=pltpu.SMEM),
            pl.BlockSpec((rows, 384), col),
            pl.BlockSpec((prompt, 128), col),
            pl.BlockSpec((prompt, 128), col),
            pl.BlockSpec((cont, 128), col),
            pl.BlockSpec((cont, 128), col),
        ],
        out_specs=[pl.BlockSpec((rows, 384), col), pl.BlockSpec((1, 8, rows), lambda i: (i, 0, 0))],
        out_shape=[
            jax.ShapeDtypeStruct(query.shape, BF),
            jax.ShapeDtypeStruct((pairs, 8, rows), F32),
        ],
        scratch_shapes=[
            pltpu.VMEM((2, 2, prompt + cont, 128), BF),
            pltpu.VMEM((2, 2, prompt + cont, 128), BF),
            pltpu.VMEM((prompt + cont, rows), F32),
            pltpu.VMEM((cont, rows), BF),
        ],
        cost_estimate=pl.CostEstimate(flops=10**6, bytes_accessed=10**6, transcendentals=0),
        name="attend",
    )(place, query, prompt_key, prompt_value, own_key, own_value)


def attend_back_kernel(place_ref, q_ref, kp_ref, vp_ref, ko_ref, vo_ref, o_ref, do_ref, lse_ref,
                       dq_ref, dkp_ref, dvp_ref, dko_ref, dvo_ref, kpad, vpad, dk_acc, dv_acc):
    rows = q_ref.shape[0]
    prompt = kp_ref.shape[0]
    cont = ko_ref.shape[0]
    step = 2 * P_DEV
    place = place_ref[0]
    for src, dst, at, size in ((kp_ref, kpad, 0, prompt), (vp_ref, vpad, 0, prompt),
                               (ko_ref, kpad, prompt, cont), (vo_ref, vpad, prompt, cont)):
        for head, pair in enumerate(placed_halves(src[...].astype(F32))):
            for half in range(2):
                dst[head, half, at:at + size, :] = pair[half]
    dk_acc[...] = jnp.zeros_like(dk_acc)
    dv_acc[...] = jnp.zeros_like(dv_acc)
    for chunk in range(3):
        lanes = slice(chunk * 128, (chunk + 1) * 128)
        scaled = q_ref[:, lanes].astype(F32) * HD ** (-0.5)
        queries = scaled.astype(BF)
        query_halves = [part.astype(BF) for part in halves(scaled)]
        outs = o_ref[:, lanes].astype(F32)
        grads_f32 = do_ref[:, lanes].astype(F32)
        grads = do_ref[:, lanes]
        grad_halves = [part.astype(BF) for part in halves(grads_f32)]
        inner = jnp.transpose(outs * grads_f32)
        total = jnp.zeros((128, rows), F32)
        for half in range(2):
            position = chunk * 2 + half
            head = position // 3
            level = lse_ref[0, position:position + 1, :]
            delta = jnp.sum(inner[half * HD:(half + 1) * HD, :], 0, keepdims=True)

            def block(at, cols, mask, queries=queries, grads=grads, query_half=query_halves[half],
                      grad_half=grad_halves[half], level=level, delta=delta, head=head, half=half):
                keys = kpad[head, half, pl.ds(at, step), :]
                values = vpad[head, half, pl.ds(at, step), :]
                scores = dot_nt(keys, queries[cols, :])
                weights = jnp.exp(mask(scores) - level[:, cols])
                grad_weights = dot_nt(values, grads[cols, :])
                grad_scores = weights * (grad_weights - delta[:, cols])
                low_weights = weights.astype(BF)
                low_scores = grad_scores.astype(BF)
                dv_acc[head, pl.ds(at, step), :] += dot_nn(low_weights, grad_half[cols, :])
                dk_acc[head, pl.ds(at, step), :] += dot_nn(low_scores, query_half[cols, :])
                return dot_tn(keys, low_scores)

            def prompt_step(i, carry):
                at = pl.multiple_of(i * step, step)

                def mask(scores):
                    key_id = at + lax.broadcasted_iota(jnp.int32, (step, P_DEV), 0)
                    row_id = lax.broadcasted_iota(jnp.int32, (step, P_DEV), 1)
                    first = jnp.where(key_id <= place * P_DEV + row_id, scores[:, 0:P_DEV], NEGATIVE)
                    return jnp.concatenate([first, scores[:, P_DEV:]], 1)

                return carry + block(at, slice(0, rows), mask)

            total = lax.fori_loop(0, prompt // step, prompt_step, total)
            for own in range(cont // step):
                start = P_DEV + own * step

                def mask(scores):
                    key_id = lax.broadcasted_iota(jnp.int32, (step, step), 0)
                    row_id = lax.broadcasted_iota(jnp.int32, (step, step), 1)
                    edge = jnp.where(key_id <= row_id, scores[:, 0:step], NEGATIVE)
                    if scores.shape[1] == step:
                        return edge
                    return jnp.concatenate([edge, scores[:, step:]], 1)

                part = block(prompt + own * step, slice(start, rows), mask)
                total = jnp.concatenate([total[:, 0:start], total[:, start:] + part], 1)
        dq_ref[:, lanes] = (jnp.transpose(total) * HD ** (-0.5)).astype(BF)
    for acc, out_prompt, out_own in ((dk_acc, dkp_ref, dko_ref), (dv_acc, dvp_ref, dvo_ref)):
        low0, high0 = halves(acc[0])
        low1, high1 = halves(acc[1])
        merged = low0 + pltpu.roll(high0, HD, 1) + high1 + pltpu.roll(low1, HD, 1)
        out_prompt[...] = merged[0:prompt].astype(BF)
        out_own[...] = merged[prompt:].astype(BF)


def attend_back(place, query, prompt_key, prompt_value, own_key, own_value, mixed, grad, lse):
    rows = query.shape[0]
    prompt = prompt_key.shape[0]
    cont = own_key.shape[0]
    pairs = prompt_key.shape[1] // 128
    col = lambda i: (0, i)
    wide = pl.BlockSpec((rows, 384), col)
    keys_p = pl.BlockSpec((prompt, 128), col)
    keys_o = pl.BlockSpec((cont, 128), col)
    return pl.pallas_call(
        attend_back_kernel,
        grid=(pairs,),
        in_specs=[
            pl.BlockSpec(memory_space=pltpu.SMEM),
            wide, keys_p, keys_p, keys_o, keys_o, wide, wide,
            pl.BlockSpec((1, 8, rows), lambda i: (i, 0, 0)),
        ],
        out_specs=[wide, keys_p, keys_p, keys_o, keys_o],
        out_shape=[
            jax.ShapeDtypeStruct(query.shape, BF),
            jax.ShapeDtypeStruct(prompt_key.shape, BF),
            jax.ShapeDtypeStruct(prompt_key.shape, BF),
            jax.ShapeDtypeStruct(own_key.shape, BF),
            jax.ShapeDtypeStruct(own_key.shape, BF),
        ],
        scratch_shapes=[
            pltpu.VMEM((2, 2, prompt + cont, 128), BF),
            pltpu.VMEM((2, 2, prompt + cont, 128), BF),
            pltpu.VMEM((2, prompt + cont, 128), F32),
            pltpu.VMEM((2, prompt + cont, 128), F32),
        ],
        cost_estimate=pl.CostEstimate(flops=10**6, bytes_accessed=10**6, transcendentals=0),
        name="attend_back",
    )(place, query, prompt_key, prompt_value, own_key, own_value, mixed, grad, lse)


SLOTS_ALIGN = 16


def gather_kernel(count, with_gates, pos_ref, *refs):
    if with_gates:
        gate_ref, rows_ref, x_ref, g_ref, pick = refs
    else:
        rows_ref, x_ref, pick = refs
    tokens = rows_ref.shape[1]
    slots = x_ref.shape[1] // count
    half = rows_ref.shape[2] // 2
    slot_id = lax.broadcasted_iota(jnp.int32, (slots, tokens), 0)
    for k in range(count):
        hit = slot_id == pos_ref[0, k:k + 1, :]
        pick[k * slots:(k + 1) * slots, :] = jnp.where(hit, 1.0, 0.0).astype(BF)
        if with_gates:
            gate = jnp.sum(jnp.where(hit, gate_ref[0, k:k + 1, :], 0.0), 1, keepdims=True)
            g_ref[0, k * slots:(k + 1) * slots, :] = jnp.broadcast_to(gate, (slots, 128))
    x_ref[0, :, 0:half] = dot_nn(pick[...], rows_ref[0, :, 0:half]).astype(BF)
    x_ref[0, :, half:] = dot_nn(pick[...], rows_ref[0, :, half:]).astype(BF)


def gather_rows(positions, gates, rows, count, slots):
    sources, tokens, width = rows.shape
    size = count * slots
    table = pl.BlockSpec((1, 8, tokens), lambda s: (s, 0, 0))
    block = lambda shape: pl.BlockSpec((1,) + shape, lambda s: (s, 0, 0))
    tables = [positions] if gates is None else [positions, gates]
    outs = [((size, width), BF)] if gates is None else [((size, width), BF), ((size, 128), F32)]
    return pl.pallas_call(
        functools.partial(gather_kernel, count, gates is not None),
        grid=(sources,),
        in_specs=[table] * len(tables) + [block((tokens, width))],
        out_specs=[block(shape) for shape, _ in outs],
        out_shape=[jax.ShapeDtypeStruct((sources,) + shape, dtype) for shape, dtype in outs],
        scratch_shapes=[pltpu.VMEM((size, tokens), BF)],
        cost_estimate=pl.CostEstimate(flops=10**6, bytes_accessed=10**6, transcendentals=0),
        name="gather_rows",
    )(*tables, rows)


def gather_split_kernel(count, lefts, rights, pos_ref, *refs):
    parts = refs[0:len(set(i for i, _ in lefts)) + len(set(i for i, _ in rights))]
    x_ref, pick, left, right, sems = refs[len(parts):]
    s = pl.program_id(0)
    sources = len(lefts)
    slots = x_ref.shape[1] // count
    tokens, half = left.shape[1:]

    def fetch(i):
        (a, at), (b, bt), slot = lefts[i], rights[i], i % 2
        return (
            pltpu.make_async_copy(parts[a].at[at], left.at[slot], sems.at[0, slot]),
            pltpu.make_async_copy(parts[b].at[bt], right.at[slot], sems.at[1, slot]),
        )

    @pl.when(s == 0)
    def _():
        for copy in fetch(0):
            copy.start()

    for i in range(1, sources):

        @pl.when(s == i - 1)
        def _(i=i):
            for copy in fetch(i):
                copy.start()

    slot_id = lax.broadcasted_iota(jnp.int32, (slots, tokens), 0)
    for k in range(count):
        hit = slot_id == pos_ref[0, k:k + 1, :]
        pick[k * slots:(k + 1) * slots, :] = jnp.where(hit, 1.0, 0.0).astype(BF)
    slot = lax.rem(s, 2)
    pltpu.make_async_copy(parts[0].at[0], left.at[slot], sems.at[0, slot]).wait()
    pltpu.make_async_copy(parts[0].at[0], right.at[slot], sems.at[1, slot]).wait()
    x_ref[0, :, 0:half] = dot_nn(pick[...], left[slot]).astype(BF)
    x_ref[0, :, half:] = dot_nn(pick[...], right[slot]).astype(BF)


def gather_split(positions, parts, lefts, rights, count, slots):
    _, tokens, half = parts[0].shape
    sources, size = len(lefts), count * slots
    return pl.pallas_call(
        functools.partial(gather_split_kernel, count, lefts, rights),
        grid=(sources,),
        in_specs=[pl.BlockSpec((1, 8, tokens), lambda s: (s, 0, 0))] + [pl.BlockSpec(memory_space=pl.ANY)] * len(parts),
        out_specs=pl.BlockSpec((1, size, 2 * half), lambda s: (s, 0, 0)),
        out_shape=jax.ShapeDtypeStruct((sources, size, 2 * half), BF),
        scratch_shapes=[
            pltpu.VMEM((size, tokens), BF),
            pltpu.VMEM((2, tokens, half), BF),
            pltpu.VMEM((2, tokens, half), BF),
            pltpu.SemaphoreType.DMA((2, 2)),
        ],
        cost_estimate=pl.CostEstimate(flops=10**6, bytes_accessed=10**6, transcendentals=0),
        name="gather_split",
    )(positions, *parts)


def expert_kernel(k, shards, slots, dp_ref, x_ref, g_ref, gate_ref, *refs):
    w_refs = refs[0:shards // 2]
    (y_out, dx_out, dg_out, keep_out, send_out,
     xs, gs, gates, ws, ys, dxs, dgs, dab, actg, stage,
     in_sem, w_sem, out_sem, grad_sem) = refs[shards // 2:]
    dp = dp_ref[0]
    sources = x_ref.shape[0]
    width = xs.shape[1]
    piece = width // shards
    hidden = ws.shape[2]
    mine = pl.ds(k * slots, slots)

    def row_copies(s):
        at = pl.ds(pl.multiple_of(s * slots, 16), slots)
        return (
            pltpu.make_async_copy(x_ref.at[s, mine, :], xs.at[at, :], in_sem.at[0, s]),
            pltpu.make_async_copy(g_ref.at[s, mine, :], gs.at[at, :], in_sem.at[1, s]),
            pltpu.make_async_copy(gate_ref.at[s, mine, :], gates.at[at, :], in_sem.at[2, s]),
        )

    weight_copies = [
        pltpu.make_async_copy(
            w_refs[(r & 1) + 2 * (r >> 2)].at[(r >> 1) & 1], ws.at[:, pl.ds(pl.multiple_of((dp ^ r) * piece, 16), piece), :], w_sem.at[r]
        )
        for r in range(shards)
    ]
    for s in range(sources):
        for copy in row_copies(s):
            copy.start()
        if s == 1:
            for copy in weight_copies:
                copy.start()
    for copy in weight_copies:
        copy.wait()
    chunk = 2 * slots

    def out_copies(c):
        at = pl.ds(pl.multiple_of(c * chunk, 32), chunk)
        return [
            pltpu.make_async_copy(src.at[at, :], dst.at[at, :], out_sem.at[i, c])
            for i, (src, dst) in enumerate(((ys, y_out), (dxs, dx_out), (dgs, dg_out)))
        ]

    def forward_chunk(c, carry):
        for copy in row_copies(2 * c) + row_copies(2 * c + 1):
            copy.wait()
        rows = pl.ds(pl.multiple_of(c * chunk, 32), chunk)
        x = xs[rows, :]
        a = dot_nn(x, ws[0])
        b = dot_nn(x, ws[1])
        pulled = dot_nn(gs[rows, :], ws[2])
        gate = gates[rows, 0:1]
        sig = jax.nn.sigmoid(a)
        silu = a * sig
        act = silu * b
        dgs[rows, :] = jnp.broadcast_to(jnp.sum(act * pulled, 1, keepdims=True), (chunk, 128))
        weighted = (gate * act).astype(BF)
        actg[rows, :] = weighted
        dact = gate * pulled
        da = (dact * b * sig * (1.0 + a * (1.0 - sig))).astype(BF)
        db = (dact * silu).astype(BF)
        dab[rows, 0:hidden] = da
        dab[rows, hidden:] = db
        ys[rows, :] = dot_nt(weighted, ws[2]).astype(BF)
        dxs[rows, :] = (dot_nt(da, ws[0]) + dot_nt(db, ws[1])).astype(BF)
        for copy in out_copies(c):
            copy.start()
        return carry

    lax.fori_loop(0, sources // 2, forward_chunk, 0)
    block = 384
    inner = block // piece
    high = dp // inner
    low = dp % inner

    def grad_copies(jr):
        slot = lax.rem(jr, 2)
        copies = []
        for ri in range(inner):
            dst = (send_out if ri % 2 else keep_out).at[jr * (inner // 2) + ri // 2]
            src = stage.at[slot, :, pl.ds(pl.multiple_of((low ^ ri) * piece, 16), piece), :]
            copies.append(pltpu.make_async_copy(src, dst, grad_sem.at[slot, ri]))
        return copies

    def grad_block(jr, carry):
        slot = lax.rem(jr, 2)

        @pl.when(jr >= 2)
        def _():
            for copy in grad_copies(jr - 2):
                copy.wait()

        cols = pl.ds(pl.multiple_of((high ^ jr) * block, 128), block)
        left = dot_tn(xs[:, cols], dab[...])
        stage[slot, 0] = left[:, 0:hidden].astype(BF)
        stage[slot, 1] = left[:, hidden:].astype(BF)
        stage[slot, 2] = dot_tn(gs[:, cols], actg[...]).astype(BF)
        for copy in grad_copies(jr):
            copy.start()
        return carry

    blocks = width // block
    lax.fori_loop(0, blocks, grad_block, 0)
    for jr in range(blocks - 2, blocks):
        for copy in grad_copies(jr):
            copy.wait()
    for c in range(sources // 2):
        for copy in out_copies(c):
            copy.wait()


def run_expert(k, dp_index, xs, gs, gates, weights, slots):
    sources, shards = xs.shape[0], 2 * len(weights)
    rows = sources * slots
    width = xs.shape[2]
    piece, hidden = weights[0].shape[2:]
    inner = 384 // piece
    anywhere = pl.BlockSpec(memory_space=pl.ANY)
    return pl.pallas_call(
        functools.partial(expert_kernel, k, shards, slots),
        in_specs=[pl.BlockSpec(memory_space=pltpu.SMEM)] + [anywhere] * (3 + shards // 2),
        out_specs=[anywhere] * 5,
        out_shape=[
            jax.ShapeDtypeStruct((rows, width), BF),
            jax.ShapeDtypeStruct((rows, width), BF),
            jax.ShapeDtypeStruct((rows, 128), F32),
            jax.ShapeDtypeStruct((shards // 2, 3, piece, hidden), BF),
            jax.ShapeDtypeStruct((shards // 2, 3, piece, hidden), BF),
        ],
        scratch_shapes=[
            pltpu.VMEM((rows, width), BF),
            pltpu.VMEM((rows, width), BF),
            pltpu.VMEM((rows, 128), F32),
            pltpu.VMEM((3, width, hidden), BF),
            pltpu.VMEM((rows, width), BF),
            pltpu.VMEM((rows, width), BF),
            pltpu.VMEM((rows, 128), F32),
            pltpu.VMEM((rows, 2 * hidden), BF),
            pltpu.VMEM((rows, hidden), BF),
            pltpu.VMEM((2, 3, 384, hidden), BF),
            pltpu.SemaphoreType.DMA((3, sources)),
            pltpu.SemaphoreType.DMA((shards,)),
            pltpu.SemaphoreType.DMA((3, sources // 2)),
            pltpu.SemaphoreType.DMA((2, inner)),
        ],
        compiler_params=pltpu.CompilerParams(vmem_limit_bytes=60 * 2**20),
        cost_estimate=pl.CostEstimate(flops=10**6, bytes_accessed=10**6, transcendentals=0),
        name="expert",
    )(dp_index, xs, gs, gates, *weights)


def combine_kernel(count, slots, pos_ref, *refs):
    y_refs = refs[0:count]
    keep, send, ys, pick = refs[count:]
    tokens = pos_ref.shape[2]
    half = keep.shape[2] // 2
    slot_id = lax.broadcasted_iota(jnp.int32, (slots, tokens), 0)
    for j, out in enumerate((keep, send)):
        for k in range(count):
            rows = slice(k * slots, (k + 1) * slots)
            ys[rows, :] = y_refs[k][j * slots:(j + 1) * slots, :]
            pick[rows, :] = jnp.where(slot_id == pos_ref[j, k:k + 1, :], 1.0, 0.0).astype(BF)
        out[0, :, 0:half] = dot_tn(pick[...], ys[:, 0:half]).astype(BF)
        out[0, :, half:] = dot_tn(pick[...], ys[:, half:]).astype(BF)


def combine_rows(positions, results, slots):
    sources, _, tokens = positions.shape
    count = len(results)
    width = results[0].shape[1]
    out = pl.BlockSpec((1, tokens, width), lambda i: (i, 0, 0))
    return pl.pallas_call(
        functools.partial(combine_kernel, count, slots),
        grid=(sources // 2,),
        in_specs=[pl.BlockSpec((2, 8, tokens), lambda i: (i, 0, 0))]
        + [pl.BlockSpec((2 * slots, width), lambda i: (i, 0))] * count,
        out_specs=[out] * 2,
        out_shape=[jax.ShapeDtypeStruct((sources // 2, tokens, width), BF)] * 2,
        scratch_shapes=[pltpu.VMEM((count * slots, width), BF), pltpu.VMEM((count * slots, tokens), BF)],
        cost_estimate=pl.CostEstimate(flops=10**6, bytes_accessed=10**6, transcendentals=0),
        name="combine_rows",
    )(positions, *results)


def barrier_with(partners):
    sem = pltpu.get_barrier_semaphore()
    for partner in partners:
        pl.semaphore_signal(sem, inc=1, device_id=partner, device_id_type=pl.DeviceIdType.MESH)
    pl.semaphore_wait(sem, len(partners))


def flipped(axis, mask):
    at = lax.axis_index(axis)
    bit = lax.rem(lax.div(at, mask), 2)
    return {axis: at + mask * (1 - 2 * bit)}


def own_bit(axis, mask):
    return lax.rem(lax.div(lax.axis_index(axis), mask), 2)


TEAM = (("dp", 2), ("expert", 2), ("expert", 1))
GROUP = (("dp", 1), ("expert", 2), ("expert", 1))
CUBE = (("dp", 4), ("dp", 2), ("dp", 1), ("expert", 2), ("expert", 1))
ROTATIONS = ((0, 1, 2, 3), (0, 2, 3, 1), (0, 3, 1, 2))


def part_of(gathered, bits, cols):
    index = tuple(pl.ds(0, 2) if dim in gathered else pl.ds(bits[dim], 1) for dim in range(5))
    return index + (slice(None), cols)


def gather_all_kernel(
    pieces, shard_ref, give_ref, routes_ref, full_ref, take_ref, team_ref, own_sem, send_sem, recv_sem, piece_sem, team_sem
):
    barrier_with([flipped(*dim) for dim in CUBE])
    mine = pltpu.make_async_copy(routes_ref, team_ref.at[0:1, 0:1, 0:1], team_sem.at[2, 0])
    mine.start()
    mine.wait()

    def routes_step(step):
        index = [pl.ds(0, 2) if d < step else pl.ds(0, 1) for d in range(3)]
        src = team_ref.at[tuple(index)]
        index[step] = pl.ds(1, 1)
        return pltpu.make_async_remote_copy(
            src_ref=src, dst_ref=team_ref.at[tuple(index)], send_sem=team_sem.at[0, step],
            recv_sem=team_sem.at[1, step], device_id=flipped(*TEAM[step]), device_id_type=pl.DeviceIdType.MESH,
        )

    bits = [own_bit(*dim) for dim in CUBE]
    width = full_ref.shape[6] // 3
    cols = [pl.ds(c * width, width) for c in range(3)]
    here = tuple(pl.ds(bit, 1) for bit in bits)
    own = pltpu.make_async_copy(shard_ref, full_ref.at[here], own_sem)
    own.start()
    own.wait()

    def spread(step, c, gathered, dim, cols):
        at = part_of(gathered, bits, cols)
        return pltpu.make_async_remote_copy(
            src_ref=full_ref.at[at], dst_ref=full_ref.at[at], send_sem=send_sem.at[step, c],
            recv_sem=recv_sem.at[step, c], device_id=flipped(*CUBE[dim]), device_id_type=pl.DeviceIdType.MESH,
        )

    def hand(k):
        return pltpu.make_async_remote_copy(
            src_ref=give_ref.at[k], dst_ref=take_ref.at[k], send_sem=piece_sem.at[0, k],
            recv_sem=piece_sem.at[1, k], device_id=flipped("dp", 2), device_id_type=pl.DeviceIdType.MESH,
        )

    copies, passed = [], []
    running = [None] * 3
    for step in range(4):
        if step > 0:
            routes_step(step - 1).wait()
        if step < 3:
            routes_step(step).start()
        for c in range(3):
            if running[c] is not None:
                running[c].wait_recv()
            copy = spread(step, c, ROTATIONS[c][:step], ROTATIONS[c][step], cols[c])
            copy.start()
            copies.append(copy)
            running[c] = copy
        if step < pieces:
            passed.append(hand(step))
            passed[-1].start()
    for c in range(3):
        running[c].wait_recv()
        copy = spread(4, c, (0, 1, 2, 3), 4, cols[c])
        copy.start()
        copies.append(copy)
        running[c] = copy
    for k in range(4, pieces):
        passed.append(hand(k))
        passed[-1].start()
    for c in range(3):
        running[c].wait_recv()
    for copy in copies:
        copy.wait_send()
    for copy in passed:
        copy.wait()


def gather_all(shard, give, routes):
    rows, width = shard.shape
    pieces = give.shape[0]
    anywhere, vmem = pl.BlockSpec(memory_space=pl.ANY), pl.BlockSpec(memory_space=pltpu.VMEM)
    full, take, team = pl.pallas_call(
        functools.partial(gather_all_kernel, pieces),
        in_specs=[vmem, anywhere, vmem],
        out_specs=[anywhere, anywhere, anywhere],
        out_shape=[
            jax.ShapeDtypeStruct((2,) * 5 + (rows, width), BF),
            jax.ShapeDtypeStruct(give.shape, BF),
            jax.ShapeDtypeStruct((2, 2, 2) + routes.shape, jnp.int32),
        ],
        scratch_shapes=[
            pltpu.SemaphoreType.DMA,
            pltpu.SemaphoreType.DMA((5, 3)),
            pltpu.SemaphoreType.DMA((5, 3)),
            pltpu.SemaphoreType.DMA((2, pieces)),
            pltpu.SemaphoreType.DMA((3, 3)),
        ],
        compiler_params=pltpu.CompilerParams(collective_id=1, has_side_effects=True),
        name="gather_all",
    )(shard.reshape((1,) * 5 + (rows, width)), give, routes.reshape((1, 1, 1) + routes.shape))
    return full.reshape(32 * rows, width), take, team.reshape((8,) + routes.shape)


def job_copies(jobs, gives, takes, sems):
    return [
        pltpu.make_async_remote_copy(
            src_ref=gives[j], dst_ref=takes[j], send_sem=sems.at[0, j], recv_sem=sems.at[1, j],
            device_id=flipped(*jobs[j]), device_id_type=pl.DeviceIdType.MESH,
        )
        for j in range(len(jobs))
    ]


def partners_of(dims, jobs):
    return [flipped(*dim) for dim in dict.fromkeys(tuple(dims) + tuple(jobs))]


def inner_plane():
    return own_bit("dp", 2) != own_bit("dp", 4)


def team_rows_kernel(jobs, relays, rows_ref, gates_ref, *refs):
    count = len(jobs)
    gives, takes = refs[0:count], refs[count + 2:2 * count + 2]
    all_ref, table_ref = refs[count:count + 2]
    own_sem, send_sem, recv_sem, job_sem = refs[2 * count + 2:]
    barrier_with(partners_of(TEAM, jobs))
    half = all_ref.shape[4] // 2
    own = [
        pltpu.make_async_copy(rows_ref, all_ref.at[0:1, 0:1, 0:1], own_sem.at[0]),
        pltpu.make_async_copy(gates_ref, table_ref.at[0:1, 0:1, 0:1], own_sem.at[1]),
    ]
    for copy in own:
        copy.start()
    for copy in own:
        copy.wait()
    flows = (
        (all_ref, (0, 1, 2), (slice(None), pl.ds(0, half))),
        (all_ref, (1, 0, 2), (slice(None), pl.ds(half, half))),
        (table_ref, (0, 1, 2), (slice(None), slice(None))),
    )
    copies = []
    running = [None] * 3
    for step in range(3):
        for f, (ref, order, tail) in enumerate(flows):
            if running[f] is not None:
                running[f].wait_recv()
            dim = order[step]
            index = [pl.ds(0, 2) if d in order[:step] else pl.ds(0, 1) for d in range(3)]
            src = ref.at[tuple(index) + tail]
            index[dim] = pl.ds(1, 1)
            copy = pltpu.make_async_remote_copy(
                src_ref=src, dst_ref=ref.at[tuple(index) + tail], send_sem=send_sem.at[step, f],
                recv_sem=recv_sem.at[step, f], device_id=flipped(*TEAM[dim]), device_id_type=pl.DeviceIdType.MESH,
            )
            copy.start()
            copies.append(copy)
            running[f] = copy
        if step == 0:
            background = job_copies(jobs, gives, takes, job_sem)
            for copy in background[relays:]:
                copy.start()
        if relays and step < 2:

            @pl.when(inner_plane() if step == 0 else jnp.logical_not(inner_plane()))
            def _():
                for copy in background[:relays]:
                    copy.start()

    for copy in running:
        copy.wait_recv()
    for copy in copies:
        copy.wait_send()
    for copy in background:
        copy.wait()


def team_rows(rows, gates, jobs=(), gives=(), relays=0):
    tokens, width = rows.shape
    table = gates.shape
    anywhere = pl.BlockSpec(memory_space=pl.ANY)
    full, tables, *takes = pl.pallas_call(
        functools.partial(team_rows_kernel, tuple(jobs), relays),
        in_specs=[pl.BlockSpec(memory_space=pltpu.VMEM)] * 2 + [anywhere] * len(jobs),
        out_specs=[anywhere] * (2 + len(jobs)),
        out_shape=[
            jax.ShapeDtypeStruct((2, 2, 2, tokens, width), BF),
            jax.ShapeDtypeStruct((2, 2, 2) + table, F32),
        ] + [jax.ShapeDtypeStruct(give.shape, give.dtype) for give in gives],
        scratch_shapes=[
            pltpu.SemaphoreType.DMA((2,)),
            pltpu.SemaphoreType.DMA((3, 3)),
            pltpu.SemaphoreType.DMA((3, 3)),
            pltpu.SemaphoreType.DMA((2, max(1, len(jobs)))),
        ],
        compiler_params=pltpu.CompilerParams(collective_id=2, has_side_effects=True),
        name="team_rows",
    )(rows.reshape(1, 1, 1, tokens, width), gates.reshape((1, 1, 1) + table), *gives)
    return full.reshape(8, tokens, width), tables.reshape((8,) + table), takes


def add_into(acc, at, other):
    acc[at] = (acc[at].astype(F32) + other.astype(F32)).astype(BF)


def return_kernel(count, slots, jobs, relays, pos_ref, *refs):
    y_refs, dg_refs = refs[0:count], refs[count:2 * count]
    refs = refs[2 * count:]
    gives, takes = refs[0:len(jobs)], refs[len(jobs) + 2:2 * len(jobs) + 2]
    out_ref, gate_ref = refs[len(jobs):len(jobs) + 2]
    (acc, core_in, row_in, pair_in, last_in, ys, pick, table, table_core, table_row, table_pair,
     load_sem, send_sem, recv_sem, job_sem) = refs[2 * len(jobs) + 2:]
    tokens, width = out_ref.shape
    half = width // 2
    barrier_with(partners_of(TEAM, jobs))
    background = job_copies(jobs, gives, takes, job_sem)
    for copy in background[relays:]:
        copy.start()
    if relays:

        @pl.when(jnp.logical_not(inner_plane()))
        def _():
            for copy in background[:relays]:
                copy.start()

    first = (lax.axis_index("expert") * 2 + own_bit("dp", 2)) * count
    slot_id = lax.broadcasted_iota(jnp.int32, (slots, tokens), 0)

    def remote(src, dst, n, dim):
        return pltpu.make_async_remote_copy(
            src_ref=src, dst_ref=dst, send_sem=send_sem.at[n], recv_sem=recv_sem.at[n],
            device_id=flipped(*TEAM[dim]), device_id_type=pl.DeviceIdType.MESH,
        )

    def loads(r, slot):
        return [
            pltpu.make_async_copy(
                y_refs[k].at[pl.ds(pl.multiple_of(r * slots, 16), slots), :],
                ys.at[slot, pl.ds(k * slots, slots), :], load_sem.at[slot, k],
            )
            for k in range(count)
        ]

    table[...] = jnp.zeros_like(table)

    def build(step, r, following):
        slot = lax.rem(step, 2)
        for copy in loads(r, slot):
            copy.wait()

        @pl.when(step < 7)
        def _():
            for copy in loads(following, 1 - slot):
                copy.start()

        for k in range(count):
            hit = slot_id == pos_ref[r, k:k + 1, :]
            pick[k * slots:(k + 1) * slots, :] = jnp.where(hit, 1.0, 0.0).astype(BF)
            pulled = dg_refs[k][pl.ds(pl.multiple_of(r * slots, 16), slots), 0:1]
            table[r, pl.ds(first + k, 1), :] = jnp.sum(jnp.where(hit, pulled, 0.0), 0, keepdims=True)
        acc[r, :, 0:half] = dot_tn(pick[...], ys[slot, :, 0:half]).astype(BF)
        acc[r, :, half:] = dot_tn(pick[...], ys[slot, :, half:]).astype(BF)

    for copy in loads(1, 0):
        copy.start()

    def odd(i, carry):
        r = 2 * i + 1
        build(i, r, jnp.where(i < 3, r + 2, 0))
        remote(acc.at[r], core_in.at[i], i, 2).start()
        return carry

    def even(i, carry):
        build(i + 4, 2 * i, 2 * i + 2)
        return carry

    lax.fori_loop(0, 4, odd, 0)
    tables = [remote(table.at[2 * i + 1], table_core.at[i], 4 + i, 2) for i in range(4)]
    for copy in tables:
        copy.start()
    lax.fori_loop(0, 4, even, 0)
    if relays:

        @pl.when(inner_plane())
        def _():
            for copy in background[:relays]:
                copy.start()

    def settle(i):
        remote(acc.at[2 * i + 1], core_in.at[i], i, 2).wait()
        add_into(acc, 2 * i, core_in[i])

    left, right = slice(0, half), slice(half, width)
    settle(3)
    a = [remote(acc.at[6, :, pl.ds(0, half)], row_in.at[1], 8, 1), remote(acc.at[6, :, pl.ds(half, half)], pair_in.at[1], 9, 0)]
    for copy in a:
        copy.start()
    settle(1)
    a.append(remote(acc.at[2, :, pl.ds(0, half)], row_in.at[0], 10, 1))
    a[-1].start()
    settle(2)
    a.append(remote(acc.at[4, :, pl.ds(half, half)], pair_in.at[0], 11, 0))
    a[-1].start()
    for i, copy in enumerate(tables):
        copy.wait()
        table[2 * i] = table[2 * i] + table_core[i]
    t = [remote(table.at[2], table_row.at[0], 12, 1), remote(table.at[6], table_row.at[1], 13, 1)]
    for copy in t:
        copy.start()
    settle(0)
    a[0].wait()
    add_into(acc, (4, slice(None), left), row_in[1])
    b = [remote(acc.at[4, :, pl.ds(0, half)], last_in.at[0], 14, 0)]
    b[0].start()
    a[1].wait()
    add_into(acc, (2, slice(None), right), pair_in[1])
    b.append(remote(acc.at[2, :, pl.ds(half, half)], last_in.at[1], 15, 1))
    b[1].start()
    for i, copy in enumerate(t):
        copy.wait()
        table[4 * i] = table[4 * i] + table_row[i]
    t = remote(table.at[4], table_pair, 16, 0)
    t.start()
    a[2].wait()
    add_into(acc, (0, slice(None), left), row_in[0])
    a[3].wait()
    add_into(acc, (0, slice(None), right), pair_in[0])
    b[0].wait()
    out_ref[:, left] = (acc[0, :, left].astype(F32) + last_in[0].astype(F32)).astype(BF)
    b[1].wait()
    out_ref[:, right] = (acc[0, :, right].astype(F32) + last_in[1].astype(F32)).astype(BF)
    t.wait()
    gate_ref[...] = table[0] + table_pair[...]
    for copy in background:
        copy.wait()


def return_rows(positions, results, gate_rows, experts, slots, jobs=(), gives=(), relays=0):
    sources, _, tokens = positions.shape
    count = len(results)
    width = results[0].shape[1]
    half = width // 2
    vmem, anywhere = pl.BlockSpec(memory_space=pltpu.VMEM), pl.BlockSpec(memory_space=pl.ANY)
    rows, gates, *takes = pl.pallas_call(
        functools.partial(return_kernel, count, slots, tuple(jobs), relays),
        in_specs=[vmem] + [anywhere] * count + [vmem] * count + [anywhere] * len(jobs),
        out_specs=[vmem, vmem] + [anywhere] * len(jobs),
        out_shape=[jax.ShapeDtypeStruct((tokens, width), BF), jax.ShapeDtypeStruct((experts, tokens), F32)]
        + [jax.ShapeDtypeStruct(give.shape, give.dtype) for give in gives],
        scratch_shapes=[
            pltpu.VMEM((8, tokens, width), BF),
            pltpu.VMEM((4, tokens, width), BF),
            pltpu.VMEM((2, tokens, half), BF),
            pltpu.VMEM((2, tokens, half), BF),
            pltpu.VMEM((2, tokens, half), BF),
            pltpu.VMEM((2, count * slots, width), BF),
            pltpu.VMEM((count * slots, tokens), BF),
            pltpu.VMEM((8, experts, tokens), F32),
            pltpu.VMEM((4, experts, tokens), F32),
            pltpu.VMEM((2, experts, tokens), F32),
            pltpu.VMEM((experts, tokens), F32),
            pltpu.SemaphoreType.DMA((2, count)),
            pltpu.SemaphoreType.DMA((17,)),
            pltpu.SemaphoreType.DMA((17,)),
            pltpu.SemaphoreType.DMA((2, max(1, len(jobs)))),
        ],
        compiler_params=pltpu.CompilerParams(collective_id=3, has_side_effects=True, vmem_limit_bytes=60 * 2**20),
        name="return_rows",
    )(positions, *results, *gate_rows, *gives)
    return rows, gates, takes


class Group:
    def __init__(self, copies):
        self.copies = copies

    def wait(self):
        for copy in self.copies:
            copy.wait()


def scatter_kernel(dims, rotations, chunks, sources, *refs):
    last = len(dims) - 1
    grads, out_ref = refs[0:sources], refs[sources]
    acc, core_in = refs[sources + 1:sources + 3]
    inboxes = refs[sources + 3:sources + 3 + last]
    load_sem, send_sem, recv_sem = refs[sources + 3 + last:]
    barrier_with([flipped(*dim) for dim in dims])
    bits = [own_bit(*dim) for dim in dims]
    every = tuple(pl.ds(0, 2) for _ in range(last))
    number = iter(range(send_sem.shape[0]))

    def remote(src, dst, dim):
        n = next(number)
        return pltpu.make_async_remote_copy(
            src_ref=src, dst_ref=dst, send_sem=send_sem.at[n], recv_sem=recv_sem.at[n],
            device_id=flipped(*dims[dim]), device_id_type=pl.DeviceIdType.MESH,
        )

    sends, loads = [], []
    for source, start, at, width in chunks:
        src, dst = (slice(None), pl.ds(start, width)), (slice(None), pl.ds(at, width))
        copy = remote(
            grads[source].at[every + (pl.ds(1 - bits[last], 1),) + src], core_in.at[every + (pl.ds(0, 1),) + dst], last
        )
        copy.start()
        sends.append(copy)
        load = pltpu.make_async_copy(
            grads[source].at[every + (pl.ds(bits[last], 1),) + src], acc.at[every + (pl.ds(0, 1),) + dst],
            load_sem.at[len(loads)],
        )
        load.start()
        loads.append(load)
    for load in loads:
        load.wait()
    for step in range(last + 1):
        for c, (_, _, start, width) in enumerate(chunks):
            cols = pl.ds(start, width)
            rest = rotations[c][:last - step]
            sends[c].wait()
            for n in range(2 ** len(rest)):
                spread = [(n >> (len(rest) - 1 - i)) & 1 for i in range(len(rest))]
                index = [bits[d] if d not in rest else spread[rest.index(d)] for d in range(last)]
                at = tuple(index) + (0, slice(None), cols)
                other = core_in[at] if step == 0 else inboxes[step - 1][n, :, cols]
                if step < last:
                    add_into(acc, at, other)
                else:
                    out_ref[:, cols] = (acc[at].astype(F32) + other.astype(F32)).astype(out_ref.dtype)
            if step < last:
                dim, spread_dims = rest[-1], rest[:-1]
                group = []
                for n in range(2 ** len(spread_dims)):
                    spread = [(n >> (len(spread_dims) - 1 - i)) & 1 for i in range(len(spread_dims))]
                    index = [
                        1 - bits[d] if d == dim else (spread[spread_dims.index(d)] if d in spread_dims else bits[d])
                        for d in range(last)
                    ]
                    copy = remote(acc.at[tuple(index) + (0, slice(None), cols)], inboxes[step].at[n, :, cols], dim)
                    copy.start()
                    group.append(copy)
                sends[c] = Group(group)


def cube_scatter(dims, rotations, chunks, grads, dtype, collective, name):
    last = len(dims) - 1
    rows = grads[0].shape[0] // 2 ** len(dims)
    width = sum(chunk[3] for chunk in chunks)
    copies = len(chunks) * 2 ** last
    return pl.pallas_call(
        functools.partial(scatter_kernel, dims, rotations, chunks, len(grads)),
        in_specs=[pl.BlockSpec(memory_space=pl.ANY)] * len(grads),
        out_specs=pl.BlockSpec(memory_space=pltpu.VMEM),
        out_shape=jax.ShapeDtypeStruct((rows, width), dtype),
        scratch_shapes=[pltpu.VMEM((2,) * last + (1, rows, width), BF)] * 2
        + [pltpu.VMEM((2 ** n, rows, width), BF) for n in reversed(range(last))]
        + [pltpu.SemaphoreType.DMA((len(chunks),)), pltpu.SemaphoreType.DMA((copies,)), pltpu.SemaphoreType.DMA((copies,))],
        compiler_params=pltpu.CompilerParams(
            collective_id=collective, has_side_effects=True, vmem_limit_bytes=60 * 2**20
        ),
        name=name,
    )(*[g.reshape((2,) * len(dims) + (rows, g.shape[1])) for g in grads])


def scatter_all(first, second):
    one, two = first.shape[1], second.shape[1]
    cut = one // 256 * 128
    chunks = ((0, 0, 0, cut), (0, cut, cut, one - cut), (1, 0, one, two))
    return cube_scatter(CUBE, ROTATIONS, chunks, [first, second], F32, 4, "scatter_all")


def group_back(grad_key, grad_value):
    width = grad_key.shape[1]
    chunks = ((0, 0, 0, width), (1, 0, width, width))
    return cube_scatter(GROUP, ((0, 1), (1, 0)), chunks, [grad_key, grad_value], BF, 6, "group_back")


def group_rows_kernel(rows_ref, key_ref, value_ref, own_sem, send_sem, recv_sem):
    barrier_with([flipped(*dim) for dim in GROUP])
    bits = [own_bit(*dim) for dim in GROUP]
    width = key_ref.shape[4]
    here = tuple(pl.ds(bit, 1) for bit in bits)
    own = [
        pltpu.make_async_copy(rows_ref.at[:, :, :, :, pl.ds(i * width, width)], ref.at[here], own_sem.at[i])
        for i, ref in enumerate((key_ref, value_ref))
    ]
    for copy in own:
        copy.start()
    for copy in own:
        copy.wait()
    copies = []
    running = [None, None]
    for step in range(3):
        for f, (ref, order) in enumerate(((key_ref, (0, 1, 2)), (value_ref, (1, 0, 2)))):
            if running[f] is not None:
                running[f].wait_recv()
            at = tuple(pl.ds(0, 2) if d in order[:step] else pl.ds(bits[d], 1) for d in range(3))
            copy = pltpu.make_async_remote_copy(
                src_ref=ref.at[at], dst_ref=ref.at[at], send_sem=send_sem.at[step, f], recv_sem=recv_sem.at[step, f],
                device_id=flipped(*GROUP[order[step]]), device_id_type=pl.DeviceIdType.MESH,
            )
            copy.start()
            copies.append(copy)
            running[f] = copy
    for copy in running:
        copy.wait_recv()
    for copy in copies:
        copy.wait_send()


def group_rows(key_value):
    rows, width = key_value.shape
    anywhere = pl.BlockSpec(memory_space=pl.ANY)
    outs = pl.pallas_call(
        group_rows_kernel,
        in_specs=[pl.BlockSpec(memory_space=pltpu.VMEM)],
        out_specs=[anywhere] * 2,
        out_shape=[jax.ShapeDtypeStruct((2, 2, 2, rows, width // 2), BF)] * 2,
        scratch_shapes=[
            pltpu.SemaphoreType.DMA((2,)),
            pltpu.SemaphoreType.DMA((3, 2)),
            pltpu.SemaphoreType.DMA((3, 2)),
        ],
        compiler_params=pltpu.CompilerParams(collective_id=5, has_side_effects=True),
        name="group_rows",
    )(key_value.reshape(1, 1, 1, rows, width))
    return [out.reshape(8 * rows, width // 2) for out in outs]


D = 1536
EPSILON = 1e-06
EVERYWHERE = ("dp", "expert")


def exchange(value, axis, mask):
    return lax.ppermute(value, axis, [(i, i ^ mask) for i in range(lax.axis_size(axis))])


def tie(first, *others):
    return lax.optimization_barrier((first, *others))[0]


def rms_scale(values):
    return lax.rsqrt(jnp.mean(values * values, axis=-1, keepdims=True) + EPSILON)


def product(left, right):
    return jnp.dot(left, right, preferred_element_type=F32)


def contract_rows(left, right):
    return jnp.einsum("ta,tb->ab", left, right, preferred_element_type=F32)


def times_transposed(left, right):
    return jnp.einsum("ta,ba->tb", left, right, preferred_element_type=F32)


def added(left, right):
    return (left.astype(F32) + right.astype(F32)).astype(BF)


def team_gather(value, order):
    pieces = {0: value}
    for axis, mask, bit in order:
        pieces.update({r | bit: exchange(v, axis, mask) for r, v in list(pieces.items())})
    return jnp.stack([pieces[r] for r in sorted(pieces)])


TEAM_BITS = (("dp", 2, 4), ("expert", 2, 2), ("expert", 1, 1))


def local(tokens, attn_gain, w_query, w_key, w_value, w_out, w_router, ffn_gain, w_gate, w_up, w_down, routes, cotangent):
    dp, expert_at = lax.axis_index("dp"), lax.axis_index("expert")
    shards, owners = lax.axis_size("dp"), lax.axis_size("expert")
    cube = shards == 8 and owners == 4
    turn = (dp >> 1) & 1
    tok_rows = tokens.shape[0]
    per_owner, piece, hidden = w_gate.shape
    count = per_owner // 2
    expert_count = per_owner * owners
    top_count = routes.shape[1]
    kvw = w_key.shape[1]
    capacity = 8 * ((17 * top_count * tok_rows + 128 * expert_count - 1) // (128 * expert_count))
    slots = SLOTS_ALIGN * (-(-capacity // SLOTS_ALIGN))
    dp_index = dp.astype(jnp.int32).reshape(1)
    wide = D + 2 * kvw

    stacked = jnp.stack([w_gate, w_up, w_down.transpose(0, 2, 1)], 1)
    own = lax.dynamic_slice_in_dim(stacked, turn * count, count, 0)
    other = lax.dynamic_slice_in_dim(stacked, (1 - turn) * count, count, 0)
    gains = jnp.stack([attn_gain, ffn_gain], 1)
    first_shard = jnp.concatenate([w_query, w_key, w_value, jnp.pad(gains, ((0, 0), (0, 126)))], 1)
    ahead = 2
    if cube:
        first_full, taken, routes_t = gather_all(first_shard, other[:ahead], routes.T)
    else:
        routes_t = team_gather(routes.T, TEAM_BITS)
        first_full = lax.all_gather(first_shard, EVERYWHERE, axis=0, tiled=True)
        taken = exchange(other[:ahead], "dp", 2)
    qkv_full = first_full[:, :wide]
    gains_full = first_full[:, wide:].astype(F32).T
    gain_first, gain_second = gains_full[0], gains_full[1]
    second_shard = jnp.concatenate([w_out, jnp.pad(w_router, ((0, 0), (0, 128 - expert_count)))], 1)
    second_full = lax.all_gather(tie(second_shard, first_full), EVERYWHERE, axis=0, tiled=True)
    out_full = second_full[:, :D]
    router_full = second_full[:, D:D + expert_count]

    relay_bits = [1 << b for b in range(2, shards.bit_length() - 1)]
    taken_late = exchange(tie(other[ahead:], first_full), "dp", 2)
    pairs = [
        jnp.stack([own[k], taken[k] if k < ahead else taken_late[k - ahead]]) for k in range(count)
    ]

    def crossed(relayed):
        return [w for v in relayed for w in (v, exchange(v, "dp", 1))]

    def relays(pair):
        pieces = [pair]
        for bit in relay_bits:
            pieces += [exchange(v, "dp", bit) for v in pieces]
        return pieces

    first_expert = expert_at * per_owner + turn * count
    local_ids = first_expert + jnp.arange(count, dtype=jnp.int32)
    hits = jnp.any(routes_t[:, None] == local_ids[None, :, None, None], axis=2)
    row_id = lax.broadcasted_iota(jnp.int32, (tok_rows, tok_rows), 0)
    col_id = lax.broadcasted_iota(jnp.int32, (tok_rows, tok_rows), 1)
    before = jnp.where(row_id < col_id, 1.0, 0.0).astype(BF)
    ranks = product(hits.astype(BF).reshape(-1, tok_rows), before).reshape(hits.shape)
    positions = jnp.where(hits, ranks.astype(jnp.int32), -1)
    positions = jnp.pad(positions, ((0, 0), (0, 8 - count), (0, 0)), constant_values=-1)

    inputs = tokens.astype(F32)
    scale_one = rms_scale(inputs)
    normed_one = inputs * scale_one
    hidden_one = (normed_one * gain_first).astype(BF)
    qkv = product(hidden_one, qkv_full).astype(BF)
    query, key_value = qkv[:, :D], qkv[:, D:]
    place = ((dp & 1) * owners + expert_at).astype(jnp.int32).reshape(1)
    prompt_key, prompt_value = group_rows(key_value[:P_DEV])
    own_key, own_value = key_value[P_DEV:, :kvw], key_value[P_DEV:, kvw:]
    half = D // 2
    early = tie(cotangent, first_full)
    left, right = early[:, :half], early[:, half:]
    left = jnp.stack([left, exchange(left, "dp", 2)])
    right = jnp.stack([right, exchange(right, "expert", 2)])
    query, left, right = lax.optimization_barrier((query, left, right))
    parts = [left, exchange(left, "expert", 2), right, exchange(right, "dp", 2)]
    mixed, levels = attend(place, query, prompt_key, prompt_value, own_key, own_value)
    second = inputs + product(mixed, out_full)
    scale_two = rms_scale(second)
    normed_two = second * scale_two
    hidden_two = (normed_two * gain_second).astype(BF)
    logits = product(hidden_two, router_full)
    expert_ids = jnp.arange(expert_count, dtype=jnp.int32)
    chosen = jnp.any(routes[:, :, None] == expert_ids, axis=1)
    peak = jnp.max(jnp.where(chosen, logits, NEGATIVE), axis=-1, keepdims=True)
    raised = jnp.where(chosen, jnp.exp(jnp.where(chosen, logits - peak, 0.0)), 0.0)
    gates = raised / jnp.sum(raised, axis=-1, keepdims=True)

    weights = [None] * count
    crossings = [exchange(pairs[k], "dp", 1) for k in range(3)]
    sent_rows, parts, crossings = lax.optimization_barrier((hidden_two, parts, crossings))
    core_jobs = (("expert", 1),) * 4
    if cube:
        jobs = (("dp", 4), ("dp", 4)) + core_jobs + (("dp", 1), ("dp", 1))
        gives = (pairs[0], pairs[1], *parts, pairs[3], pairs[4])
        rows, gates_t, takes = team_rows(sent_rows, gates.T, jobs, gives, 2)
        parts = parts + takes[2:6]
        crossings = crossings + takes[6:8]
        relayed_pairs = takes[0:2]
        for k in range(2, count):
            relayed_pairs.append(exchange(tie(pairs[k], rows), "dp", 4))
        for k in range(count):
            weights[k] = [pairs[k], crossings[k], relayed_pairs[k]]
    else:
        rows, gates_t, takes = team_rows(sent_rows, gates.T, core_jobs, parts)
        parts = parts + takes
        for k in range(count):
            weights[k] = crossed(relays(tie(pairs[k], rows)))
    lefts = tuple((r % 2 * 4 + r // 2 % 2, r // 4) for r in range(8))
    rights = tuple((r % 2 * 4 + 2 + r // 4, r // 2 % 2) for r in range(8))
    gates_t = lax.dynamic_slice_in_dim(gates_t, first_expert, count, 1)
    gates_t = jnp.pad(gates_t, ((0, 0), (0, 8 - count), (0, 0)))
    grad_slots = gather_split(positions, parts, lefts, rights, count, slots)
    row_slots, gate_slots = gather_rows(positions, gates_t, rows, count, slots)

    results, backs, gate_rows, sums = [], [], [], []
    expert_index = dp_index
    for k in range(count):
        if cube:
            relayed_pair = weights[k][2] if k < 2 else tie(weights[k][2], gate_rows[k - 2])
            weights[k].append(exchange(relayed_pair, "dp", 1))
        y, dx, dg, keep, send = run_expert(k, expert_index, row_slots, grad_slots, gate_slots, weights[k], slots)
        results.append(y)
        backs.append(dx)
        gate_rows.append(dg)
        sums.append((keep, send))
        expert_index = tie(dp_index, dg)

    before_return = added(sums[0][0], exchange(sums[0][1], "dp", 1))
    jobs, gives, relays_in = (("dp", 1),) * 2, (sums[1][1], sums[2][1]), 0
    if cube:
        jobs, gives, relays_in = (("dp", 4),) + jobs, (before_return[2:],) + gives, 1
    routed_back, gate_grad, takes = return_rows(
        positions, backs, gate_rows, expert_count, slots, jobs, gives, relays_in
    )
    halved = [before_return, added(sums[1][0], takes[-2]), added(sums[2][0], takes[-1])]
    crossed_back = [exchange(tie(sums[k][1], routed_back), "dp", 1) for k in range(3, count)]
    relay_bits = relay_bits[::-1]

    def sent_on(keep):
        return exchange(keep[keep.shape[0] // 2:], "dp", relay_bits[0])

    def settled(keep, came):
        keep = added(keep[:keep.shape[0] // 2], came)
        for bit in relay_bits[1:]:
            middle = keep.shape[0] // 2
            keep = added(keep[:middle], exchange(keep[middle:], "dp", bit))
        return keep

    relay_came = [takes[0] if cube else sent_on(before_return)] + [sent_on(keep) for keep in halved[1:]]
    out_keep, out_send = combine_rows(tie(positions, routed_back), results, slots)
    gate_grad = gate_grad.T
    routed_back = routed_back.astype(F32)

    grad_output = cotangent.astype(F32)
    picked = jnp.where(chosen, gate_grad, 0.0)
    grad_logits = (gates * (picked - jnp.sum(gates * picked, axis=-1, keepdims=True))).astype(BF)
    grad_hidden_two = times_transposed(grad_logits, router_full) + routed_back
    grad_normed_two = grad_hidden_two * gain_second
    grad_second = grad_output + scale_two * (
        grad_normed_two - normed_two * jnp.mean(grad_normed_two * normed_two, axis=-1, keepdims=True)
    )
    grad_branch = grad_second.astype(BF)
    ones = jnp.ones((tok_rows, 128), BF)
    lane = lax.broadcasted_iota(jnp.int32, (tok_rows, 128), 1)
    wide_logits = jnp.pad(grad_logits, ((0, 0), (0, 128 - expert_count)))
    small = contract_rows(hidden_two, wide_logits) + contract_rows(
        (grad_hidden_two * normed_two).astype(BF), jnp.where(lane == expert_count, ones, jnp.zeros_like(ones))
    )
    second_grads = jnp.concatenate([contract_rows(mixed, grad_branch).astype(BF), small.astype(BF)], 1)
    grad_mixed = times_transposed(grad_branch, out_full).astype(BF)

    total = added(out_keep, exchange(out_send, "expert", 1)).reshape(2, 2, tok_rows, D)
    row_sent = total[:, 1]
    grad_mixed, total, row_sent = lax.optimization_barrier((grad_mixed, total, row_sent, halved))[:3]
    row_came = exchange(row_sent, "expert", 2)
    grad_query, dkp, dvp, dko, dvo = attend_back(
        place, query, prompt_key, prompt_value, own_key, own_value, mixed, grad_mixed, levels
    )
    halved, relay_came, crossed_back, grad_query, total, row_came = lax.optimization_barrier(
        (halved, relay_came, crossed_back, grad_query, total, row_came)
    )
    relayed = [settled(halved[k], relay_came[k]) for k in range(3)]
    halved += [added(sums[k][0], crossed_back[k - 3]) for k in range(3, count)]
    relay_came += [sent_on(keep) for keep in halved[3:]]
    theirs = exchange(jnp.stack([keep[1] for keep in relayed]), "dp", 2)
    grad_prompt = group_back(dkp, dvp)
    total = added(total[:, 0], row_came)
    pair_came = exchange(total[1], "dp", 2)
    grad_qkv = jnp.concatenate([
        grad_query, jnp.concatenate([grad_prompt, jnp.concatenate([dko, dvo], 1)], 0)
    ], 1)
    grad_hidden_one = times_transposed(grad_qkv, qkv_full)
    first_grads = jnp.concatenate([
        contract_rows(hidden_one, grad_qkv).astype(BF),
        contract_rows((grad_hidden_one * normed_one).astype(BF), ones).astype(BF),
    ], 1)
    if cube:
        share = scatter_all(first_grads, second_grads)
    else:
        share = lax.psum_scatter(
            jnp.concatenate([first_grads, second_grads], 1), EVERYWHERE, scatter_dimension=0, tiled=True
        ).astype(F32)
    grad_normed_one = grad_hidden_one * gain_first
    grad_input = grad_second + scale_one * (
        grad_normed_one - normed_one * jnp.mean(grad_normed_one * normed_one, axis=-1, keepdims=True)
    )

    share, halved, relay_came, total, pair_came = lax.optimization_barrier(
        (share, halved, relay_came, total, pair_came)
    )
    output = (second + added(total[0], pair_came).astype(F32)).astype(BF)
    first_share, second_share = share[:, :wide + 128], share[:, wide + 128:]
    relayed += [settled(halved[k], relay_came[k]) for k in range(3, count)]
    theirs = jnp.concatenate([theirs, exchange(jnp.stack([keep[1] for keep in relayed[3:]]), "dp", 2)])
    mine = jnp.stack([keep[0] for keep in relayed])
    lower = jnp.where(turn == 0, mine, theirs)
    upper = jnp.where(turn == 0, theirs, mine)
    expert_grads = jnp.concatenate([lower, upper]).astype(F32)
    return (
        output,
        grad_input.astype(BF),
        first_share[:, wide],
        first_share[:, :D],
        first_share[:, D:D + kvw],
        first_share[:, D + kvw:wide],
        second_share[:, :D].astype(F32),
        second_share[:, D:D + expert_count].astype(F32),
        second_share[:, D + expert_count].astype(F32),
        expert_grads[:, 0],
        expert_grads[:, 1],
        expert_grads[:, 2].transpose(0, 2, 1),
    )


def solution(mesh):
    rows, line = P(("dp", "expert"), None), P(("dp", "expert"))
    gate, down = P("expert", "dp", None), P("expert", None, "dp")
    return jax.shard_map(
        local,
        mesh=mesh,
        in_specs=(rows, line, rows, rows, rows, rows, rows, line, gate, gate, down, rows, rows),
        out_specs=(rows, rows, line, rows, rows, rows, rows, rows, line, gate, gate, down),
        check_vma=False,
    )
```

```python
import functools
import jax
import jax.numpy as jnp
from jax import lax
from jax.sharding import PartitionSpec as P
from jax.experimental import pallas as pl
from jax.experimental.pallas import tpu as pltpu

HD = 64
P_DEV = 128
NEGATIVE = -1e30
F32 = jnp.float32
BF = jnp.bfloat16


def dot_nt(a, b):
    return lax.dot_general(a, b, (((1,), (1,)), ((), ())), preferred_element_type=F32)


def dot_nn(a, b):
    return lax.dot_general(a, b, (((1,), (0,)), ((), ())), preferred_element_type=F32)


def dot_tn(a, b):
    return lax.dot_general(a, b, (((0,), (0,)), ((), ())), preferred_element_type=F32)


def halves(pair):
    lane = lax.broadcasted_iota(jnp.int32, pair.shape, 1)
    zero = jnp.zeros_like(pair)
    return jnp.where(lane < HD, pair, zero), jnp.where(lane < HD, zero, pair)


def placed_halves(pair_f32):
    low0, high1 = halves(pair_f32)
    high0 = pltpu.roll(low0, HD, 1)
    low1 = pltpu.roll(high1, HD, 1)
    return ((low0.astype(BF), high0.astype(BF)), (low1.astype(BF), high1.astype(BF)))


def attend_kernel(place_ref, q_ref, kp_ref, vp_ref, ko_ref, vo_ref, o_ref, lse_ref, kpad, vpad, s_scr, p_scr):
    rows = q_ref.shape[0]
    prompt = kp_ref.shape[0]
    cont = ko_ref.shape[0]
    place = place_ref[0]
    for src, dst in ((kp_ref, kpad), (vp_ref, vpad)):
        for head, pair in enumerate(placed_halves(src[...].astype(F32))):
            for half in range(2):
                dst[head, half, 0:prompt, :] = pair[half]
    for src, dst in ((ko_ref, kpad), (vo_ref, vpad)):
        for head, pair in enumerate(placed_halves(src[...].astype(F32))):
            for half in range(2):
                dst[head, half, prompt:prompt + cont, :] = pair[half]
    key_id = lax.broadcasted_iota(jnp.int32, (prompt, P_DEV), 0)
    row_id = lax.broadcasted_iota(jnp.int32, (prompt, P_DEV), 1)
    seen_prompt = key_id <= place * P_DEV + row_id
    diag = lax.broadcasted_iota(jnp.int32, (P_DEV, P_DEV), 0) <= lax.broadcasted_iota(jnp.int32, (P_DEV, P_DEV), 1)
    blocks = cont // P_DEV
    stats = []
    for chunk in range(3):
        queries = (q_ref[:, chunk * 128:(chunk + 1) * 128].astype(F32) * HD ** (-0.5)).astype(BF)
        total = None
        for half in range(2):
            position = chunk * 2 + half
            head = position // 3
            keys = kpad.at[head, half]
            scores = dot_nt(keys[0:prompt, :], queries)
            first = jnp.where(seen_prompt, scores[:, 0:P_DEV], NEGATIVE)
            rest = scores[:, P_DEV:]
            s_scr[0:prompt, 0:P_DEV] = first
            s_scr[0:prompt, P_DEV:] = rest
            top = jnp.concatenate([jnp.max(first, 0, keepdims=True), jnp.max(rest, 0, keepdims=True)], 1)
            tops = [top[:, i * P_DEV:(i + 1) * P_DEV] for i in range(1 + blocks)]
            for block in range(blocks):
                start = (1 + block) * P_DEV
                at = prompt + block * P_DEV
                own = dot_nt(keys[at:at + P_DEV, :], queries[start:, :])
                edge = jnp.where(diag, own[:, 0:P_DEV], NEGATIVE)
                s_scr[at:at + P_DEV, start:start + P_DEV] = edge
                tops[1 + block] = jnp.maximum(tops[1 + block], jnp.max(edge, 0, keepdims=True))
                if block + 1 < blocks:
                    later = own[:, P_DEV:]
                    s_scr[at:at + P_DEV, start + P_DEV:] = later
                    best = jnp.max(later, 0, keepdims=True)
                    for i in range(block + 1, blocks):
                        at_i = (i - block - 1) * P_DEV
                        tops[1 + i] = jnp.maximum(tops[1 + i], best[:, at_i:at_i + P_DEV])
            top = jnp.concatenate(tops, 1)
            weights = jnp.exp(s_scr[0:prompt, :] - top)
            mass = jnp.sum(weights, 0, keepdims=True)
            masses = [mass[:, i * P_DEV:(i + 1) * P_DEV] for i in range(1 + blocks)]
            values = vpad.at[head, half]
            mixed = dot_tn(values[0:prompt, :], weights.astype(BF))
            for block in range(blocks):
                start = (1 + block) * P_DEV
                at = prompt + block * P_DEV
                part = jnp.exp(s_scr[at:at + P_DEV, start:] - top[:, start:])
                p_scr[block * P_DEV:(block + 1) * P_DEV, start:] = part.astype(BF)
                if block:
                    p_scr[block * P_DEV:(block + 1) * P_DEV, P_DEV:start] = jnp.zeros((P_DEV, block * P_DEV), BF)
                part_mass = jnp.sum(part, 0, keepdims=True)
                for i in range(block, blocks):
                    at_i = (i - block) * P_DEV
                    masses[1 + i] = masses[1 + i] + part_mass[:, at_i:at_i + P_DEV]
            own_mixed = dot_tn(values[prompt:prompt + cont, :], p_scr[:, P_DEV:])
            mass = jnp.concatenate(masses, 1)
            scale = 1.0 / mass
            mixed = jnp.concatenate([mixed[:, 0:P_DEV], mixed[:, P_DEV:] + own_mixed], 1) * scale
            total = mixed if total is None else total + mixed
            stats.append(top + jnp.log(mass))
        o_ref[:, chunk * 128:(chunk + 1) * 128] = jnp.transpose(total).astype(BF)
    lse_ref[0] = jnp.concatenate(stats + [jnp.zeros((2, rows), F32)], 0)


def attend(place, query, prompt_key, prompt_value, own_key, own_value):
    rows = query.shape[0]
    prompt = prompt_key.shape[0]
    cont = own_key.shape[0]
    pairs = prompt_key.shape[1] // 128
    col = lambda i: (0, i)
    return pl.pallas_call(
        attend_kernel,
        grid=(pairs,),
        in_specs=[
            pl.BlockSpec(memory_space=pltpu.SMEM),
            pl.BlockSpec((rows, 384), col),
            pl.BlockSpec((prompt, 128), col),
            pl.BlockSpec((prompt, 128), col),
            pl.BlockSpec((cont, 128), col),
            pl.BlockSpec((cont, 128), col),
        ],
        out_specs=[pl.BlockSpec((rows, 384), col), pl.BlockSpec((1, 8, rows), lambda i: (i, 0, 0))],
        out_shape=[
            jax.ShapeDtypeStruct(query.shape, BF),
            jax.ShapeDtypeStruct((pairs, 8, rows), F32),
        ],
        scratch_shapes=[
            pltpu.VMEM((2, 2, prompt + cont, 128), BF),
            pltpu.VMEM((2, 2, prompt + cont, 128), BF),
            pltpu.VMEM((prompt + cont, rows), F32),
            pltpu.VMEM((cont, rows), BF),
        ],
        cost_estimate=pl.CostEstimate(flops=10**6, bytes_accessed=10**6, transcendentals=0),
        name="attend",
    )(place, query, prompt_key, prompt_value, own_key, own_value)


def attend_back_kernel(place_ref, q_ref, kp_ref, vp_ref, ko_ref, vo_ref, o_ref, do_ref, lse_ref,
                       dq_ref, dkp_ref, dvp_ref, dko_ref, dvo_ref, kpad, vpad, dk_acc, dv_acc):
    rows = q_ref.shape[0]
    prompt = kp_ref.shape[0]
    cont = ko_ref.shape[0]
    step = 2 * P_DEV
    place = place_ref[0]
    for src, dst, at, size in ((kp_ref, kpad, 0, prompt), (vp_ref, vpad, 0, prompt),
                               (ko_ref, kpad, prompt, cont), (vo_ref, vpad, prompt, cont)):
        for head, pair in enumerate(placed_halves(src[...].astype(F32))):
            for half in range(2):
                dst[head, half, at:at + size, :] = pair[half]
    dk_acc[...] = jnp.zeros_like(dk_acc)
    dv_acc[...] = jnp.zeros_like(dv_acc)
    for chunk in range(3):
        lanes = slice(chunk * 128, (chunk + 1) * 128)
        scaled = q_ref[:, lanes].astype(F32) * HD ** (-0.5)
        queries = scaled.astype(BF)
        query_halves = [part.astype(BF) for part in halves(scaled)]
        outs = o_ref[:, lanes].astype(F32)
        grads_f32 = do_ref[:, lanes].astype(F32)
        grads = do_ref[:, lanes]
        grad_halves = [part.astype(BF) for part in halves(grads_f32)]
        inner = jnp.transpose(outs * grads_f32)
        total = jnp.zeros((128, rows), F32)
        for half in range(2):
            position = chunk * 2 + half
            head = position // 3
            level = lse_ref[0, position:position + 1, :]
            delta = jnp.sum(inner[half * HD:(half + 1) * HD, :], 0, keepdims=True)

            def block(at, cols, mask, queries=queries, grads=grads, query_half=query_halves[half],
                      grad_half=grad_halves[half], level=level, delta=delta, head=head, half=half):
                keys = kpad[head, half, pl.ds(at, step), :]
                values = vpad[head, half, pl.ds(at, step), :]
                scores = dot_nt(keys, queries[cols, :])
                weights = jnp.exp(mask(scores) - level[:, cols])
                grad_weights = dot_nt(values, grads[cols, :])
                grad_scores = weights * (grad_weights - delta[:, cols])
                low_weights = weights.astype(BF)
                low_scores = grad_scores.astype(BF)
                dv_acc[head, pl.ds(at, step), :] += dot_nn(low_weights, grad_half[cols, :])
                dk_acc[head, pl.ds(at, step), :] += dot_nn(low_scores, query_half[cols, :])
                return dot_tn(keys, low_scores)

            def prompt_step(i, carry):
                at = pl.multiple_of(i * step, step)

                def mask(scores):
                    key_id = at + lax.broadcasted_iota(jnp.int32, (step, P_DEV), 0)
                    row_id = lax.broadcasted_iota(jnp.int32, (step, P_DEV), 1)
                    first = jnp.where(key_id <= place * P_DEV + row_id, scores[:, 0:P_DEV], NEGATIVE)
                    return jnp.concatenate([first, scores[:, P_DEV:]], 1)

                return carry + block(at, slice(0, rows), mask)

            total = lax.fori_loop(0, prompt // step, prompt_step, total)
            for own in range(cont // step):
                start = P_DEV + own * step

                def mask(scores):
                    key_id = lax.broadcasted_iota(jnp.int32, (step, step), 0)
                    row_id = lax.broadcasted_iota(jnp.int32, (step, step), 1)
                    edge = jnp.where(key_id <= row_id, scores[:, 0:step], NEGATIVE)
                    if scores.shape[1] == step:
                        return edge
                    return jnp.concatenate([edge, scores[:, step:]], 1)

                part = block(prompt + own * step, slice(start, rows), mask)
                total = jnp.concatenate([total[:, 0:start], total[:, start:] + part], 1)
        dq_ref[:, lanes] = (jnp.transpose(total) * HD ** (-0.5)).astype(BF)
    for acc, out_prompt, out_own in ((dk_acc, dkp_ref, dko_ref), (dv_acc, dvp_ref, dvo_ref)):
        low0, high0 = halves(acc[0])
        low1, high1 = halves(acc[1])
        merged = low0 + pltpu.roll(high0, HD, 1) + high1 + pltpu.roll(low1, HD, 1)
        out_prompt[...] = merged[0:prompt].astype(BF)
        out_own[...] = merged[prompt:].astype(BF)


def attend_back(place, query, prompt_key, prompt_value, own_key, own_value, mixed, grad, lse):
    rows = query.shape[0]
    prompt = prompt_key.shape[0]
    cont = own_key.shape[0]
    pairs = prompt_key.shape[1] // 128
    col = lambda i: (0, i)
    wide = pl.BlockSpec((rows, 384), col)
    keys_p = pl.BlockSpec((prompt, 128), col)
    keys_o = pl.BlockSpec((cont, 128), col)
    return pl.pallas_call(
        attend_back_kernel,
        grid=(pairs,),
        in_specs=[
            pl.BlockSpec(memory_space=pltpu.SMEM),
            wide, keys_p, keys_p, keys_o, keys_o, wide, wide,
            pl.BlockSpec((1, 8, rows), lambda i: (i, 0, 0)),
        ],
        out_specs=[wide, keys_p, keys_p, keys_o, keys_o],
        out_shape=[
            jax.ShapeDtypeStruct(query.shape, BF),
            jax.ShapeDtypeStruct(prompt_key.shape, BF),
            jax.ShapeDtypeStruct(prompt_key.shape, BF),
            jax.ShapeDtypeStruct(own_key.shape, BF),
            jax.ShapeDtypeStruct(own_key.shape, BF),
        ],
        scratch_shapes=[
            pltpu.VMEM((2, 2, prompt + cont, 128), BF),
            pltpu.VMEM((2, 2, prompt + cont, 128), BF),
            pltpu.VMEM((2, prompt + cont, 128), F32),
            pltpu.VMEM((2, prompt + cont, 128), F32),
        ],
        cost_estimate=pl.CostEstimate(flops=10**6, bytes_accessed=10**6, transcendentals=0),
        name="attend_back",
    )(place, query, prompt_key, prompt_value, own_key, own_value, mixed, grad, lse)


SLOTS_ALIGN = 16


def gather_kernel(count, with_gates, pos_ref, *refs):
    if with_gates:
        gate_ref, rows_ref, x_ref, g_ref, pick = refs
    else:
        rows_ref, x_ref, pick = refs
    tokens = rows_ref.shape[1]
    slots = x_ref.shape[1] // count
    half = rows_ref.shape[2] // 2
    slot_id = lax.broadcasted_iota(jnp.int32, (slots, tokens), 0)
    for k in range(count):
        hit = slot_id == pos_ref[0, k:k + 1, :]
        pick[k * slots:(k + 1) * slots, :] = jnp.where(hit, 1.0, 0.0).astype(BF)
        if with_gates:
            gate = jnp.sum(jnp.where(hit, gate_ref[0, k:k + 1, :], 0.0), 1, keepdims=True)
            g_ref[0, k * slots:(k + 1) * slots, :] = jnp.broadcast_to(gate, (slots, 128))
    x_ref[0, :, 0:half] = dot_nn(pick[...], rows_ref[0, :, 0:half]).astype(BF)
    x_ref[0, :, half:] = dot_nn(pick[...], rows_ref[0, :, half:]).astype(BF)


def gather_rows(positions, gates, rows, count, slots):
    sources, tokens, width = rows.shape
    size = count * slots
    table = pl.BlockSpec((1, 8, tokens), lambda s: (s, 0, 0))
    block = lambda shape: pl.BlockSpec((1,) + shape, lambda s: (s, 0, 0))
    tables = [positions] if gates is None else [positions, gates]
    outs = [((size, width), BF)] if gates is None else [((size, width), BF), ((size, 128), F32)]
    return pl.pallas_call(
        functools.partial(gather_kernel, count, gates is not None),
        grid=(sources,),
        in_specs=[table] * len(tables) + [block((tokens, width))],
        out_specs=[block(shape) for shape, _ in outs],
        out_shape=[jax.ShapeDtypeStruct((sources,) + shape, dtype) for shape, dtype in outs],
        scratch_shapes=[pltpu.VMEM((size, tokens), BF)],
        cost_estimate=pl.CostEstimate(flops=10**6, bytes_accessed=10**6, transcendentals=0),
        name="gather_rows",
    )(*tables, rows)


def gather_split_kernel(count, lefts, rights, pos_ref, *refs):
    parts = refs[0:len(set(i for i, _ in lefts)) + len(set(i for i, _ in rights))]
    x_ref, pick, left, right, sems = refs[len(parts):]
    s = pl.program_id(0)
    sources = len(lefts)
    slots = x_ref.shape[1] // count
    tokens, half = left.shape[1:]

    def fetch(i):
        (a, at), (b, bt), slot = lefts[i], rights[i], i % 2
        return (
            pltpu.make_async_copy(parts[a].at[at], left.at[slot], sems.at[0, slot]),
            pltpu.make_async_copy(parts[b].at[bt], right.at[slot], sems.at[1, slot]),
        )

    @pl.when(s == 0)
    def _():
        for copy in fetch(0):
            copy.start()

    for i in range(1, sources):

        @pl.when(s == i - 1)
        def _(i=i):
            for copy in fetch(i):
                copy.start()

    slot_id = lax.broadcasted_iota(jnp.int32, (slots, tokens), 0)
    for k in range(count):
        hit = slot_id == pos_ref[0, k:k + 1, :]
        pick[k * slots:(k + 1) * slots, :] = jnp.where(hit, 1.0, 0.0).astype(BF)
    slot = lax.rem(s, 2)
    pltpu.make_async_copy(parts[0].at[0], left.at[slot], sems.at[0, slot]).wait()
    pltpu.make_async_copy(parts[0].at[0], right.at[slot], sems.at[1, slot]).wait()
    x_ref[0, :, 0:half] = dot_nn(pick[...], left[slot]).astype(BF)
    x_ref[0, :, half:] = dot_nn(pick[...], right[slot]).astype(BF)


def gather_split(positions, parts, lefts, rights, count, slots):
    _, tokens, half = parts[0].shape
    sources, size = len(lefts), count * slots
    return pl.pallas_call(
        functools.partial(gather_split_kernel, count, lefts, rights),
        grid=(sources,),
        in_specs=[pl.BlockSpec((1, 8, tokens), lambda s: (s, 0, 0))] + [pl.BlockSpec(memory_space=pl.ANY)] * len(parts),
        out_specs=pl.BlockSpec((1, size, 2 * half), lambda s: (s, 0, 0)),
        out_shape=jax.ShapeDtypeStruct((sources, size, 2 * half), BF),
        scratch_shapes=[
            pltpu.VMEM((size, tokens), BF),
            pltpu.VMEM((2, tokens, half), BF),
            pltpu.VMEM((2, tokens, half), BF),
            pltpu.SemaphoreType.DMA((2, 2)),
        ],
        cost_estimate=pl.CostEstimate(flops=10**6, bytes_accessed=10**6, transcendentals=0),
        name="gather_split",
    )(positions, *parts)


def expert_kernel(k, shards, slots, dp_ref, x_ref, g_ref, gate_ref, *refs):
    w_refs = refs[0:shards // 2]
    (y_out, dx_out, dg_out, keep_out, send_out,
     xs, gs, gates, ws, ys, dxs, dgs, dab, actg, stage,
     in_sem, w_sem, out_sem, grad_sem) = refs[shards // 2:]
    dp = dp_ref[0]
    sources = x_ref.shape[0]
    width = xs.shape[1]
    piece = width // shards
    hidden = ws.shape[2]
    mine = pl.ds(k * slots, slots)

    def row_copies(s):
        at = pl.ds(pl.multiple_of(s * slots, 16), slots)
        return (
            pltpu.make_async_copy(x_ref.at[s, mine, :], xs.at[at, :], in_sem.at[0, s]),
            pltpu.make_async_copy(g_ref.at[s, mine, :], gs.at[at, :], in_sem.at[1, s]),
            pltpu.make_async_copy(gate_ref.at[s, mine, :], gates.at[at, :], in_sem.at[2, s]),
        )

    weight_copies = [
        pltpu.make_async_copy(
            w_refs[(r & 1) + 2 * (r >> 2)].at[(r >> 1) & 1], ws.at[:, pl.ds(pl.multiple_of((dp ^ r) * piece, 16), piece), :], w_sem.at[r]
        )
        for r in range(shards)
    ]
    for s in range(sources):
        for copy in row_copies(s):
            copy.start()
        if s == 1:
            for copy in weight_copies:
                copy.start()
    for copy in weight_copies:
        copy.wait()
    chunk = 2 * slots

    def out_copies(c):
        at = pl.ds(pl.multiple_of(c * chunk, 32), chunk)
        return [
            pltpu.make_async_copy(src.at[at, :], dst.at[at, :], out_sem.at[i, c])
            for i, (src, dst) in enumerate(((ys, y_out), (dxs, dx_out), (dgs, dg_out)))
        ]

    def forward_chunk(c, carry):
        for copy in row_copies(2 * c) + row_copies(2 * c + 1):
            copy.wait()
        rows = pl.ds(pl.multiple_of(c * chunk, 32), chunk)
        x = xs[rows, :]
        a = dot_nn(x, ws[0])
        b = dot_nn(x, ws[1])
        pulled = dot_nn(gs[rows, :], ws[2])
        gate = gates[rows, 0:1]
        sig = jax.nn.sigmoid(a)
        silu = a * sig
        act = silu * b
        dgs[rows, :] = jnp.broadcast_to(jnp.sum(act * pulled, 1, keepdims=True), (chunk, 128))
        weighted = (gate * act).astype(BF)
        actg[rows, :] = weighted
        dact = gate * pulled
        da = (dact * b * sig * (1.0 + a * (1.0 - sig))).astype(BF)
        db = (dact * silu).astype(BF)
        dab[rows, 0:hidden] = da
        dab[rows, hidden:] = db
        ys[rows, :] = dot_nt(weighted, ws[2]).astype(BF)
        dxs[rows, :] = (dot_nt(da, ws[0]) + dot_nt(db, ws[1])).astype(BF)
        for copy in out_copies(c):
            copy.start()
        return carry

    lax.fori_loop(0, sources // 2, forward_chunk, 0)
    block = 384
    inner = block // piece
    high = dp // inner
    low = dp % inner

    def grad_copies(jr):
        slot = lax.rem(jr, 2)
        copies = []
        for ri in range(inner):
            dst = (send_out if ri % 2 else keep_out).at[jr * (inner // 2) + ri // 2]
            src = stage.at[slot, :, pl.ds(pl.multiple_of((low ^ ri) * piece, 16), piece), :]
            copies.append(pltpu.make_async_copy(src, dst, grad_sem.at[slot, ri]))
        return copies

    def grad_block(jr, carry):
        slot = lax.rem(jr, 2)

        @pl.when(jr >= 2)
        def _():
            for copy in grad_copies(jr - 2):
                copy.wait()

        cols = pl.ds(pl.multiple_of((high ^ jr) * block, 128), block)
        left = dot_tn(xs[:, cols], dab[...])
        stage[slot, 0] = left[:, 0:hidden].astype(BF)
        stage[slot, 1] = left[:, hidden:].astype(BF)
        stage[slot, 2] = dot_tn(gs[:, cols], actg[...]).astype(BF)
        for copy in grad_copies(jr):
            copy.start()
        return carry

    blocks = width // block
    lax.fori_loop(0, blocks, grad_block, 0)
    for jr in range(blocks - 2, blocks):
        for copy in grad_copies(jr):
            copy.wait()
    for c in range(sources // 2):
        for copy in out_copies(c):
            copy.wait()


def run_expert(k, dp_index, xs, gs, gates, weights, slots):
    sources, shards = xs.shape[0], 2 * len(weights)
    rows = sources * slots
    width = xs.shape[2]
    piece, hidden = weights[0].shape[2:]
    inner = 384 // piece
    anywhere = pl.BlockSpec(memory_space=pl.ANY)
    return pl.pallas_call(
        functools.partial(expert_kernel, k, shards, slots),
        in_specs=[pl.BlockSpec(memory_space=pltpu.SMEM)] + [anywhere] * (3 + shards // 2),
        out_specs=[anywhere] * 5,
        out_shape=[
            jax.ShapeDtypeStruct((rows, width), BF),
            jax.ShapeDtypeStruct((rows, width), BF),
            jax.ShapeDtypeStruct((rows, 128), F32),
            jax.ShapeDtypeStruct((shards // 2, 3, piece, hidden), BF),
            jax.ShapeDtypeStruct((shards // 2, 3, piece, hidden), BF),
        ],
        scratch_shapes=[
            pltpu.VMEM((rows, width), BF),
            pltpu.VMEM((rows, width), BF),
            pltpu.VMEM((rows, 128), F32),
            pltpu.VMEM((3, width, hidden), BF),
            pltpu.VMEM((rows, width), BF),
            pltpu.VMEM((rows, width), BF),
            pltpu.VMEM((rows, 128), F32),
            pltpu.VMEM((rows, 2 * hidden), BF),
            pltpu.VMEM((rows, hidden), BF),
            pltpu.VMEM((2, 3, 384, hidden), BF),
            pltpu.SemaphoreType.DMA((3, sources)),
            pltpu.SemaphoreType.DMA((shards,)),
            pltpu.SemaphoreType.DMA((3, sources // 2)),
            pltpu.SemaphoreType.DMA((2, inner)),
        ],
        compiler_params=pltpu.CompilerParams(vmem_limit_bytes=60 * 2**20),
        cost_estimate=pl.CostEstimate(flops=10**6, bytes_accessed=10**6, transcendentals=0),
        name="expert",
    )(dp_index, xs, gs, gates, *weights)


def combine_kernel(count, slots, pos_ref, *refs):
    y_refs = refs[0:count]
    keep, send, ys, pick = refs[count:]
    tokens = pos_ref.shape[2]
    half = keep.shape[2] // 2
    slot_id = lax.broadcasted_iota(jnp.int32, (slots, tokens), 0)
    for j, out in enumerate((keep, send)):
        for k in range(count):
            rows = slice(k * slots, (k + 1) * slots)
            ys[rows, :] = y_refs[k][j * slots:(j + 1) * slots, :]
            pick[rows, :] = jnp.where(slot_id == pos_ref[j, k:k + 1, :], 1.0, 0.0).astype(BF)
        out[0, :, 0:half] = dot_tn(pick[...], ys[:, 0:half]).astype(BF)
        out[0, :, half:] = dot_tn(pick[...], ys[:, half:]).astype(BF)


def combine_rows(positions, results, slots):
    sources, _, tokens = positions.shape
    count = len(results)
    width = results[0].shape[1]
    out = pl.BlockSpec((1, tokens, width), lambda i: (i, 0, 0))
    return pl.pallas_call(
        functools.partial(combine_kernel, count, slots),
        grid=(sources // 2,),
        in_specs=[pl.BlockSpec((2, 8, tokens), lambda i: (i, 0, 0))]
        + [pl.BlockSpec((2 * slots, width), lambda i: (i, 0))] * count,
        out_specs=[out] * 2,
        out_shape=[jax.ShapeDtypeStruct((sources // 2, tokens, width), BF)] * 2,
        scratch_shapes=[pltpu.VMEM((count * slots, width), BF), pltpu.VMEM((count * slots, tokens), BF)],
        cost_estimate=pl.CostEstimate(flops=10**6, bytes_accessed=10**6, transcendentals=0),
        name="combine_rows",
    )(positions, *results)


def barrier_with(partners):
    sem = pltpu.get_barrier_semaphore()
    for partner in partners:
        pl.semaphore_signal(sem, inc=1, device_id=partner, device_id_type=pl.DeviceIdType.MESH)
    pl.semaphore_wait(sem, len(partners))


def flipped(axis, mask):
    at = lax.axis_index(axis)
    bit = lax.rem(lax.div(at, mask), 2)
    return {axis: at + mask * (1 - 2 * bit)}


def own_bit(axis, mask):
    return lax.rem(lax.div(lax.axis_index(axis), mask), 2)


TEAM = (("dp", 2), ("expert", 2), ("expert", 1))
GROUP = (("dp", 1), ("expert", 2), ("expert", 1))
CUBE = (("dp", 4), ("dp", 2), ("dp", 1), ("expert", 2), ("expert", 1))
ROTATIONS = ((0, 1, 2, 3), (0, 2, 3, 1), (0, 3, 1, 2))


def gather_all_kernel(pieces, segments, count, *refs):
    shards, give_ref, routes_ref = refs[0:count], refs[count], refs[count + 1]
    fulls, take_ref, team_ref = refs[count + 2:2 * count + 2], refs[2 * count + 2], refs[2 * count + 3]
    own_sem, send_sem, recv_sem, piece_sem, team_sem = refs[2 * count + 4:]
    barrier_with([flipped(*dim) for dim in CUBE])
    bits = [own_bit(*dim) for dim in CUBE]
    here = tuple(pl.ds(bit, 1) for bit in bits)
    own = [pltpu.make_async_copy(shards[i], fulls[i].at[here], own_sem.at[i]) for i in range(count)]
    own.append(pltpu.make_async_copy(routes_ref, team_ref.at[0:1, 0:1, 0:1], own_sem.at[count]))
    for copy in own:
        copy.start()
    for copy in own:
        copy.wait()

    def routes_step(step):
        index = [pl.ds(0, 2) if d < step else pl.ds(0, 1) for d in range(3)]
        src = team_ref.at[tuple(index)]
        index[step] = pl.ds(1, 1)
        return pltpu.make_async_remote_copy(
            src_ref=src, dst_ref=team_ref.at[tuple(index)], send_sem=team_sem.at[0, step],
            recv_sem=team_sem.at[1, step], device_id=flipped(*TEAM[step]), device_id_type=pl.DeviceIdType.MESH,
        )

    def spread(step, n, gathered, dim):
        source, start, width, _ = segments[n]
        at = tuple(pl.ds(0, 2) if d in gathered else pl.ds(bits[d], 1) for d in range(5))
        ref = fulls[source].at[at + (slice(None), pl.ds(start, width))]
        return pltpu.make_async_remote_copy(
            src_ref=ref, dst_ref=ref, send_sem=send_sem.at[step, n], recv_sem=recv_sem.at[step, n],
            device_id=flipped(*CUBE[dim]), device_id_type=pl.DeviceIdType.MESH,
        )

    def hand(k):
        return pltpu.make_async_remote_copy(
            src_ref=give_ref.at[k], dst_ref=take_ref.at[k], send_sem=piece_sem.at[0, k],
            recv_sem=piece_sem.at[1, k], device_id=flipped("dp", 2), device_id_type=pl.DeviceIdType.MESH,
        )

    copies, passed = [], []
    running = [None] * len(segments)
    for step in range(5):
        if 0 < step < 4:
            routes_step(step - 1).wait()
        if step < 3:
            routes_step(step).start()
        for n, segment in enumerate(segments):
            if running[n] is not None:
                running[n].wait_recv()
            order = ROTATIONS[segment[3]] + (4,)
            copy = spread(step, n, order[:step], order[step])
            copy.start()
            copies.append(copy)
            running[n] = copy
        for k in range(pieces) if step == 4 else range(step, min(step + 1, pieces)):
            if step == 4 and k < 4:
                continue
            passed.append(hand(k))
            passed[-1].start()
    for copy in running:
        copy.wait_recv()
    for copy in copies:
        copy.wait_send()
    for copy in passed:
        copy.wait()


def gather_all(shards, segments, give, routes):
    rows = shards[0].shape[0]
    count, pieces = len(shards), give.shape[0]
    anywhere, vmem = pl.BlockSpec(memory_space=pl.ANY), pl.BlockSpec(memory_space=pltpu.VMEM)
    outs = pl.pallas_call(
        functools.partial(gather_all_kernel, pieces, segments, count),
        in_specs=[vmem] * count + [anywhere, vmem],
        out_specs=[anywhere] * (count + 2),
        out_shape=[jax.ShapeDtypeStruct((2,) * 5 + shard.shape, BF) for shard in shards]
        + [jax.ShapeDtypeStruct(give.shape, BF), jax.ShapeDtypeStruct((2, 2, 2) + routes.shape, jnp.int32)],
        scratch_shapes=[
            pltpu.SemaphoreType.DMA((count + 1,)),
            pltpu.SemaphoreType.DMA((5, len(segments))),
            pltpu.SemaphoreType.DMA((5, len(segments))),
            pltpu.SemaphoreType.DMA((2, pieces)),
            pltpu.SemaphoreType.DMA((2, 3)),
        ],
        compiler_params=pltpu.CompilerParams(collective_id=1, has_side_effects=True),
        name="gather_all",
    )(*[shard.reshape((1,) * 5 + shard.shape) for shard in shards], give, routes.reshape((1, 1, 1) + routes.shape))
    fulls = [full.reshape(32 * rows, full.shape[-1]) for full in outs[:count]]
    return fulls, outs[count], outs[count + 1].reshape((8,) + routes.shape)


def job_copies(jobs, gives, takes, sems):
    return [
        pltpu.make_async_remote_copy(
            src_ref=gives[j], dst_ref=takes[j], send_sem=sems.at[0, j], recv_sem=sems.at[1, j],
            device_id=flipped(*jobs[j]), device_id_type=pl.DeviceIdType.MESH,
        )
        for j in range(len(jobs))
    ]


def partners_of(dims, jobs):
    return [flipped(*dim) for dim in dict.fromkeys(tuple(dims) + tuple(jobs))]


def inner_plane():
    return own_bit("dp", 2) != own_bit("dp", 4)


def across():
    at = lax.axis_index("dp")
    return {"dp": at + 2 * (1 - 2 * own_bit("dp", 2)) + 4 * (1 - 2 * own_bit("dp", 4))}


def team_rows_kernel(jobs, relays, rows_ref, gates_ref, *refs):
    count, lanes = len(jobs), len(relays)
    gives, pairs = refs[0:count], refs[count:count + lanes]
    refs = refs[count + lanes:]
    if lanes:
        other_ref, refs = refs[0], refs[1:]
    all_ref, table_ref = refs[0:2]
    takes, far = refs[2:2 + count], refs[2 + count:2 + count + lanes]
    own_sem, send_sem, recv_sem, job_sem, relay_sem = refs[2 + count + lanes:]
    partners = partners_of(TEAM, jobs)
    if lanes:
        partners += [flipped("dp", 4), across()]
    barrier_with(partners)
    half = all_ref.shape[4] // 2
    own = [
        pltpu.make_async_copy(rows_ref, all_ref.at[0:1, 0:1, 0:1], own_sem.at[0]),
        pltpu.make_async_copy(gates_ref, table_ref.at[0:1, 0:1, 0:1], own_sem.at[1]),
    ]
    for copy in own:
        copy.start()

    def leg(j, n):
        src = (pairs[j].at[0], pairs[j].at[1], other_ref.at[relays[j]])[n]
        return pltpu.make_async_remote_copy(
            src_ref=src, dst_ref=far[j].at[min(n, 1)], send_sem=relay_sem.at[n, j],
            recv_sem=relay_sem.at[3 + min(n, 1), j], device_id=across() if n == 2 else flipped("dp", 4),
            device_id_type=pl.DeviceIdType.MESH,
        )

    for copy in own:
        copy.wait()
    flows = (
        (all_ref, (0, 1, 2), (slice(None), pl.ds(0, half))),
        (all_ref, (1, 0, 2), (slice(None), pl.ds(half, half))),
        (table_ref, (0, 1, 2), (slice(None), slice(None))),
    )
    copies = []
    running = [None] * 3
    for step in range(3):
        for f, (ref, order, tail) in enumerate(flows):
            if running[f] is not None:
                running[f].wait_recv()
            dim = order[step]
            index = [pl.ds(0, 2) if d in order[:step] else pl.ds(0, 1) for d in range(3)]
            src = ref.at[tuple(index) + tail]
            index[dim] = pl.ds(1, 1)
            copy = pltpu.make_async_remote_copy(
                src_ref=src, dst_ref=ref.at[tuple(index) + tail], send_sem=send_sem.at[step, f],
                recv_sem=recv_sem.at[step, f], device_id=flipped(*TEAM[dim]), device_id_type=pl.DeviceIdType.MESH,
            )
            copy.start()
            copies.append(copy)
            running[f] = copy
        if step == 0:
            background = job_copies(jobs, gives, takes, job_sem)
            for copy in background:
                copy.start()
            if lanes:

                @pl.when(inner_plane())
                def _():
                    for j in range(lanes):
                        for n in range(3):
                            leg(j, n).start()

        if step == 1 and lanes:

            @pl.when(jnp.logical_not(inner_plane()))
            def _():
                for j in range(lanes):
                    leg(j, 0).start()

    for copy in running:
        copy.wait_recv()
    for copy in copies:
        copy.wait_send()
    for copy in background:
        copy.wait()
    for j in range(lanes):
        leg(j, 0).wait()
        leg(j, 1).wait_recv()
    if lanes:

        @pl.when(inner_plane())
        def _():
            for j in range(lanes):
                leg(j, 1).wait_send()
                leg(j, 2).wait_send()


def team_rows(rows, gates, jobs=(), gives=(), relays=(), pairs=(), other=None):
    tokens, width = rows.shape
    table = gates.shape
    anywhere = pl.BlockSpec(memory_space=pl.ANY)
    extra = [] if other is None else [other]
    full, tables, *takes = pl.pallas_call(
        functools.partial(team_rows_kernel, tuple(jobs), tuple(relays)),
        in_specs=[pl.BlockSpec(memory_space=pltpu.VMEM)] * 2 + [anywhere] * (len(jobs) + len(pairs) + len(extra)),
        out_specs=[anywhere] * (2 + len(jobs) + len(pairs)),
        out_shape=[
            jax.ShapeDtypeStruct((2, 2, 2, tokens, width), BF),
            jax.ShapeDtypeStruct((2, 2, 2) + table, F32),
        ] + [jax.ShapeDtypeStruct(give.shape, give.dtype) for give in list(gives) + list(pairs)],
        scratch_shapes=[
            pltpu.SemaphoreType.DMA((2,)),
            pltpu.SemaphoreType.DMA((3, 3)),
            pltpu.SemaphoreType.DMA((3, 3)),
            pltpu.SemaphoreType.DMA((2, max(1, len(jobs)))),
            pltpu.SemaphoreType.DMA((5, max(1, len(relays)))),
        ],
        compiler_params=pltpu.CompilerParams(collective_id=2, has_side_effects=True),
        name="team_rows",
    )(rows.reshape(1, 1, 1, tokens, width), gates.reshape((1, 1, 1) + table), *gives, *pairs, *extra)
    return full.reshape(8, tokens, width), tables.reshape((8,) + table), takes


def add_into(acc, at, other):
    acc[at] = (acc[at].astype(F32) + other.astype(F32)).astype(BF)


def return_kernel(count, slots, jobs, relays, pos_ref, *refs):
    y_refs, dg_refs = refs[0:count], refs[count:2 * count]
    refs = refs[2 * count:]
    gives, takes = refs[0:len(jobs)], refs[len(jobs) + 2:2 * len(jobs) + 2]
    out_ref, gate_ref = refs[len(jobs):len(jobs) + 2]
    (acc, core_in, row_in, pair_in, last_in, ys, pick, table, table_core, table_row, table_pair,
     load_sem, send_sem, recv_sem, job_sem) = refs[2 * len(jobs) + 2:]
    tokens, width = out_ref.shape
    half = width // 2
    barrier_with(partners_of(TEAM, jobs))
    background = job_copies(jobs, gives, takes, job_sem)
    for copy in background[relays:]:
        copy.start()
    if relays:

        @pl.when(jnp.logical_not(inner_plane()))
        def _():
            for copy in background[:relays]:
                copy.start()

    first = (lax.axis_index("expert") * 2 + own_bit("dp", 2)) * count
    slot_id = lax.broadcasted_iota(jnp.int32, (slots, tokens), 0)

    def remote(src, dst, n, dim):
        return pltpu.make_async_remote_copy(
            src_ref=src, dst_ref=dst, send_sem=send_sem.at[n], recv_sem=recv_sem.at[n],
            device_id=flipped(*TEAM[dim]), device_id_type=pl.DeviceIdType.MESH,
        )

    def loads(r, slot):
        return [
            pltpu.make_async_copy(
                y_refs[k].at[pl.ds(pl.multiple_of(r * slots, 16), slots), :],
                ys.at[slot, pl.ds(k * slots, slots), :], load_sem.at[slot, k],
            )
            for k in range(count)
        ]

    table[...] = jnp.zeros_like(table)

    def build(step, r, following):
        slot = lax.rem(step, 2)
        for copy in loads(r, slot):
            copy.wait()

        @pl.when(step < 7)
        def _():
            for copy in loads(following, 1 - slot):
                copy.start()

        for k in range(count):
            hit = slot_id == pos_ref[r, k:k + 1, :]
            pick[k * slots:(k + 1) * slots, :] = jnp.where(hit, 1.0, 0.0).astype(BF)
            pulled = dg_refs[k][pl.ds(pl.multiple_of(r * slots, 16), slots), 0:1]
            table[r, pl.ds(first + k, 1), :] = jnp.sum(jnp.where(hit, pulled, 0.0), 0, keepdims=True)
        acc[r, :, 0:half] = dot_tn(pick[...], ys[slot, :, 0:half]).astype(BF)
        acc[r, :, half:] = dot_tn(pick[...], ys[slot, :, half:]).astype(BF)

    for copy in loads(1, 0):
        copy.start()

    def odd(i, carry):
        r = 2 * i + 1
        build(i, r, jnp.where(i < 3, r + 2, 0))
        remote(acc.at[r], core_in.at[i], i, 2).start()
        return carry

    def even(i, carry):
        build(i + 4, 2 * i, 2 * i + 2)
        return carry

    lax.fori_loop(0, 4, odd, 0)
    tables = [remote(table.at[2 * i + 1], table_core.at[i], 4 + i, 2) for i in range(4)]
    for copy in tables:
        copy.start()
    lax.fori_loop(0, 4, even, 0)
    if relays:

        @pl.when(inner_plane())
        def _():
            for copy in background[:relays]:
                copy.start()

    def settle(i):
        remote(acc.at[2 * i + 1], core_in.at[i], i, 2).wait()
        add_into(acc, 2 * i, core_in[i])

    left, right = slice(0, half), slice(half, width)
    settle(3)
    a = [remote(acc.at[6, :, pl.ds(0, half)], row_in.at[1], 8, 1), remote(acc.at[6, :, pl.ds(half, half)], pair_in.at[1], 9, 0)]
    for copy in a:
        copy.start()
    settle(1)
    a.append(remote(acc.at[2, :, pl.ds(0, half)], row_in.at[0], 10, 1))
    a[-1].start()
    settle(2)
    a.append(remote(acc.at[4, :, pl.ds(half, half)], pair_in.at[0], 11, 0))
    a[-1].start()
    for i, copy in enumerate(tables):
        copy.wait()
        table[2 * i] = table[2 * i] + table_core[i]
    t = [remote(table.at[2], table_row.at[0], 12, 1), remote(table.at[6], table_row.at[1], 13, 1)]
    for copy in t:
        copy.start()
    settle(0)
    a[0].wait()
    add_into(acc, (4, slice(None), left), row_in[1])
    b = [remote(acc.at[4, :, pl.ds(0, half)], last_in.at[0], 14, 0)]
    b[0].start()
    a[1].wait()
    add_into(acc, (2, slice(None), right), pair_in[1])
    b.append(remote(acc.at[2, :, pl.ds(half, half)], last_in.at[1], 15, 1))
    b[1].start()
    for i, copy in enumerate(t):
        copy.wait()
        table[4 * i] = table[4 * i] + table_row[i]
    t = remote(table.at[4], table_pair, 16, 0)
    t.start()
    a[2].wait()
    add_into(acc, (0, slice(None), left), row_in[0])
    a[3].wait()
    add_into(acc, (0, slice(None), right), pair_in[0])
    b[0].wait()
    out_ref[:, left] = (acc[0, :, left].astype(F32) + last_in[0].astype(F32)).astype(BF)
    b[1].wait()
    out_ref[:, right] = (acc[0, :, right].astype(F32) + last_in[1].astype(F32)).astype(BF)
    t.wait()
    gate_ref[...] = table[0] + table_pair[...]
    for copy in background:
        copy.wait()


def return_rows(positions, results, gate_rows, experts, slots, jobs=(), gives=(), relays=0):
    sources, _, tokens = positions.shape
    count = len(results)
    width = results[0].shape[1]
    half = width // 2
    vmem, anywhere = pl.BlockSpec(memory_space=pltpu.VMEM), pl.BlockSpec(memory_space=pl.ANY)
    rows, gates, *takes = pl.pallas_call(
        functools.partial(return_kernel, count, slots, tuple(jobs), relays),
        in_specs=[vmem] + [anywhere] * count + [vmem] * count + [anywhere] * len(jobs),
        out_specs=[vmem, vmem] + [anywhere] * len(jobs),
        out_shape=[jax.ShapeDtypeStruct((tokens, width), BF), jax.ShapeDtypeStruct((experts, tokens), F32)]
        + [jax.ShapeDtypeStruct(give.shape, give.dtype) for give in gives],
        scratch_shapes=[
            pltpu.VMEM((8, tokens, width), BF),
            pltpu.VMEM((4, tokens, width), BF),
            pltpu.VMEM((2, tokens, half), BF),
            pltpu.VMEM((2, tokens, half), BF),
            pltpu.VMEM((2, tokens, half), BF),
            pltpu.VMEM((2, count * slots, width), BF),
            pltpu.VMEM((count * slots, tokens), BF),
            pltpu.VMEM((8, experts, tokens), F32),
            pltpu.VMEM((4, experts, tokens), F32),
            pltpu.VMEM((2, experts, tokens), F32),
            pltpu.VMEM((experts, tokens), F32),
            pltpu.SemaphoreType.DMA((2, count)),
            pltpu.SemaphoreType.DMA((17,)),
            pltpu.SemaphoreType.DMA((17,)),
            pltpu.SemaphoreType.DMA((2, max(1, len(jobs)))),
        ],
        compiler_params=pltpu.CompilerParams(collective_id=3, has_side_effects=True, vmem_limit_bytes=60 * 2**20),
        name="return_rows",
    )(positions, *results, *gate_rows, *gives)
    return rows, gates, takes


class Group:
    def __init__(self, copies):
        self.copies = copies

    def wait(self):
        for copy in self.copies:
            copy.wait()


def scatter_kernel(dims, rotations, chunks, segments, sources, *refs):
    last = len(dims) - 1
    grads, out_ref = refs[0:sources], refs[sources]
    acc, core_in = refs[sources + 1:sources + 3]
    inboxes = refs[sources + 3:sources + 3 + last]
    load_sem, send_sem, recv_sem = refs[sources + 3 + last:]
    barrier_with([flipped(*dim) for dim in dims])
    bits = [own_bit(*dim) for dim in dims]
    every = tuple(pl.ds(0, 2) for _ in range(last))
    number = iter(range(send_sem.shape[0]))

    def remote(src, dst, dim):
        n = next(number)
        return pltpu.make_async_remote_copy(
            src_ref=src, dst_ref=dst, send_sem=send_sem.at[n], recv_sem=recv_sem.at[n],
            device_id=flipped(*dims[dim]), device_id_type=pl.DeviceIdType.MESH,
        )

    firsts, loads = [[] for _ in chunks], []
    for source, start, at, width, chunk in segments:
        src, dst = (slice(None), pl.ds(start, width)), (slice(None), pl.ds(at, width))
        copy = remote(
            grads[source].at[every + (pl.ds(1 - bits[last], 1),) + src], core_in.at[every + (pl.ds(0, 1),) + dst], last
        )
        copy.start()
        firsts[chunk].append(copy)
        load = pltpu.make_async_copy(
            grads[source].at[every + (pl.ds(bits[last], 1),) + src], acc.at[every + (pl.ds(0, 1),) + dst],
            load_sem.at[len(loads)],
        )
        load.start()
        loads.append(load)
    for load in loads:
        load.wait()
    sends = [Group(copies) for copies in firsts]
    for step in range(last + 1):
        for c, (start, width) in enumerate(chunks):
            cols = pl.ds(start, width)
            rest = rotations[c][:last - step]
            sends[c].wait()
            for n in range(2 ** len(rest)):
                spread = [(n >> (len(rest) - 1 - i)) & 1 for i in range(len(rest))]
                index = [bits[d] if d not in rest else spread[rest.index(d)] for d in range(last)]
                at = tuple(index) + (0, slice(None), cols)
                other = core_in[at] if step == 0 else inboxes[step - 1][n, :, cols]
                if step < last:
                    add_into(acc, at, other)
                else:
                    out_ref[:, cols] = (acc[at].astype(F32) + other.astype(F32)).astype(out_ref.dtype)
            if step < last:
                dim, spread_dims = rest[-1], rest[:-1]
                group = []
                for n in range(2 ** len(spread_dims)):
                    spread = [(n >> (len(spread_dims) - 1 - i)) & 1 for i in range(len(spread_dims))]
                    index = [
                        1 - bits[d] if d == dim else (spread[spread_dims.index(d)] if d in spread_dims else bits[d])
                        for d in range(last)
                    ]
                    copy = remote(acc.at[tuple(index) + (0, slice(None), cols)], inboxes[step].at[n, :, cols], dim)
                    copy.start()
                    group.append(copy)
                sends[c] = Group(group)


def cube_scatter(dims, rotations, chunks, segments, grads, dtype, collective, name):
    last = len(dims) - 1
    rows = grads[0].shape[0] // 2 ** len(dims)
    width = sum(chunk[1] for chunk in chunks)
    copies = len(segments) + len(chunks) * (2 ** last - 1)
    return pl.pallas_call(
        functools.partial(scatter_kernel, dims, rotations, chunks, segments, len(grads)),
        in_specs=[pl.BlockSpec(memory_space=pl.ANY)] * len(grads),
        out_specs=pl.BlockSpec(memory_space=pltpu.VMEM),
        out_shape=jax.ShapeDtypeStruct((rows, width), dtype),
        scratch_shapes=[pltpu.VMEM((2,) * last + (1, rows, width), BF)] * 2
        + [pltpu.VMEM((2 ** n, rows, width), BF) for n in reversed(range(last))]
        + [
            pltpu.SemaphoreType.DMA((len(segments),)),
            pltpu.SemaphoreType.DMA((copies,)),
            pltpu.SemaphoreType.DMA((copies,)),
        ],
        compiler_params=pltpu.CompilerParams(
            collective_id=collective, has_side_effects=True, vmem_limit_bytes=60 * 2**20
        ),
        name=name,
    )(*[g.reshape((2,) * len(dims) + (rows, g.shape[1])) for g in grads])


def dense_segments(wide):
    cut = wide // 256 * 128 + 128
    return ((0, 0, cut, 0), (0, cut, wide - cut, 1), (1, 0, 128, 1), (2, 0, 1536, 2), (3, 0, 128, 2))


def scatter_all(grads):
    segments, chunks, at = [], [0, 0, 0], 0
    for source, start, width, chunk in dense_segments(grads[0].shape[1]):
        segments.append((source, start, at, width, chunk))
        chunks[chunk] += width
        at += width
    starts = (0, chunks[0], chunks[0] + chunks[1])
    return cube_scatter(
        CUBE, ROTATIONS, tuple(zip(starts, chunks)), tuple(segments), grads, F32, 4, "scatter_all"
    )


def group_back(grad_key, grad_value):
    width = grad_key.shape[1]
    segments = ((0, 0, 0, width, 0), (1, 0, width, width, 1))
    return cube_scatter(
        GROUP, ((0, 1), (1, 0)), ((0, width), (width, width)), segments, [grad_key, grad_value], BF, 6, "group_back"
    )


def group_rows_kernel(rows_ref, key_ref, value_ref, own_sem, send_sem, recv_sem):
    barrier_with([flipped(*dim) for dim in GROUP])
    bits = [own_bit(*dim) for dim in GROUP]
    width = key_ref.shape[4]
    here = tuple(pl.ds(bit, 1) for bit in bits)
    own = [
        pltpu.make_async_copy(rows_ref.at[:, :, :, :, pl.ds(i * width, width)], ref.at[here], own_sem.at[i])
        for i, ref in enumerate((key_ref, value_ref))
    ]
    for copy in own:
        copy.start()
    for copy in own:
        copy.wait()
    copies = []
    running = [None, None]
    for step in range(3):
        for f, (ref, order) in enumerate(((key_ref, (0, 1, 2)), (value_ref, (1, 0, 2)))):
            if running[f] is not None:
                running[f].wait_recv()
            at = tuple(pl.ds(0, 2) if d in order[:step] else pl.ds(bits[d], 1) for d in range(3))
            copy = pltpu.make_async_remote_copy(
                src_ref=ref.at[at], dst_ref=ref.at[at], send_sem=send_sem.at[step, f], recv_sem=recv_sem.at[step, f],
                device_id=flipped(*GROUP[order[step]]), device_id_type=pl.DeviceIdType.MESH,
            )
            copy.start()
            copies.append(copy)
            running[f] = copy
    for copy in running:
        copy.wait_recv()
    for copy in copies:
        copy.wait_send()


def group_rows(key_value):
    rows, width = key_value.shape
    anywhere = pl.BlockSpec(memory_space=pl.ANY)
    outs = pl.pallas_call(
        group_rows_kernel,
        in_specs=[pl.BlockSpec(memory_space=pltpu.VMEM)],
        out_specs=[anywhere] * 2,
        out_shape=[jax.ShapeDtypeStruct((2, 2, 2, rows, width // 2), BF)] * 2,
        scratch_shapes=[
            pltpu.SemaphoreType.DMA((2,)),
            pltpu.SemaphoreType.DMA((3, 2)),
            pltpu.SemaphoreType.DMA((3, 2)),
        ],
        compiler_params=pltpu.CompilerParams(collective_id=5, has_side_effects=True),
        name="group_rows",
    )(key_value.reshape(1, 1, 1, rows, width))
    return [out.reshape(8 * rows, width // 2) for out in outs]


D = 1536
EPSILON = 1e-06
EVERYWHERE = ("dp", "expert")


def exchange(value, axis, mask):
    return lax.ppermute(value, axis, [(i, i ^ mask) for i in range(lax.axis_size(axis))])


def tie(first, *others):
    return lax.optimization_barrier((first, *others))[0]


def rms_scale(values):
    return lax.rsqrt(jnp.mean(values * values, axis=-1, keepdims=True) + EPSILON)


def product(left, right):
    return jnp.dot(left, right, preferred_element_type=F32)


def contract_rows(left, right):
    return jnp.einsum("ta,tb->ab", left, right, preferred_element_type=F32)


def times_transposed(left, right):
    return jnp.einsum("ta,ba->tb", left, right, preferred_element_type=F32)


def added(left, right):
    return (left.astype(F32) + right.astype(F32)).astype(BF)


def team_gather(value, order):
    pieces = {0: value}
    for axis, mask, bit in order:
        pieces.update({r | bit: exchange(v, axis, mask) for r, v in list(pieces.items())})
    return jnp.stack([pieces[r] for r in sorted(pieces)])


TEAM_BITS = (("dp", 2, 4), ("expert", 2, 2), ("expert", 1, 1))


def local(tokens, attn_gain, w_query, w_key, w_value, w_out, w_router, ffn_gain, w_gate, w_up, w_down, routes, cotangent):
    dp, expert_at = lax.axis_index("dp"), lax.axis_index("expert")
    shards, owners = lax.axis_size("dp"), lax.axis_size("expert")
    cube = shards == 8 and owners == 4
    turn = (dp >> 1) & 1
    tok_rows = tokens.shape[0]
    per_owner, piece, hidden = w_gate.shape
    count = per_owner // 2
    expert_count = per_owner * owners
    top_count = routes.shape[1]
    kvw = w_key.shape[1]
    capacity = 8 * ((17 * top_count * tok_rows + 128 * expert_count - 1) // (128 * expert_count))
    slots = SLOTS_ALIGN * (-(-capacity // SLOTS_ALIGN))
    dp_index = dp.astype(jnp.int32).reshape(1)
    wide = D + 2 * kvw

    stacked = jnp.stack([w_gate, w_up, w_down.transpose(0, 2, 1)], 1)
    own = lax.dynamic_slice_in_dim(stacked, turn * count, count, 0)
    other = lax.dynamic_slice_in_dim(stacked, (1 - turn) * count, count, 0)
    gains = jnp.pad(jnp.stack([attn_gain, ffn_gain], 1), ((0, 0), (0, 126)))
    dense = [
        jnp.concatenate([w_query, w_key, w_value], 1), gains, w_out,
        jnp.pad(w_router, ((0, 0), (0, 128 - expert_count))),
    ]
    ahead = 2
    if cube:
        dense_full, taken, routes_t = gather_all(dense, dense_segments(wide), other[:ahead], routes.T)
    else:
        routes_t = team_gather(routes.T, TEAM_BITS)
        dense_full = [lax.all_gather(shard, EVERYWHERE, axis=0, tiled=True) for shard in dense]
        taken = exchange(other[:ahead], "dp", 2)
    qkv_full, gains_full, out_full, router_full = dense_full
    gains_full = gains_full.astype(F32).T
    gain_first, gain_second = gains_full[0], gains_full[1]

    relay_bits = [1 << b for b in range(2, shards.bit_length() - 1)]
    taken_late = exchange(tie(other[ahead:], qkv_full), "dp", 2)
    pairs = [
        jnp.stack([own[k], taken[k] if k < ahead else taken_late[k - ahead]]) for k in range(count)
    ]

    def crossed(relayed):
        return [w for v in relayed for w in (v, exchange(v, "dp", 1))]

    def relays(pair):
        pieces = [pair]
        for bit in relay_bits:
            pieces += [exchange(v, "dp", bit) for v in pieces]
        return pieces

    first_expert = expert_at * per_owner + turn * count
    local_ids = first_expert + jnp.arange(count, dtype=jnp.int32)
    hits = jnp.any(routes_t[:, None] == local_ids[None, :, None, None], axis=2)
    row_id = lax.broadcasted_iota(jnp.int32, (tok_rows, tok_rows), 0)
    col_id = lax.broadcasted_iota(jnp.int32, (tok_rows, tok_rows), 1)
    before = jnp.where(row_id < col_id, 1.0, 0.0).astype(BF)
    ranks = product(hits.astype(BF).reshape(-1, tok_rows), before).reshape(hits.shape)
    positions = jnp.where(hits, ranks.astype(jnp.int32), -1)
    positions = jnp.pad(positions, ((0, 0), (0, 8 - count), (0, 0)), constant_values=-1)

    inputs = tokens.astype(F32)
    scale_one = rms_scale(inputs)
    normed_one = inputs * scale_one
    hidden_one = (normed_one * gain_first).astype(BF)
    qkv = product(hidden_one, qkv_full).astype(BF)
    query, key_value = qkv[:, :D], qkv[:, D:]
    place = ((dp & 1) * owners + expert_at).astype(jnp.int32).reshape(1)
    prompt_key, prompt_value = group_rows(key_value[:P_DEV])
    own_key, own_value = key_value[P_DEV:, :kvw], key_value[P_DEV:, kvw:]
    half = D // 2
    early = tie(cotangent, qkv_full)
    left, right = early[:, :half], early[:, half:]
    left = jnp.stack([left, exchange(left, "dp", 2)])
    right = jnp.stack([right, exchange(right, "expert", 2)])
    query, left, right, pairs, prompt_key = lax.optimization_barrier((query, left, right, pairs, prompt_key))
    parts = [left, exchange(left, "expert", 2), right, exchange(right, "dp", 2)]
    crossings = [exchange(pairs[k], "dp", 1) for k in range(2)]
    mixed, levels = attend(place, query, prompt_key, prompt_value, own_key, own_value)
    second = inputs + product(mixed, out_full)
    scale_two = rms_scale(second)
    normed_two = second * scale_two
    hidden_two = (normed_two * gain_second).astype(BF)
    logits = product(hidden_two, router_full)[:, :expert_count]
    expert_ids = jnp.arange(expert_count, dtype=jnp.int32)
    chosen = jnp.any(routes[:, :, None] == expert_ids, axis=1)
    peak = jnp.max(jnp.where(chosen, logits, NEGATIVE), axis=-1, keepdims=True)
    raised = jnp.where(chosen, jnp.exp(jnp.where(chosen, logits - peak, 0.0)), 0.0)
    gates = raised / jnp.sum(raised, axis=-1, keepdims=True)

    weights = [None] * count
    if cube:
        near = exchange(tie(pairs[0], parts[0]), "dp", 4)
        sent_rows, parts, crossings, near = lax.optimization_barrier((hidden_two, parts, crossings, near))
    else:
        sent_rows, parts, crossings = lax.optimization_barrier((hidden_two, parts, crossings))
    core_jobs = (("expert", 1),) * 4
    if cube:
        rows, gates_t, takes = team_rows(
            sent_rows, gates.T, core_jobs + (("dp", 1),) * 3, (*parts, *pairs[2:]), (1, 2), pairs[1:3], other
        )
        parts = parts + takes[0:4]
        crossings = crossings + takes[4:7]
        relayed_pairs = [near] + takes[7:9]
        for k in range(3, count):
            relayed_pairs.append(exchange(tie(pairs[k], rows), "dp", 4))
        for k in range(count):
            weights[k] = [pairs[k], crossings[k], relayed_pairs[k]]
    else:
        rows, gates_t, takes = team_rows(sent_rows, gates.T, core_jobs, parts)
        parts = parts + takes
        for k in range(count):
            weights[k] = crossed(relays(tie(pairs[k], rows)))
    lefts = tuple((r % 2 * 4 + r // 2 % 2, r // 4) for r in range(8))
    rights = tuple((r % 2 * 4 + 2 + r // 4, r // 2 % 2) for r in range(8))
    gates_t = lax.dynamic_slice_in_dim(gates_t, first_expert, count, 1)
    gates_t = jnp.pad(gates_t, ((0, 0), (0, 8 - count), (0, 0)))
    grad_slots = gather_split(positions, parts, lefts, rights, count, slots)
    row_slots, gate_slots = gather_rows(positions, gates_t, rows, count, slots)

    results, backs, gate_rows, sums = [], [], [], []
    expert_index = dp_index
    for k in range(count):
        if cube:
            relayed_pair = weights[k][2] if k < 3 else tie(weights[k][2], gate_rows[k - 2])
            weights[k].append(exchange(relayed_pair, "dp", 1))
        y, dx, dg, keep, send = run_expert(k, expert_index, row_slots, grad_slots, gate_slots, weights[k], slots)
        results.append(y)
        backs.append(dx)
        gate_rows.append(dg)
        sums.append((keep, send))
        expert_index = tie(dp_index, dg)

    before_return = added(sums[0][0], exchange(sums[0][1], "dp", 1))
    jobs, gives, relays_in = (("dp", 1),) * 2, (sums[1][1], sums[2][1]), 0
    if cube:
        jobs, gives, relays_in = (("dp", 4),) + jobs, (before_return[2:],) + gives, 1
    routed_back, gate_grad, takes = return_rows(
        positions, backs, gate_rows, expert_count, slots, jobs, gives, relays_in
    )
    halved = [before_return, added(sums[1][0], takes[-2]), added(sums[2][0], takes[-1])]
    crossed_back = [exchange(tie(sums[k][1], routed_back), "dp", 1) for k in range(3, count)]
    relay_bits = relay_bits[::-1]

    def sent_on(keep):
        return exchange(keep[keep.shape[0] // 2:], "dp", relay_bits[0])

    def settled(keep, came):
        keep = added(keep[:keep.shape[0] // 2], came)
        for bit in relay_bits[1:]:
            middle = keep.shape[0] // 2
            keep = added(keep[:middle], exchange(keep[middle:], "dp", bit))
        return keep

    relay_came = [takes[0] if cube else sent_on(before_return)] + [sent_on(keep) for keep in halved[1:]]
    out_keep, out_send = combine_rows(tie(positions, routed_back), results, slots)
    gate_grad = gate_grad.T
    routed_back = routed_back.astype(F32)

    grad_output = cotangent.astype(F32)
    picked = jnp.where(chosen, gate_grad, 0.0)
    grad_logits = (gates * (picked - jnp.sum(gates * picked, axis=-1, keepdims=True))).astype(BF)
    wide_logits = jnp.pad(grad_logits, ((0, 0), (0, 128 - expert_count)))
    grad_hidden_two = times_transposed(wide_logits, router_full) + routed_back
    grad_normed_two = grad_hidden_two * gain_second
    grad_second = grad_output + scale_two * (
        grad_normed_two - normed_two * jnp.mean(grad_normed_two * normed_two, axis=-1, keepdims=True)
    )
    grad_branch = grad_second.astype(BF)
    ones = jnp.ones((tok_rows, 128), BF)
    lane = lax.broadcasted_iota(jnp.int32, (tok_rows, 128), 1)
    small = contract_rows(hidden_two, wide_logits) + contract_rows(
        (grad_hidden_two * normed_two).astype(BF), jnp.where(lane == expert_count, ones, jnp.zeros_like(ones))
    )
    out_grad = contract_rows(mixed, grad_branch).astype(BF)
    grad_mixed = times_transposed(grad_branch, out_full).astype(BF)

    out_keep, core_came, relay_came[1], crossed_back[0] = lax.optimization_barrier(
        (out_keep, exchange(out_send, "expert", 1), relay_came[1], crossed_back[0])
    )
    total = added(out_keep, core_came).reshape(2, 2, tok_rows, D)
    halved.append(added(sums[3][0], crossed_back[0]))
    relay_came.append(sent_on(halved[3]))
    row_sent = total[:, 1]
    grad_mixed, total, row_sent, halved = lax.optimization_barrier((grad_mixed, total, row_sent, halved))
    row_came = exchange(row_sent, "expert", 2)
    grad_query, dkp, dvp, dko, dvo = attend_back(
        place, query, prompt_key, prompt_value, own_key, own_value, mixed, grad_mixed, levels
    )
    halved, relay_came, crossed_back, grad_query, total, row_came, dkp = lax.optimization_barrier(
        (halved, relay_came, crossed_back, grad_query, total, row_came, dkp)
    )
    halved.append(added(sums[4][0], crossed_back[1]))
    relay_came.append(sent_on(halved[4]))
    grad_prompt = group_back(dkp, dvp)
    total = added(total[:, 0], row_came)
    pair_came = exchange(total[1], "dp", 2)
    grad_qkv = jnp.concatenate([
        grad_query, jnp.concatenate([grad_prompt, jnp.concatenate([dko, dvo], 1)], 0)
    ], 1)
    grad_hidden_one = times_transposed(grad_qkv, qkv_full)
    dense_grads = [
        contract_rows(hidden_one, grad_qkv).astype(BF),
        contract_rows((grad_hidden_one * normed_one).astype(BF), ones).astype(BF),
        out_grad, small.astype(BF),
    ]
    dense_grads, relay_came = lax.optimization_barrier((dense_grads, relay_came))
    if cube:
        share = scatter_all(dense_grads)
    else:
        share = lax.psum_scatter(
            jnp.concatenate(dense_grads, 1), EVERYWHERE, scatter_dimension=0, tiled=True
        ).astype(F32)
    grad_normed_one = grad_hidden_one * gain_first
    grad_input = grad_second + scale_one * (
        grad_normed_one - normed_one * jnp.mean(grad_normed_one * normed_one, axis=-1, keepdims=True)
    )

    share, halved, relay_came, total, pair_came = lax.optimization_barrier(
        (share, halved, relay_came, total, pair_came)
    )
    output = (second + added(total[0], pair_came).astype(F32)).astype(BF)
    first_share, second_share = share[:, :wide + 128], share[:, wide + 128:]
    relayed = [settled(halved[k], relay_came[k]) for k in range(count)]
    theirs = exchange(jnp.stack([keep[1] for keep in relayed]), "dp", 2)
    mine = jnp.stack([keep[0] for keep in relayed])
    lower = jnp.where(turn == 0, mine, theirs)
    upper = jnp.where(turn == 0, theirs, mine)
    expert_grads = jnp.concatenate([lower, upper]).astype(F32)
    return (
        output,
        grad_input.astype(BF),
        first_share[:, wide],
        first_share[:, :D],
        first_share[:, D:D + kvw],
        first_share[:, D + kvw:wide],
        second_share[:, :D].astype(F32),
        second_share[:, D:D + expert_count].astype(F32),
        second_share[:, D + expert_count].astype(F32),
        expert_grads[:, 0],
        expert_grads[:, 1],
        expert_grads[:, 2].transpose(0, 2, 1),
    )


def solution(mesh):
    rows, line = P(("dp", "expert"), None), P(("dp", "expert"))
    gate, down = P("expert", "dp", None), P("expert", None, "dp")
    return jax.shard_map(
        local,
        mesh=mesh,
        in_specs=(rows, line, rows, rows, rows, rows, rows, line, gate, gate, down, rows, rows),
        out_specs=(rows, rows, line, rows, rows, rows, rows, rows, line, gate, gate, down),
        check_vma=False,
    )
```

```python
import functools
import jax
import jax.numpy as jnp
from jax import lax
from jax.sharding import PartitionSpec as P
from jax.experimental import pallas as pl
from jax.experimental.pallas import tpu as pltpu

HD = 64
P_DEV = 128
NEGATIVE = -1e30
F32 = jnp.float32
BF = jnp.bfloat16


def dot_nt(a, b):
    return lax.dot_general(a, b, (((1,), (1,)), ((), ())), preferred_element_type=F32)


def dot_nn(a, b):
    return lax.dot_general(a, b, (((1,), (0,)), ((), ())), preferred_element_type=F32)


def dot_tn(a, b):
    return lax.dot_general(a, b, (((0,), (0,)), ((), ())), preferred_element_type=F32)


def halves(pair):
    lane = lax.broadcasted_iota(jnp.int32, pair.shape, 1)
    zero = jnp.zeros_like(pair)
    return jnp.where(lane < HD, pair, zero), jnp.where(lane < HD, zero, pair)


def placed_halves(pair_f32):
    low0, high1 = halves(pair_f32)
    high0 = pltpu.roll(low0, HD, 1)
    low1 = pltpu.roll(high1, HD, 1)
    return ((low0.astype(BF), high0.astype(BF)), (low1.astype(BF), high1.astype(BF)))


def attend_kernel(place_ref, q_ref, kp_ref, vp_ref, ko_ref, vo_ref, o_ref, lse_ref, kpad, vpad, s_scr, p_scr):
    rows = q_ref.shape[0]
    prompt = kp_ref.shape[0]
    cont = ko_ref.shape[0]
    place = place_ref[0]
    for src, dst in ((kp_ref, kpad), (vp_ref, vpad)):
        for head, pair in enumerate(placed_halves(src[...].astype(F32))):
            for half in range(2):
                dst[head, half, 0:prompt, :] = pair[half]
    for src, dst in ((ko_ref, kpad), (vo_ref, vpad)):
        for head, pair in enumerate(placed_halves(src[...].astype(F32))):
            for half in range(2):
                dst[head, half, prompt:prompt + cont, :] = pair[half]
    key_id = lax.broadcasted_iota(jnp.int32, (prompt, P_DEV), 0)
    row_id = lax.broadcasted_iota(jnp.int32, (prompt, P_DEV), 1)
    seen_prompt = key_id <= place * P_DEV + row_id
    diag = lax.broadcasted_iota(jnp.int32, (P_DEV, P_DEV), 0) <= lax.broadcasted_iota(jnp.int32, (P_DEV, P_DEV), 1)
    blocks = cont // P_DEV
    stats = []
    for chunk in range(3):
        queries = (q_ref[:, chunk * 128:(chunk + 1) * 128].astype(F32) * HD ** (-0.5)).astype(BF)
        total = None
        for half in range(2):
            position = chunk * 2 + half
            head = position // 3
            keys = kpad.at[head, half]
            scores = dot_nt(keys[0:prompt, :], queries)
            first = jnp.where(seen_prompt, scores[:, 0:P_DEV], NEGATIVE)
            rest = scores[:, P_DEV:]
            s_scr[0:prompt, 0:P_DEV] = first
            s_scr[0:prompt, P_DEV:] = rest
            top = jnp.concatenate([jnp.max(first, 0, keepdims=True), jnp.max(rest, 0, keepdims=True)], 1)
            tops = [top[:, i * P_DEV:(i + 1) * P_DEV] for i in range(1 + blocks)]
            for block in range(blocks):
                start = (1 + block) * P_DEV
                at = prompt + block * P_DEV
                own = dot_nt(keys[at:at + P_DEV, :], queries[start:, :])
                edge = jnp.where(diag, own[:, 0:P_DEV], NEGATIVE)
                s_scr[at:at + P_DEV, start:start + P_DEV] = edge
                tops[1 + block] = jnp.maximum(tops[1 + block], jnp.max(edge, 0, keepdims=True))
                if block + 1 < blocks:
                    later = own[:, P_DEV:]
                    s_scr[at:at + P_DEV, start + P_DEV:] = later
                    best = jnp.max(later, 0, keepdims=True)
                    for i in range(block + 1, blocks):
                        at_i = (i - block - 1) * P_DEV
                        tops[1 + i] = jnp.maximum(tops[1 + i], best[:, at_i:at_i + P_DEV])
            top = jnp.concatenate(tops, 1)
            weights = jnp.exp(s_scr[0:prompt, :] - top)
            mass = jnp.sum(weights, 0, keepdims=True)
            masses = [mass[:, i * P_DEV:(i + 1) * P_DEV] for i in range(1 + blocks)]
            values = vpad.at[head, half]
            mixed = dot_tn(values[0:prompt, :], weights.astype(BF))
            for block in range(blocks):
                start = (1 + block) * P_DEV
                at = prompt + block * P_DEV
                part = jnp.exp(s_scr[at:at + P_DEV, start:] - top[:, start:])
                p_scr[block * P_DEV:(block + 1) * P_DEV, start:] = part.astype(BF)
                if block:
                    p_scr[block * P_DEV:(block + 1) * P_DEV, P_DEV:start] = jnp.zeros((P_DEV, block * P_DEV), BF)
                part_mass = jnp.sum(part, 0, keepdims=True)
                for i in range(block, blocks):
                    at_i = (i - block) * P_DEV
                    masses[1 + i] = masses[1 + i] + part_mass[:, at_i:at_i + P_DEV]
            own_mixed = dot_tn(values[prompt:prompt + cont, :], p_scr[:, P_DEV:])
            mass = jnp.concatenate(masses, 1)
            scale = 1.0 / mass
            mixed = jnp.concatenate([mixed[:, 0:P_DEV], mixed[:, P_DEV:] + own_mixed], 1) * scale
            total = mixed if total is None else total + mixed
            stats.append(top + jnp.log(mass))
        o_ref[:, chunk * 128:(chunk + 1) * 128] = jnp.transpose(total).astype(BF)
    lse_ref[0] = jnp.concatenate(stats + [jnp.zeros((2, rows), F32)], 0)


def attend(place, query, prompt_key, prompt_value, own_key, own_value):
    rows = query.shape[0]
    prompt = prompt_key.shape[0]
    cont = own_key.shape[0]
    pairs = prompt_key.shape[1] // 128
    col = lambda i: (0, i)
    return pl.pallas_call(
        attend_kernel,
        grid=(pairs,),
        in_specs=[
            pl.BlockSpec(memory_space=pltpu.SMEM),
            pl.BlockSpec((rows, 384), col),
            pl.BlockSpec((prompt, 128), col),
            pl.BlockSpec((prompt, 128), col),
            pl.BlockSpec((cont, 128), col),
            pl.BlockSpec((cont, 128), col),
        ],
        out_specs=[pl.BlockSpec((rows, 384), col), pl.BlockSpec((1, 8, rows), lambda i: (i, 0, 0))],
        out_shape=[
            jax.ShapeDtypeStruct(query.shape, BF),
            jax.ShapeDtypeStruct((pairs, 8, rows), F32),
        ],
        scratch_shapes=[
            pltpu.VMEM((2, 2, prompt + cont, 128), BF),
            pltpu.VMEM((2, 2, prompt + cont, 128), BF),
            pltpu.VMEM((prompt + cont, rows), F32),
            pltpu.VMEM((cont, rows), BF),
        ],
        cost_estimate=pl.CostEstimate(flops=10**6, bytes_accessed=10**6, transcendentals=0),
        name="attend",
    )(place, query, prompt_key, prompt_value, own_key, own_value)


def attend_back_kernel(place_ref, q_ref, kp_ref, vp_ref, ko_ref, vo_ref, o_ref, do_ref, lse_ref,
                       dq_ref, dkp_ref, dvp_ref, dko_ref, dvo_ref, kpad, vpad, dk_acc, dv_acc):
    rows = q_ref.shape[0]
    prompt = kp_ref.shape[0]
    cont = ko_ref.shape[0]
    step = 2 * P_DEV
    place = place_ref[0]
    for src, dst, at, size in ((kp_ref, kpad, 0, prompt), (vp_ref, vpad, 0, prompt),
                               (ko_ref, kpad, prompt, cont), (vo_ref, vpad, prompt, cont)):
        for head, pair in enumerate(placed_halves(src[...].astype(F32))):
            for half in range(2):
                dst[head, half, at:at + size, :] = pair[half]
    dk_acc[...] = jnp.zeros_like(dk_acc)
    dv_acc[...] = jnp.zeros_like(dv_acc)
    for chunk in range(3):
        lanes = slice(chunk * 128, (chunk + 1) * 128)
        scaled = q_ref[:, lanes].astype(F32) * HD ** (-0.5)
        queries = scaled.astype(BF)
        query_halves = [part.astype(BF) for part in halves(scaled)]
        outs = o_ref[:, lanes].astype(F32)
        grads_f32 = do_ref[:, lanes].astype(F32)
        grads = do_ref[:, lanes]
        grad_halves = [part.astype(BF) for part in halves(grads_f32)]
        inner = jnp.transpose(outs * grads_f32)
        total = jnp.zeros((128, rows), F32)
        for half in range(2):
            position = chunk * 2 + half
            head = position // 3
            level = lse_ref[0, position:position + 1, :]
            delta = jnp.sum(inner[half * HD:(half + 1) * HD, :], 0, keepdims=True)

            def block(at, cols, mask, queries=queries, grads=grads, query_half=query_halves[half],
                      grad_half=grad_halves[half], level=level, delta=delta, head=head, half=half):
                keys = kpad[head, half, pl.ds(at, step), :]
                values = vpad[head, half, pl.ds(at, step), :]
                scores = dot_nt(keys, queries[cols, :])
                weights = jnp.exp(mask(scores) - level[:, cols])
                grad_weights = dot_nt(values, grads[cols, :])
                grad_scores = weights * (grad_weights - delta[:, cols])
                low_weights = weights.astype(BF)
                low_scores = grad_scores.astype(BF)
                dv_acc[head, pl.ds(at, step), :] += dot_nn(low_weights, grad_half[cols, :])
                dk_acc[head, pl.ds(at, step), :] += dot_nn(low_scores, query_half[cols, :])
                return dot_tn(keys, low_scores)

            def prompt_step(i, carry):
                at = pl.multiple_of(i * step, step)

                def mask(scores):
                    key_id = at + lax.broadcasted_iota(jnp.int32, (step, P_DEV), 0)
                    row_id = lax.broadcasted_iota(jnp.int32, (step, P_DEV), 1)
                    first = jnp.where(key_id <= place * P_DEV + row_id, scores[:, 0:P_DEV], NEGATIVE)
                    return jnp.concatenate([first, scores[:, P_DEV:]], 1)

                return carry + block(at, slice(0, rows), mask)

            total = lax.fori_loop(0, prompt // step, prompt_step, total)
            for own in range(cont // step):
                start = P_DEV + own * step

                def mask(scores):
                    key_id = lax.broadcasted_iota(jnp.int32, (step, step), 0)
                    row_id = lax.broadcasted_iota(jnp.int32, (step, step), 1)
                    edge = jnp.where(key_id <= row_id, scores[:, 0:step], NEGATIVE)
                    if scores.shape[1] == step:
                        return edge
                    return jnp.concatenate([edge, scores[:, step:]], 1)

                part = block(prompt + own * step, slice(start, rows), mask)
                total = jnp.concatenate([total[:, 0:start], total[:, start:] + part], 1)
        dq_ref[:, lanes] = (jnp.transpose(total) * HD ** (-0.5)).astype(BF)
    for acc, out_prompt, out_own in ((dk_acc, dkp_ref, dko_ref), (dv_acc, dvp_ref, dvo_ref)):
        low0, high0 = halves(acc[0])
        low1, high1 = halves(acc[1])
        merged = low0 + pltpu.roll(high0, HD, 1) + high1 + pltpu.roll(low1, HD, 1)
        out_prompt[...] = merged[0:prompt].astype(BF)
        out_own[...] = merged[prompt:].astype(BF)


def attend_back(place, query, prompt_key, prompt_value, own_key, own_value, mixed, grad, lse):
    rows = query.shape[0]
    prompt = prompt_key.shape[0]
    cont = own_key.shape[0]
    pairs = prompt_key.shape[1] // 128
    col = lambda i: (0, i)
    wide = pl.BlockSpec((rows, 384), col)
    keys_p = pl.BlockSpec((prompt, 128), col)
    keys_o = pl.BlockSpec((cont, 128), col)
    return pl.pallas_call(
        attend_back_kernel,
        grid=(pairs,),
        in_specs=[
            pl.BlockSpec(memory_space=pltpu.SMEM),
            wide, keys_p, keys_p, keys_o, keys_o, wide, wide,
            pl.BlockSpec((1, 8, rows), lambda i: (i, 0, 0)),
        ],
        out_specs=[wide, keys_p, keys_p, keys_o, keys_o],
        out_shape=[
            jax.ShapeDtypeStruct(query.shape, BF),
            jax.ShapeDtypeStruct(prompt_key.shape, BF),
            jax.ShapeDtypeStruct(prompt_key.shape, BF),
            jax.ShapeDtypeStruct(own_key.shape, BF),
            jax.ShapeDtypeStruct(own_key.shape, BF),
        ],
        scratch_shapes=[
            pltpu.VMEM((2, 2, prompt + cont, 128), BF),
            pltpu.VMEM((2, 2, prompt + cont, 128), BF),
            pltpu.VMEM((2, prompt + cont, 128), F32),
            pltpu.VMEM((2, prompt + cont, 128), F32),
        ],
        cost_estimate=pl.CostEstimate(flops=10**6, bytes_accessed=10**6, transcendentals=0),
        name="attend_back",
    )(place, query, prompt_key, prompt_value, own_key, own_value, mixed, grad, lse)


SLOTS_ALIGN = 16


def gather_kernel(count, with_gates, pos_ref, *refs):
    if with_gates:
        gate_ref, rows_ref, x_ref, g_ref, pick = refs
    else:
        rows_ref, x_ref, pick = refs
    tokens = rows_ref.shape[1]
    slots = x_ref.shape[1] // count
    half = rows_ref.shape[2] // 2
    slot_id = lax.broadcasted_iota(jnp.int32, (slots, tokens), 0)
    for k in range(count):
        hit = slot_id == pos_ref[0, k:k + 1, :]
        pick[k * slots:(k + 1) * slots, :] = jnp.where(hit, 1.0, 0.0).astype(BF)
        if with_gates:
            gate = jnp.sum(jnp.where(hit, gate_ref[0, k:k + 1, :], 0.0), 1, keepdims=True)
            g_ref[0, k * slots:(k + 1) * slots, :] = jnp.broadcast_to(gate, (slots, 128))
    x_ref[0, :, 0:half] = dot_nn(pick[...], rows_ref[0, :, 0:half]).astype(BF)
    x_ref[0, :, half:] = dot_nn(pick[...], rows_ref[0, :, half:]).astype(BF)


def gather_rows(positions, gates, rows, count, slots):
    sources, tokens, width = rows.shape
    size = count * slots
    table = pl.BlockSpec((1, 8, tokens), lambda s: (s, 0, 0))
    block = lambda shape: pl.BlockSpec((1,) + shape, lambda s: (s, 0, 0))
    tables = [positions] if gates is None else [positions, gates]
    outs = [((size, width), BF)] if gates is None else [((size, width), BF), ((size, 128), F32)]
    return pl.pallas_call(
        functools.partial(gather_kernel, count, gates is not None),
        grid=(sources,),
        in_specs=[table] * len(tables) + [block((tokens, width))],
        out_specs=[block(shape) for shape, _ in outs],
        out_shape=[jax.ShapeDtypeStruct((sources,) + shape, dtype) for shape, dtype in outs],
        scratch_shapes=[pltpu.VMEM((size, tokens), BF)],
        cost_estimate=pl.CostEstimate(flops=10**6, bytes_accessed=10**6, transcendentals=0),
        name="gather_rows",
    )(*tables, rows)


def gather_parts_kernel(count, sources, pos_ref, *refs):
    parts = refs[0:sources]
    x_ref, pick, rows, sems = refs[sources:]
    s = pl.program_id(0)
    slots = x_ref.shape[1] // count
    tokens, width = rows.shape[1:]
    half = width // 2

    for i in range(sources):

        @pl.when(s == max(i - 1, 0))
        def _(i=i):
            pltpu.make_async_copy(parts[i], rows.at[i % 2], sems.at[i % 2]).start()

    slot_id = lax.broadcasted_iota(jnp.int32, (slots, tokens), 0)
    for k in range(count):
        hit = slot_id == pos_ref[0, k:k + 1, :]
        pick[k * slots:(k + 1) * slots, :] = jnp.where(hit, 1.0, 0.0).astype(BF)
    slot = lax.rem(s, 2)
    pltpu.make_async_copy(parts[0], rows.at[slot], sems.at[slot]).wait()
    x_ref[0, :, 0:half] = dot_nn(pick[...], rows[slot, :, 0:half]).astype(BF)
    x_ref[0, :, half:] = dot_nn(pick[...], rows[slot, :, half:]).astype(BF)


def gather_parts(positions, parts, count, slots):
    tokens, width = parts[0].shape
    sources, size = len(parts), count * slots
    return pl.pallas_call(
        functools.partial(gather_parts_kernel, count, sources),
        grid=(sources,),
        in_specs=[pl.BlockSpec((1, 8, tokens), lambda s: (s, 0, 0))] + [pl.BlockSpec(memory_space=pl.ANY)] * sources,
        out_specs=pl.BlockSpec((1, size, width), lambda s: (s, 0, 0)),
        out_shape=jax.ShapeDtypeStruct((sources, size, width), BF),
        scratch_shapes=[
            pltpu.VMEM((size, tokens), BF),
            pltpu.VMEM((2, tokens, width), BF),
            pltpu.SemaphoreType.DMA((2,)),
        ],
        cost_estimate=pl.CostEstimate(flops=10**6, bytes_accessed=10**6, transcendentals=0),
        name="gather_parts",
    )(positions, *parts)


def expert_kernel(k, shards, slots, dp_ref, x_ref, g_ref, gate_ref, *refs):
    w_refs = refs[0:shards // 2]
    (y_out, dx_out, dg_out, keep_out, send_out,
     xs, gs, gates, ws, ys, dxs, dgs, dab, actg, stage,
     in_sem, w_sem, out_sem, grad_sem) = refs[shards // 2:]
    dp = dp_ref[0]
    sources = x_ref.shape[0]
    width = xs.shape[1]
    piece = width // shards
    hidden = ws.shape[2]
    mine = pl.ds(k * slots, slots)

    def row_copies(s):
        at = pl.ds(pl.multiple_of(s * slots, 16), slots)
        return (
            pltpu.make_async_copy(x_ref.at[s, mine, :], xs.at[at, :], in_sem.at[0, s]),
            pltpu.make_async_copy(g_ref.at[s, mine, :], gs.at[at, :], in_sem.at[1, s]),
            pltpu.make_async_copy(gate_ref.at[s, mine, :], gates.at[at, :], in_sem.at[2, s]),
        )

    weight_copies = [
        pltpu.make_async_copy(
            w_refs[(r & 1) + 2 * (r >> 2)].at[(r >> 1) & 1], ws.at[:, pl.ds(pl.multiple_of((dp ^ r) * piece, 16), piece), :], w_sem.at[r]
        )
        for r in range(shards)
    ]
    for s in range(sources):
        for copy in row_copies(s):
            copy.start()
        if s == 1:
            for copy in weight_copies:
                copy.start()
    for copy in weight_copies:
        copy.wait()
    chunk = 2 * slots

    def out_copies(c):
        at = pl.ds(pl.multiple_of(c * chunk, 32), chunk)
        return [
            pltpu.make_async_copy(src.at[at, :], dst.at[at, :], out_sem.at[i, c])
            for i, (src, dst) in enumerate(((ys, y_out), (dxs, dx_out), (dgs, dg_out)))
        ]

    def forward_chunk(c, carry):
        for copy in row_copies(2 * c) + row_copies(2 * c + 1):
            copy.wait()
        rows = pl.ds(pl.multiple_of(c * chunk, 32), chunk)
        x = xs[rows, :]
        a = dot_nn(x, ws[0])
        b = dot_nn(x, ws[1])
        pulled = dot_nn(gs[rows, :], ws[2])
        gate = gates[rows, 0:1]
        sig = jax.nn.sigmoid(a)
        silu = a * sig
        act = silu * b
        dgs[rows, :] = jnp.broadcast_to(jnp.sum(act * pulled, 1, keepdims=True), (chunk, 128))
        weighted = (gate * act).astype(BF)
        actg[rows, :] = weighted
        dact = gate * pulled
        da = (dact * b * sig * (1.0 + a * (1.0 - sig))).astype(BF)
        db = (dact * silu).astype(BF)
        dab[rows, 0:hidden] = da
        dab[rows, hidden:] = db
        ys[rows, :] = dot_nt(weighted, ws[2]).astype(BF)
        dxs[rows, :] = (dot_nt(da, ws[0]) + dot_nt(db, ws[1])).astype(BF)
        for copy in out_copies(c):
            copy.start()
        return carry

    lax.fori_loop(0, sources // 2, forward_chunk, 0)
    block = 384
    inner = block // piece
    high = dp // inner
    low = dp % inner

    def grad_copies(jr):
        slot = lax.rem(jr, 2)
        copies = []
        for ri in range(inner):
            dst = (send_out if ri % 2 else keep_out).at[jr * (inner // 2) + ri // 2]
            src = stage.at[slot, :, pl.ds(pl.multiple_of((low ^ ri) * piece, 16), piece), :]
            copies.append(pltpu.make_async_copy(src, dst, grad_sem.at[slot, ri]))
        return copies

    def grad_block(jr, carry):
        slot = lax.rem(jr, 2)

        @pl.when(jr >= 2)
        def _():
            for copy in grad_copies(jr - 2):
                copy.wait()

        cols = pl.ds(pl.multiple_of((high ^ jr) * block, 128), block)
        left = dot_tn(xs[:, cols], dab[...])
        stage[slot, 0] = left[:, 0:hidden].astype(BF)
        stage[slot, 1] = left[:, hidden:].astype(BF)
        stage[slot, 2] = dot_tn(gs[:, cols], actg[...]).astype(BF)
        for copy in grad_copies(jr):
            copy.start()
        return carry

    blocks = width // block
    lax.fori_loop(0, blocks, grad_block, 0)
    for jr in range(blocks - 2, blocks):
        for copy in grad_copies(jr):
            copy.wait()
    for c in range(sources // 2):
        for copy in out_copies(c):
            copy.wait()


def run_expert(k, dp_index, xs, gs, gates, weights, slots):
    sources, shards = xs.shape[0], 2 * len(weights)
    rows = sources * slots
    width = xs.shape[2]
    piece, hidden = weights[0].shape[2:]
    inner = 384 // piece
    anywhere = pl.BlockSpec(memory_space=pl.ANY)
    return pl.pallas_call(
        functools.partial(expert_kernel, k, shards, slots),
        in_specs=[pl.BlockSpec(memory_space=pltpu.SMEM)] + [anywhere] * (3 + shards // 2),
        out_specs=[anywhere] * 5,
        out_shape=[
            jax.ShapeDtypeStruct((rows, width), BF),
            jax.ShapeDtypeStruct((rows, width), BF),
            jax.ShapeDtypeStruct((rows, 128), F32),
            jax.ShapeDtypeStruct((shards // 2, 3, piece, hidden), BF),
            jax.ShapeDtypeStruct((shards // 2, 3, piece, hidden), BF),
        ],
        scratch_shapes=[
            pltpu.VMEM((rows, width), BF),
            pltpu.VMEM((rows, width), BF),
            pltpu.VMEM((rows, 128), F32),
            pltpu.VMEM((3, width, hidden), BF),
            pltpu.VMEM((rows, width), BF),
            pltpu.VMEM((rows, width), BF),
            pltpu.VMEM((rows, 128), F32),
            pltpu.VMEM((rows, 2 * hidden), BF),
            pltpu.VMEM((rows, hidden), BF),
            pltpu.VMEM((2, 3, 384, hidden), BF),
            pltpu.SemaphoreType.DMA((3, sources)),
            pltpu.SemaphoreType.DMA((shards,)),
            pltpu.SemaphoreType.DMA((3, sources // 2)),
            pltpu.SemaphoreType.DMA((2, inner)),
        ],
        compiler_params=pltpu.CompilerParams(vmem_limit_bytes=60 * 2**20),
        cost_estimate=pl.CostEstimate(flops=10**6, bytes_accessed=10**6, transcendentals=0),
        name="expert",
    )(dp_index, xs, gs, gates, *weights)


def barrier_with(partners):
    sem = pltpu.get_barrier_semaphore()
    for partner in partners:
        pl.semaphore_signal(sem, inc=1, device_id=partner, device_id_type=pl.DeviceIdType.MESH)
    pl.semaphore_wait(sem, len(partners))


def flipped(axis, mask):
    at = lax.axis_index(axis)
    bit = lax.rem(lax.div(at, mask), 2)
    return {axis: at + mask * (1 - 2 * bit)}


def own_bit(axis, mask):
    return lax.rem(lax.div(lax.axis_index(axis), mask), 2)


TEAM = (("dp", 2), ("expert", 2), ("expert", 1))
GROUP = (("dp", 1), ("expert", 2), ("expert", 1))
CUBE = (("dp", 4), ("dp", 2), ("dp", 1), ("expert", 2), ("expert", 1))
ROTATIONS = ((0, 1, 2, 3), (0, 2, 3, 1), (0, 3, 1, 2))


def gather_all_kernel(pieces, segments, count, *refs):
    shards, give_ref, routes_ref = refs[0:count], refs[count], refs[count + 1]
    fulls, take_ref, team_ref = refs[count + 2:2 * count + 2], refs[2 * count + 2], refs[2 * count + 3]
    own_sem, send_sem, recv_sem, piece_sem, team_sem = refs[2 * count + 4:]
    barrier_with([flipped(*dim) for dim in CUBE])
    bits = [own_bit(*dim) for dim in CUBE]
    here = tuple(pl.ds(bit, 1) for bit in bits)
    own = [pltpu.make_async_copy(shards[i], fulls[i].at[here], own_sem.at[i]) for i in range(count)]
    own.append(pltpu.make_async_copy(routes_ref, team_ref.at[0:1, 0:1, 0:1], own_sem.at[count]))
    for copy in own:
        copy.start()
    for copy in own:
        copy.wait()

    def routes_step(step):
        index = [pl.ds(0, 2) if d < step else pl.ds(0, 1) for d in range(3)]
        src = team_ref.at[tuple(index)]
        index[step] = pl.ds(1, 1)
        return pltpu.make_async_remote_copy(
            src_ref=src, dst_ref=team_ref.at[tuple(index)], send_sem=team_sem.at[0, step],
            recv_sem=team_sem.at[1, step], device_id=flipped(*TEAM[step]), device_id_type=pl.DeviceIdType.MESH,
        )

    def spread(step, n, gathered, dim):
        source, start, width, _ = segments[n]
        at = tuple(pl.ds(0, 2) if d in gathered else pl.ds(bits[d], 1) for d in range(5))
        ref = fulls[source].at[at + (slice(None), pl.ds(start, width))]
        return pltpu.make_async_remote_copy(
            src_ref=ref, dst_ref=ref, send_sem=send_sem.at[step, n], recv_sem=recv_sem.at[step, n],
            device_id=flipped(*CUBE[dim]), device_id_type=pl.DeviceIdType.MESH,
        )

    def hand(k):
        return pltpu.make_async_remote_copy(
            src_ref=give_ref.at[k], dst_ref=take_ref.at[k], send_sem=piece_sem.at[0, k],
            recv_sem=piece_sem.at[1, k], device_id=flipped("dp", 2), device_id_type=pl.DeviceIdType.MESH,
        )

    copies, passed = [], []
    running = [None] * len(segments)
    for step in range(5):
        if 0 < step < 4:
            routes_step(step - 1).wait()
        if step < 3:
            routes_step(step).start()
        for n, segment in enumerate(segments):
            if running[n] is not None:
                running[n].wait_recv()
            order = ROTATIONS[segment[3]] + (4,)
            copy = spread(step, n, order[:step], order[step])
            copy.start()
            copies.append(copy)
            running[n] = copy
        for k in range(pieces) if step == 4 else range(step, min(step + 1, pieces)):
            if step == 4 and k < 4:
                continue
            passed.append(hand(k))
            passed[-1].start()
    for copy in running:
        copy.wait_recv()
    for copy in copies:
        copy.wait_send()
    for copy in passed:
        copy.wait()


def gather_all(shards, segments, give, routes):
    rows = shards[0].shape[0]
    count, pieces = len(shards), give.shape[0]
    anywhere, vmem = pl.BlockSpec(memory_space=pl.ANY), pl.BlockSpec(memory_space=pltpu.VMEM)
    outs = pl.pallas_call(
        functools.partial(gather_all_kernel, pieces, segments, count),
        in_specs=[vmem] * count + [anywhere, vmem],
        out_specs=[anywhere] * (count + 2),
        out_shape=[jax.ShapeDtypeStruct((2,) * 5 + shard.shape, BF) for shard in shards]
        + [jax.ShapeDtypeStruct(give.shape, BF), jax.ShapeDtypeStruct((2, 2, 2) + routes.shape, jnp.int32)],
        scratch_shapes=[
            pltpu.SemaphoreType.DMA((count + 1,)),
            pltpu.SemaphoreType.DMA((5, len(segments))),
            pltpu.SemaphoreType.DMA((5, len(segments))),
            pltpu.SemaphoreType.DMA((2, pieces)),
            pltpu.SemaphoreType.DMA((2, 3)),
        ],
        compiler_params=pltpu.CompilerParams(collective_id=1, has_side_effects=True),
        name="gather_all",
    )(*[shard.reshape((1,) * 5 + shard.shape) for shard in shards], give, routes.reshape((1, 1, 1) + routes.shape))
    fulls = [full.reshape(32 * rows, full.shape[-1]) for full in outs[:count]]
    return fulls, outs[count], outs[count + 1].reshape((8,) + routes.shape)


def job_copies(jobs, gives, takes, sems):
    return [
        pltpu.make_async_remote_copy(
            src_ref=gives[j], dst_ref=takes[j], send_sem=sems.at[0, j], recv_sem=sems.at[1, j],
            device_id=flipped(*jobs[j]), device_id_type=pl.DeviceIdType.MESH,
        )
        for j in range(len(jobs))
    ]


def partners_of(dims, jobs):
    return [flipped(*dim) for dim in dict.fromkeys(tuple(dims) + tuple(jobs))]


def inner_plane():
    return own_bit("dp", 2) != own_bit("dp", 4)


def across():
    at = lax.axis_index("dp")
    return {"dp": at + 2 * (1 - 2 * own_bit("dp", 2)) + 4 * (1 - 2 * own_bit("dp", 4))}


def team_rows_kernel(jobs, relays, rows_ref, gates_ref, *refs):
    count, lanes = len(jobs), len(relays)
    gives, pairs = refs[0:count], refs[count:count + lanes]
    refs = refs[count + lanes:]
    if lanes:
        other_ref, refs = refs[0], refs[1:]
    all_ref, table_ref = refs[0:2]
    takes, far = refs[2:2 + count], refs[2 + count:2 + count + lanes]
    own_sem, send_sem, recv_sem, job_sem, relay_sem = refs[2 + count + lanes:]
    partners = partners_of(TEAM, jobs)
    if lanes:
        partners += [flipped("dp", 4), across()]
    barrier_with(partners)
    own = [
        pltpu.make_async_copy(rows_ref, all_ref.at[0:1, 0:1, 0:1], own_sem.at[0]),
        pltpu.make_async_copy(gates_ref, table_ref.at[0:1, 0:1, 0:1], own_sem.at[1]),
    ]
    for copy in own:
        copy.start()

    def leg(j, n):
        src = (pairs[j].at[0], pairs[j].at[1], other_ref.at[relays[j]])[n]
        return pltpu.make_async_remote_copy(
            src_ref=src, dst_ref=far[j].at[min(n, 1)], send_sem=relay_sem.at[n, j],
            recv_sem=relay_sem.at[3 + min(n, 1), j], device_id=across() if n == 2 else flipped("dp", 4),
            device_id_type=pl.DeviceIdType.MESH,
        )

    for copy in own:
        copy.wait()
    parts = 4
    width = all_ref.shape[4] // parts
    flows = [(all_ref, (slice(None), pl.ds(c * width, width))) for c in range(parts)]
    flows.append((table_ref, (slice(None), slice(None))))

    def hop(step, f):
        ref, tail = flows[f]
        index = [pl.ds(0, 2) if d < step else pl.ds(0, 1) for d in range(3)]
        src = ref.at[tuple(index) + tail]
        index[step] = pl.ds(1, 1)
        return pltpu.make_async_remote_copy(
            src_ref=src, dst_ref=ref.at[tuple(index) + tail], send_sem=send_sem.at[step, f],
            recv_sem=recv_sem.at[step, f], device_id=flipped(*TEAM[step]), device_id_type=pl.DeviceIdType.MESH,
        )

    order = [parts] + list(range(parts))
    for f in order:
        hop(0, f).start()
    background = job_copies(jobs, gives, takes, job_sem)
    for copy in background:
        copy.start()
    if lanes:

        @pl.when(inner_plane())
        def _():
            for n in (2, 0, 1):
                for j in range(lanes):
                    leg(j, n).start()

        @pl.when(jnp.logical_not(inner_plane()))
        def _():
            for j in range(lanes):
                leg(j, 0).start()

    for step in range(1, 3):
        for f in order:
            hop(step - 1, f).wait_recv()
            hop(step, f).start()
    for f in order:
        hop(2, f).wait_recv()
    for step in range(3):
        for f in order:
            hop(step, f).wait_send()
    for copy in background:
        copy.wait()
    for j in range(lanes):
        leg(j, 0).wait()
        leg(j, 1).wait_recv()
    if lanes:

        @pl.when(inner_plane())
        def _():
            for j in range(lanes):
                leg(j, 1).wait_send()
                leg(j, 2).wait_send()


def team_rows(rows, gates, jobs=(), gives=(), relays=(), pairs=(), other=None):
    tokens, width = rows.shape
    table = gates.shape
    anywhere = pl.BlockSpec(memory_space=pl.ANY)
    extra = [] if other is None else [other]
    full, tables, *takes = pl.pallas_call(
        functools.partial(team_rows_kernel, tuple(jobs), tuple(relays)),
        in_specs=[pl.BlockSpec(memory_space=pltpu.VMEM)] * 2 + [anywhere] * (len(jobs) + len(pairs) + len(extra)),
        out_specs=[anywhere] * (2 + len(jobs) + len(pairs)),
        out_shape=[
            jax.ShapeDtypeStruct((2, 2, 2, tokens, width), BF),
            jax.ShapeDtypeStruct((2, 2, 2) + table, F32),
        ] + [jax.ShapeDtypeStruct(give.shape, give.dtype) for give in list(gives) + list(pairs)],
        scratch_shapes=[
            pltpu.SemaphoreType.DMA((2,)),
            pltpu.SemaphoreType.DMA((3, 5)),
            pltpu.SemaphoreType.DMA((3, 5)),
            pltpu.SemaphoreType.DMA((2, max(1, len(jobs)))),
            pltpu.SemaphoreType.DMA((5, max(1, len(relays)))),
        ],
        compiler_params=pltpu.CompilerParams(collective_id=2, has_side_effects=True),
        name="team_rows",
    )(rows.reshape(1, 1, 1, tokens, width), gates.reshape((1, 1, 1) + table), *gives, *pairs, *extra)
    return full.reshape(8, tokens, width), tables.reshape((8,) + table), takes


def add_into(acc, at, other):
    acc[at] = (acc[at].astype(F32) + other.astype(F32)).astype(BF)


def return_kernel(count, slots, jobs, relays, pos_ref, *refs):
    x_refs, y_refs, dg_refs = refs[0:count], refs[count:2 * count], refs[2 * count:3 * count]
    refs = refs[3 * count:]
    gives, takes = refs[0:len(jobs)], refs[len(jobs) + 4:2 * len(jobs) + 4]
    out_ref, gate_ref, kept_ref, sent_ref = refs[len(jobs):len(jobs) + 4]
    (acc, core_in, even_out, row_in, pair_in, last_in, ys, pick, table, table_core, table_row, table_pair,
     load_sem, send_sem, recv_sem, job_sem, store_sem, free_sem) = refs[2 * len(jobs) + 4:]
    tokens, width = out_ref.shape
    half = width // 2
    barrier_with(partners_of(TEAM, jobs))
    background = job_copies(jobs, gives, takes, job_sem)
    for copy in background[relays:]:
        copy.start()
    if relays:

        @pl.when(jnp.logical_not(inner_plane()))
        def _():
            for copy in background[:relays]:
                copy.start()

    first = (lax.axis_index("expert") * 2 + own_bit("dp", 2)) * count
    slot_id = lax.broadcasted_iota(jnp.int32, (slots, tokens), 0)

    def remote(src, dst, n, dim):
        return pltpu.make_async_remote_copy(
            src_ref=src, dst_ref=dst, send_sem=send_sem.at[n], recv_sem=recv_sem.at[n],
            device_id=flipped(*TEAM[dim]), device_id_type=pl.DeviceIdType.MESH,
        )

    def loads(parts, r, slot):
        return [
            pltpu.make_async_copy(
                parts[k].at[pl.ds(pl.multiple_of(r * slots, 16), slots), :],
                ys.at[slot, pl.ds(k * slots, slots), :], load_sem.at[slot, k],
            )
            for k in range(count)
        ]

    table[...] = jnp.zeros_like(table)

    def build(parts, step, r, following, dst, at, with_gates):
        slot = lax.rem(step, 2)
        for copy in loads(parts, r, slot):
            copy.wait()

        @pl.when(step < 7)
        def _():
            for copy in loads(parts, following, 1 - slot):
                copy.start()

        for k in range(count):
            hit = slot_id == pos_ref[r, k:k + 1, :]
            pick[k * slots:(k + 1) * slots, :] = jnp.where(hit, 1.0, 0.0).astype(BF)
            if with_gates:
                pulled = dg_refs[k][pl.ds(pl.multiple_of(r * slots, 16), slots), 0:1]
                table[r, pl.ds(first + k, 1), :] = jnp.sum(jnp.where(hit, pulled, 0.0), 0, keepdims=True)
        dst[at, :, 0:half] = dot_tn(pick[...], ys[slot, :, 0:half]).astype(BF)
        dst[at, :, half:] = dot_tn(pick[...], ys[slot, :, half:]).astype(BF)

    def core_copy(i, base):
        return remote(acc.at[2 * i + 1], core_in.at[i], base + i, 2)

    def build_odd(parts, base, with_gates):
        def odd(i, carry):
            r = 2 * i + 1
            build(parts, i, r, jnp.where(i < 3, r + 2, 0), acc, r, with_gates)
            core_copy(i, base).start()
            return carry

        lax.fori_loop(0, 4, odd, 0)

    for copy in loads(x_refs, 1, 0):
        copy.start()
    build_odd(x_refs, 0, True)
    tables = [remote(table.at[2 * i + 1], table_core.at[i], 4 + i, 2) for i in range(4)]
    for copy in tables:
        copy.start()

    def even(i, carry):
        build(x_refs, i + 4, 2 * i, 2 * i + 2, acc, 2 * i, True)
        return carry

    lax.fori_loop(0, 4, even, 0)
    if relays:

        @pl.when(inner_plane())
        def _():
            for copy in background[:relays]:
                copy.start()

    for copy in loads(y_refs, 1, 0):
        copy.start()

    def settle(i):
        core_copy(i, 0).wait()
        add_into(acc, 2 * i, core_in[i])

    left, right = slice(0, half), slice(half, width)
    settle(3)
    a = [remote(acc.at[6, :, pl.ds(0, half)], row_in.at[1], 8, 1), remote(acc.at[6, :, pl.ds(half, half)], pair_in.at[1], 9, 0)]
    for copy in a:
        copy.start()
    settle(1)
    a.append(remote(acc.at[2, :, pl.ds(0, half)], row_in.at[0], 10, 1))
    a[-1].start()
    settle(2)
    a.append(remote(acc.at[4, :, pl.ds(half, half)], pair_in.at[0], 11, 0))
    a[-1].start()
    settle(0)
    pl.semaphore_signal(free_sem, inc=1, device_id=flipped(*TEAM[2]), device_id_type=pl.DeviceIdType.MESH)
    for i, copy in enumerate(tables):
        copy.wait()
        table[2 * i] = table[2 * i] + table_core[i]
    t = [remote(table.at[2], table_row.at[0], 12, 1), remote(table.at[6], table_row.at[1], 13, 1)]
    for copy in t:
        copy.start()
    pl.semaphore_wait(free_sem, 1)
    build_odd(y_refs, 17, False)
    a[0].wait()
    add_into(acc, (4, slice(None), left), row_in[1])
    b = [remote(acc.at[4, :, pl.ds(0, half)], last_in.at[0], 14, 0)]
    b[0].start()
    a[1].wait()
    add_into(acc, (2, slice(None), right), pair_in[1])
    b.append(remote(acc.at[2, :, pl.ds(half, half)], last_in.at[1], 15, 1))
    b[1].start()
    for i, copy in enumerate(t):
        copy.wait()
        table[4 * i] = table[4 * i] + table_row[i]
    t = remote(table.at[4], table_pair, 16, 0)
    t.start()

    def even_y(i, carry):
        build(y_refs, i + 4, 2 * i, 2 * i + 2, even_out, i, False)
        return carry

    lax.fori_loop(0, 4, even_y, 0)
    stores = []
    for i in range(4):
        core_copy(i, 17).wait()
        add_into(even_out, i, core_in[i])
        stores.append(
            pltpu.make_async_copy(even_out.at[i], (sent_ref if i % 2 else kept_ref).at[i // 2], store_sem.at[i])
        )
        stores[-1].start()
    a[2].wait()
    add_into(acc, (0, slice(None), left), row_in[0])
    a[3].wait()
    add_into(acc, (0, slice(None), right), pair_in[0])
    b[0].wait()
    out_ref[:, left] = (acc[0, :, left].astype(F32) + last_in[0].astype(F32)).astype(BF)
    b[1].wait()
    out_ref[:, right] = (acc[0, :, right].astype(F32) + last_in[1].astype(F32)).astype(BF)
    t.wait()
    gate_ref[...] = table[0] + table_pair[...]
    for copy in stores:
        copy.wait()
    for copy in background:
        copy.wait()


def return_rows(positions, backs, results, gate_rows, experts, slots, jobs=(), gives=(), relays=0):
    sources, _, tokens = positions.shape
    count = len(results)
    width = results[0].shape[1]
    half = width // 2
    vmem, anywhere = pl.BlockSpec(memory_space=pltpu.VMEM), pl.BlockSpec(memory_space=pl.ANY)
    rows, gates, kept, sent, *takes = pl.pallas_call(
        functools.partial(return_kernel, count, slots, tuple(jobs), relays),
        in_specs=[vmem] + [anywhere] * (2 * count) + [vmem] * count + [anywhere] * len(jobs),
        out_specs=[vmem, vmem] + [anywhere] * (2 + len(jobs)),
        out_shape=[jax.ShapeDtypeStruct((tokens, width), BF), jax.ShapeDtypeStruct((experts, tokens), F32)]
        + [jax.ShapeDtypeStruct((2, tokens, width), BF)] * 2
        + [jax.ShapeDtypeStruct(give.shape, give.dtype) for give in gives],
        scratch_shapes=[
            pltpu.VMEM((8, tokens, width), BF),
            pltpu.VMEM((4, tokens, width), BF),
            pltpu.VMEM((4, tokens, width), BF),
            pltpu.VMEM((2, tokens, half), BF),
            pltpu.VMEM((2, tokens, half), BF),
            pltpu.VMEM((2, tokens, half), BF),
            pltpu.VMEM((2, count * slots, width), BF),
            pltpu.VMEM((count * slots, tokens), BF),
            pltpu.VMEM((8, experts, tokens), F32),
            pltpu.VMEM((4, experts, tokens), F32),
            pltpu.VMEM((2, experts, tokens), F32),
            pltpu.VMEM((experts, tokens), F32),
            pltpu.SemaphoreType.DMA((2, count)),
            pltpu.SemaphoreType.DMA((21,)),
            pltpu.SemaphoreType.DMA((21,)),
            pltpu.SemaphoreType.DMA((2, max(1, len(jobs)))),
            pltpu.SemaphoreType.DMA((4,)),
            pltpu.SemaphoreType.REGULAR,
        ],
        compiler_params=pltpu.CompilerParams(collective_id=3, has_side_effects=True, vmem_limit_bytes=63 * 2**20),
        name="return_rows",
    )(positions, *backs, *results, *gate_rows, *gives)
    return rows, gates, kept, sent, takes


class Group:
    def __init__(self, copies):
        self.copies = copies

    def wait(self):
        for copy in self.copies:
            copy.wait()


def scatter_kernel(dims, rotations, chunks, segments, sources, *refs):
    last = len(dims) - 1
    grads, out_ref = refs[0:sources], refs[sources]
    acc, core_in = refs[sources + 1:sources + 3]
    inboxes = refs[sources + 3:sources + 3 + last]
    load_sem, send_sem, recv_sem = refs[sources + 3 + last:]
    barrier_with([flipped(*dim) for dim in dims])
    bits = [own_bit(*dim) for dim in dims]
    every = tuple(pl.ds(0, 2) for _ in range(last))
    number = iter(range(send_sem.shape[0]))

    def remote(src, dst, dim):
        n = next(number)
        return pltpu.make_async_remote_copy(
            src_ref=src, dst_ref=dst, send_sem=send_sem.at[n], recv_sem=recv_sem.at[n],
            device_id=flipped(*dims[dim]), device_id_type=pl.DeviceIdType.MESH,
        )

    firsts, loads = [[] for _ in chunks], []
    for source, start, at, width, chunk in segments:
        src, dst = (slice(None), pl.ds(start, width)), (slice(None), pl.ds(at, width))
        copy = remote(
            grads[source].at[every + (pl.ds(1 - bits[last], 1),) + src], core_in.at[every + (pl.ds(0, 1),) + dst], last
        )
        copy.start()
        firsts[chunk].append(copy)
        load = pltpu.make_async_copy(
            grads[source].at[every + (pl.ds(bits[last], 1),) + src], acc.at[every + (pl.ds(0, 1),) + dst],
            load_sem.at[len(loads)],
        )
        load.start()
        loads.append(load)
    for load in loads:
        load.wait()
    sends = [Group(copies) for copies in firsts]
    for step in range(last + 1):
        for c, (start, width) in enumerate(chunks):
            cols = pl.ds(start, width)
            rest = rotations[c][:last - step]
            sends[c].wait()
            for n in range(2 ** len(rest)):
                spread = [(n >> (len(rest) - 1 - i)) & 1 for i in range(len(rest))]
                index = [bits[d] if d not in rest else spread[rest.index(d)] for d in range(last)]
                at = tuple(index) + (0, slice(None), cols)
                other = core_in[at] if step == 0 else inboxes[step - 1][n, :, cols]
                if step < last:
                    add_into(acc, at, other)
                else:
                    out_ref[:, cols] = (acc[at].astype(F32) + other.astype(F32)).astype(out_ref.dtype)
            if step < last:
                dim, spread_dims = rest[-1], rest[:-1]
                group = []
                for n in range(2 ** len(spread_dims)):
                    spread = [(n >> (len(spread_dims) - 1 - i)) & 1 for i in range(len(spread_dims))]
                    index = [
                        1 - bits[d] if d == dim else (spread[spread_dims.index(d)] if d in spread_dims else bits[d])
                        for d in range(last)
                    ]
                    copy = remote(acc.at[tuple(index) + (0, slice(None), cols)], inboxes[step].at[n, :, cols], dim)
                    copy.start()
                    group.append(copy)
                sends[c] = Group(group)


def cube_scatter(dims, rotations, chunks, segments, grads, dtype, collective, name):
    last = len(dims) - 1
    rows = grads[0].shape[0] // 2 ** len(dims)
    width = sum(chunk[1] for chunk in chunks)
    copies = len(segments) + len(chunks) * (2 ** last - 1)
    return pl.pallas_call(
        functools.partial(scatter_kernel, dims, rotations, chunks, segments, len(grads)),
        in_specs=[pl.BlockSpec(memory_space=pl.ANY)] * len(grads),
        out_specs=pl.BlockSpec(memory_space=pltpu.VMEM),
        out_shape=jax.ShapeDtypeStruct((rows, width), dtype),
        scratch_shapes=[pltpu.VMEM((2,) * last + (1, rows, width), BF)] * 2
        + [pltpu.VMEM((2 ** n, rows, width), BF) for n in reversed(range(last))]
        + [
            pltpu.SemaphoreType.DMA((len(segments),)),
            pltpu.SemaphoreType.DMA((copies,)),
            pltpu.SemaphoreType.DMA((copies,)),
        ],
        compiler_params=pltpu.CompilerParams(
            collective_id=collective, has_side_effects=True, vmem_limit_bytes=60 * 2**20
        ),
        name=name,
    )(*[g.reshape((2,) * len(dims) + (rows, g.shape[1])) for g in grads])


def dense_segments(wide):
    cut = wide // 256 * 128 + 128
    return ((0, 0, cut, 0), (0, cut, wide - cut, 1), (1, 0, 128, 1), (2, 0, 1536, 2), (3, 0, 128, 2))


def scatter_all(grads):
    segments, chunks, at = [], [0, 0, 0], 0
    for source, start, width, chunk in dense_segments(grads[0].shape[1]):
        segments.append((source, start, at, width, chunk))
        chunks[chunk] += width
        at += width
    starts = (0, chunks[0], chunks[0] + chunks[1])
    return cube_scatter(
        CUBE, ROTATIONS, tuple(zip(starts, chunks)), tuple(segments), grads, F32, 4, "scatter_all"
    )


def group_back(grad_key, grad_value):
    width = grad_key.shape[1]
    segments = ((0, 0, 0, width, 0), (1, 0, width, width, 1))
    return cube_scatter(
        GROUP, ((0, 1), (1, 0)), ((0, width), (width, width)), segments, [grad_key, grad_value], BF, 6, "group_back"
    )


def group_rows_kernel(rows_ref, key_ref, value_ref, own_sem, send_sem, recv_sem):
    barrier_with([flipped(*dim) for dim in GROUP])
    bits = [own_bit(*dim) for dim in GROUP]
    width = key_ref.shape[4]
    here = tuple(pl.ds(bit, 1) for bit in bits)
    own = [
        pltpu.make_async_copy(rows_ref.at[:, :, :, :, pl.ds(i * width, width)], ref.at[here], own_sem.at[i])
        for i, ref in enumerate((key_ref, value_ref))
    ]
    for copy in own:
        copy.start()
    for copy in own:
        copy.wait()
    copies = []
    running = [None, None]
    for step in range(3):
        for f, (ref, order) in enumerate(((key_ref, (0, 1, 2)), (value_ref, (1, 0, 2)))):
            if running[f] is not None:
                running[f].wait_recv()
            at = tuple(pl.ds(0, 2) if d in order[:step] else pl.ds(bits[d], 1) for d in range(3))
            copy = pltpu.make_async_remote_copy(
                src_ref=ref.at[at], dst_ref=ref.at[at], send_sem=send_sem.at[step, f], recv_sem=recv_sem.at[step, f],
                device_id=flipped(*GROUP[order[step]]), device_id_type=pl.DeviceIdType.MESH,
            )
            copy.start()
            copies.append(copy)
            running[f] = copy
    for copy in running:
        copy.wait_recv()
    for copy in copies:
        copy.wait_send()


def group_rows(key_value):
    rows, width = key_value.shape
    anywhere = pl.BlockSpec(memory_space=pl.ANY)
    outs = pl.pallas_call(
        group_rows_kernel,
        in_specs=[pl.BlockSpec(memory_space=pltpu.VMEM)],
        out_specs=[anywhere] * 2,
        out_shape=[jax.ShapeDtypeStruct((2, 2, 2, rows, width // 2), BF)] * 2,
        scratch_shapes=[
            pltpu.SemaphoreType.DMA((2,)),
            pltpu.SemaphoreType.DMA((3, 2)),
            pltpu.SemaphoreType.DMA((3, 2)),
        ],
        compiler_params=pltpu.CompilerParams(collective_id=5, has_side_effects=True),
        name="group_rows",
    )(key_value.reshape(1, 1, 1, rows, width))
    return [out.reshape(8 * rows, width // 2) for out in outs]


D = 1536
EPSILON = 1e-06
EVERYWHERE = ("dp", "expert")


def exchange(value, axis, mask):
    return lax.ppermute(value, axis, [(i, i ^ mask) for i in range(lax.axis_size(axis))])


def tie(first, *others):
    return lax.optimization_barrier((first, *others))[0]


def rms_scale(values):
    return lax.rsqrt(jnp.mean(values * values, axis=-1, keepdims=True) + EPSILON)


def product(left, right):
    return jnp.dot(left, right, preferred_element_type=F32)


def contract_rows(left, right):
    return jnp.einsum("ta,tb->ab", left, right, preferred_element_type=F32)


def times_transposed(left, right):
    return jnp.einsum("ta,ba->tb", left, right, preferred_element_type=F32)


def added(left, right):
    return (left.astype(F32) + right.astype(F32)).astype(BF)


def team_gather(value, order):
    pieces = {0: value}
    for axis, mask, bit in order:
        pieces.update({r | bit: exchange(v, axis, mask) for r, v in list(pieces.items())})
    return jnp.stack([pieces[r] for r in sorted(pieces)])


TEAM_BITS = (("dp", 2, 4), ("expert", 2, 2), ("expert", 1, 1))


def local(tokens, attn_gain, w_query, w_key, w_value, w_out, w_router, ffn_gain, w_gate, w_up, w_down, routes, cotangent):
    dp, expert_at = lax.axis_index("dp"), lax.axis_index("expert")
    shards, owners = lax.axis_size("dp"), lax.axis_size("expert")
    cube = shards == 8 and owners == 4
    turn = (dp >> 1) & 1
    tok_rows = tokens.shape[0]
    per_owner, piece, hidden = w_gate.shape
    count = per_owner // 2
    expert_count = per_owner * owners
    top_count = routes.shape[1]
    kvw = w_key.shape[1]
    capacity = 8 * ((17 * top_count * tok_rows + 128 * expert_count - 1) // (128 * expert_count))
    slots = SLOTS_ALIGN * (-(-capacity // SLOTS_ALIGN))
    dp_index = dp.astype(jnp.int32).reshape(1)
    wide = D + 2 * kvw

    stacked = jnp.stack([w_gate, w_up, w_down.transpose(0, 2, 1)], 1)
    own = lax.dynamic_slice_in_dim(stacked, turn * count, count, 0)
    other = lax.dynamic_slice_in_dim(stacked, (1 - turn) * count, count, 0)
    gains = jnp.pad(jnp.stack([attn_gain, ffn_gain], 1), ((0, 0), (0, 126)))
    dense = [
        jnp.concatenate([w_query, w_key, w_value], 1), gains, w_out,
        jnp.pad(w_router, ((0, 0), (0, 128 - expert_count))),
    ]
    ahead = 2
    if cube:
        dense_full, taken, routes_t = gather_all(dense, dense_segments(wide), other[:ahead], routes.T)
    else:
        routes_t = team_gather(routes.T, TEAM_BITS)
        dense_full = [lax.all_gather(shard, EVERYWHERE, axis=0, tiled=True) for shard in dense]
        taken = exchange(other[:ahead], "dp", 2)
    qkv_full, gains_full, out_full, router_full = dense_full
    gains_full = gains_full.astype(F32).T
    gain_first, gain_second = gains_full[0], gains_full[1]

    relay_bits = [1 << b for b in range(2, shards.bit_length() - 1)]
    pairs = [jnp.stack([own[k], taken[k]]) for k in range(ahead)]

    def crossed(relayed):
        return [w for v in relayed for w in (v, exchange(v, "dp", 1))]

    def relays(pair):
        pieces = [pair]
        for bit in relay_bits:
            pieces += [exchange(v, "dp", bit) for v in pieces]
        return pieces

    first_expert = expert_at * per_owner + turn * count
    local_ids = first_expert + jnp.arange(count, dtype=jnp.int32)
    hits = jnp.any(routes_t[:, None] == local_ids[None, :, None, None], axis=2)
    row_id = lax.broadcasted_iota(jnp.int32, (tok_rows, tok_rows), 0)
    col_id = lax.broadcasted_iota(jnp.int32, (tok_rows, tok_rows), 1)
    before = jnp.where(row_id < col_id, 1.0, 0.0).astype(BF)
    ranks = product(hits.astype(BF).reshape(-1, tok_rows), before).reshape(hits.shape)
    positions = jnp.where(hits, ranks.astype(jnp.int32), -1)
    positions = jnp.pad(positions, ((0, 0), (0, 8 - count), (0, 0)), constant_values=-1)

    inputs = tokens.astype(F32)
    scale_one = rms_scale(inputs)
    normed_one = inputs * scale_one
    hidden_one = (normed_one * gain_first).astype(BF)
    qkv = product(hidden_one, qkv_full).astype(BF)
    query, key_value = qkv[:, :D], qkv[:, D:]
    place = ((dp & 1) * owners + expert_at).astype(jnp.int32).reshape(1)
    prompt_key, prompt_value = group_rows(key_value[:P_DEV])
    own_key, own_value = key_value[P_DEV:, :kvw], key_value[P_DEV:, kvw:]
    early = tie(cotangent, qkv_full)
    paired = exchange(early, "dp", 2)
    query, early, paired, prompt_key, pairs[:2], late = lax.optimization_barrier(
        (query, early, paired, prompt_key, pairs[:2], other[ahead:])
    )
    parts = [early, exchange(early, "expert", 2), paired, exchange(paired, "expert", 2)]
    taken_late = exchange(late, "dp", 2)
    pairs += [jnp.stack([own[k], taken_late[k - ahead]]) for k in range(ahead, count)]
    crossings = [exchange(pairs[k], "dp", 1) for k in range(2)]
    mixed, levels = attend(place, query, prompt_key, prompt_value, own_key, own_value)
    second = inputs + product(mixed, out_full)
    scale_two = rms_scale(second)
    normed_two = second * scale_two
    hidden_two = (normed_two * gain_second).astype(BF)
    logits = product(hidden_two, router_full)[:, :expert_count]
    expert_ids = jnp.arange(expert_count, dtype=jnp.int32)
    chosen = jnp.any(routes[:, :, None] == expert_ids, axis=1)
    peak = jnp.max(jnp.where(chosen, logits, NEGATIVE), axis=-1, keepdims=True)
    raised = jnp.where(chosen, jnp.exp(jnp.where(chosen, logits - peak, 0.0)), 0.0)
    gates = raised / jnp.sum(raised, axis=-1, keepdims=True)

    weights = [None] * count
    near = exchange(tie(pairs[0], taken_late), "dp", 4) if cube else None
    sent_rows, parts, crossings = lax.optimization_barrier((hidden_two, parts, crossings))
    core_jobs = (("expert", 1),) * 4
    if cube:
        rows, gates_t, takes = team_rows(
            sent_rows, gates.T, core_jobs + (("dp", 1),) * 3, (*parts, *pairs[2:]), (1, 2), pairs[1:3], other
        )
        parts = parts + takes[0:4]
        crossings = crossings + takes[4:7]
        relayed_pairs = [near] + takes[7:9]
        for k in range(3, count):
            relayed_pairs.append(exchange(tie(pairs[k], rows), "dp", 4))
        for k in range(count):
            weights[k] = [pairs[k], crossings[k], relayed_pairs[k]]
    else:
        rows, gates_t, takes = team_rows(sent_rows, gates.T, core_jobs, parts)
        parts = parts + takes
        for k in range(count):
            weights[k] = crossed(relays(tie(pairs[k], rows)))
    parts = [parts[r % 2 * 4 + r // 2] for r in range(8)]
    gates_t = lax.dynamic_slice_in_dim(gates_t, first_expert, count, 1)
    gates_t = jnp.pad(gates_t, ((0, 0), (0, 8 - count), (0, 0)))
    grad_slots = gather_parts(positions, parts, count, slots)
    row_slots, gate_slots = gather_rows(positions, gates_t, rows, count, slots)

    results, backs, gate_rows, sums = [], [], [], []
    expert_index = dp_index
    for k in range(count):
        if cube:
            relayed_pair = tie(weights[k][2], rows) if k < 3 else tie(weights[k][2], gate_rows[k - 2])
            weights[k].append(exchange(relayed_pair, "dp", 1))
        y, dx, dg, keep, send = run_expert(k, expert_index, row_slots, grad_slots, gate_slots, weights[k], slots)
        results.append(y)
        backs.append(dx)
        gate_rows.append(dg)
        sums.append((keep, send))
        expert_index = tie(dp_index, dg)

    before_return = added(sums[0][0], exchange(sums[0][1], "dp", 1))
    jobs, gives, relays_in = (("dp", 1),) * 2, (sums[1][1], sums[2][1]), 0
    if cube:
        jobs, gives, relays_in = (("dp", 4),) + jobs, (before_return[2:],) + gives, 1
    routed_back, gate_grad, out_keep, out_sent, takes = return_rows(
        positions, backs, results, gate_rows, expert_count, slots, jobs, gives, relays_in
    )
    halved = [before_return, added(sums[1][0], takes[-2]), added(sums[2][0], takes[-1])]
    crossed_back = [exchange(tie(sums[3][1], routed_back), "dp", 1)]
    relay_bits = relay_bits[::-1]

    def sent_on(keep):
        return exchange(keep[keep.shape[0] // 2:], "dp", relay_bits[0])

    def settled(keep, came):
        keep = added(keep[:keep.shape[0] // 2], came)
        for bit in relay_bits[1:]:
            middle = keep.shape[0] // 2
            keep = added(keep[:middle], exchange(keep[middle:], "dp", bit))
        return keep

    relay_came = [takes[0] if cube else sent_on(before_return)] + [sent_on(keep) for keep in halved[1:]]
    gate_grad = gate_grad.T
    routed_back = routed_back.astype(F32)

    grad_output = cotangent.astype(F32)
    picked = jnp.where(chosen, gate_grad, 0.0)
    grad_logits = (gates * (picked - jnp.sum(gates * picked, axis=-1, keepdims=True))).astype(BF)
    wide_logits = jnp.pad(grad_logits, ((0, 0), (0, 128 - expert_count)))
    grad_hidden_two = times_transposed(wide_logits, router_full) + routed_back
    grad_normed_two = grad_hidden_two * gain_second
    grad_second = grad_output + scale_two * (
        grad_normed_two - normed_two * jnp.mean(grad_normed_two * normed_two, axis=-1, keepdims=True)
    )
    grad_branch = grad_second.astype(BF)
    ones = jnp.ones((tok_rows, 128), BF)
    lane = lax.broadcasted_iota(jnp.int32, (tok_rows, 128), 1)
    small = contract_rows(hidden_two, wide_logits) + contract_rows(
        (grad_hidden_two * normed_two).astype(BF), jnp.where(lane == expert_count, ones, jnp.zeros_like(ones))
    )
    out_grad = contract_rows(mixed, grad_branch).astype(BF)
    grad_mixed = times_transposed(grad_branch, out_full).astype(BF)

    grad_mixed, relay_came[1], crossed_back[0] = lax.optimization_barrier(
        (grad_mixed, relay_came[1], crossed_back[0])
    )
    halved.append(added(sums[3][0], crossed_back[0]))
    crossed_back.append(exchange(tie(sums[4][1], crossed_back[0]), "dp", 1))
    relay_came.append(sent_on(halved[3]))
    grad_mixed, halved = lax.optimization_barrier((grad_mixed, halved))
    row_came = exchange(out_sent, "expert", 2)
    grad_query, dkp, dvp, dko, dvo = attend_back(
        place, query, prompt_key, prompt_value, own_key, own_value, mixed, grad_mixed, levels
    )
    halved, relay_came, crossed_back, grad_query, row_came, dkp = lax.optimization_barrier(
        (halved, relay_came, crossed_back, grad_query, row_came, dkp)
    )
    halved.append(added(sums[4][0], crossed_back[1]))
    relay_came.append(sent_on(halved[4]))
    grad_prompt = group_back(dkp, dvp)
    total = tie(added(out_keep, row_came), grad_prompt)
    pair_came = exchange(total[1], "dp", 2)
    grad_qkv = jnp.concatenate([
        grad_query, jnp.concatenate([grad_prompt, jnp.concatenate([dko, dvo], 1)], 0)
    ], 1)
    grad_hidden_one = times_transposed(grad_qkv, qkv_full)
    dense_grads = [
        contract_rows(hidden_one, grad_qkv).astype(BF),
        contract_rows((grad_hidden_one * normed_one).astype(BF), ones).astype(BF),
        out_grad, small.astype(BF),
    ]
    dense_grads, relay_came = lax.optimization_barrier((dense_grads, relay_came))
    if cube:
        share = scatter_all(dense_grads)
    else:
        share = lax.psum_scatter(
            jnp.concatenate(dense_grads, 1), EVERYWHERE, scatter_dimension=0, tiled=True
        ).astype(F32)
    grad_normed_one = grad_hidden_one * gain_first
    grad_input = grad_second + scale_one * (
        grad_normed_one - normed_one * jnp.mean(grad_normed_one * normed_one, axis=-1, keepdims=True)
    )

    share, halved, relay_came, total, pair_came = lax.optimization_barrier(
        (share, halved, relay_came, total, pair_came)
    )
    output = (second + added(total[0], pair_came).astype(F32)).astype(BF)
    first_share, second_share = share[:, :wide + 128], share[:, wide + 128:]
    relayed = [settled(halved[k], relay_came[k]) for k in range(count)]
    theirs = exchange(jnp.stack([keep[1] for keep in relayed]), "dp", 2)
    mine = jnp.stack([keep[0] for keep in relayed])
    lower = jnp.where(turn == 0, mine, theirs)
    upper = jnp.where(turn == 0, theirs, mine)
    expert_grads = jnp.concatenate([lower, upper]).astype(F32)
    return (
        output,
        grad_input.astype(BF),
        first_share[:, wide],
        first_share[:, :D],
        first_share[:, D:D + kvw],
        first_share[:, D + kvw:wide],
        second_share[:, :D].astype(F32),
        second_share[:, D:D + expert_count].astype(F32),
        second_share[:, D + expert_count].astype(F32),
        expert_grads[:, 0],
        expert_grads[:, 1],
        expert_grads[:, 2].transpose(0, 2, 1),
    )


def solution(mesh):
    rows, line = P(("dp", "expert"), None), P(("dp", "expert"))
    gate, down = P("expert", "dp", None), P("expert", None, "dp")
    return jax.shard_map(
        local,
        mesh=mesh,
        in_specs=(rows, line, rows, rows, rows, rows, rows, line, gate, gate, down, rows, rows),
        out_specs=(rows, rows, line, rows, rows, rows, rows, rows, line, gate, gate, down),
        check_vma=False,
    )
```

```python
import functools
import jax
import jax.numpy as jnp
from jax import lax
from jax.sharding import PartitionSpec as P
from jax.experimental import pallas as pl
from jax.experimental.pallas import tpu as pltpu

HD = 64
P_DEV = 128
NEGATIVE = -1e30
F32 = jnp.float32
BF = jnp.bfloat16


def dot_nt(a, b):
    return lax.dot_general(a, b, (((1,), (1,)), ((), ())), preferred_element_type=F32)


def dot_nn(a, b):
    return lax.dot_general(a, b, (((1,), (0,)), ((), ())), preferred_element_type=F32)


def dot_tn(a, b):
    return lax.dot_general(a, b, (((0,), (0,)), ((), ())), preferred_element_type=F32)


def halves(pair):
    lane = lax.broadcasted_iota(jnp.int32, pair.shape, 1)
    zero = jnp.zeros_like(pair)
    return jnp.where(lane < HD, pair, zero), jnp.where(lane < HD, zero, pair)


def placed_halves(pair_f32):
    low0, high1 = halves(pair_f32)
    high0 = pltpu.roll(low0, HD, 1)
    low1 = pltpu.roll(high1, HD, 1)
    return ((low0.astype(BF), high0.astype(BF)), (low1.astype(BF), high1.astype(BF)))


def attend_kernel(place_ref, q_ref, kp_ref, vp_ref, ko_ref, vo_ref, o_ref, lse_ref, kpad, vpad, s_scr, p_scr):
    rows = q_ref.shape[0]
    prompt = kp_ref.shape[0]
    cont = ko_ref.shape[0]
    place = place_ref[0]
    for src, dst in ((kp_ref, kpad), (vp_ref, vpad)):
        for head, pair in enumerate(placed_halves(src[...].astype(F32))):
            for half in range(2):
                dst[head, half, 0:prompt, :] = pair[half]
    for src, dst in ((ko_ref, kpad), (vo_ref, vpad)):
        for head, pair in enumerate(placed_halves(src[...].astype(F32))):
            for half in range(2):
                dst[head, half, prompt:prompt + cont, :] = pair[half]
    key_id = lax.broadcasted_iota(jnp.int32, (prompt, P_DEV), 0)
    row_id = lax.broadcasted_iota(jnp.int32, (prompt, P_DEV), 1)
    seen_prompt = key_id <= place * P_DEV + row_id
    diag = lax.broadcasted_iota(jnp.int32, (P_DEV, P_DEV), 0) <= lax.broadcasted_iota(jnp.int32, (P_DEV, P_DEV), 1)
    blocks = cont // P_DEV
    stats = []
    for chunk in range(3):
        queries = (q_ref[:, chunk * 128:(chunk + 1) * 128].astype(F32) * HD ** (-0.5)).astype(BF)
        total = None
        for half in range(2):
            position = chunk * 2 + half
            head = position // 3
            keys = kpad.at[head, half]
            scores = dot_nt(keys[0:prompt, :], queries)
            first = jnp.where(seen_prompt, scores[:, 0:P_DEV], NEGATIVE)
            rest = scores[:, P_DEV:]
            s_scr[0:prompt, 0:P_DEV] = first
            s_scr[0:prompt, P_DEV:] = rest
            top = jnp.concatenate([jnp.max(first, 0, keepdims=True), jnp.max(rest, 0, keepdims=True)], 1)
            tops = [top[:, i * P_DEV:(i + 1) * P_DEV] for i in range(1 + blocks)]
            for block in range(blocks):
                start = (1 + block) * P_DEV
                at = prompt + block * P_DEV
                own = dot_nt(keys[at:at + P_DEV, :], queries[start:, :])
                edge = jnp.where(diag, own[:, 0:P_DEV], NEGATIVE)
                s_scr[at:at + P_DEV, start:start + P_DEV] = edge
                tops[1 + block] = jnp.maximum(tops[1 + block], jnp.max(edge, 0, keepdims=True))
                if block + 1 < blocks:
                    later = own[:, P_DEV:]
                    s_scr[at:at + P_DEV, start + P_DEV:] = later
                    best = jnp.max(later, 0, keepdims=True)
                    for i in range(block + 1, blocks):
                        at_i = (i - block - 1) * P_DEV
                        tops[1 + i] = jnp.maximum(tops[1 + i], best[:, at_i:at_i + P_DEV])
            top = jnp.concatenate(tops, 1)
            weights = jnp.exp(s_scr[0:prompt, :] - top)
            mass = jnp.sum(weights, 0, keepdims=True)
            masses = [mass[:, i * P_DEV:(i + 1) * P_DEV] for i in range(1 + blocks)]
            values = vpad.at[head, half]
            mixed = dot_tn(values[0:prompt, :], weights.astype(BF))
            for block in range(blocks):
                start = (1 + block) * P_DEV
                at = prompt + block * P_DEV
                part = jnp.exp(s_scr[at:at + P_DEV, start:] - top[:, start:])
                p_scr[block * P_DEV:(block + 1) * P_DEV, start:] = part.astype(BF)
                if block:
                    p_scr[block * P_DEV:(block + 1) * P_DEV, P_DEV:start] = jnp.zeros((P_DEV, block * P_DEV), BF)
                part_mass = jnp.sum(part, 0, keepdims=True)
                for i in range(block, blocks):
                    at_i = (i - block) * P_DEV
                    masses[1 + i] = masses[1 + i] + part_mass[:, at_i:at_i + P_DEV]
            own_mixed = dot_tn(values[prompt:prompt + cont, :], p_scr[:, P_DEV:])
            mass = jnp.concatenate(masses, 1)
            scale = 1.0 / mass
            mixed = jnp.concatenate([mixed[:, 0:P_DEV], mixed[:, P_DEV:] + own_mixed], 1) * scale
            total = mixed if total is None else total + mixed
            stats.append(top + jnp.log(mass))
        o_ref[:, chunk * 128:(chunk + 1) * 128] = jnp.transpose(total).astype(BF)
    lse_ref[0] = jnp.concatenate(stats + [jnp.zeros((2, rows), F32)], 0)


def attend(place, query, prompt_key, prompt_value, own_key, own_value):
    rows = query.shape[0]
    prompt = prompt_key.shape[0]
    cont = own_key.shape[0]
    pairs = prompt_key.shape[1] // 128
    col = lambda i: (0, i)
    return pl.pallas_call(
        attend_kernel,
        grid=(pairs,),
        in_specs=[
            pl.BlockSpec(memory_space=pltpu.SMEM),
            pl.BlockSpec((rows, 384), col),
            pl.BlockSpec((prompt, 128), col),
            pl.BlockSpec((prompt, 128), col),
            pl.BlockSpec((cont, 128), col),
            pl.BlockSpec((cont, 128), col),
        ],
        out_specs=[pl.BlockSpec((rows, 384), col), pl.BlockSpec((1, 8, rows), lambda i: (i, 0, 0))],
        out_shape=[
            jax.ShapeDtypeStruct(query.shape, BF),
            jax.ShapeDtypeStruct((pairs, 8, rows), F32),
        ],
        scratch_shapes=[
            pltpu.VMEM((2, 2, prompt + cont, 128), BF),
            pltpu.VMEM((2, 2, prompt + cont, 128), BF),
            pltpu.VMEM((prompt + cont, rows), F32),
            pltpu.VMEM((cont, rows), BF),
        ],
        cost_estimate=pl.CostEstimate(flops=10**6, bytes_accessed=10**6, transcendentals=0),
        name="attend",
    )(place, query, prompt_key, prompt_value, own_key, own_value)


def attend_back_kernel(place_ref, q_ref, kp_ref, vp_ref, ko_ref, vo_ref, o_ref, do_ref, lse_ref,
                       dq_ref, dkp_ref, dvp_ref, dko_ref, dvo_ref, kpad, vpad, dk_acc, dv_acc):
    rows = q_ref.shape[0]
    prompt = kp_ref.shape[0]
    cont = ko_ref.shape[0]
    step = 2 * P_DEV
    place = place_ref[0]
    for src, dst, at, size in ((kp_ref, kpad, 0, prompt), (vp_ref, vpad, 0, prompt),
                               (ko_ref, kpad, prompt, cont), (vo_ref, vpad, prompt, cont)):
        for head, pair in enumerate(placed_halves(src[...].astype(F32))):
            for half in range(2):
                dst[head, half, at:at + size, :] = pair[half]
    dk_acc[...] = jnp.zeros_like(dk_acc)
    dv_acc[...] = jnp.zeros_like(dv_acc)
    for chunk in range(3):
        lanes = slice(chunk * 128, (chunk + 1) * 128)
        scaled = q_ref[:, lanes].astype(F32) * HD ** (-0.5)
        queries = scaled.astype(BF)
        query_halves = [part.astype(BF) for part in halves(scaled)]
        outs = o_ref[:, lanes].astype(F32)
        grads_f32 = do_ref[:, lanes].astype(F32)
        grads = do_ref[:, lanes]
        grad_halves = [part.astype(BF) for part in halves(grads_f32)]
        inner = jnp.transpose(outs * grads_f32)
        total = jnp.zeros((128, rows), F32)
        for half in range(2):
            position = chunk * 2 + half
            head = position // 3
            level = lse_ref[0, position:position + 1, :]
            delta = jnp.sum(inner[half * HD:(half + 1) * HD, :], 0, keepdims=True)

            def block(at, cols, mask, queries=queries, grads=grads, query_half=query_halves[half],
                      grad_half=grad_halves[half], level=level, delta=delta, head=head, half=half):
                keys = kpad[head, half, pl.ds(at, step), :]
                values = vpad[head, half, pl.ds(at, step), :]
                scores = dot_nt(keys, queries[cols, :])
                weights = jnp.exp(mask(scores) - level[:, cols])
                grad_weights = dot_nt(values, grads[cols, :])
                grad_scores = weights * (grad_weights - delta[:, cols])
                low_weights = weights.astype(BF)
                low_scores = grad_scores.astype(BF)
                dv_acc[head, pl.ds(at, step), :] += dot_nn(low_weights, grad_half[cols, :])
                dk_acc[head, pl.ds(at, step), :] += dot_nn(low_scores, query_half[cols, :])
                return dot_tn(keys, low_scores)

            def prompt_step(i, carry):
                at = pl.multiple_of(i * step, step)

                def mask(scores):
                    key_id = at + lax.broadcasted_iota(jnp.int32, (step, P_DEV), 0)
                    row_id = lax.broadcasted_iota(jnp.int32, (step, P_DEV), 1)
                    first = jnp.where(key_id <= place * P_DEV + row_id, scores[:, 0:P_DEV], NEGATIVE)
                    return jnp.concatenate([first, scores[:, P_DEV:]], 1)

                return carry + block(at, slice(0, rows), mask)

            total = lax.fori_loop(0, prompt // step, prompt_step, total)
            for own in range(cont // step):
                start = P_DEV + own * step

                def mask(scores):
                    key_id = lax.broadcasted_iota(jnp.int32, (step, step), 0)
                    row_id = lax.broadcasted_iota(jnp.int32, (step, step), 1)
                    edge = jnp.where(key_id <= row_id, scores[:, 0:step], NEGATIVE)
                    if scores.shape[1] == step:
                        return edge
                    return jnp.concatenate([edge, scores[:, step:]], 1)

                part = block(prompt + own * step, slice(start, rows), mask)
                total = jnp.concatenate([total[:, 0:start], total[:, start:] + part], 1)
        dq_ref[:, lanes] = (jnp.transpose(total) * HD ** (-0.5)).astype(BF)
    for acc, out_prompt, out_own in ((dk_acc, dkp_ref, dko_ref), (dv_acc, dvp_ref, dvo_ref)):
        low0, high0 = halves(acc[0])
        low1, high1 = halves(acc[1])
        merged = low0 + pltpu.roll(high0, HD, 1) + high1 + pltpu.roll(low1, HD, 1)
        out_prompt[...] = merged[0:prompt].astype(BF)
        out_own[...] = merged[prompt:].astype(BF)


def attend_back(place, query, prompt_key, prompt_value, own_key, own_value, mixed, grad, lse):
    rows = query.shape[0]
    prompt = prompt_key.shape[0]
    cont = own_key.shape[0]
    pairs = prompt_key.shape[1] // 128
    col = lambda i: (0, i)
    wide = pl.BlockSpec((rows, 384), col)
    keys_p = pl.BlockSpec((prompt, 128), col)
    keys_o = pl.BlockSpec((cont, 128), col)
    return pl.pallas_call(
        attend_back_kernel,
        grid=(pairs,),
        in_specs=[
            pl.BlockSpec(memory_space=pltpu.SMEM),
            wide, keys_p, keys_p, keys_o, keys_o, wide, wide,
            pl.BlockSpec((1, 8, rows), lambda i: (i, 0, 0)),
        ],
        out_specs=[wide, keys_p, keys_p, keys_o, keys_o],
        out_shape=[
            jax.ShapeDtypeStruct(query.shape, BF),
            jax.ShapeDtypeStruct(prompt_key.shape, BF),
            jax.ShapeDtypeStruct(prompt_key.shape, BF),
            jax.ShapeDtypeStruct(own_key.shape, BF),
            jax.ShapeDtypeStruct(own_key.shape, BF),
        ],
        scratch_shapes=[
            pltpu.VMEM((2, 2, prompt + cont, 128), BF),
            pltpu.VMEM((2, 2, prompt + cont, 128), BF),
            pltpu.VMEM((2, prompt + cont, 128), F32),
            pltpu.VMEM((2, prompt + cont, 128), F32),
        ],
        cost_estimate=pl.CostEstimate(flops=10**6, bytes_accessed=10**6, transcendentals=0),
        name="attend_back",
    )(place, query, prompt_key, prompt_value, own_key, own_value, mixed, grad, lse)


SLOTS_ALIGN = 16


def gather_kernel(count, with_gates, pos_ref, *refs):
    if with_gates:
        gate_ref, rows_ref, x_ref, g_ref, pick = refs
    else:
        rows_ref, x_ref, pick = refs
    tokens = rows_ref.shape[1]
    slots = x_ref.shape[1] // count
    half = rows_ref.shape[2] // 2
    slot_id = lax.broadcasted_iota(jnp.int32, (slots, tokens), 0)
    for k in range(count):
        hit = slot_id == pos_ref[0, k:k + 1, :]
        pick[k * slots:(k + 1) * slots, :] = jnp.where(hit, 1.0, 0.0).astype(BF)
        if with_gates:
            gate = jnp.sum(jnp.where(hit, gate_ref[0, k:k + 1, :], 0.0), 1, keepdims=True)
            g_ref[0, k * slots:(k + 1) * slots, :] = jnp.broadcast_to(gate, (slots, 128))
    x_ref[0, :, 0:half] = dot_nn(pick[...], rows_ref[0, :, 0:half]).astype(BF)
    x_ref[0, :, half:] = dot_nn(pick[...], rows_ref[0, :, half:]).astype(BF)


def gather_rows(positions, gates, rows, count, slots):
    sources, tokens, width = rows.shape
    size = count * slots
    table = pl.BlockSpec((1, 8, tokens), lambda s: (s, 0, 0))
    block = lambda shape: pl.BlockSpec((1,) + shape, lambda s: (s, 0, 0))
    tables = [positions] if gates is None else [positions, gates]
    outs = [((size, width), BF)] if gates is None else [((size, width), BF), ((size, 128), F32)]
    return pl.pallas_call(
        functools.partial(gather_kernel, count, gates is not None),
        grid=(sources,),
        in_specs=[table] * len(tables) + [block((tokens, width))],
        out_specs=[block(shape) for shape, _ in outs],
        out_shape=[jax.ShapeDtypeStruct((sources,) + shape, dtype) for shape, dtype in outs],
        scratch_shapes=[pltpu.VMEM((size, tokens), BF)],
        cost_estimate=pl.CostEstimate(flops=10**6, bytes_accessed=10**6, transcendentals=0),
        name="gather_rows",
    )(*tables, rows)


def expert_kernel(k, shards, slots, dp_ref, x_ref, g_ref, gate_ref, *refs):
    w_refs = refs[0:shards // 2]
    (y_out, dx_out, dg_out, keep_out, send_out,
     xs, gs, gates, ws, ys, dxs, dgs, dab, actg, stage,
     in_sem, w_sem, out_sem, grad_sem) = refs[shards // 2:]
    dp = dp_ref[0]
    sources = x_ref.shape[0]
    width = xs.shape[1]
    piece = width // shards
    hidden = ws.shape[2]
    mine = pl.ds(k * slots, slots)

    def row_copies(s):
        at = pl.ds(pl.multiple_of(s * slots, 16), slots)
        return (
            pltpu.make_async_copy(x_ref.at[s, mine, :], xs.at[at, :], in_sem.at[0, s]),
            pltpu.make_async_copy(g_ref.at[s, mine, :], gs.at[at, :], in_sem.at[1, s]),
            pltpu.make_async_copy(gate_ref.at[s, mine, :], gates.at[at, :], in_sem.at[2, s]),
        )

    weight_copies = [
        pltpu.make_async_copy(
            w_refs[(r & 1) + 2 * (r >> 2)].at[(r >> 1) & 1], ws.at[:, pl.ds(pl.multiple_of((dp ^ r) * piece, 16), piece), :], w_sem.at[r]
        )
        for r in range(shards)
    ]
    for s in range(sources):
        for copy in row_copies(s):
            copy.start()
        if s == 1:
            for copy in weight_copies:
                copy.start()
    for copy in weight_copies:
        copy.wait()
    chunk = 2 * slots

    def out_copies(c):
        at = pl.ds(pl.multiple_of(c * chunk, 32), chunk)
        return [
            pltpu.make_async_copy(src.at[at, :], dst.at[at, :], out_sem.at[i, c])
            for i, (src, dst) in enumerate(((ys, y_out), (dxs, dx_out), (dgs, dg_out)))
        ]

    def forward_chunk(c, carry):
        for copy in row_copies(2 * c) + row_copies(2 * c + 1):
            copy.wait()
        rows = pl.ds(pl.multiple_of(c * chunk, 32), chunk)
        x = xs[rows, :]
        a = dot_nn(x, ws[0])
        b = dot_nn(x, ws[1])
        pulled = dot_nn(gs[rows, :], ws[2])
        gate = gates[rows, 0:1]
        sig = jax.nn.sigmoid(a)
        silu = a * sig
        act = silu * b
        dgs[rows, :] = jnp.broadcast_to(jnp.sum(act * pulled, 1, keepdims=True), (chunk, 128))
        weighted = (gate * act).astype(BF)
        actg[rows, :] = weighted
        dact = gate * pulled
        da = (dact * b * sig * (1.0 + a * (1.0 - sig))).astype(BF)
        db = (dact * silu).astype(BF)
        dab[rows, 0:hidden] = da
        dab[rows, hidden:] = db
        ys[rows, :] = dot_nt(weighted, ws[2]).astype(BF)
        dxs[rows, :] = (dot_nt(da, ws[0]) + dot_nt(db, ws[1])).astype(BF)
        for copy in out_copies(c):
            copy.start()
        return carry

    lax.fori_loop(0, sources // 2, forward_chunk, 0)
    block = 384
    inner = block // piece
    high = dp // inner
    low = dp % inner

    def grad_copies(jr):
        slot = lax.rem(jr, 2)
        copies = []
        for ri in range(inner):
            dst = (send_out if ri % 2 else keep_out).at[jr * (inner // 2) + ri // 2]
            src = stage.at[slot, :, pl.ds(pl.multiple_of((low ^ ri) * piece, 16), piece), :]
            copies.append(pltpu.make_async_copy(src, dst, grad_sem.at[slot, ri]))
        return copies

    def grad_block(jr, carry):
        slot = lax.rem(jr, 2)

        @pl.when(jr >= 2)
        def _():
            for copy in grad_copies(jr - 2):
                copy.wait()

        cols = pl.ds(pl.multiple_of((high ^ jr) * block, 128), block)
        left = dot_tn(xs[:, cols], dab[...])
        stage[slot, 0] = left[:, 0:hidden].astype(BF)
        stage[slot, 1] = left[:, hidden:].astype(BF)
        stage[slot, 2] = dot_tn(gs[:, cols], actg[...]).astype(BF)
        for copy in grad_copies(jr):
            copy.start()
        return carry

    blocks = width // block
    lax.fori_loop(0, blocks, grad_block, 0)
    for jr in range(blocks - 2, blocks):
        for copy in grad_copies(jr):
            copy.wait()
    for c in range(sources // 2):
        for copy in out_copies(c):
            copy.wait()


def run_expert(k, dp_index, xs, gs, gates, weights, slots):
    sources, shards = xs.shape[0], 2 * len(weights)
    rows = sources * slots
    width = xs.shape[2]
    piece, hidden = weights[0].shape[2:]
    inner = 384 // piece
    anywhere = pl.BlockSpec(memory_space=pl.ANY)
    return pl.pallas_call(
        functools.partial(expert_kernel, k, shards, slots),
        in_specs=[pl.BlockSpec(memory_space=pltpu.SMEM)] + [anywhere] * (3 + shards // 2),
        out_specs=[anywhere] * 5,
        out_shape=[
            jax.ShapeDtypeStruct((rows, width), BF),
            jax.ShapeDtypeStruct((rows, width), BF),
            jax.ShapeDtypeStruct((rows, 128), F32),
            jax.ShapeDtypeStruct((shards // 2, 3, piece, hidden), BF),
            jax.ShapeDtypeStruct((shards // 2, 3, piece, hidden), BF),
        ],
        scratch_shapes=[
            pltpu.VMEM((rows, width), BF),
            pltpu.VMEM((rows, width), BF),
            pltpu.VMEM((rows, 128), F32),
            pltpu.VMEM((3, width, hidden), BF),
            pltpu.VMEM((rows, width), BF),
            pltpu.VMEM((rows, width), BF),
            pltpu.VMEM((rows, 128), F32),
            pltpu.VMEM((rows, 2 * hidden), BF),
            pltpu.VMEM((rows, hidden), BF),
            pltpu.VMEM((2, 3, 384, hidden), BF),
            pltpu.SemaphoreType.DMA((3, sources)),
            pltpu.SemaphoreType.DMA((shards,)),
            pltpu.SemaphoreType.DMA((3, sources // 2)),
            pltpu.SemaphoreType.DMA((2, inner)),
        ],
        compiler_params=pltpu.CompilerParams(vmem_limit_bytes=60 * 2**20),
        cost_estimate=pl.CostEstimate(flops=10**6, bytes_accessed=10**6, transcendentals=0),
        name="expert",
    )(dp_index, xs, gs, gates, *weights)


def barrier_with(partners):
    sem = pltpu.get_barrier_semaphore()
    for partner in partners:
        pl.semaphore_signal(sem, inc=1, device_id=partner, device_id_type=pl.DeviceIdType.MESH)
    pl.semaphore_wait(sem, len(partners))


def flipped(axis, mask):
    at = lax.axis_index(axis)
    bit = lax.rem(lax.div(at, mask), 2)
    return {axis: at + mask * (1 - 2 * bit)}


def own_bit(axis, mask):
    return lax.rem(lax.div(lax.axis_index(axis), mask), 2)


TEAM = (("dp", 2), ("expert", 2), ("expert", 1))
GROUP = (("dp", 1), ("expert", 2), ("expert", 1))
CUBE = (("dp", 4), ("dp", 2), ("dp", 1), ("expert", 2), ("expert", 1))
ROTATIONS = ((0, 1, 2, 3), (0, 2, 3, 1), (0, 3, 1, 2))


def gather_all_kernel(pieces, segments, count, *refs):
    shards, give_ref, routes_ref = refs[0:count], refs[count], refs[count + 1]
    fulls, take_ref, team_ref = refs[count + 2:2 * count + 2], refs[2 * count + 2], refs[2 * count + 3]
    own_sem, send_sem, recv_sem, piece_sem, team_sem = refs[2 * count + 4:]
    barrier_with([flipped(*dim) for dim in CUBE])
    bits = [own_bit(*dim) for dim in CUBE]
    here = tuple(pl.ds(bit, 1) for bit in bits)
    own = [pltpu.make_async_copy(shards[i], fulls[i].at[here], own_sem.at[i]) for i in range(count)]
    own.append(pltpu.make_async_copy(routes_ref, team_ref.at[0:1, 0:1, 0:1], own_sem.at[count]))
    for copy in own:
        copy.start()
    for copy in own:
        copy.wait()

    def routes_step(step):
        index = [pl.ds(0, 2) if d < step else pl.ds(0, 1) for d in range(3)]
        src = team_ref.at[tuple(index)]
        index[step] = pl.ds(1, 1)
        return pltpu.make_async_remote_copy(
            src_ref=src, dst_ref=team_ref.at[tuple(index)], send_sem=team_sem.at[0, step],
            recv_sem=team_sem.at[1, step], device_id=flipped(*TEAM[step]), device_id_type=pl.DeviceIdType.MESH,
        )

    def spread(step, n, gathered, dim):
        source, start, width, _ = segments[n]
        at = tuple(pl.ds(0, 2) if d in gathered else pl.ds(bits[d], 1) for d in range(5))
        ref = fulls[source].at[at + (slice(None), pl.ds(start, width))]
        return pltpu.make_async_remote_copy(
            src_ref=ref, dst_ref=ref, send_sem=send_sem.at[step, n], recv_sem=recv_sem.at[step, n],
            device_id=flipped(*CUBE[dim]), device_id_type=pl.DeviceIdType.MESH,
        )

    def hand(k):
        return pltpu.make_async_remote_copy(
            src_ref=give_ref.at[k], dst_ref=take_ref.at[k], send_sem=piece_sem.at[0, k],
            recv_sem=piece_sem.at[1, k], device_id=flipped("dp", 2), device_id_type=pl.DeviceIdType.MESH,
        )

    copies, passed = [], []
    running = [None] * len(segments)
    for step in range(5):
        if 0 < step < 4:
            routes_step(step - 1).wait()
        if step < 3:
            routes_step(step).start()
        for n, segment in enumerate(segments):
            if running[n] is not None:
                running[n].wait_recv()
            order = ROTATIONS[segment[3]] + (4,)
            copy = spread(step, n, order[:step], order[step])
            copy.start()
            copies.append(copy)
            running[n] = copy
        for k in range(pieces) if step == 4 else range(step, min(step + 1, pieces)):
            if step == 4 and k < 4:
                continue
            passed.append(hand(k))
            passed[-1].start()
    for copy in running:
        copy.wait_recv()
    for copy in copies:
        copy.wait_send()
    for copy in passed:
        copy.wait()


def gather_all(shards, segments, give, routes):
    rows = shards[0].shape[0]
    count, pieces = len(shards), give.shape[0]
    anywhere, vmem = pl.BlockSpec(memory_space=pl.ANY), pl.BlockSpec(memory_space=pltpu.VMEM)
    outs = pl.pallas_call(
        functools.partial(gather_all_kernel, pieces, segments, count),
        in_specs=[vmem] * count + [anywhere, vmem],
        out_specs=[anywhere] * (count + 2),
        out_shape=[jax.ShapeDtypeStruct((2,) * 5 + shard.shape, BF) for shard in shards]
        + [jax.ShapeDtypeStruct(give.shape, BF), jax.ShapeDtypeStruct((2, 2, 2) + routes.shape, jnp.int32)],
        scratch_shapes=[
            pltpu.SemaphoreType.DMA((count + 1,)),
            pltpu.SemaphoreType.DMA((5, len(segments))),
            pltpu.SemaphoreType.DMA((5, len(segments))),
            pltpu.SemaphoreType.DMA((2, pieces)),
            pltpu.SemaphoreType.DMA((2, 3)),
        ],
        compiler_params=pltpu.CompilerParams(collective_id=1, has_side_effects=True),
        name="gather_all",
    )(*[shard.reshape((1,) * 5 + shard.shape) for shard in shards], give, routes.reshape((1, 1, 1) + routes.shape))
    fulls = [full.reshape(32 * rows, full.shape[-1]) for full in outs[:count]]
    return fulls, outs[count], outs[count + 1].reshape((8,) + routes.shape)


def job_copies(jobs, gives, takes, sems):
    return [
        pltpu.make_async_remote_copy(
            src_ref=gives[j], dst_ref=takes[j], send_sem=sems.at[0, j], recv_sem=sems.at[1, j],
            device_id=flipped(*jobs[j]), device_id_type=pl.DeviceIdType.MESH,
        )
        for j in range(len(jobs))
    ]


def partners_of(dims, jobs):
    return [flipped(*dim) for dim in dict.fromkeys(tuple(dims) + tuple(jobs))]


def inner_plane():
    return own_bit("dp", 2) != own_bit("dp", 4)


def across():
    at = lax.axis_index("dp")
    return {"dp": at + 2 * (1 - 2 * own_bit("dp", 2)) + 4 * (1 - 2 * own_bit("dp", 4))}


def team_rows_kernel(jobs, relays, layout, experts, rows_ref, gates_ref, pos_ref, *refs):
    count, lanes = len(jobs), len(relays)
    gives, pairs = refs[0:count], refs[count:count + lanes]
    refs = refs[count + lanes:]
    if lanes:
        other_ref, refs = refs[0], refs[1:]
    all_ref, table_ref = refs[0:2]
    takes, far = refs[2:2 + count], refs[2 + count:2 + count + lanes]
    picked_ref, pick, held, built = refs[2 + count + lanes:6 + count + lanes]
    own_sem, send_sem, recv_sem, job_sem, relay_sem, held_sem, built_sem = refs[6 + count + lanes:]
    partners = partners_of(TEAM, jobs)
    if lanes:
        partners += [flipped("dp", 4), across()]
    barrier_with(partners)
    own = [
        pltpu.make_async_copy(rows_ref, all_ref.at[0:1, 0:1, 0:1], own_sem.at[0]),
        pltpu.make_async_copy(gates_ref, table_ref.at[0:1, 0:1, 0:1], own_sem.at[1]),
    ]
    for copy in own:
        copy.start()

    def leg(j, n):
        src = (pairs[j].at[0], pairs[j].at[1], other_ref.at[relays[j]])[n]
        return pltpu.make_async_remote_copy(
            src_ref=src, dst_ref=far[j].at[min(n, 1)], send_sem=relay_sem.at[n, j],
            recv_sem=relay_sem.at[3 + min(n, 1), j], device_id=across() if n == 2 else flipped("dp", 4),
            device_id_type=pl.DeviceIdType.MESH,
        )

    for copy in own:
        copy.wait()
    parts = 4
    width = all_ref.shape[4] // parts
    flows = [(all_ref, (slice(None), pl.ds(c * width, width))) for c in range(parts)]
    flows.append((table_ref, (slice(None), slice(None))))

    def hop(step, f):
        ref, tail = flows[f]
        index = [pl.ds(0, 2) if d < step else pl.ds(0, 1) for d in range(3)]
        src = ref.at[tuple(index) + tail]
        index[step] = pl.ds(1, 1)
        return pltpu.make_async_remote_copy(
            src_ref=src, dst_ref=ref.at[tuple(index) + tail], send_sem=send_sem.at[step, f],
            recv_sem=recv_sem.at[step, f], device_id=flipped(*TEAM[step]), device_id_type=pl.DeviceIdType.MESH,
        )

    order = [parts] + list(range(parts))
    for f in order:
        hop(0, f).start()
    background = job_copies(jobs, gives, takes, job_sem)
    for copy in background:
        copy.start()
    if lanes:

        @pl.when(inner_plane())
        def _():
            for n in (2, 0, 1):
                for j in range(lanes):
                    leg(j, n).start()

        @pl.when(jnp.logical_not(inner_plane()))
        def _():
            for j in range(lanes):
                leg(j, 0).start()

    tokens = rows_ref.shape[3]
    slots = pick.shape[0] // experts
    middle = all_ref.shape[4] // 2
    slot_id = lax.broadcasted_iota(jnp.int32, (slots, tokens), 0)
    turns = [(core, source) for core in range(2) for source in range(4)]

    def fetches(turn):
        core, source = turns[turn]
        copies, at = [], 0
        for n, job in enumerate(layout[source]):
            ref = (takes if core else gives)[job]
            size = ref.shape[0]
            copies.append(pltpu.make_async_copy(ref, held.at[turn % 2, pl.ds(at, size), :], held_sem.at[turn % 2, n]))
            at += size
        return copies

    def store(turn):
        core, source = turns[turn]
        return pltpu.make_async_copy(built.at[turn % 2], picked_ref.at[2 * source + core], built_sem.at[turn % 2])

    def begin(turn):
        if turns[turn][0]:
            for job in layout[turns[turn][1]]:
                background[job].wait()
        for copy in fetches(turn):
            copy.start()

    def gather(turn):
        core, source = turns[turn]
        slot = turn % 2
        for copy in fetches(turn):
            copy.wait()
        if turn + 1 < len(turns):
            begin(turn + 1)
        for k in range(experts):
            hit = slot_id == pos_ref[2 * source + core, k:k + 1, :]
            pick[k * slots:(k + 1) * slots, :] = jnp.where(hit, 1.0, 0.0).astype(BF)
        if turn >= 2:
            store(turn - 2).wait()
        built[slot, :, 0:middle] = dot_nn(pick[...], held[slot, :, 0:middle]).astype(BF)
        built[slot, :, middle:] = dot_nn(pick[...], held[slot, :, middle:]).astype(BF)
        store(turn).start()

    begin(0)
    for step in range(1, 3):
        for n, f in enumerate(order):
            hop(step - 1, f).wait_recv()
            hop(step, f).start()
            if n:
                gather(4 * (step - 1) + n - 1)
    for f in order:
        hop(2, f).wait_recv()
    store(6).wait()
    store(7).wait()
    for step in range(3):
        for f in order:
            hop(step, f).wait_send()
    used = [job for jobs_of in layout for job in jobs_of]
    for job, copy in enumerate(background):
        if job not in used:
            copy.wait()
    for j in range(lanes):
        leg(j, 0).wait()
        leg(j, 1).wait_recv()
    if lanes:

        @pl.when(inner_plane())
        def _():
            for j in range(lanes):
                leg(j, 1).wait_send()
                leg(j, 2).wait_send()


def team_rows(rows, gates, positions, layout, experts, slots, jobs=(), gives=(), relays=(), pairs=(), other=None):
    tokens, width = rows.shape
    size = experts * slots
    table = gates.shape
    anywhere = pl.BlockSpec(memory_space=pl.ANY)
    extra = [] if other is None else [other]
    full, tables, *takes = pl.pallas_call(
        functools.partial(team_rows_kernel, tuple(jobs), tuple(relays), layout, experts),
        in_specs=[pl.BlockSpec(memory_space=pltpu.VMEM)] * 3 + [anywhere] * (len(jobs) + len(pairs) + len(extra)),
        out_specs=[anywhere] * (3 + len(jobs) + len(pairs)),
        out_shape=[
            jax.ShapeDtypeStruct((2, 2, 2, tokens, width), BF),
            jax.ShapeDtypeStruct((2, 2, 2) + table, F32),
        ] + [jax.ShapeDtypeStruct(give.shape, give.dtype) for give in list(gives) + list(pairs)]
        + [jax.ShapeDtypeStruct((8, size, width), BF)],
        scratch_shapes=[
            pltpu.VMEM((size, tokens), BF),
            pltpu.VMEM((2, tokens, width), BF),
            pltpu.VMEM((2, size, width), BF),
            pltpu.SemaphoreType.DMA((2,)),
            pltpu.SemaphoreType.DMA((3, 5)),
            pltpu.SemaphoreType.DMA((3, 5)),
            pltpu.SemaphoreType.DMA((2, max(1, len(jobs)))),
            pltpu.SemaphoreType.DMA((5, max(1, len(relays)))),
            pltpu.SemaphoreType.DMA((2, 2)),
            pltpu.SemaphoreType.DMA((2,)),
        ],
        compiler_params=pltpu.CompilerParams(collective_id=2, has_side_effects=True, vmem_limit_bytes=60 * 2**20),
        name="team_rows",
    )(rows.reshape(1, 1, 1, tokens, width), gates.reshape((1, 1, 1) + table), positions, *gives, *pairs, *extra)
    *takes, picked = takes
    return full.reshape(8, tokens, width), tables.reshape((8,) + table), takes, picked


def add_into(acc, at, other):
    acc[at] = (acc[at].astype(F32) + other.astype(F32)).astype(BF)


def return_kernel(count, slots, jobs, relays, pos_ref, *refs):
    x_refs, y_refs, dg_refs = refs[0:count], refs[count:2 * count], refs[2 * count:3 * count]
    refs = refs[3 * count:]
    gives, takes = refs[0:len(jobs)], refs[len(jobs) + 4:2 * len(jobs) + 4]
    out_ref, gate_ref, kept_ref, sent_ref = refs[len(jobs):len(jobs) + 4]
    (acc, core_in, even_out, row_in, pair_in, last_in, ys, pick, table, table_core, table_row, table_pair,
     load_sem, send_sem, recv_sem, job_sem, store_sem, free_sem) = refs[2 * len(jobs) + 4:]
    tokens, width = out_ref.shape
    half = width // 2
    barrier_with(partners_of(TEAM, jobs))
    background = job_copies(jobs, gives, takes, job_sem)
    for copy in background[relays:]:
        copy.start()
    if relays:

        @pl.when(jnp.logical_not(inner_plane()))
        def _():
            for copy in background[:relays]:
                copy.start()

    first = (lax.axis_index("expert") * 2 + own_bit("dp", 2)) * count
    slot_id = lax.broadcasted_iota(jnp.int32, (slots, tokens), 0)

    def remote(src, dst, n, dim):
        return pltpu.make_async_remote_copy(
            src_ref=src, dst_ref=dst, send_sem=send_sem.at[n], recv_sem=recv_sem.at[n],
            device_id=flipped(*TEAM[dim]), device_id_type=pl.DeviceIdType.MESH,
        )

    def loads(parts, r, slot):
        return [
            pltpu.make_async_copy(
                parts[k].at[pl.ds(pl.multiple_of(r * slots, 16), slots), :],
                ys.at[slot, pl.ds(k * slots, slots), :], load_sem.at[slot, k],
            )
            for k in range(count)
        ]

    table[...] = jnp.zeros_like(table)

    def build(parts, step, r, following, dst, at, with_gates):
        slot = lax.rem(step, 2)
        for copy in loads(parts, r, slot):
            copy.wait()

        @pl.when(step < 7)
        def _():
            for copy in loads(parts, following, 1 - slot):
                copy.start()

        for k in range(count):
            hit = slot_id == pos_ref[r, k:k + 1, :]
            pick[k * slots:(k + 1) * slots, :] = jnp.where(hit, 1.0, 0.0).astype(BF)
            if with_gates:
                pulled = dg_refs[k][pl.ds(pl.multiple_of(r * slots, 16), slots), 0:1]
                table[r, pl.ds(first + k, 1), :] = jnp.sum(jnp.where(hit, pulled, 0.0), 0, keepdims=True)
        dst[at, :, 0:half] = dot_tn(pick[...], ys[slot, :, 0:half]).astype(BF)
        dst[at, :, half:] = dot_tn(pick[...], ys[slot, :, half:]).astype(BF)

    def core_copy(i, base):
        return remote(acc.at[2 * i + 1], core_in.at[i], base + i, 2)

    def build_odd(parts, base, with_gates):
        def odd(i, carry):
            r = 2 * i + 1
            build(parts, i, r, jnp.where(i < 3, r + 2, 0), acc, r, with_gates)
            core_copy(i, base).start()
            return carry

        lax.fori_loop(0, 4, odd, 0)

    for copy in loads(x_refs, 1, 0):
        copy.start()
    build_odd(x_refs, 0, True)
    tables = [remote(table.at[2 * i + 1], table_core.at[i], 4 + i, 2) for i in range(4)]
    for copy in tables:
        copy.start()

    def even(i, carry):
        build(x_refs, i + 4, 2 * i, 2 * i + 2, acc, 2 * i, True)
        return carry

    lax.fori_loop(0, 4, even, 0)
    if relays:

        @pl.when(inner_plane())
        def _():
            for copy in background[:relays]:
                copy.start()

    for copy in loads(y_refs, 1, 0):
        copy.start()

    def settle(i):
        core_copy(i, 0).wait()
        add_into(acc, 2 * i, core_in[i])

    left, right = slice(0, half), slice(half, width)
    settle(3)
    a = [remote(acc.at[6, :, pl.ds(0, half)], row_in.at[1], 8, 1), remote(acc.at[6, :, pl.ds(half, half)], pair_in.at[1], 9, 0)]
    for copy in a:
        copy.start()
    settle(1)
    a.append(remote(acc.at[2, :, pl.ds(0, half)], row_in.at[0], 10, 1))
    a[-1].start()
    settle(2)
    a.append(remote(acc.at[4, :, pl.ds(half, half)], pair_in.at[0], 11, 0))
    a[-1].start()
    settle(0)
    pl.semaphore_signal(free_sem, inc=1, device_id=flipped(*TEAM[2]), device_id_type=pl.DeviceIdType.MESH)
    for i, copy in enumerate(tables):
        copy.wait()
        table[2 * i] = table[2 * i] + table_core[i]
    t = [remote(table.at[2], table_row.at[0], 12, 1), remote(table.at[6], table_row.at[1], 13, 1)]
    for copy in t:
        copy.start()
    pl.semaphore_wait(free_sem, 1)
    build_odd(y_refs, 17, False)
    a[0].wait()
    add_into(acc, (4, slice(None), left), row_in[1])
    b = [remote(acc.at[4, :, pl.ds(0, half)], last_in.at[0], 14, 0)]
    b[0].start()
    a[1].wait()
    add_into(acc, (2, slice(None), right), pair_in[1])
    b.append(remote(acc.at[2, :, pl.ds(half, half)], last_in.at[1], 15, 1))
    b[1].start()
    for i, copy in enumerate(t):
        copy.wait()
        table[4 * i] = table[4 * i] + table_row[i]
    t = remote(table.at[4], table_pair, 16, 0)
    t.start()

    def even_y(i, carry):
        build(y_refs, i + 4, 2 * i, 2 * i + 2, even_out, i, False)
        return carry

    lax.fori_loop(0, 4, even_y, 0)
    stores = []
    for i in range(4):
        core_copy(i, 17).wait()
        add_into(even_out, i, core_in[i])
        stores.append(
            pltpu.make_async_copy(even_out.at[i], (sent_ref if i % 2 else kept_ref).at[i // 2], store_sem.at[i])
        )
        stores[-1].start()
    a[2].wait()
    add_into(acc, (0, slice(None), left), row_in[0])
    a[3].wait()
    add_into(acc, (0, slice(None), right), pair_in[0])
    b[0].wait()
    out_ref[:, left] = (acc[0, :, left].astype(F32) + last_in[0].astype(F32)).astype(BF)
    b[1].wait()
    out_ref[:, right] = (acc[0, :, right].astype(F32) + last_in[1].astype(F32)).astype(BF)
    t.wait()
    gate_ref[...] = table[0] + table_pair[...]
    for copy in stores:
        copy.wait()
    for copy in background:
        copy.wait()


def return_rows(positions, backs, results, gate_rows, experts, slots, jobs=(), gives=(), relays=0):
    sources, _, tokens = positions.shape
    count = len(results)
    width = results[0].shape[1]
    half = width // 2
    vmem, anywhere = pl.BlockSpec(memory_space=pltpu.VMEM), pl.BlockSpec(memory_space=pl.ANY)
    rows, gates, kept, sent, *takes = pl.pallas_call(
        functools.partial(return_kernel, count, slots, tuple(jobs), relays),
        in_specs=[vmem] + [anywhere] * (2 * count) + [vmem] * count + [anywhere] * len(jobs),
        out_specs=[vmem, vmem] + [anywhere] * (2 + len(jobs)),
        out_shape=[jax.ShapeDtypeStruct((tokens, width), BF), jax.ShapeDtypeStruct((experts, tokens), F32)]
        + [jax.ShapeDtypeStruct((2, tokens, width), BF)] * 2
        + [jax.ShapeDtypeStruct(give.shape, give.dtype) for give in gives],
        scratch_shapes=[
            pltpu.VMEM((8, tokens, width), BF),
            pltpu.VMEM((4, tokens, width), BF),
            pltpu.VMEM((4, tokens, width), BF),
            pltpu.VMEM((2, tokens, half), BF),
            pltpu.VMEM((2, tokens, half), BF),
            pltpu.VMEM((2, tokens, half), BF),
            pltpu.VMEM((2, count * slots, width), BF),
            pltpu.VMEM((count * slots, tokens), BF),
            pltpu.VMEM((8, experts, tokens), F32),
            pltpu.VMEM((4, experts, tokens), F32),
            pltpu.VMEM((2, experts, tokens), F32),
            pltpu.VMEM((experts, tokens), F32),
            pltpu.SemaphoreType.DMA((2, count)),
            pltpu.SemaphoreType.DMA((21,)),
            pltpu.SemaphoreType.DMA((21,)),
            pltpu.SemaphoreType.DMA((2, max(1, len(jobs)))),
            pltpu.SemaphoreType.DMA((4,)),
            pltpu.SemaphoreType.REGULAR,
        ],
        compiler_params=pltpu.CompilerParams(collective_id=3, has_side_effects=True, vmem_limit_bytes=63 * 2**20),
        name="return_rows",
    )(positions, *backs, *results, *gate_rows, *gives)
    return rows, gates, kept, sent, takes


class Group:
    def __init__(self, copies):
        self.copies = copies

    def wait(self):
        for copy in self.copies:
            copy.wait()


def scatter_kernel(dims, rotations, chunks, segments, sources, relays, *refs):
    last = len(dims) - 1
    grads, refs = refs[0:sources], refs[sources:]
    gives, takes = refs[0:relays], refs[relays + 1:2 * relays + 1]
    out_ref, refs = refs[relays], refs[2 * relays + 1:]
    acc, core_in = refs[0:2]
    inboxes = refs[2:2 + last]
    load_sem, send_sem, recv_sem, job_sem = refs[2 + last:]
    barrier_with([flipped(*dim) for dim in dims])
    background = job_copies((("dp", 4),) * relays, gives, takes, job_sem)

    def relay(outer):
        if relays:

            @pl.when(jnp.logical_not(inner_plane()) if outer else inner_plane())
            def _():
                for copy in background:
                    copy.start()

    bits = [own_bit(*dim) for dim in dims]
    every = tuple(pl.ds(0, 2) for _ in range(last))
    number = iter(range(send_sem.shape[0]))

    def remote(src, dst, dim):
        n = next(number)
        return pltpu.make_async_remote_copy(
            src_ref=src, dst_ref=dst, send_sem=send_sem.at[n], recv_sem=recv_sem.at[n],
            device_id=flipped(*dims[dim]), device_id_type=pl.DeviceIdType.MESH,
        )

    firsts, loads = [[] for _ in chunks], []
    for source, start, at, width, chunk in segments:
        src, dst = (slice(None), pl.ds(start, width)), (slice(None), pl.ds(at, width))
        copy = remote(
            grads[source].at[every + (pl.ds(1 - bits[last], 1),) + src], core_in.at[every + (pl.ds(0, 1),) + dst], last
        )
        copy.start()
        firsts[chunk].append(copy)
        load = pltpu.make_async_copy(
            grads[source].at[every + (pl.ds(bits[last], 1),) + src], acc.at[every + (pl.ds(0, 1),) + dst],
            load_sem.at[len(loads)],
        )
        load.start()
        loads.append(load)
    for load in loads:
        load.wait()
    sends = [Group(copies) for copies in firsts]
    relay(True)
    for step in range(last + 1):
        for c, (start, width) in enumerate(chunks):
            cols = pl.ds(start, width)
            rest = rotations[c][:last - step]
            sends[c].wait()
            for n in range(2 ** len(rest)):
                spread = [(n >> (len(rest) - 1 - i)) & 1 for i in range(len(rest))]
                index = [bits[d] if d not in rest else spread[rest.index(d)] for d in range(last)]
                at = tuple(index) + (0, slice(None), cols)
                other = core_in[at] if step == 0 else inboxes[step - 1][n, :, cols]
                if step < last:
                    add_into(acc, at, other)
                else:
                    out_ref[:, cols] = (acc[at].astype(F32) + other.astype(F32)).astype(out_ref.dtype)
            if step < last:
                dim, spread_dims = rest[-1], rest[:-1]
                group = []
                for n in range(2 ** len(spread_dims)):
                    spread = [(n >> (len(spread_dims) - 1 - i)) & 1 for i in range(len(spread_dims))]
                    index = [
                        1 - bits[d] if d == dim else (spread[spread_dims.index(d)] if d in spread_dims else bits[d])
                        for d in range(last)
                    ]
                    copy = remote(acc.at[tuple(index) + (0, slice(None), cols)], inboxes[step].at[n, :, cols], dim)
                    copy.start()
                    group.append(copy)
                sends[c] = Group(group)
        if step == 0:
            relay(False)
    for copy in background:
        copy.wait()


def cube_scatter(dims, rotations, chunks, segments, grads, dtype, collective, name, gives=()):
    last = len(dims) - 1
    rows = grads[0].shape[0] // 2 ** len(dims)
    width = sum(chunk[1] for chunk in chunks)
    copies = len(segments) + len(chunks) * (2 ** last - 1)
    out, *takes = pl.pallas_call(
        functools.partial(scatter_kernel, dims, rotations, chunks, segments, len(grads), len(gives)),
        in_specs=[pl.BlockSpec(memory_space=pl.ANY)] * (len(grads) + len(gives)),
        out_specs=[pl.BlockSpec(memory_space=pltpu.VMEM)] + [pl.BlockSpec(memory_space=pl.ANY)] * len(gives),
        out_shape=[jax.ShapeDtypeStruct((rows, width), dtype)]
        + [jax.ShapeDtypeStruct(give.shape, give.dtype) for give in gives],
        scratch_shapes=[pltpu.VMEM((2,) * last + (1, rows, width), BF)] * 2
        + [pltpu.VMEM((2 ** n, rows, width), BF) for n in reversed(range(last))]
        + [
            pltpu.SemaphoreType.DMA((len(segments),)),
            pltpu.SemaphoreType.DMA((copies,)),
            pltpu.SemaphoreType.DMA((copies,)),
            pltpu.SemaphoreType.DMA((2, max(1, len(gives)))),
        ],
        compiler_params=pltpu.CompilerParams(
            collective_id=collective, has_side_effects=True, vmem_limit_bytes=60 * 2**20
        ),
        name=name,
    )(*[g.reshape((2,) * len(dims) + (rows, g.shape[1])) for g in grads], *gives)
    return out, takes


def dense_segments(wide):
    cut = wide // 256 * 128 + 128
    return ((0, 0, cut, 0), (0, cut, wide - cut, 1), (1, 0, 128, 1), (2, 0, 1536, 2), (3, 0, 128, 2))


def scatter_all(grads, gives):
    segments, chunks, at = [], [0, 0, 0], 0
    for source, start, width, chunk in dense_segments(grads[0].shape[1]):
        segments.append((source, start, at, width, chunk))
        chunks[chunk] += width
        at += width
    starts = (0, chunks[0], chunks[0] + chunks[1])
    return cube_scatter(
        CUBE, ROTATIONS, tuple(zip(starts, chunks)), tuple(segments), grads, F32, 4, "scatter_all", gives
    )


def group_back(grad_key, grad_value):
    width = grad_key.shape[1]
    segments = ((0, 0, 0, width, 0), (1, 0, width, width, 1))
    return cube_scatter(
        GROUP, ((0, 1), (1, 0)), ((0, width), (width, width)), segments, [grad_key, grad_value], BF, 6, "group_back"
    )[0]


def group_rows_kernel(rows_ref, key_ref, value_ref, own_sem, send_sem, recv_sem):
    barrier_with([flipped(*dim) for dim in GROUP])
    bits = [own_bit(*dim) for dim in GROUP]
    width = key_ref.shape[4]
    here = tuple(pl.ds(bit, 1) for bit in bits)
    own = [
        pltpu.make_async_copy(rows_ref.at[:, :, :, :, pl.ds(i * width, width)], ref.at[here], own_sem.at[i])
        for i, ref in enumerate((key_ref, value_ref))
    ]
    for copy in own:
        copy.start()
    for copy in own:
        copy.wait()
    copies = []
    running = [None, None]
    for step in range(3):
        for f, (ref, order) in enumerate(((key_ref, (0, 1, 2)), (value_ref, (1, 0, 2)))):
            if running[f] is not None:
                running[f].wait_recv()
            at = tuple(pl.ds(0, 2) if d in order[:step] else pl.ds(bits[d], 1) for d in range(3))
            copy = pltpu.make_async_remote_copy(
                src_ref=ref.at[at], dst_ref=ref.at[at], send_sem=send_sem.at[step, f], recv_sem=recv_sem.at[step, f],
                device_id=flipped(*GROUP[order[step]]), device_id_type=pl.DeviceIdType.MESH,
            )
            copy.start()
            copies.append(copy)
            running[f] = copy
    for copy in running:
        copy.wait_recv()
    for copy in copies:
        copy.wait_send()


def group_rows(key_value):
    rows, width = key_value.shape
    anywhere = pl.BlockSpec(memory_space=pl.ANY)
    outs = pl.pallas_call(
        group_rows_kernel,
        in_specs=[pl.BlockSpec(memory_space=pltpu.VMEM)],
        out_specs=[anywhere] * 2,
        out_shape=[jax.ShapeDtypeStruct((2, 2, 2, rows, width // 2), BF)] * 2,
        scratch_shapes=[
            pltpu.SemaphoreType.DMA((2,)),
            pltpu.SemaphoreType.DMA((3, 2)),
            pltpu.SemaphoreType.DMA((3, 2)),
        ],
        compiler_params=pltpu.CompilerParams(collective_id=5, has_side_effects=True),
        name="group_rows",
    )(key_value.reshape(1, 1, 1, rows, width))
    return [out.reshape(8 * rows, width // 2) for out in outs]


D = 1536
EPSILON = 1e-06
EVERYWHERE = ("dp", "expert")


def exchange(value, axis, mask):
    return lax.ppermute(value, axis, [(i, i ^ mask) for i in range(lax.axis_size(axis))])


def tie(first, *others):
    return lax.optimization_barrier((first, *others))[0]


def rms_scale(values):
    return lax.rsqrt(jnp.mean(values * values, axis=-1, keepdims=True) + EPSILON)


def product(left, right):
    return jnp.dot(left, right, preferred_element_type=F32)


def contract_rows(left, right):
    return jnp.einsum("ta,tb->ab", left, right, preferred_element_type=F32)


def times_transposed(left, right):
    return jnp.einsum("ta,ba->tb", left, right, preferred_element_type=F32)


def added(left, right):
    return (left.astype(F32) + right.astype(F32)).astype(BF)


def team_gather(value, order):
    pieces = {0: value}
    for axis, mask, bit in order:
        pieces.update({r | bit: exchange(v, axis, mask) for r, v in list(pieces.items())})
    return jnp.stack([pieces[r] for r in sorted(pieces)])


TEAM_BITS = (("dp", 2, 4), ("expert", 2, 2), ("expert", 1, 1))


def local(tokens, attn_gain, w_query, w_key, w_value, w_out, w_router, ffn_gain, w_gate, w_up, w_down, routes, cotangent):
    dp, expert_at = lax.axis_index("dp"), lax.axis_index("expert")
    shards, owners = lax.axis_size("dp"), lax.axis_size("expert")
    cube = shards == 8 and owners == 4
    turn = (dp >> 1) & 1
    tok_rows = tokens.shape[0]
    per_owner, piece, hidden = w_gate.shape
    count = per_owner // 2
    expert_count = per_owner * owners
    top_count = routes.shape[1]
    kvw = w_key.shape[1]
    capacity = 8 * ((17 * top_count * tok_rows + 128 * expert_count - 1) // (128 * expert_count))
    slots = SLOTS_ALIGN * (-(-capacity // SLOTS_ALIGN))
    dp_index = dp.astype(jnp.int32).reshape(1)
    wide = D + 2 * kvw

    stacked = jnp.stack([w_gate, w_up, w_down.transpose(0, 2, 1)], 1)
    own = lax.dynamic_slice_in_dim(stacked, turn * count, count, 0)
    other = lax.dynamic_slice_in_dim(stacked, (1 - turn) * count, count, 0)
    gains = jnp.pad(jnp.stack([attn_gain, ffn_gain], 1), ((0, 0), (0, 126)))
    dense = [
        jnp.concatenate([w_query, w_key, w_value], 1), gains, w_out,
        jnp.pad(w_router, ((0, 0), (0, 128 - expert_count))),
    ]
    ahead = 2
    if cube:
        dense_full, taken, routes_t = gather_all(dense, dense_segments(wide), other[:ahead], routes.T)
    else:
        routes_t = team_gather(routes.T, TEAM_BITS)
        dense_full = [lax.all_gather(shard, EVERYWHERE, axis=0, tiled=True) for shard in dense]
        taken = exchange(other[:ahead], "dp", 2)
    qkv_full, gains_full, out_full, router_full = dense_full
    gains_full = gains_full.astype(F32).T
    gain_first, gain_second = gains_full[0], gains_full[1]

    relay_bits = [1 << b for b in range(2, shards.bit_length() - 1)]
    pairs = [jnp.stack([own[k], taken[k]]) for k in range(ahead)]

    def crossed(relayed):
        return [w for v in relayed for w in (v, exchange(v, "dp", 1))]

    def relays(pair):
        pieces = [pair]
        for bit in relay_bits:
            pieces += [exchange(v, "dp", bit) for v in pieces]
        return pieces

    first_expert = expert_at * per_owner + turn * count
    local_ids = first_expert + jnp.arange(count, dtype=jnp.int32)
    hits = jnp.any(routes_t[:, None] == local_ids[None, :, None, None], axis=2)
    row_id = lax.broadcasted_iota(jnp.int32, (tok_rows, tok_rows), 0)
    col_id = lax.broadcasted_iota(jnp.int32, (tok_rows, tok_rows), 1)
    before = jnp.where(row_id < col_id, 1.0, 0.0).astype(BF)
    ranks = product(hits.astype(BF).reshape(-1, tok_rows), before).reshape(hits.shape)
    positions = jnp.where(hits, ranks.astype(jnp.int32), -1)
    positions = jnp.pad(positions, ((0, 0), (0, 8 - count), (0, 0)), constant_values=-1)

    inputs = tokens.astype(F32)
    scale_one = rms_scale(inputs)
    normed_one = inputs * scale_one
    hidden_one = (normed_one * gain_first).astype(BF)
    qkv = product(hidden_one, qkv_full).astype(BF)
    query, key_value = qkv[:, :D], qkv[:, D:]
    place = ((dp & 1) * owners + expert_at).astype(jnp.int32).reshape(1)
    prompt_key, prompt_value = group_rows(key_value[:P_DEV])
    own_key, own_value = key_value[P_DEV:, :kvw], key_value[P_DEV:, kvw:]
    early = tie(cotangent, qkv_full)
    middle = tok_rows // 2
    paired = exchange(early, "dp", 2)
    upper = exchange(early[:middle], "expert", 2)
    query, early, paired, prompt_key, pairs[:2], late = lax.optimization_barrier(
        (query, early, paired, prompt_key, pairs[:2], other[ahead:])
    )
    parts = [early, paired, upper, None, exchange(paired, "expert", 2)]
    layout = ((0,), (2, 3), (1,), (4,))
    taken_late = exchange(late, "dp", 2)
    pairs += [jnp.stack([own[k], taken_late[k - ahead]]) for k in range(ahead, count)]
    crossings = [exchange(pairs[k], "dp", 1) for k in range(2)]
    mixed, levels = attend(place, query, prompt_key, prompt_value, own_key, own_value)
    mixed, parts[4] = lax.optimization_barrier((mixed, parts[4]))
    parts[3] = exchange(tie(early[middle:], parts[4]), "expert", 2)
    second = inputs + product(mixed, out_full)
    scale_two = rms_scale(second)
    normed_two = second * scale_two
    hidden_two = (normed_two * gain_second).astype(BF)
    logits = product(hidden_two, router_full)[:, :expert_count]
    expert_ids = jnp.arange(expert_count, dtype=jnp.int32)
    chosen = jnp.any(routes[:, :, None] == expert_ids, axis=1)
    peak = jnp.max(jnp.where(chosen, logits, NEGATIVE), axis=-1, keepdims=True)
    raised = jnp.where(chosen, jnp.exp(jnp.where(chosen, logits - peak, 0.0)), 0.0)
    gates = raised / jnp.sum(raised, axis=-1, keepdims=True)

    weights = [None] * count
    near = exchange(tie(pairs[0], taken_late), "dp", 4) if cube else None
    sent_rows, parts, crossings = lax.optimization_barrier((hidden_two, parts, crossings))
    core_jobs = (("expert", 1),) * 5
    if cube:
        rows, gates_t, takes, grad_slots = team_rows(
            sent_rows, gates.T, positions, layout, count, slots,
            core_jobs + (("dp", 1),) * 3, (*parts, *pairs[2:]), (1, 2), pairs[1:3], other,
        )
        crossings = crossings + takes[5:8]
        relayed_pairs = [near] + takes[8:10]
        for k in range(3, count):
            relayed_pairs.append(exchange(tie(pairs[k], rows), "dp", 4))
        for k in range(count):
            weights[k] = [pairs[k], crossings[k], relayed_pairs[k]]
    else:
        rows, gates_t, _, grad_slots = team_rows(
            sent_rows, gates.T, positions, layout, count, slots, core_jobs, parts
        )
        for k in range(count):
            weights[k] = crossed(relays(tie(pairs[k], rows)))
    gates_t = lax.dynamic_slice_in_dim(gates_t, first_expert, count, 1)
    gates_t = jnp.pad(gates_t, ((0, 0), (0, 8 - count), (0, 0)))
    row_slots, gate_slots = gather_rows(positions, gates_t, rows, count, slots)

    results, backs, gate_rows, sums = [], [], [], []
    expert_index = dp_index
    for k in range(count):
        if cube:
            relayed_pair = tie(weights[k][2], rows) if k < 3 else tie(weights[k][2], gate_rows[k - 2], weights[k - 1][3])
            weights[k].append(exchange(relayed_pair, "dp", 1))
        y, dx, dg, keep, send = run_expert(k, expert_index, row_slots, grad_slots, gate_slots, weights[k], slots)
        results.append(y)
        backs.append(dx)
        gate_rows.append(dg)
        sums.append((keep, send))
        expert_index = tie(dp_index, dg)

    before_return = added(sums[0][0], exchange(tie(sums[0][1], gate_rows[1], weights[4]), "dp", 1))
    jobs, gives, relays_in = (("dp", 1),) * 2, (sums[1][1], sums[2][1]), 0
    if cube:
        jobs, gives, relays_in = (("dp", 4),) + jobs, (before_return[2:],) + gives, 1
    routed_back, gate_grad, out_keep, out_sent, takes = return_rows(
        positions, backs, results, gate_rows, expert_count, slots, jobs, gives, relays_in
    )
    halved = [before_return, added(sums[1][0], takes[-2]), added(sums[2][0], takes[-1])]
    crossed_back = [exchange(tie(sums[k][1], routed_back), "dp", 1) for k in range(3, count)]
    relay_bits = relay_bits[::-1]

    def sent_on(keep):
        return exchange(keep[keep.shape[0] // 2:], "dp", relay_bits[0])

    def settled(keep, came):
        keep = added(keep[:keep.shape[0] // 2], came)
        for bit in relay_bits[1:]:
            middle = keep.shape[0] // 2
            keep = added(keep[:middle], exchange(keep[middle:], "dp", bit))
        return keep

    relay_came = [takes[0] if cube else sent_on(before_return)] + [sent_on(keep) for keep in halved[1:]]
    gate_grad = gate_grad.T
    routed_back = routed_back.astype(F32)

    grad_output = cotangent.astype(F32)
    picked = jnp.where(chosen, gate_grad, 0.0)
    grad_logits = (gates * (picked - jnp.sum(gates * picked, axis=-1, keepdims=True))).astype(BF)
    wide_logits = jnp.pad(grad_logits, ((0, 0), (0, 128 - expert_count)))
    grad_hidden_two = times_transposed(wide_logits, router_full) + routed_back
    grad_normed_two = grad_hidden_two * gain_second
    grad_second = grad_output + scale_two * (
        grad_normed_two - normed_two * jnp.mean(grad_normed_two * normed_two, axis=-1, keepdims=True)
    )
    grad_branch = grad_second.astype(BF)
    ones = jnp.ones((tok_rows, 128), BF)
    lane = lax.broadcasted_iota(jnp.int32, (tok_rows, 128), 1)
    small = contract_rows(hidden_two, wide_logits) + contract_rows(
        (grad_hidden_two * normed_two).astype(BF), jnp.where(lane == expert_count, ones, jnp.zeros_like(ones))
    )
    out_grad = contract_rows(mixed, grad_branch).astype(BF)
    grad_mixed = times_transposed(grad_branch, out_full).astype(BF)

    grad_mixed, halved = lax.optimization_barrier((grad_mixed, halved))
    row_came = exchange(out_sent, "expert", 2)
    grad_query, dkp, dvp, dko, dvo = attend_back(
        place, query, prompt_key, prompt_value, own_key, own_value, mixed, grad_mixed, levels
    )
    halved, relay_came, crossed_back, grad_query, row_came, dkp = lax.optimization_barrier(
        (halved, relay_came, crossed_back, grad_query, row_came, dkp)
    )
    halved += [added(sums[k][0], crossed_back[k - 3]) for k in range(3, count)]
    relay_came += [sent_on(halved[3])]
    grad_prompt = group_back(dkp, dvp)
    total = tie(added(out_keep, row_came), grad_prompt)
    pair_came = exchange(total[1], "dp", 2)
    grad_qkv = jnp.concatenate([
        grad_query, jnp.concatenate([grad_prompt, jnp.concatenate([dko, dvo], 1)], 0)
    ], 1)
    grad_hidden_one = times_transposed(grad_qkv, qkv_full)
    dense_grads = [
        contract_rows(hidden_one, grad_qkv).astype(BF),
        contract_rows((grad_hidden_one * normed_one).astype(BF), ones).astype(BF),
        out_grad, small.astype(BF),
    ]
    dense_grads, relay_came = lax.optimization_barrier((dense_grads, relay_came))
    if cube:
        share, takes = scatter_all(dense_grads, (halved[4][2:],))
        relay_came += takes
    else:
        share = lax.psum_scatter(
            jnp.concatenate(dense_grads, 1), EVERYWHERE, scatter_dimension=0, tiled=True
        ).astype(F32)
        relay_came.append(sent_on(halved[4]))
    grad_normed_one = grad_hidden_one * gain_first
    grad_input = grad_second + scale_one * (
        grad_normed_one - normed_one * jnp.mean(grad_normed_one * normed_one, axis=-1, keepdims=True)
    )

    share, halved, relay_came, total, pair_came = lax.optimization_barrier(
        (share, halved, relay_came, total, pair_came)
    )
    output = (second + added(total[0], pair_came).astype(F32)).astype(BF)
    first_share, second_share = share[:, :wide + 128], share[:, wide + 128:]
    relayed = [settled(halved[k], relay_came[k]) for k in range(count)]
    theirs = exchange(jnp.stack([keep[1] for keep in relayed]), "dp", 2)
    mine = jnp.stack([keep[0] for keep in relayed])
    lower = jnp.where(turn == 0, mine, theirs)
    upper = jnp.where(turn == 0, theirs, mine)
    expert_grads = jnp.concatenate([lower, upper]).astype(F32)
    return (
        output,
        grad_input.astype(BF),
        first_share[:, wide],
        first_share[:, :D],
        first_share[:, D:D + kvw],
        first_share[:, D + kvw:wide],
        second_share[:, :D].astype(F32),
        second_share[:, D:D + expert_count].astype(F32),
        second_share[:, D + expert_count].astype(F32),
        expert_grads[:, 0],
        expert_grads[:, 1],
        expert_grads[:, 2].transpose(0, 2, 1),
    )


def solution(mesh):
    rows, line = P(("dp", "expert"), None), P(("dp", "expert"))
    gate, down = P("expert", "dp", None), P("expert", None, "dp")
    return jax.shard_map(
        local,
        mesh=mesh,
        in_specs=(rows, line, rows, rows, rows, rows, rows, line, gate, gate, down, rows, rows),
        out_specs=(rows, rows, line, rows, rows, rows, rows, rows, line, gate, gate, down),
        check_vma=False,
    )
```

```python
import functools
import jax
import jax.numpy as jnp
from jax import lax
from jax.sharding import PartitionSpec as P
from jax.experimental import pallas as pl
from jax.experimental.pallas import tpu as pltpu

HD = 64
P_DEV = 128
NEGATIVE = -1e30
F32 = jnp.float32
BF = jnp.bfloat16


def dot_nt(a, b):
    return lax.dot_general(a, b, (((1,), (1,)), ((), ())), preferred_element_type=F32)


def dot_nn(a, b):
    return lax.dot_general(a, b, (((1,), (0,)), ((), ())), preferred_element_type=F32)


def dot_tn(a, b):
    return lax.dot_general(a, b, (((0,), (0,)), ((), ())), preferred_element_type=F32)


def halves(pair):
    lane = lax.broadcasted_iota(jnp.int32, pair.shape, 1)
    zero = jnp.zeros_like(pair)
    return jnp.where(lane < HD, pair, zero), jnp.where(lane < HD, zero, pair)


def placed_halves(pair_f32):
    low0, high1 = halves(pair_f32)
    high0 = pltpu.roll(low0, HD, 1)
    low1 = pltpu.roll(high1, HD, 1)
    return ((low0.astype(BF), high0.astype(BF)), (low1.astype(BF), high1.astype(BF)))


def attend_kernel(place_ref, q_ref, kp_ref, vp_ref, ko_ref, vo_ref, o_ref, lse_ref, kpad, vpad, s_scr, p_scr):
    rows = q_ref.shape[0]
    prompt = kp_ref.shape[0]
    cont = ko_ref.shape[0]
    place = place_ref[0]
    for src, dst in ((kp_ref, kpad), (vp_ref, vpad)):
        for head, pair in enumerate(placed_halves(src[...].astype(F32))):
            for half in range(2):
                dst[head, half, 0:prompt, :] = pair[half]
    for src, dst in ((ko_ref, kpad), (vo_ref, vpad)):
        for head, pair in enumerate(placed_halves(src[...].astype(F32))):
            for half in range(2):
                dst[head, half, prompt:prompt + cont, :] = pair[half]
    key_id = lax.broadcasted_iota(jnp.int32, (prompt, P_DEV), 0)
    row_id = lax.broadcasted_iota(jnp.int32, (prompt, P_DEV), 1)
    seen_prompt = key_id <= place * P_DEV + row_id
    diag = lax.broadcasted_iota(jnp.int32, (P_DEV, P_DEV), 0) <= lax.broadcasted_iota(jnp.int32, (P_DEV, P_DEV), 1)
    blocks = cont // P_DEV
    stats = []
    for chunk in range(3):
        queries = (q_ref[:, chunk * 128:(chunk + 1) * 128].astype(F32) * HD ** (-0.5)).astype(BF)
        total = None
        for half in range(2):
            position = chunk * 2 + half
            head = position // 3
            keys = kpad.at[head, half]
            scores = dot_nt(keys[0:prompt, :], queries)
            first = jnp.where(seen_prompt, scores[:, 0:P_DEV], NEGATIVE)
            rest = scores[:, P_DEV:]
            s_scr[0:prompt, 0:P_DEV] = first
            s_scr[0:prompt, P_DEV:] = rest
            top = jnp.concatenate([jnp.max(first, 0, keepdims=True), jnp.max(rest, 0, keepdims=True)], 1)
            tops = [top[:, i * P_DEV:(i + 1) * P_DEV] for i in range(1 + blocks)]
            for block in range(blocks):
                start = (1 + block) * P_DEV
                at = prompt + block * P_DEV
                own = dot_nt(keys[at:at + P_DEV, :], queries[start:, :])
                edge = jnp.where(diag, own[:, 0:P_DEV], NEGATIVE)
                s_scr[at:at + P_DEV, start:start + P_DEV] = edge
                tops[1 + block] = jnp.maximum(tops[1 + block], jnp.max(edge, 0, keepdims=True))
                if block + 1 < blocks:
                    later = own[:, P_DEV:]
                    s_scr[at:at + P_DEV, start + P_DEV:] = later
                    best = jnp.max(later, 0, keepdims=True)
                    for i in range(block + 1, blocks):
                        at_i = (i - block - 1) * P_DEV
                        tops[1 + i] = jnp.maximum(tops[1 + i], best[:, at_i:at_i + P_DEV])
            top = jnp.concatenate(tops, 1)
            weights = jnp.exp(s_scr[0:prompt, :] - top)
            mass = jnp.sum(weights, 0, keepdims=True)
            masses = [mass[:, i * P_DEV:(i + 1) * P_DEV] for i in range(1 + blocks)]
            values = vpad.at[head, half]
            mixed = dot_tn(values[0:prompt, :], weights.astype(BF))
            for block in range(blocks):
                start = (1 + block) * P_DEV
                at = prompt + block * P_DEV
                part = jnp.exp(s_scr[at:at + P_DEV, start:] - top[:, start:])
                p_scr[block * P_DEV:(block + 1) * P_DEV, start:] = part.astype(BF)
                if block:
                    p_scr[block * P_DEV:(block + 1) * P_DEV, P_DEV:start] = jnp.zeros((P_DEV, block * P_DEV), BF)
                part_mass = jnp.sum(part, 0, keepdims=True)
                for i in range(block, blocks):
                    at_i = (i - block) * P_DEV
                    masses[1 + i] = masses[1 + i] + part_mass[:, at_i:at_i + P_DEV]
            own_mixed = dot_tn(values[prompt:prompt + cont, :], p_scr[:, P_DEV:])
            mass = jnp.concatenate(masses, 1)
            scale = 1.0 / mass
            mixed = jnp.concatenate([mixed[:, 0:P_DEV], mixed[:, P_DEV:] + own_mixed], 1) * scale
            total = mixed if total is None else total + mixed
            stats.append(top + jnp.log(mass))
        o_ref[:, chunk * 128:(chunk + 1) * 128] = jnp.transpose(total).astype(BF)
    lse_ref[0] = jnp.concatenate(stats + [jnp.zeros((2, rows), F32)], 0)


def attend(place, query, prompt_key, prompt_value, own_key, own_value):
    rows = query.shape[0]
    prompt = prompt_key.shape[0]
    cont = own_key.shape[0]
    pairs = prompt_key.shape[1] // 128
    col = lambda i: (0, i)
    return pl.pallas_call(
        attend_kernel,
        grid=(pairs,),
        in_specs=[
            pl.BlockSpec(memory_space=pltpu.SMEM),
            pl.BlockSpec((rows, 384), col),
            pl.BlockSpec((prompt, 128), col),
            pl.BlockSpec((prompt, 128), col),
            pl.BlockSpec((cont, 128), col),
            pl.BlockSpec((cont, 128), col),
        ],
        out_specs=[pl.BlockSpec((rows, 384), col), pl.BlockSpec((1, 8, rows), lambda i: (i, 0, 0))],
        out_shape=[
            jax.ShapeDtypeStruct(query.shape, BF),
            jax.ShapeDtypeStruct((pairs, 8, rows), F32),
        ],
        scratch_shapes=[
            pltpu.VMEM((2, 2, prompt + cont, 128), BF),
            pltpu.VMEM((2, 2, prompt + cont, 128), BF),
            pltpu.VMEM((prompt + cont, rows), F32),
            pltpu.VMEM((cont, rows), BF),
        ],
        cost_estimate=pl.CostEstimate(flops=10**6, bytes_accessed=10**6, transcendentals=0),
        name="attend",
    )(place, query, prompt_key, prompt_value, own_key, own_value)


def attend_back_kernel(place_ref, q_ref, kp_ref, vp_ref, ko_ref, vo_ref, o_ref, do_ref, lse_ref,
                       dq_ref, dkp_ref, dvp_ref, dko_ref, dvo_ref, kpad, vpad, dk_acc, dv_acc):
    rows = q_ref.shape[0]
    prompt = kp_ref.shape[0]
    cont = ko_ref.shape[0]
    step = 2 * P_DEV
    place = place_ref[0]
    for src, dst, at, size in ((kp_ref, kpad, 0, prompt), (vp_ref, vpad, 0, prompt),
                               (ko_ref, kpad, prompt, cont), (vo_ref, vpad, prompt, cont)):
        for head, pair in enumerate(placed_halves(src[...].astype(F32))):
            for half in range(2):
                dst[head, half, at:at + size, :] = pair[half]
    dk_acc[...] = jnp.zeros_like(dk_acc)
    dv_acc[...] = jnp.zeros_like(dv_acc)
    for chunk in range(3):
        lanes = slice(chunk * 128, (chunk + 1) * 128)
        scaled = q_ref[:, lanes].astype(F32) * HD ** (-0.5)
        queries = scaled.astype(BF)
        query_halves = [part.astype(BF) for part in halves(scaled)]
        outs = o_ref[:, lanes].astype(F32)
        grads_f32 = do_ref[:, lanes].astype(F32)
        grads = do_ref[:, lanes]
        grad_halves = [part.astype(BF) for part in halves(grads_f32)]
        inner = jnp.transpose(outs * grads_f32)
        total = jnp.zeros((128, rows), F32)
        for half in range(2):
            position = chunk * 2 + half
            head = position // 3
            level = lse_ref[0, position:position + 1, :]
            delta = jnp.sum(inner[half * HD:(half + 1) * HD, :], 0, keepdims=True)

            def block(at, cols, mask, queries=queries, grads=grads, query_half=query_halves[half],
                      grad_half=grad_halves[half], level=level, delta=delta, head=head, half=half):
                keys = kpad[head, half, pl.ds(at, step), :]
                values = vpad[head, half, pl.ds(at, step), :]
                scores = dot_nt(keys, queries[cols, :])
                weights = jnp.exp(mask(scores) - level[:, cols])
                grad_weights = dot_nt(values, grads[cols, :])
                grad_scores = weights * (grad_weights - delta[:, cols])
                low_weights = weights.astype(BF)
                low_scores = grad_scores.astype(BF)
                dv_acc[head, pl.ds(at, step), :] += dot_nn(low_weights, grad_half[cols, :])
                dk_acc[head, pl.ds(at, step), :] += dot_nn(low_scores, query_half[cols, :])
                return dot_tn(keys, low_scores)

            def prompt_step(i, carry):
                at = pl.multiple_of(i * step, step)

                def mask(scores):
                    key_id = at + lax.broadcasted_iota(jnp.int32, (step, P_DEV), 0)
                    row_id = lax.broadcasted_iota(jnp.int32, (step, P_DEV), 1)
                    first = jnp.where(key_id <= place * P_DEV + row_id, scores[:, 0:P_DEV], NEGATIVE)
                    return jnp.concatenate([first, scores[:, P_DEV:]], 1)

                return carry + block(at, slice(0, rows), mask)

            total = lax.fori_loop(0, prompt // step, prompt_step, total)
            for own in range(cont // step):
                start = P_DEV + own * step

                def mask(scores):
                    key_id = lax.broadcasted_iota(jnp.int32, (step, step), 0)
                    row_id = lax.broadcasted_iota(jnp.int32, (step, step), 1)
                    edge = jnp.where(key_id <= row_id, scores[:, 0:step], NEGATIVE)
                    if scores.shape[1] == step:
                        return edge
                    return jnp.concatenate([edge, scores[:, step:]], 1)

                part = block(prompt + own * step, slice(start, rows), mask)
                total = jnp.concatenate([total[:, 0:start], total[:, start:] + part], 1)
        dq_ref[:, lanes] = (jnp.transpose(total) * HD ** (-0.5)).astype(BF)
    for acc, out_prompt, out_own in ((dk_acc, dkp_ref, dko_ref), (dv_acc, dvp_ref, dvo_ref)):
        low0, high0 = halves(acc[0])
        low1, high1 = halves(acc[1])
        merged = low0 + pltpu.roll(high0, HD, 1) + high1 + pltpu.roll(low1, HD, 1)
        out_prompt[...] = merged[0:prompt].astype(BF)
        out_own[...] = merged[prompt:].astype(BF)


def attend_back(place, query, prompt_key, prompt_value, own_key, own_value, mixed, grad, lse):
    rows = query.shape[0]
    prompt = prompt_key.shape[0]
    cont = own_key.shape[0]
    pairs = prompt_key.shape[1] // 128
    col = lambda i: (0, i)
    wide = pl.BlockSpec((rows, 384), col)
    keys_p = pl.BlockSpec((prompt, 128), col)
    keys_o = pl.BlockSpec((cont, 128), col)
    return pl.pallas_call(
        attend_back_kernel,
        grid=(pairs,),
        in_specs=[
            pl.BlockSpec(memory_space=pltpu.SMEM),
            wide, keys_p, keys_p, keys_o, keys_o, wide, wide,
            pl.BlockSpec((1, 8, rows), lambda i: (i, 0, 0)),
        ],
        out_specs=[wide, keys_p, keys_p, keys_o, keys_o],
        out_shape=[
            jax.ShapeDtypeStruct(query.shape, BF),
            jax.ShapeDtypeStruct(prompt_key.shape, BF),
            jax.ShapeDtypeStruct(prompt_key.shape, BF),
            jax.ShapeDtypeStruct(own_key.shape, BF),
            jax.ShapeDtypeStruct(own_key.shape, BF),
        ],
        scratch_shapes=[
            pltpu.VMEM((2, 2, prompt + cont, 128), BF),
            pltpu.VMEM((2, 2, prompt + cont, 128), BF),
            pltpu.VMEM((2, prompt + cont, 128), F32),
            pltpu.VMEM((2, prompt + cont, 128), F32),
        ],
        cost_estimate=pl.CostEstimate(flops=10**6, bytes_accessed=10**6, transcendentals=0),
        name="attend_back",
    )(place, query, prompt_key, prompt_value, own_key, own_value, mixed, grad, lse)


SLOTS_ALIGN = 16


def gather_kernel(count, with_gates, pos_ref, *refs):
    if with_gates:
        gate_ref, rows_ref, x_ref, g_ref, pick = refs
    else:
        rows_ref, x_ref, pick = refs
    tokens = rows_ref.shape[1]
    slots = x_ref.shape[1] // count
    half = rows_ref.shape[2] // 2
    slot_id = lax.broadcasted_iota(jnp.int32, (slots, tokens), 0)
    for k in range(count):
        hit = slot_id == pos_ref[0, k:k + 1, :]
        pick[k * slots:(k + 1) * slots, :] = jnp.where(hit, 1.0, 0.0).astype(BF)
        if with_gates:
            gate = jnp.sum(jnp.where(hit, gate_ref[0, k:k + 1, :], 0.0), 1, keepdims=True)
            g_ref[0, k * slots:(k + 1) * slots, :] = jnp.broadcast_to(gate, (slots, 128))
    x_ref[0, :, 0:half] = dot_nn(pick[...], rows_ref[0, :, 0:half]).astype(BF)
    x_ref[0, :, half:] = dot_nn(pick[...], rows_ref[0, :, half:]).astype(BF)


def gather_rows(positions, gates, rows, count, slots):
    sources, tokens, width = rows.shape
    size = count * slots
    table = pl.BlockSpec((1, 8, tokens), lambda s: (s, 0, 0))
    block = lambda shape: pl.BlockSpec((1,) + shape, lambda s: (s, 0, 0))
    tables = [positions] if gates is None else [positions, gates]
    outs = [((size, width), BF)] if gates is None else [((size, width), BF), ((size, 128), F32)]
    return pl.pallas_call(
        functools.partial(gather_kernel, count, gates is not None),
        grid=(sources,),
        in_specs=[table] * len(tables) + [block((tokens, width))],
        out_specs=[block(shape) for shape, _ in outs],
        out_shape=[jax.ShapeDtypeStruct((sources,) + shape, dtype) for shape, dtype in outs],
        scratch_shapes=[pltpu.VMEM((size, tokens), BF)],
        cost_estimate=pl.CostEstimate(flops=10**6, bytes_accessed=10**6, transcendentals=0),
        name="gather_rows",
    )(*tables, rows)


def expert_kernel(k, shards, slots, dp_ref, x_ref, g_ref, gate_ref, *refs):
    w_refs = refs[0:shards // 2]
    (y_out, dx_out, dg_out, keep_out, send_out,
     xs, gs, gates, ws, ys, dxs, dgs, dab, actg, stage,
     in_sem, w_sem, out_sem, grad_sem) = refs[shards // 2:]
    dp = dp_ref[0]
    sources = x_ref.shape[0]
    width = xs.shape[1]
    piece = width // shards
    hidden = ws.shape[2]
    mine = pl.ds(k * slots, slots)

    def row_copies(s):
        at = pl.ds(pl.multiple_of(s * slots, 16), slots)
        return (
            pltpu.make_async_copy(x_ref.at[s, mine, :], xs.at[at, :], in_sem.at[0, s]),
            pltpu.make_async_copy(g_ref.at[s, mine, :], gs.at[at, :], in_sem.at[1, s]),
            pltpu.make_async_copy(gate_ref.at[s, mine, :], gates.at[at, :], in_sem.at[2, s]),
        )

    weight_copies = [
        pltpu.make_async_copy(
            w_refs[(r & 1) + 2 * (r >> 2)].at[(r >> 1) & 1], ws.at[:, pl.ds(pl.multiple_of((dp ^ r) * piece, 16), piece), :], w_sem.at[r]
        )
        for r in range(shards)
    ]
    for s in range(sources):
        for copy in row_copies(s):
            copy.start()
        if s == 1:
            for copy in weight_copies:
                copy.start()
    for copy in weight_copies:
        copy.wait()
    chunk = 2 * slots

    def out_copies(c):
        at = pl.ds(pl.multiple_of(c * chunk, 32), chunk)
        return [
            pltpu.make_async_copy(src.at[at, :], dst.at[at, :], out_sem.at[i, c])
            for i, (src, dst) in enumerate(((ys, y_out), (dxs, dx_out), (dgs, dg_out)))
        ]

    def forward_chunk(c, carry):
        for copy in row_copies(2 * c) + row_copies(2 * c + 1):
            copy.wait()
        rows = pl.ds(pl.multiple_of(c * chunk, 32), chunk)
        x = xs[rows, :]
        a = dot_nn(x, ws[0])
        b = dot_nn(x, ws[1])
        pulled = dot_nn(gs[rows, :], ws[2])
        gate = gates[rows, 0:1]
        sig = jax.nn.sigmoid(a)
        silu = a * sig
        act = silu * b
        dgs[rows, :] = jnp.broadcast_to(jnp.sum(act * pulled, 1, keepdims=True), (chunk, 128))
        weighted = (gate * act).astype(BF)
        actg[rows, :] = weighted
        dact = gate * pulled
        da = (dact * b * sig * (1.0 + a * (1.0 - sig))).astype(BF)
        db = (dact * silu).astype(BF)
        dab[rows, 0:hidden] = da
        dab[rows, hidden:] = db
        ys[rows, :] = dot_nt(weighted, ws[2]).astype(BF)
        dxs[rows, :] = (dot_nt(da, ws[0]) + dot_nt(db, ws[1])).astype(BF)
        for copy in out_copies(c):
            copy.start()
        return carry

    lax.fori_loop(0, sources // 2, forward_chunk, 0)
    block = 384
    inner = block // piece
    high = dp // inner
    low = dp % inner

    def grad_copies(jr):
        slot = lax.rem(jr, 2)
        copies = []
        for ri in range(inner):
            dst = (send_out if ri % 2 else keep_out).at[jr * (inner // 2) + ri // 2]
            src = stage.at[slot, :, pl.ds(pl.multiple_of((low ^ ri) * piece, 16), piece), :]
            copies.append(pltpu.make_async_copy(src, dst, grad_sem.at[slot, ri]))
        return copies

    def grad_block(jr, carry):
        slot = lax.rem(jr, 2)

        @pl.when(jr >= 2)
        def _():
            for copy in grad_copies(jr - 2):
                copy.wait()

        cols = pl.ds(pl.multiple_of((high ^ jr) * block, 128), block)
        left = dot_tn(xs[:, cols], dab[...])
        stage[slot, 0] = left[:, 0:hidden].astype(BF)
        stage[slot, 1] = left[:, hidden:].astype(BF)
        stage[slot, 2] = dot_tn(gs[:, cols], actg[...]).astype(BF)
        for copy in grad_copies(jr):
            copy.start()
        return carry

    blocks = width // block
    lax.fori_loop(0, blocks, grad_block, 0)
    for jr in range(blocks - 2, blocks):
        for copy in grad_copies(jr):
            copy.wait()
    for c in range(sources // 2):
        for copy in out_copies(c):
            copy.wait()


def run_expert(k, dp_index, xs, gs, gates, weights, slots):
    sources, shards = xs.shape[0], 2 * len(weights)
    rows = sources * slots
    width = xs.shape[2]
    piece, hidden = weights[0].shape[2:]
    inner = 384 // piece
    anywhere = pl.BlockSpec(memory_space=pl.ANY)
    return pl.pallas_call(
        functools.partial(expert_kernel, k, shards, slots),
        in_specs=[pl.BlockSpec(memory_space=pltpu.SMEM)] + [anywhere] * (3 + shards // 2),
        out_specs=[anywhere] * 5,
        out_shape=[
            jax.ShapeDtypeStruct((rows, width), BF),
            jax.ShapeDtypeStruct((rows, width), BF),
            jax.ShapeDtypeStruct((rows, 128), F32),
            jax.ShapeDtypeStruct((shards // 2, 3, piece, hidden), BF),
            jax.ShapeDtypeStruct((shards // 2, 3, piece, hidden), BF),
        ],
        scratch_shapes=[
            pltpu.VMEM((rows, width), BF),
            pltpu.VMEM((rows, width), BF),
            pltpu.VMEM((rows, 128), F32),
            pltpu.VMEM((3, width, hidden), BF),
            pltpu.VMEM((rows, width), BF),
            pltpu.VMEM((rows, width), BF),
            pltpu.VMEM((rows, 128), F32),
            pltpu.VMEM((rows, 2 * hidden), BF),
            pltpu.VMEM((rows, hidden), BF),
            pltpu.VMEM((2, 3, 384, hidden), BF),
            pltpu.SemaphoreType.DMA((3, sources)),
            pltpu.SemaphoreType.DMA((shards,)),
            pltpu.SemaphoreType.DMA((3, sources // 2)),
            pltpu.SemaphoreType.DMA((2, inner)),
        ],
        compiler_params=pltpu.CompilerParams(vmem_limit_bytes=60 * 2**20),
        cost_estimate=pl.CostEstimate(flops=10**6, bytes_accessed=10**6, transcendentals=0),
        name="expert",
    )(dp_index, xs, gs, gates, *weights)


def barrier_with(partners):
    sem = pltpu.get_barrier_semaphore()
    for partner in partners:
        pl.semaphore_signal(sem, inc=1, device_id=partner, device_id_type=pl.DeviceIdType.MESH)
    pl.semaphore_wait(sem, len(partners))


def flipped(axis, mask):
    at = lax.axis_index(axis)
    bit = lax.rem(lax.div(at, mask), 2)
    return {axis: at + mask * (1 - 2 * bit)}


def own_bit(axis, mask):
    return lax.rem(lax.div(lax.axis_index(axis), mask), 2)


TEAM = (("dp", 2), ("expert", 2), ("expert", 1))
GROUP = (("dp", 1), ("expert", 2), ("expert", 1))
CUBE = (("dp", 4), ("dp", 2), ("dp", 1), ("expert", 2), ("expert", 1))
ROTATIONS = ((0, 1, 2, 3), (0, 2, 3, 1), (0, 3, 1, 2))


def gather_all_kernel(pieces, segments, count, *refs):
    shards, give_ref, routes_ref = refs[0:count], refs[count], refs[count + 1]
    fulls, take_ref, team_ref = refs[count + 2:2 * count + 2], refs[2 * count + 2], refs[2 * count + 3]
    own_sem, send_sem, recv_sem, piece_sem, team_sem = refs[2 * count + 4:]
    barrier_with([flipped(*dim) for dim in CUBE])
    bits = [own_bit(*dim) for dim in CUBE]
    here = tuple(pl.ds(bit, 1) for bit in bits)
    own = [pltpu.make_async_copy(shards[i], fulls[i].at[here], own_sem.at[i]) for i in range(count)]
    own.append(pltpu.make_async_copy(routes_ref, team_ref.at[0:1, 0:1, 0:1], own_sem.at[count]))
    for copy in own:
        copy.start()
    for copy in own:
        copy.wait()

    def routes_step(step):
        index = [pl.ds(0, 2) if d < step else pl.ds(0, 1) for d in range(3)]
        src = team_ref.at[tuple(index)]
        index[step] = pl.ds(1, 1)
        return pltpu.make_async_remote_copy(
            src_ref=src, dst_ref=team_ref.at[tuple(index)], send_sem=team_sem.at[0, step],
            recv_sem=team_sem.at[1, step], device_id=flipped(*TEAM[step]), device_id_type=pl.DeviceIdType.MESH,
        )

    def spread(step, n, gathered, dim):
        source, start, width, _ = segments[n]
        at = tuple(pl.ds(0, 2) if d in gathered else pl.ds(bits[d], 1) for d in range(5))
        ref = fulls[source].at[at + (slice(None), pl.ds(start, width))]
        return pltpu.make_async_remote_copy(
            src_ref=ref, dst_ref=ref, send_sem=send_sem.at[step, n], recv_sem=recv_sem.at[step, n],
            device_id=flipped(*CUBE[dim]), device_id_type=pl.DeviceIdType.MESH,
        )

    def hand(k):
        return pltpu.make_async_remote_copy(
            src_ref=give_ref.at[k], dst_ref=take_ref.at[k], send_sem=piece_sem.at[0, k],
            recv_sem=piece_sem.at[1, k], device_id=flipped("dp", 2), device_id_type=pl.DeviceIdType.MESH,
        )

    copies, passed = [], []
    running = [None] * len(segments)
    for step in range(5):
        if 0 < step < 4:
            routes_step(step - 1).wait()
        if step < 3:
            routes_step(step).start()
        for n, segment in enumerate(segments):
            if running[n] is not None:
                running[n].wait_recv()
            order = ROTATIONS[segment[3]] + (4,)
            copy = spread(step, n, order[:step], order[step])
            copy.start()
            copies.append(copy)
            running[n] = copy
        for k in range(pieces) if step == 4 else range(step, min(step + 1, pieces)):
            if step == 4 and k < 4:
                continue
            passed.append(hand(k))
            passed[-1].start()
    for copy in running:
        copy.wait_recv()
    for copy in copies:
        copy.wait_send()
    for copy in passed:
        copy.wait()


def gather_all(shards, segments, give, routes):
    rows = shards[0].shape[0]
    count, pieces = len(shards), give.shape[0]
    anywhere, vmem = pl.BlockSpec(memory_space=pl.ANY), pl.BlockSpec(memory_space=pltpu.VMEM)
    outs = pl.pallas_call(
        functools.partial(gather_all_kernel, pieces, segments, count),
        in_specs=[vmem] * count + [anywhere, vmem],
        out_specs=[anywhere] * (count + 2),
        out_shape=[jax.ShapeDtypeStruct((2,) * 5 + shard.shape, BF) for shard in shards]
        + [jax.ShapeDtypeStruct(give.shape, BF), jax.ShapeDtypeStruct((2, 2, 2) + routes.shape, jnp.int32)],
        scratch_shapes=[
            pltpu.SemaphoreType.DMA((count + 1,)),
            pltpu.SemaphoreType.DMA((5, len(segments))),
            pltpu.SemaphoreType.DMA((5, len(segments))),
            pltpu.SemaphoreType.DMA((2, pieces)),
            pltpu.SemaphoreType.DMA((2, 3)),
        ],
        compiler_params=pltpu.CompilerParams(collective_id=1, has_side_effects=True),
        name="gather_all",
    )(*[shard.reshape((1,) * 5 + shard.shape) for shard in shards], give, routes.reshape((1, 1, 1) + routes.shape))
    fulls = [full.reshape(32 * rows, full.shape[-1]) for full in outs[:count]]
    return fulls, outs[count], outs[count + 1].reshape((8,) + routes.shape)


def job_copies(jobs, gives, takes, sems):
    return [
        pltpu.make_async_remote_copy(
            src_ref=gives[j], dst_ref=takes[j], send_sem=sems.at[0, j], recv_sem=sems.at[1, j],
            device_id=flipped(*jobs[j]), device_id_type=pl.DeviceIdType.MESH,
        )
        for j in range(len(jobs))
    ]


def partners_of(dims, jobs):
    return [flipped(*dim) for dim in dict.fromkeys(tuple(dims) + tuple(jobs))]


def inner_plane():
    return own_bit("dp", 2) != own_bit("dp", 4)


def across():
    at = lax.axis_index("dp")
    return {"dp": at + 2 * (1 - 2 * own_bit("dp", 2)) + 4 * (1 - 2 * own_bit("dp", 4))}


def team_rows_kernel(jobs, relays, layout, experts, rows_ref, gates_ref, pos_ref, *refs):
    count, lanes = len(jobs), len(relays)
    gives, pairs = refs[0:count], refs[count:count + lanes]
    refs = refs[count + lanes:]
    if lanes:
        other_ref, refs = refs[0], refs[1:]
    all_ref, table_ref = refs[0:2]
    takes, far = refs[2:2 + count], refs[2 + count:2 + count + lanes]
    picked_ref, pick, held, built = refs[2 + count + lanes:6 + count + lanes]
    own_sem, send_sem, recv_sem, job_sem, relay_sem, held_sem, built_sem = refs[6 + count + lanes:]
    partners = partners_of(TEAM, jobs)
    if lanes:
        partners += [flipped("dp", 4), across()]
    barrier_with(partners)
    own = [
        pltpu.make_async_copy(rows_ref, all_ref.at[0:1, 0:1, 0:1], own_sem.at[0]),
        pltpu.make_async_copy(gates_ref, table_ref.at[0:1, 0:1, 0:1], own_sem.at[1]),
    ]
    for copy in own:
        copy.start()

    def leg(j, n):
        src = (pairs[j].at[0], pairs[j].at[1], other_ref.at[relays[j]])[n]
        return pltpu.make_async_remote_copy(
            src_ref=src, dst_ref=far[j].at[min(n, 1)], send_sem=relay_sem.at[n, j],
            recv_sem=relay_sem.at[3 + min(n, 1), j], device_id=across() if n == 2 else flipped("dp", 4),
            device_id_type=pl.DeviceIdType.MESH,
        )

    for copy in own:
        copy.wait()
    parts = 4
    width = all_ref.shape[4] // parts
    flows = [(all_ref, (slice(None), pl.ds(c * width, width))) for c in range(parts)]
    flows.append((table_ref, (slice(None), slice(None))))

    def hop(step, f):
        ref, tail = flows[f]
        index = [pl.ds(0, 2) if d < step else pl.ds(0, 1) for d in range(3)]
        src = ref.at[tuple(index) + tail]
        index[step] = pl.ds(1, 1)
        return pltpu.make_async_remote_copy(
            src_ref=src, dst_ref=ref.at[tuple(index) + tail], send_sem=send_sem.at[step, f],
            recv_sem=recv_sem.at[step, f], device_id=flipped(*TEAM[step]), device_id_type=pl.DeviceIdType.MESH,
        )

    order = [parts] + list(range(parts))
    for f in order:
        hop(0, f).start()
    background = job_copies(jobs, gives, takes, job_sem)
    for copy in background:
        copy.start()
    if lanes:

        @pl.when(inner_plane())
        def _():
            for n in (2, 0, 1):
                for j in range(lanes):
                    leg(j, n).start()

        @pl.when(jnp.logical_not(inner_plane()))
        def _():
            for j in range(lanes):
                leg(j, 0).start()

    tokens = rows_ref.shape[3]
    slots = pick.shape[0] // experts
    middle = all_ref.shape[4] // 2
    slot_id = lax.broadcasted_iota(jnp.int32, (slots, tokens), 0)
    turns = [(core, source) for core in range(2) for source in range(4)]

    def fetches(turn):
        core, source = turns[turn]
        copies, at = [], 0
        for n, job in enumerate(layout[source]):
            ref = (takes if core else gives)[job]
            size = ref.shape[0]
            copies.append(pltpu.make_async_copy(ref, held.at[turn % 2, pl.ds(at, size), :], held_sem.at[turn % 2, n]))
            at += size
        return copies

    def store(turn):
        core, source = turns[turn]
        return pltpu.make_async_copy(built.at[turn % 2], picked_ref.at[2 * source + core], built_sem.at[turn % 2])

    def begin(turn):
        if turns[turn][0]:
            for job in layout[turns[turn][1]]:
                background[job].wait()
        for copy in fetches(turn):
            copy.start()

    def gather(turn):
        core, source = turns[turn]
        slot = turn % 2
        for copy in fetches(turn):
            copy.wait()
        if turn + 1 < len(turns):
            begin(turn + 1)
        for k in range(experts):
            hit = slot_id == pos_ref[2 * source + core, k:k + 1, :]
            pick[k * slots:(k + 1) * slots, :] = jnp.where(hit, 1.0, 0.0).astype(BF)
        if turn >= 2:
            store(turn - 2).wait()
        built[slot, :, 0:middle] = dot_nn(pick[...], held[slot, :, 0:middle]).astype(BF)
        built[slot, :, middle:] = dot_nn(pick[...], held[slot, :, middle:]).astype(BF)
        store(turn).start()

    begin(0)
    for step in range(1, 3):
        for n, f in enumerate(order):
            hop(step - 1, f).wait_recv()
            hop(step, f).start()
            if n:
                gather(4 * (step - 1) + n - 1)
    for f in order:
        hop(2, f).wait_recv()
    store(6).wait()
    store(7).wait()
    for step in range(3):
        for f in order:
            hop(step, f).wait_send()
    used = [job for jobs_of in layout for job in jobs_of]
    for job, copy in enumerate(background):
        if job not in used:
            copy.wait()
    for j in range(lanes):
        leg(j, 0).wait()
        leg(j, 1).wait_recv()
    if lanes:

        @pl.when(inner_plane())
        def _():
            for j in range(lanes):
                leg(j, 1).wait_send()
                leg(j, 2).wait_send()


def team_rows(rows, gates, positions, layout, experts, slots, jobs=(), gives=(), relays=(), pairs=(), other=None):
    tokens, width = rows.shape
    size = experts * slots
    table = gates.shape
    anywhere = pl.BlockSpec(memory_space=pl.ANY)
    extra = [] if other is None else [other]
    full, tables, *takes = pl.pallas_call(
        functools.partial(team_rows_kernel, tuple(jobs), tuple(relays), layout, experts),
        in_specs=[pl.BlockSpec(memory_space=pltpu.VMEM)] * 3 + [anywhere] * (len(jobs) + len(pairs) + len(extra)),
        out_specs=[anywhere] * (3 + len(jobs) + len(pairs)),
        out_shape=[
            jax.ShapeDtypeStruct((2, 2, 2, tokens, width), BF),
            jax.ShapeDtypeStruct((2, 2, 2) + table, F32),
        ] + [jax.ShapeDtypeStruct(give.shape, give.dtype) for give in list(gives) + list(pairs)]
        + [jax.ShapeDtypeStruct((8, size, width), BF)],
        scratch_shapes=[
            pltpu.VMEM((size, tokens), BF),
            pltpu.VMEM((2, tokens, width), BF),
            pltpu.VMEM((2, size, width), BF),
            pltpu.SemaphoreType.DMA((2,)),
            pltpu.SemaphoreType.DMA((3, 5)),
            pltpu.SemaphoreType.DMA((3, 5)),
            pltpu.SemaphoreType.DMA((2, max(1, len(jobs)))),
            pltpu.SemaphoreType.DMA((5, max(1, len(relays)))),
            pltpu.SemaphoreType.DMA((2, 2)),
            pltpu.SemaphoreType.DMA((2,)),
        ],
        compiler_params=pltpu.CompilerParams(collective_id=2, has_side_effects=True, vmem_limit_bytes=60 * 2**20),
        name="team_rows",
    )(rows.reshape(1, 1, 1, tokens, width), gates.reshape((1, 1, 1) + table), positions, *gives, *pairs, *extra)
    *takes, picked = takes
    return full.reshape(8, tokens, width), tables.reshape((8,) + table), takes, picked


def add_into(acc, at, other):
    acc[at] = (acc[at].astype(F32) + other.astype(F32)).astype(BF)


def return_kernel(count, slots, jobs, relays, pos_ref, *refs):
    x_refs, y_refs, dg_refs = refs[0:count], refs[count:2 * count], refs[2 * count:3 * count]
    refs = refs[3 * count:]
    gives, takes = refs[0:len(jobs)], refs[len(jobs) + 4:2 * len(jobs) + 4]
    out_ref, gate_ref, kept_ref, sent_ref = refs[len(jobs):len(jobs) + 4]
    (acc, core_in, even_out, row_in, pair_in, last_in, ys, pick, table, table_core, table_row, table_pair,
     load_sem, send_sem, recv_sem, job_sem, store_sem, free_sem) = refs[2 * len(jobs) + 4:]
    tokens, width = out_ref.shape
    half = width // 2
    barrier_with(partners_of(TEAM, jobs))
    background = job_copies(jobs, gives, takes, job_sem)
    for copy in background[relays:]:
        copy.start()
    if relays:

        @pl.when(jnp.logical_not(inner_plane()))
        def _():
            for copy in background[:relays]:
                copy.start()

    first = (lax.axis_index("expert") * 2 + own_bit("dp", 2)) * count
    slot_id = lax.broadcasted_iota(jnp.int32, (slots, tokens), 0)

    def remote(src, dst, n, dim):
        return pltpu.make_async_remote_copy(
            src_ref=src, dst_ref=dst, send_sem=send_sem.at[n], recv_sem=recv_sem.at[n],
            device_id=flipped(*TEAM[dim]), device_id_type=pl.DeviceIdType.MESH,
        )

    def loads(parts, r, slot):
        return [
            pltpu.make_async_copy(
                parts[k].at[pl.ds(pl.multiple_of(r * slots, 16), slots), :],
                ys.at[slot, pl.ds(k * slots, slots), :], load_sem.at[slot, k],
            )
            for k in range(count)
        ]

    table[...] = jnp.zeros_like(table)

    def build(parts, step, r, following, dst, at, with_gates):
        slot = lax.rem(step, 2)
        for copy in loads(parts, r, slot):
            copy.wait()

        @pl.when(step < 7)
        def _():
            for copy in loads(parts, following, 1 - slot):
                copy.start()

        for k in range(count):
            hit = slot_id == pos_ref[r, k:k + 1, :]
            pick[k * slots:(k + 1) * slots, :] = jnp.where(hit, 1.0, 0.0).astype(BF)
            if with_gates:
                pulled = dg_refs[k][pl.ds(pl.multiple_of(r * slots, 16), slots), 0:1]
                table[r, pl.ds(first + k, 1), :] = jnp.sum(jnp.where(hit, pulled, 0.0), 0, keepdims=True)
        dst[at, :, 0:half] = dot_tn(pick[...], ys[slot, :, 0:half]).astype(BF)
        dst[at, :, half:] = dot_tn(pick[...], ys[slot, :, half:]).astype(BF)

    def core_copy(i, base):
        return remote(acc.at[2 * i + 1], core_in.at[i], base + i, 2)

    def build_odd(parts, base, with_gates):
        def odd(i, carry):
            r = 2 * i + 1
            build(parts, i, r, jnp.where(i < 3, r + 2, 0), acc, r, with_gates)
            core_copy(i, base).start()
            return carry

        lax.fori_loop(0, 4, odd, 0)

    for copy in loads(x_refs, 1, 0):
        copy.start()
    build_odd(x_refs, 0, True)
    tables = [remote(table.at[2 * i + 1], table_core.at[i], 4 + i, 2) for i in range(4)]
    for copy in tables:
        copy.start()

    def even(i, carry):
        build(x_refs, i + 4, 2 * i, 2 * i + 2, acc, 2 * i, True)
        return carry

    lax.fori_loop(0, 4, even, 0)
    if relays:

        @pl.when(inner_plane())
        def _():
            for copy in background[:relays]:
                copy.start()

    for copy in loads(y_refs, 1, 0):
        copy.start()

    def settle(i):
        core_copy(i, 0).wait()
        add_into(acc, 2 * i, core_in[i])

    left, right = slice(0, half), slice(half, width)
    settle(3)
    a = [remote(acc.at[6, :, pl.ds(0, half)], row_in.at[1], 8, 1), remote(acc.at[6, :, pl.ds(half, half)], pair_in.at[1], 9, 0)]
    for copy in a:
        copy.start()
    settle(1)
    a.append(remote(acc.at[2, :, pl.ds(0, half)], row_in.at[0], 10, 1))
    a[-1].start()
    settle(2)
    a.append(remote(acc.at[4, :, pl.ds(half, half)], pair_in.at[0], 11, 0))
    a[-1].start()
    settle(0)
    pl.semaphore_signal(free_sem, inc=1, device_id=flipped(*TEAM[2]), device_id_type=pl.DeviceIdType.MESH)
    for i, copy in enumerate(tables):
        copy.wait()
        table[2 * i] = table[2 * i] + table_core[i]
    t = [remote(table.at[2], table_row.at[0], 12, 1), remote(table.at[6], table_row.at[1], 13, 1)]
    for copy in t:
        copy.start()
    pl.semaphore_wait(free_sem, 1)
    build_odd(y_refs, 17, False)
    a[0].wait()
    add_into(acc, (4, slice(None), left), row_in[1])
    b = [remote(acc.at[4, :, pl.ds(0, half)], last_in.at[0], 14, 0)]
    b[0].start()
    a[1].wait()
    add_into(acc, (2, slice(None), right), pair_in[1])
    b.append(remote(acc.at[2, :, pl.ds(half, half)], last_in.at[1], 15, 1))
    b[1].start()
    for i, copy in enumerate(t):
        copy.wait()
        table[4 * i] = table[4 * i] + table_row[i]
    t = remote(table.at[4], table_pair, 16, 0)
    t.start()

    def even_y(i, carry):
        build(y_refs, i + 4, 2 * i, 2 * i + 2, even_out, i, False)
        return carry

    lax.fori_loop(0, 4, even_y, 0)
    stores = []
    for i in range(4):
        core_copy(i, 17).wait()
        add_into(even_out, i, core_in[i])
        stores.append(
            pltpu.make_async_copy(even_out.at[i], (sent_ref if i % 2 else kept_ref).at[i // 2], store_sem.at[i])
        )
        stores[-1].start()
    a[2].wait()
    add_into(acc, (0, slice(None), left), row_in[0])
    a[3].wait()
    add_into(acc, (0, slice(None), right), pair_in[0])
    b[0].wait()
    out_ref[:, left] = (acc[0, :, left].astype(F32) + last_in[0].astype(F32)).astype(BF)
    b[1].wait()
    out_ref[:, right] = (acc[0, :, right].astype(F32) + last_in[1].astype(F32)).astype(BF)
    t.wait()
    gate_ref[...] = table[0] + table_pair[...]
    for copy in stores:
        copy.wait()
    for copy in background:
        copy.wait()


def return_rows(positions, backs, results, gate_rows, experts, slots, jobs=(), gives=(), relays=0):
    sources, _, tokens = positions.shape
    count = len(results)
    width = results[0].shape[1]
    half = width // 2
    vmem, anywhere = pl.BlockSpec(memory_space=pltpu.VMEM), pl.BlockSpec(memory_space=pl.ANY)
    rows, gates, kept, sent, *takes = pl.pallas_call(
        functools.partial(return_kernel, count, slots, tuple(jobs), relays),
        in_specs=[vmem] + [anywhere] * (2 * count) + [vmem] * count + [anywhere] * len(jobs),
        out_specs=[vmem, vmem] + [anywhere] * (2 + len(jobs)),
        out_shape=[jax.ShapeDtypeStruct((tokens, width), BF), jax.ShapeDtypeStruct((experts, tokens), F32)]
        + [jax.ShapeDtypeStruct((2, tokens, width), BF)] * 2
        + [jax.ShapeDtypeStruct(give.shape, give.dtype) for give in gives],
        scratch_shapes=[
            pltpu.VMEM((8, tokens, width), BF),
            pltpu.VMEM((4, tokens, width), BF),
            pltpu.VMEM((4, tokens, width), BF),
            pltpu.VMEM((2, tokens, half), BF),
            pltpu.VMEM((2, tokens, half), BF),
            pltpu.VMEM((2, tokens, half), BF),
            pltpu.VMEM((2, count * slots, width), BF),
            pltpu.VMEM((count * slots, tokens), BF),
            pltpu.VMEM((8, experts, tokens), F32),
            pltpu.VMEM((4, experts, tokens), F32),
            pltpu.VMEM((2, experts, tokens), F32),
            pltpu.VMEM((experts, tokens), F32),
            pltpu.SemaphoreType.DMA((2, count)),
            pltpu.SemaphoreType.DMA((21,)),
            pltpu.SemaphoreType.DMA((21,)),
            pltpu.SemaphoreType.DMA((2, max(1, len(jobs)))),
            pltpu.SemaphoreType.DMA((4,)),
            pltpu.SemaphoreType.REGULAR,
        ],
        compiler_params=pltpu.CompilerParams(collective_id=3, has_side_effects=True, vmem_limit_bytes=63 * 2**20),
        name="return_rows",
    )(positions, *backs, *results, *gate_rows, *gives)
    return rows, gates, kept, sent, takes


class Group:
    def __init__(self, copies):
        self.copies = copies

    def wait(self):
        for copy in self.copies:
            copy.wait()


def scatter_kernel(dims, rotations, chunks, segments, sources, relays, *refs):
    last = len(dims) - 1
    grads, refs = refs[0:sources], refs[sources:]
    gives, takes = refs[0:relays], refs[relays + 1:2 * relays + 1]
    out_ref, refs = refs[relays], refs[2 * relays + 1:]
    acc, core_in = refs[0:2]
    inboxes = refs[2:2 + last]
    load_sem, send_sem, recv_sem, job_sem = refs[2 + last:]
    barrier_with([flipped(*dim) for dim in dims])
    background = job_copies(((("dp", 4), ("dp", 2)) * relays)[:relays], gives, takes, job_sem)

    def relay(outer):
        if relays:

            @pl.when(jnp.logical_not(inner_plane()) if outer else inner_plane())
            def _():
                background[0].start()

    bits = [own_bit(*dim) for dim in dims]
    every = tuple(pl.ds(0, 2) for _ in range(last))
    number = iter(range(send_sem.shape[0]))

    def remote(src, dst, dim):
        n = next(number)
        return pltpu.make_async_remote_copy(
            src_ref=src, dst_ref=dst, send_sem=send_sem.at[n], recv_sem=recv_sem.at[n],
            device_id=flipped(*dims[dim]), device_id_type=pl.DeviceIdType.MESH,
        )

    firsts, loads = [[] for _ in chunks], []
    for source, start, at, width, chunk in segments:
        src, dst = (slice(None), pl.ds(start, width)), (slice(None), pl.ds(at, width))
        copy = remote(
            grads[source].at[every + (pl.ds(1 - bits[last], 1),) + src], core_in.at[every + (pl.ds(0, 1),) + dst], last
        )
        copy.start()
        firsts[chunk].append(copy)
        load = pltpu.make_async_copy(
            grads[source].at[every + (pl.ds(bits[last], 1),) + src], acc.at[every + (pl.ds(0, 1),) + dst],
            load_sem.at[len(loads)],
        )
        load.start()
        loads.append(load)
    for load in loads:
        load.wait()
    sends = [Group(copies) for copies in firsts]
    relay(True)
    for step in range(last + 1):
        for c, (start, width) in enumerate(chunks):
            cols = pl.ds(start, width)
            rest = rotations[c][:last - step]
            sends[c].wait()
            for n in range(2 ** len(rest)):
                spread = [(n >> (len(rest) - 1 - i)) & 1 for i in range(len(rest))]
                index = [bits[d] if d not in rest else spread[rest.index(d)] for d in range(last)]
                at = tuple(index) + (0, slice(None), cols)
                other = core_in[at] if step == 0 else inboxes[step - 1][n, :, cols]
                if step < last:
                    add_into(acc, at, other)
                else:
                    out_ref[:, cols] = (acc[at].astype(F32) + other.astype(F32)).astype(out_ref.dtype)
            if step < last:
                dim, spread_dims = rest[-1], rest[:-1]
                group = []
                for n in range(2 ** len(spread_dims)):
                    spread = [(n >> (len(spread_dims) - 1 - i)) & 1 for i in range(len(spread_dims))]
                    index = [
                        1 - bits[d] if d == dim else (spread[spread_dims.index(d)] if d in spread_dims else bits[d])
                        for d in range(last)
                    ]
                    copy = remote(acc.at[tuple(index) + (0, slice(None), cols)], inboxes[step].at[n, :, cols], dim)
                    copy.start()
                    group.append(copy)
                sends[c] = Group(group)
        if step == 0:
            relay(False)
        if step == last - 1:
            for copy in background[1:]:
                copy.start()
    for copy in background:
        copy.wait()


def cube_scatter(dims, rotations, chunks, segments, grads, dtype, collective, name, gives=()):
    last = len(dims) - 1
    rows = grads[0].shape[0] // 2 ** len(dims)
    width = sum(chunk[1] for chunk in chunks)
    copies = len(segments) + len(chunks) * (2 ** last - 1)
    out, *takes = pl.pallas_call(
        functools.partial(scatter_kernel, dims, rotations, chunks, segments, len(grads), len(gives)),
        in_specs=[pl.BlockSpec(memory_space=pl.ANY)] * (len(grads) + len(gives)),
        out_specs=[pl.BlockSpec(memory_space=pltpu.VMEM)] + [pl.BlockSpec(memory_space=pl.ANY)] * len(gives),
        out_shape=[jax.ShapeDtypeStruct((rows, width), dtype)]
        + [jax.ShapeDtypeStruct(give.shape, give.dtype) for give in gives],
        scratch_shapes=[pltpu.VMEM((2,) * last + (1, rows, width), BF)] * 2
        + [pltpu.VMEM((2 ** n, rows, width), BF) for n in reversed(range(last))]
        + [
            pltpu.SemaphoreType.DMA((len(segments),)),
            pltpu.SemaphoreType.DMA((copies,)),
            pltpu.SemaphoreType.DMA((copies,)),
            pltpu.SemaphoreType.DMA((2, max(1, len(gives)))),
        ],
        compiler_params=pltpu.CompilerParams(
            collective_id=collective, has_side_effects=True, vmem_limit_bytes=60 * 2**20
        ),
        name=name,
    )(*[g.reshape((2,) * len(dims) + (rows, g.shape[1])) for g in grads], *gives)
    return out, takes


def dense_segments(wide):
    cut = wide // 256 * 128 + 128
    return ((0, 0, cut, 0), (0, cut, wide - cut, 1), (1, 0, 128, 1), (2, 0, 1536, 2), (3, 0, 128, 2))


def scatter_all(grads, gives):
    segments, chunks, at = [], [0, 0, 0], 0
    for source, start, width, chunk in dense_segments(grads[0].shape[1]):
        segments.append((source, start, at, width, chunk))
        chunks[chunk] += width
        at += width
    starts = (0, chunks[0], chunks[0] + chunks[1])
    return cube_scatter(
        CUBE, ROTATIONS, tuple(zip(starts, chunks)), tuple(segments), grads, F32, 4, "scatter_all", gives
    )


def group_back(grad_key, grad_value):
    width = grad_key.shape[1]
    segments = ((0, 0, 0, width, 0), (1, 0, width, width, 1))
    return cube_scatter(
        GROUP, ((0, 1), (1, 0)), ((0, width), (width, width)), segments, [grad_key, grad_value], BF, 6, "group_back"
    )[0]


def group_rows_kernel(rows_ref, key_ref, value_ref, own_sem, send_sem, recv_sem):
    barrier_with([flipped(*dim) for dim in GROUP])
    bits = [own_bit(*dim) for dim in GROUP]
    width = key_ref.shape[4]
    here = tuple(pl.ds(bit, 1) for bit in bits)
    own = [
        pltpu.make_async_copy(rows_ref.at[:, :, :, :, pl.ds(i * width, width)], ref.at[here], own_sem.at[i])
        for i, ref in enumerate((key_ref, value_ref))
    ]
    for copy in own:
        copy.start()
    for copy in own:
        copy.wait()
    copies = []
    running = [None, None]
    for step in range(3):
        for f, (ref, order) in enumerate(((key_ref, (0, 1, 2)), (value_ref, (1, 0, 2)))):
            if running[f] is not None:
                running[f].wait_recv()
            at = tuple(pl.ds(0, 2) if d in order[:step] else pl.ds(bits[d], 1) for d in range(3))
            copy = pltpu.make_async_remote_copy(
                src_ref=ref.at[at], dst_ref=ref.at[at], send_sem=send_sem.at[step, f], recv_sem=recv_sem.at[step, f],
                device_id=flipped(*GROUP[order[step]]), device_id_type=pl.DeviceIdType.MESH,
            )
            copy.start()
            copies.append(copy)
            running[f] = copy
    for copy in running:
        copy.wait_recv()
    for copy in copies:
        copy.wait_send()


def group_rows(key_value):
    rows, width = key_value.shape
    anywhere = pl.BlockSpec(memory_space=pl.ANY)
    outs = pl.pallas_call(
        group_rows_kernel,
        in_specs=[pl.BlockSpec(memory_space=pltpu.VMEM)],
        out_specs=[anywhere] * 2,
        out_shape=[jax.ShapeDtypeStruct((2, 2, 2, rows, width // 2), BF)] * 2,
        scratch_shapes=[
            pltpu.SemaphoreType.DMA((2,)),
            pltpu.SemaphoreType.DMA((3, 2)),
            pltpu.SemaphoreType.DMA((3, 2)),
        ],
        compiler_params=pltpu.CompilerParams(collective_id=5, has_side_effects=True),
        name="group_rows",
    )(key_value.reshape(1, 1, 1, rows, width))
    return [out.reshape(8 * rows, width // 2) for out in outs]


D = 1536
EPSILON = 1e-06
EVERYWHERE = ("dp", "expert")


def exchange(value, axis, mask):
    return lax.ppermute(value, axis, [(i, i ^ mask) for i in range(lax.axis_size(axis))])


def tie(first, *others):
    return lax.optimization_barrier((first, *others))[0]


def rms_scale(values):
    return lax.rsqrt(jnp.mean(values * values, axis=-1, keepdims=True) + EPSILON)


def product(left, right):
    return jnp.dot(left, right, preferred_element_type=F32)


def contract_rows(left, right):
    return jnp.einsum("ta,tb->ab", left, right, preferred_element_type=F32)


def times_transposed(left, right):
    return jnp.einsum("ta,ba->tb", left, right, preferred_element_type=F32)


def added(left, right):
    return (left.astype(F32) + right.astype(F32)).astype(BF)


def team_gather(value, order):
    pieces = {0: value}
    for axis, mask, bit in order:
        pieces.update({r | bit: exchange(v, axis, mask) for r, v in list(pieces.items())})
    return jnp.stack([pieces[r] for r in sorted(pieces)])


TEAM_BITS = (("dp", 2, 4), ("expert", 2, 2), ("expert", 1, 1))


def local(tokens, attn_gain, w_query, w_key, w_value, w_out, w_router, ffn_gain, w_gate, w_up, w_down, routes, cotangent):
    dp, expert_at = lax.axis_index("dp"), lax.axis_index("expert")
    shards, owners = lax.axis_size("dp"), lax.axis_size("expert")
    cube = shards == 8 and owners == 4
    turn = (dp >> 1) & 1
    tok_rows = tokens.shape[0]
    per_owner, piece, hidden = w_gate.shape
    count = per_owner // 2
    expert_count = per_owner * owners
    top_count = routes.shape[1]
    kvw = w_key.shape[1]
    capacity = 8 * ((17 * top_count * tok_rows + 128 * expert_count - 1) // (128 * expert_count))
    slots = SLOTS_ALIGN * (-(-capacity // SLOTS_ALIGN))
    dp_index = dp.astype(jnp.int32).reshape(1)
    wide = D + 2 * kvw

    stacked = jnp.stack([w_gate, w_up, w_down.transpose(0, 2, 1)], 1)
    own = lax.dynamic_slice_in_dim(stacked, turn * count, count, 0)
    other = lax.dynamic_slice_in_dim(stacked, (1 - turn) * count, count, 0)
    gains = jnp.pad(jnp.stack([attn_gain, ffn_gain], 1), ((0, 0), (0, 126)))
    dense = [
        jnp.concatenate([w_query, w_key, w_value], 1), gains, w_out,
        jnp.pad(w_router, ((0, 0), (0, 128 - expert_count))),
    ]
    ahead = 2
    if cube:
        dense_full, taken, routes_t = gather_all(dense, dense_segments(wide), other[:ahead], routes.T)
    else:
        routes_t = team_gather(routes.T, TEAM_BITS)
        dense_full = [lax.all_gather(shard, EVERYWHERE, axis=0, tiled=True) for shard in dense]
        taken = exchange(other[:ahead], "dp", 2)
    qkv_full, gains_full, out_full, router_full = dense_full
    gains_full = gains_full.astype(F32).T
    gain_first, gain_second = gains_full[0], gains_full[1]

    relay_bits = [1 << b for b in range(2, shards.bit_length() - 1)]
    pairs = [jnp.stack([own[k], taken[k]]) for k in range(ahead)]

    def crossed(relayed):
        return [w for v in relayed for w in (v, exchange(v, "dp", 1))]

    def relays(pair):
        pieces = [pair]
        for bit in relay_bits:
            pieces += [exchange(v, "dp", bit) for v in pieces]
        return pieces

    first_expert = expert_at * per_owner + turn * count
    local_ids = first_expert + jnp.arange(count, dtype=jnp.int32)
    hits = jnp.any(routes_t[:, None] == local_ids[None, :, None, None], axis=2)
    row_id = lax.broadcasted_iota(jnp.int32, (tok_rows, tok_rows), 0)
    col_id = lax.broadcasted_iota(jnp.int32, (tok_rows, tok_rows), 1)
    before = jnp.where(row_id < col_id, 1.0, 0.0).astype(BF)
    ranks = product(hits.astype(BF).reshape(-1, tok_rows), before).reshape(hits.shape)
    positions = jnp.where(hits, ranks.astype(jnp.int32), -1)
    positions = jnp.pad(positions, ((0, 0), (0, 8 - count), (0, 0)), constant_values=-1)

    inputs = tokens.astype(F32)
    scale_one = rms_scale(inputs)
    normed_one = inputs * scale_one
    hidden_one = (normed_one * gain_first).astype(BF)
    qkv = product(hidden_one, qkv_full).astype(BF)
    query, key_value = qkv[:, :D], qkv[:, D:]
    place = ((dp & 1) * owners + expert_at).astype(jnp.int32).reshape(1)
    prompt_key, prompt_value = group_rows(key_value[:P_DEV])
    own_key, own_value = key_value[P_DEV:, :kvw], key_value[P_DEV:, kvw:]
    early = tie(cotangent, qkv_full)
    middle = tok_rows // 2
    paired = exchange(early, "dp", 2)
    upper = exchange(early[:middle], "expert", 2)
    query, early, paired, prompt_key, pairs[:2], late = lax.optimization_barrier(
        (query, early, paired, prompt_key, pairs[:2], other[ahead:])
    )
    parts = [early, paired, upper, None, exchange(paired, "expert", 2)]
    layout = ((0,), (2, 3), (1,), (4,))
    taken_late = exchange(late, "dp", 2)
    pairs += [jnp.stack([own[k], taken_late[k - ahead]]) for k in range(ahead, count)]
    crossings = [exchange(pairs[k], "dp", 1) for k in range(2)]
    mixed, levels = attend(place, query, prompt_key, prompt_value, own_key, own_value)
    parts[3] = exchange(early[middle:], "expert", 2)
    second = inputs + product(mixed, out_full)
    second, parts[3:5] = lax.optimization_barrier((second, parts[3:5]))
    scale_two = rms_scale(second)
    normed_two = second * scale_two
    hidden_two = (normed_two * gain_second).astype(BF)
    logits = product(hidden_two, router_full)[:, :expert_count]
    expert_ids = jnp.arange(expert_count, dtype=jnp.int32)
    chosen = jnp.any(routes[:, :, None] == expert_ids, axis=1)
    peak = jnp.max(jnp.where(chosen, logits, NEGATIVE), axis=-1, keepdims=True)
    raised = jnp.where(chosen, jnp.exp(jnp.where(chosen, logits - peak, 0.0)), 0.0)
    gates = raised / jnp.sum(raised, axis=-1, keepdims=True)

    weights = [None] * count
    near = exchange(tie(pairs[0], taken_late), "dp", 4) if cube else None
    sent_rows, parts, crossings = lax.optimization_barrier((hidden_two, parts, crossings))
    core_jobs = (("expert", 1),) * 5
    if cube:
        rows, gates_t, takes, grad_slots = team_rows(
            sent_rows, gates.T, positions, layout, count, slots,
            core_jobs + (("dp", 1),) * 3, (*parts, *pairs[2:]), (1, 2), pairs[1:3], other,
        )
        crossings = crossings + takes[5:8]
        relayed_pairs = [near] + takes[8:10]
        for k in range(3, count):
            relayed_pairs.append(exchange(tie(pairs[k], rows), "dp", 4))
        for k in range(count):
            weights[k] = [pairs[k], crossings[k], relayed_pairs[k]]
    else:
        rows, gates_t, _, grad_slots = team_rows(
            sent_rows, gates.T, positions, layout, count, slots, core_jobs, parts
        )
        for k in range(count):
            weights[k] = crossed(relays(tie(pairs[k], rows)))
    gates_t = lax.dynamic_slice_in_dim(gates_t, first_expert, count, 1)
    gates_t = jnp.pad(gates_t, ((0, 0), (0, 8 - count), (0, 0)))
    row_slots, gate_slots = gather_rows(positions, gates_t, rows, count, slots)

    results, backs, gate_rows, sums = [], [], [], []
    expert_index = dp_index
    for k in range(count):
        if cube:
            relayed_pair = tie(weights[k][2], rows) if k < 3 else tie(weights[k][2], gate_rows[k - 2], weights[k - 1][3])
            weights[k].append(exchange(relayed_pair, "dp", 1))
        y, dx, dg, keep, send = run_expert(k, expert_index, row_slots, grad_slots, gate_slots, weights[k], slots)
        results.append(y)
        backs.append(dx)
        gate_rows.append(dg)
        sums.append((keep, send))
        expert_index = tie(dp_index, dg)

    before_return = added(sums[0][0], exchange(tie(sums[0][1], gate_rows[1], weights[4]), "dp", 1))
    jobs, gives, relays_in = (("dp", 1),) * 2, (sums[1][1], sums[2][1]), 0
    if cube:
        jobs, gives, relays_in = (("dp", 4),) + jobs, (before_return[2:],) + gives, 1
    routed_back, gate_grad, out_keep, out_sent, takes = return_rows(
        positions, backs, results, gate_rows, expert_count, slots, jobs, gives, relays_in
    )
    halved = [before_return, added(sums[1][0], takes[-2]), added(sums[2][0], takes[-1])]
    crossed_back = [exchange(tie(sums[k][1], routed_back), "dp", 1) for k in range(3, count)]
    relay_bits = relay_bits[::-1]

    def sent_on(keep):
        return exchange(keep[keep.shape[0] // 2:], "dp", relay_bits[0])

    def settled(keep, came):
        keep = added(keep[:keep.shape[0] // 2], came)
        for bit in relay_bits[1:]:
            middle = keep.shape[0] // 2
            keep = added(keep[:middle], exchange(keep[middle:], "dp", bit))
        return keep

    relay_came = [takes[0] if cube else sent_on(before_return)] + [sent_on(keep) for keep in halved[1:]]
    gate_grad = gate_grad.T
    routed_back = routed_back.astype(F32)

    grad_output = cotangent.astype(F32)
    picked = jnp.where(chosen, gate_grad, 0.0)
    grad_logits = (gates * (picked - jnp.sum(gates * picked, axis=-1, keepdims=True))).astype(BF)
    wide_logits = jnp.pad(grad_logits, ((0, 0), (0, 128 - expert_count)))
    grad_hidden_two = times_transposed(wide_logits, router_full) + routed_back
    grad_normed_two = grad_hidden_two * gain_second
    grad_second = grad_output + scale_two * (
        grad_normed_two - normed_two * jnp.mean(grad_normed_two * normed_two, axis=-1, keepdims=True)
    )
    grad_branch = grad_second.astype(BF)
    ones = jnp.ones((tok_rows, 128), BF)
    lane = lax.broadcasted_iota(jnp.int32, (tok_rows, 128), 1)
    small = contract_rows(hidden_two, wide_logits) + contract_rows(
        (grad_hidden_two * normed_two).astype(BF), jnp.where(lane == expert_count, ones, jnp.zeros_like(ones))
    )
    out_grad = contract_rows(mixed, grad_branch).astype(BF)
    grad_mixed = times_transposed(grad_branch, out_full).astype(BF)

    grad_mixed, halved = lax.optimization_barrier((grad_mixed, halved))
    row_came = exchange(out_sent, "expert", 2)
    grad_query, dkp, dvp, dko, dvo = attend_back(
        place, query, prompt_key, prompt_value, own_key, own_value, mixed, grad_mixed, levels
    )
    halved, relay_came, crossed_back, grad_query, row_came, dkp = lax.optimization_barrier(
        (halved, relay_came, crossed_back, grad_query, row_came, dkp)
    )
    halved += [added(sums[k][0], crossed_back[k - 3]) for k in range(3, count)]
    relay_came += [sent_on(halved[3])]
    grad_prompt = group_back(dkp, dvp)
    grad_qkv = jnp.concatenate([
        grad_query, jnp.concatenate([grad_prompt, jnp.concatenate([dko, dvo], 1)], 0)
    ], 1)
    grad_hidden_one = times_transposed(grad_qkv, qkv_full)
    weight_rows, grad_hidden_one, relay_came[3] = lax.optimization_barrier((grad_qkv, grad_hidden_one, relay_came[3]))
    total = tie(added(out_keep, row_came), weight_rows)
    pair_came = exchange(total[1], "dp", 2)
    relayed = [settled(halved[k], relay_came[k]) for k in range(3)]
    passing = jnp.stack([keep[1] for keep in relayed])
    dense_grads = [
        contract_rows(hidden_one, weight_rows).astype(BF),
        contract_rows((grad_hidden_one * normed_one).astype(BF), ones).astype(BF),
        out_grad, small.astype(BF),
    ]
    if cube:
        share, takes = scatter_all(dense_grads, (halved[4][2:], passing))
        relay_came.append(takes[0])
        theirs = takes[1]
    else:
        share = lax.psum_scatter(
            jnp.concatenate(dense_grads, 1), EVERYWHERE, scatter_dimension=0, tiled=True
        ).astype(F32)
        relay_came.append(sent_on(halved[4]))
        theirs = exchange(passing, "dp", 2)
    grad_normed_one = grad_hidden_one * gain_first
    grad_input = grad_second + scale_one * (
        grad_normed_one - normed_one * jnp.mean(grad_normed_one * normed_one, axis=-1, keepdims=True)
    )

    share, halved, relay_came, total, pair_came = lax.optimization_barrier(
        (share, halved, relay_came, total, pair_came)
    )
    output = (second + added(total[0], pair_came).astype(F32)).astype(BF)
    first_share, second_share = share[:, :wide + 128], share[:, wide + 128:]
    relayed += [settled(halved[k], relay_came[k]) for k in range(3, count)]
    theirs = jnp.concatenate([theirs, exchange(jnp.stack([keep[1] for keep in relayed[3:]]), "dp", 2)])
    mine = jnp.stack([keep[0] for keep in relayed])
    lower = jnp.where(turn == 0, mine, theirs)
    upper = jnp.where(turn == 0, theirs, mine)
    expert_grads = jnp.concatenate([lower, upper]).astype(F32)
    return (
        output,
        grad_input.astype(BF),
        first_share[:, wide],
        first_share[:, :D],
        first_share[:, D:D + kvw],
        first_share[:, D + kvw:wide],
        second_share[:, :D].astype(F32),
        second_share[:, D:D + expert_count].astype(F32),
        second_share[:, D + expert_count].astype(F32),
        expert_grads[:, 0],
        expert_grads[:, 1],
        expert_grads[:, 2].transpose(0, 2, 1),
    )


def solution(mesh):
    rows, line = P(("dp", "expert"), None), P(("dp", "expert"))
    gate, down = P("expert", "dp", None), P("expert", None, "dp")
    return jax.shard_map(
        local,
        mesh=mesh,
        in_specs=(rows, line, rows, rows, rows, rows, rows, line, gate, gate, down, rows, rows),
        out_specs=(rows, rows, line, rows, rows, rows, rows, rows, line, gate, gate, down),
        check_vma=False,
    )
```

```python
import functools
import jax
import jax.numpy as jnp
from jax import lax
from jax.sharding import PartitionSpec as P
from jax.experimental import pallas as pl
from jax.experimental.pallas import tpu as pltpu

HD = 64
P_DEV = 128
NEGATIVE = -1e30
F32 = jnp.float32
BF = jnp.bfloat16


def dot_nt(a, b):
    return lax.dot_general(a, b, (((1,), (1,)), ((), ())), preferred_element_type=F32)


def dot_nn(a, b):
    return lax.dot_general(a, b, (((1,), (0,)), ((), ())), preferred_element_type=F32)


def dot_tn(a, b):
    return lax.dot_general(a, b, (((0,), (0,)), ((), ())), preferred_element_type=F32)


def halves(pair):
    lane = lax.broadcasted_iota(jnp.int32, pair.shape, 1)
    zero = jnp.zeros_like(pair)
    return jnp.where(lane < HD, pair, zero), jnp.where(lane < HD, zero, pair)


def placed_halves(pair_f32):
    low0, high1 = halves(pair_f32)
    high0 = pltpu.roll(low0, HD, 1)
    low1 = pltpu.roll(high1, HD, 1)
    return ((low0.astype(BF), high0.astype(BF)), (low1.astype(BF), high1.astype(BF)))


def attend_kernel(place_ref, q_ref, kp_ref, vp_ref, ko_ref, vo_ref, o_ref, lse_ref, kpad, vpad, s_scr, p_scr):
    rows = q_ref.shape[0]
    prompt = kp_ref.shape[0]
    cont = ko_ref.shape[0]
    place = place_ref[0]
    for src, dst in ((kp_ref, kpad), (vp_ref, vpad)):
        for head, pair in enumerate(placed_halves(src[...].astype(F32))):
            for half in range(2):
                dst[head, half, 0:prompt, :] = pair[half]
    for src, dst in ((ko_ref, kpad), (vo_ref, vpad)):
        for head, pair in enumerate(placed_halves(src[...].astype(F32))):
            for half in range(2):
                dst[head, half, prompt:prompt + cont, :] = pair[half]
    key_id = lax.broadcasted_iota(jnp.int32, (prompt, P_DEV), 0)
    row_id = lax.broadcasted_iota(jnp.int32, (prompt, P_DEV), 1)
    seen_prompt = key_id <= place * P_DEV + row_id
    diag = lax.broadcasted_iota(jnp.int32, (P_DEV, P_DEV), 0) <= lax.broadcasted_iota(jnp.int32, (P_DEV, P_DEV), 1)
    blocks = cont // P_DEV
    stats = []
    for chunk in range(3):
        queries = (q_ref[:, chunk * 128:(chunk + 1) * 128].astype(F32) * HD ** (-0.5)).astype(BF)
        total = None
        for half in range(2):
            position = chunk * 2 + half
            head = position // 3
            keys = kpad.at[head, half]
            scores = dot_nt(keys[0:prompt, :], queries)
            first = jnp.where(seen_prompt, scores[:, 0:P_DEV], NEGATIVE)
            rest = scores[:, P_DEV:]
            s_scr[0:prompt, 0:P_DEV] = first
            s_scr[0:prompt, P_DEV:] = rest
            top = jnp.concatenate([jnp.max(first, 0, keepdims=True), jnp.max(rest, 0, keepdims=True)], 1)
            tops = [top[:, i * P_DEV:(i + 1) * P_DEV] for i in range(1 + blocks)]
            for block in range(blocks):
                start = (1 + block) * P_DEV
                at = prompt + block * P_DEV
                own = dot_nt(keys[at:at + P_DEV, :], queries[start:, :])
                edge = jnp.where(diag, own[:, 0:P_DEV], NEGATIVE)
                s_scr[at:at + P_DEV, start:start + P_DEV] = edge
                tops[1 + block] = jnp.maximum(tops[1 + block], jnp.max(edge, 0, keepdims=True))
                if block + 1 < blocks:
                    later = own[:, P_DEV:]
                    s_scr[at:at + P_DEV, start + P_DEV:] = later
                    best = jnp.max(later, 0, keepdims=True)
                    for i in range(block + 1, blocks):
                        at_i = (i - block - 1) * P_DEV
                        tops[1 + i] = jnp.maximum(tops[1 + i], best[:, at_i:at_i + P_DEV])
            top = jnp.concatenate(tops, 1)
            weights = jnp.exp(s_scr[0:prompt, :] - top)
            mass = jnp.sum(weights, 0, keepdims=True)
            masses = [mass[:, i * P_DEV:(i + 1) * P_DEV] for i in range(1 + blocks)]
            values = vpad.at[head, half]
            mixed = dot_tn(values[0:prompt, :], weights.astype(BF))
            for block in range(blocks):
                start = (1 + block) * P_DEV
                at = prompt + block * P_DEV
                part = jnp.exp(s_scr[at:at + P_DEV, start:] - top[:, start:])
                p_scr[block * P_DEV:(block + 1) * P_DEV, start:] = part.astype(BF)
                if block:
                    p_scr[block * P_DEV:(block + 1) * P_DEV, P_DEV:start] = jnp.zeros((P_DEV, block * P_DEV), BF)
                part_mass = jnp.sum(part, 0, keepdims=True)
                for i in range(block, blocks):
                    at_i = (i - block) * P_DEV
                    masses[1 + i] = masses[1 + i] + part_mass[:, at_i:at_i + P_DEV]
            own_mixed = dot_tn(values[prompt:prompt + cont, :], p_scr[:, P_DEV:])
            mass = jnp.concatenate(masses, 1)
            scale = 1.0 / mass
            mixed = jnp.concatenate([mixed[:, 0:P_DEV], mixed[:, P_DEV:] + own_mixed], 1) * scale
            total = mixed if total is None else total + mixed
            stats.append(top + jnp.log(mass))
        o_ref[:, chunk * 128:(chunk + 1) * 128] = jnp.transpose(total).astype(BF)
    lse_ref[0] = jnp.concatenate(stats + [jnp.zeros((2, rows), F32)], 0)


def attend(place, query, prompt_key, prompt_value, own_key, own_value):
    rows = query.shape[0]
    prompt = prompt_key.shape[0]
    cont = own_key.shape[0]
    pairs = prompt_key.shape[1] // 128
    col = lambda i: (0, i)
    return pl.pallas_call(
        attend_kernel,
        grid=(pairs,),
        in_specs=[
            pl.BlockSpec(memory_space=pltpu.SMEM),
            pl.BlockSpec((rows, 384), col),
            pl.BlockSpec((prompt, 128), col),
            pl.BlockSpec((prompt, 128), col),
            pl.BlockSpec((cont, 128), col),
            pl.BlockSpec((cont, 128), col),
        ],
        out_specs=[pl.BlockSpec((rows, 384), col), pl.BlockSpec((1, 8, rows), lambda i: (i, 0, 0))],
        out_shape=[
            jax.ShapeDtypeStruct(query.shape, BF),
            jax.ShapeDtypeStruct((pairs, 8, rows), F32),
        ],
        scratch_shapes=[
            pltpu.VMEM((2, 2, prompt + cont, 128), BF),
            pltpu.VMEM((2, 2, prompt + cont, 128), BF),
            pltpu.VMEM((prompt + cont, rows), F32),
            pltpu.VMEM((cont, rows), BF),
        ],
        cost_estimate=pl.CostEstimate(flops=10**6, bytes_accessed=10**6, transcendentals=0),
        name="attend",
    )(place, query, prompt_key, prompt_value, own_key, own_value)


def attend_back_kernel(place_ref, q_ref, kp_ref, vp_ref, ko_ref, vo_ref, o_ref, do_ref, lse_ref,
                       dq_ref, dkp_ref, dvp_ref, dko_ref, dvo_ref, kpad, vpad, dk_acc, dv_acc):
    rows = q_ref.shape[0]
    prompt = kp_ref.shape[0]
    cont = ko_ref.shape[0]
    step = 2 * P_DEV
    place = place_ref[0]
    for src, dst, at, size in ((kp_ref, kpad, 0, prompt), (vp_ref, vpad, 0, prompt),
                               (ko_ref, kpad, prompt, cont), (vo_ref, vpad, prompt, cont)):
        for head, pair in enumerate(placed_halves(src[...].astype(F32))):
            for half in range(2):
                dst[head, half, at:at + size, :] = pair[half]
    dk_acc[...] = jnp.zeros_like(dk_acc)
    dv_acc[...] = jnp.zeros_like(dv_acc)
    for chunk in range(3):
        lanes = slice(chunk * 128, (chunk + 1) * 128)
        scaled = q_ref[:, lanes].astype(F32) * HD ** (-0.5)
        queries = scaled.astype(BF)
        query_halves = [part.astype(BF) for part in halves(scaled)]
        outs = o_ref[:, lanes].astype(F32)
        grads_f32 = do_ref[:, lanes].astype(F32)
        grads = do_ref[:, lanes]
        grad_halves = [part.astype(BF) for part in halves(grads_f32)]
        inner = jnp.transpose(outs * grads_f32)
        total = jnp.zeros((128, rows), F32)
        for half in range(2):
            position = chunk * 2 + half
            head = position // 3
            level = lse_ref[0, position:position + 1, :]
            delta = jnp.sum(inner[half * HD:(half + 1) * HD, :], 0, keepdims=True)

            def block(at, cols, mask, queries=queries, grads=grads, query_half=query_halves[half],
                      grad_half=grad_halves[half], level=level, delta=delta, head=head, half=half):
                keys = kpad[head, half, pl.ds(at, step), :]
                values = vpad[head, half, pl.ds(at, step), :]
                scores = dot_nt(keys, queries[cols, :])
                weights = jnp.exp(mask(scores) - level[:, cols])
                grad_weights = dot_nt(values, grads[cols, :])
                grad_scores = weights * (grad_weights - delta[:, cols])
                low_weights = weights.astype(BF)
                low_scores = grad_scores.astype(BF)
                dv_acc[head, pl.ds(at, step), :] += dot_nn(low_weights, grad_half[cols, :])
                dk_acc[head, pl.ds(at, step), :] += dot_nn(low_scores, query_half[cols, :])
                return dot_tn(keys, low_scores)

            def prompt_step(i, carry):
                at = pl.multiple_of(i * step, step)

                def mask(scores):
                    key_id = at + lax.broadcasted_iota(jnp.int32, (step, P_DEV), 0)
                    row_id = lax.broadcasted_iota(jnp.int32, (step, P_DEV), 1)
                    first = jnp.where(key_id <= place * P_DEV + row_id, scores[:, 0:P_DEV], NEGATIVE)
                    return jnp.concatenate([first, scores[:, P_DEV:]], 1)

                return carry + block(at, slice(0, rows), mask)

            total = lax.fori_loop(0, prompt // step, prompt_step, total)
            for own in range(cont // step):
                start = P_DEV + own * step

                def mask(scores):
                    key_id = lax.broadcasted_iota(jnp.int32, (step, step), 0)
                    row_id = lax.broadcasted_iota(jnp.int32, (step, step), 1)
                    edge = jnp.where(key_id <= row_id, scores[:, 0:step], NEGATIVE)
                    if scores.shape[1] == step:
                        return edge
                    return jnp.concatenate([edge, scores[:, step:]], 1)

                part = block(prompt + own * step, slice(start, rows), mask)
                total = jnp.concatenate([total[:, 0:start], total[:, start:] + part], 1)
        dq_ref[:, lanes] = (jnp.transpose(total) * HD ** (-0.5)).astype(BF)
    for acc, out_prompt, out_own in ((dk_acc, dkp_ref, dko_ref), (dv_acc, dvp_ref, dvo_ref)):
        low0, high0 = halves(acc[0])
        low1, high1 = halves(acc[1])
        merged = low0 + pltpu.roll(high0, HD, 1) + high1 + pltpu.roll(low1, HD, 1)
        out_prompt[...] = merged[0:prompt].astype(BF)
        out_own[...] = merged[prompt:].astype(BF)


def attend_back(place, query, prompt_key, prompt_value, own_key, own_value, mixed, grad, lse):
    rows = query.shape[0]
    prompt = prompt_key.shape[0]
    cont = own_key.shape[0]
    pairs = prompt_key.shape[1] // 128
    col = lambda i: (0, i)
    wide = pl.BlockSpec((rows, 384), col)
    keys_p = pl.BlockSpec((prompt, 128), col)
    keys_o = pl.BlockSpec((cont, 128), col)
    return pl.pallas_call(
        attend_back_kernel,
        grid=(pairs,),
        in_specs=[
            pl.BlockSpec(memory_space=pltpu.SMEM),
            wide, keys_p, keys_p, keys_o, keys_o, wide, wide,
            pl.BlockSpec((1, 8, rows), lambda i: (i, 0, 0)),
        ],
        out_specs=[wide, keys_p, keys_p, keys_o, keys_o],
        out_shape=[
            jax.ShapeDtypeStruct(query.shape, BF),
            jax.ShapeDtypeStruct(prompt_key.shape, BF),
            jax.ShapeDtypeStruct(prompt_key.shape, BF),
            jax.ShapeDtypeStruct(own_key.shape, BF),
            jax.ShapeDtypeStruct(own_key.shape, BF),
        ],
        scratch_shapes=[
            pltpu.VMEM((2, 2, prompt + cont, 128), BF),
            pltpu.VMEM((2, 2, prompt + cont, 128), BF),
            pltpu.VMEM((2, prompt + cont, 128), F32),
            pltpu.VMEM((2, prompt + cont, 128), F32),
        ],
        cost_estimate=pl.CostEstimate(flops=10**6, bytes_accessed=10**6, transcendentals=0),
        name="attend_back",
    )(place, query, prompt_key, prompt_value, own_key, own_value, mixed, grad, lse)


SLOTS_ALIGN = 16


def gather_kernel(count, with_gates, pos_ref, *refs):
    if with_gates:
        gate_ref, rows_ref, x_ref, g_ref, pick = refs
    else:
        rows_ref, x_ref, pick = refs
    tokens = rows_ref.shape[1]
    slots = x_ref.shape[1] // count
    half = rows_ref.shape[2] // 2
    slot_id = lax.broadcasted_iota(jnp.int32, (slots, tokens), 0)
    for k in range(count):
        hit = slot_id == pos_ref[0, k:k + 1, :]
        pick[k * slots:(k + 1) * slots, :] = jnp.where(hit, 1.0, 0.0).astype(BF)
        if with_gates:
            gate = jnp.sum(jnp.where(hit, gate_ref[0, k:k + 1, :], 0.0), 1, keepdims=True)
            g_ref[0, k * slots:(k + 1) * slots, :] = jnp.broadcast_to(gate, (slots, 128))
    x_ref[0, :, 0:half] = dot_nn(pick[...], rows_ref[0, :, 0:half]).astype(BF)
    x_ref[0, :, half:] = dot_nn(pick[...], rows_ref[0, :, half:]).astype(BF)


def gather_rows(positions, gates, rows, count, slots):
    sources, tokens, width = rows.shape
    size = count * slots
    table = pl.BlockSpec((1, 8, tokens), lambda s: (s, 0, 0))
    block = lambda shape: pl.BlockSpec((1,) + shape, lambda s: (s, 0, 0))
    tables = [positions] if gates is None else [positions, gates]
    outs = [((size, width), BF)] if gates is None else [((size, width), BF), ((size, 128), F32)]
    return pl.pallas_call(
        functools.partial(gather_kernel, count, gates is not None),
        grid=(sources,),
        in_specs=[table] * len(tables) + [block((tokens, width))],
        out_specs=[block(shape) for shape, _ in outs],
        out_shape=[jax.ShapeDtypeStruct((sources,) + shape, dtype) for shape, dtype in outs],
        scratch_shapes=[pltpu.VMEM((size, tokens), BF)],
        cost_estimate=pl.CostEstimate(flops=10**6, bytes_accessed=10**6, transcendentals=0),
        name="gather_rows",
    )(*tables, rows)


def expert_kernel(k, shards, slots, dp_ref, x_ref, g_ref, gate_ref, *refs):
    w_refs = refs[0:shards // 2]
    (y_out, dx_out, dg_out, keep_out, send_out,
     xs, gs, gates, ws, ys, dxs, dgs, dab, actg, stage,
     in_sem, w_sem, out_sem, grad_sem) = refs[shards // 2:]
    dp = dp_ref[0]
    sources = x_ref.shape[0]
    width = xs.shape[1]
    piece = width // shards
    hidden = ws.shape[2]
    mine = pl.ds(k * slots, slots)

    def row_copies(s):
        at = pl.ds(pl.multiple_of(s * slots, 16), slots)
        return (
            pltpu.make_async_copy(x_ref.at[s, mine, :], xs.at[at, :], in_sem.at[0, s]),
            pltpu.make_async_copy(g_ref.at[s, mine, :], gs.at[at, :], in_sem.at[1, s]),
            pltpu.make_async_copy(gate_ref.at[s, mine, :], gates.at[at, :], in_sem.at[2, s]),
        )

    weight_copies = [
        pltpu.make_async_copy(
            w_refs[(r & 1) + 2 * (r >> 2)].at[(r >> 1) & 1], ws.at[:, pl.ds(pl.multiple_of((dp ^ r) * piece, 16), piece), :], w_sem.at[r]
        )
        for r in range(shards)
    ]
    for s in range(sources):
        for copy in row_copies(s):
            copy.start()
        if s == 1:
            for copy in weight_copies:
                copy.start()
    for copy in weight_copies:
        copy.wait()
    chunk = 2 * slots

    def out_copies(c):
        at = pl.ds(pl.multiple_of(c * chunk, 32), chunk)
        return [
            pltpu.make_async_copy(src.at[at, :], dst.at[at, :], out_sem.at[i, c])
            for i, (src, dst) in enumerate(((ys, y_out), (dxs, dx_out), (dgs, dg_out)))
        ]

    def forward_chunk(c, carry):
        for copy in row_copies(2 * c) + row_copies(2 * c + 1):
            copy.wait()
        rows = pl.ds(pl.multiple_of(c * chunk, 32), chunk)
        x = xs[rows, :]
        a = dot_nn(x, ws[0])
        b = dot_nn(x, ws[1])
        pulled = dot_nn(gs[rows, :], ws[2])
        gate = gates[rows, 0:1]
        sig = jax.nn.sigmoid(a)
        silu = a * sig
        act = silu * b
        dgs[rows, :] = jnp.broadcast_to(jnp.sum(act * pulled, 1, keepdims=True), (chunk, 128))
        weighted = (gate * act).astype(BF)
        actg[rows, :] = weighted
        dact = gate * pulled
        da = (dact * b * sig * (1.0 + a * (1.0 - sig))).astype(BF)
        db = (dact * silu).astype(BF)
        dab[rows, 0:hidden] = da
        dab[rows, hidden:] = db
        ys[rows, :] = dot_nt(weighted, ws[2]).astype(BF)
        dxs[rows, :] = (dot_nt(da, ws[0]) + dot_nt(db, ws[1])).astype(BF)
        for copy in out_copies(c):
            copy.start()
        return carry

    lax.fori_loop(0, sources // 2, forward_chunk, 0)
    block = 384
    inner = block // piece
    high = dp // inner
    low = dp % inner

    def grad_copies(jr):
        slot = lax.rem(jr, 2)
        copies = []
        for ri in range(inner):
            dst = (send_out if ri % 2 else keep_out).at[jr * (inner // 2) + ri // 2]
            src = stage.at[slot, :, pl.ds(pl.multiple_of((low ^ ri) * piece, 16), piece), :]
            copies.append(pltpu.make_async_copy(src, dst, grad_sem.at[slot, ri]))
        return copies

    def grad_block(jr, carry):
        slot = lax.rem(jr, 2)

        @pl.when(jr >= 2)
        def _():
            for copy in grad_copies(jr - 2):
                copy.wait()

        cols = pl.ds(pl.multiple_of((high ^ jr) * block, 128), block)
        left = dot_tn(xs[:, cols], dab[...])
        stage[slot, 0] = left[:, 0:hidden].astype(BF)
        stage[slot, 1] = left[:, hidden:].astype(BF)
        stage[slot, 2] = dot_tn(gs[:, cols], actg[...]).astype(BF)
        for copy in grad_copies(jr):
            copy.start()
        return carry

    blocks = width // block
    lax.fori_loop(0, blocks, grad_block, 0)
    for jr in range(blocks - 2, blocks):
        for copy in grad_copies(jr):
            copy.wait()
    for c in range(sources // 2):
        for copy in out_copies(c):
            copy.wait()


def run_expert(k, dp_index, xs, gs, gates, weights, slots):
    sources, shards = xs.shape[0], 2 * len(weights)
    rows = sources * slots
    width = xs.shape[2]
    piece, hidden = weights[0].shape[2:]
    inner = 384 // piece
    anywhere = pl.BlockSpec(memory_space=pl.ANY)
    return pl.pallas_call(
        functools.partial(expert_kernel, k, shards, slots),
        in_specs=[pl.BlockSpec(memory_space=pltpu.SMEM)] + [anywhere] * (3 + shards // 2),
        out_specs=[anywhere] * 5,
        out_shape=[
            jax.ShapeDtypeStruct((rows, width), BF),
            jax.ShapeDtypeStruct((rows, width), BF),
            jax.ShapeDtypeStruct((rows, 128), F32),
            jax.ShapeDtypeStruct((shards // 2, 3, piece, hidden), BF),
            jax.ShapeDtypeStruct((shards // 2, 3, piece, hidden), BF),
        ],
        scratch_shapes=[
            pltpu.VMEM((rows, width), BF),
            pltpu.VMEM((rows, width), BF),
            pltpu.VMEM((rows, 128), F32),
            pltpu.VMEM((3, width, hidden), BF),
            pltpu.VMEM((rows, width), BF),
            pltpu.VMEM((rows, width), BF),
            pltpu.VMEM((rows, 128), F32),
            pltpu.VMEM((rows, 2 * hidden), BF),
            pltpu.VMEM((rows, hidden), BF),
            pltpu.VMEM((2, 3, 384, hidden), BF),
            pltpu.SemaphoreType.DMA((3, sources)),
            pltpu.SemaphoreType.DMA((shards,)),
            pltpu.SemaphoreType.DMA((3, sources // 2)),
            pltpu.SemaphoreType.DMA((2, inner)),
        ],
        compiler_params=pltpu.CompilerParams(vmem_limit_bytes=60 * 2**20),
        cost_estimate=pl.CostEstimate(flops=10**6, bytes_accessed=10**6, transcendentals=0),
        name="expert",
    )(dp_index, xs, gs, gates, *weights)


def barrier_with(partners):
    sem = pltpu.get_barrier_semaphore()
    for partner in partners:
        pl.semaphore_signal(sem, inc=1, device_id=partner, device_id_type=pl.DeviceIdType.MESH)
    pl.semaphore_wait(sem, len(partners))


def flipped(axis, mask):
    at = lax.axis_index(axis)
    bit = lax.rem(lax.div(at, mask), 2)
    return {axis: at + mask * (1 - 2 * bit)}


def own_bit(axis, mask):
    return lax.rem(lax.div(lax.axis_index(axis), mask), 2)


TEAM = (("dp", 2), ("expert", 2), ("expert", 1))
GROUP = (("dp", 1), ("expert", 2), ("expert", 1))
CUBE = (("dp", 4), ("dp", 2), ("dp", 1), ("expert", 2), ("expert", 1))
ROTATIONS = ((0, 1, 2, 3), (0, 2, 3, 1), (0, 3, 1, 2))


def gather_all_kernel(pieces, segments, count, *refs):
    shards, give_ref, routes_ref = refs[0:count], refs[count], refs[count + 1]
    fulls, take_ref, team_ref = refs[count + 2:2 * count + 2], refs[2 * count + 2], refs[2 * count + 3]
    own_sem, send_sem, recv_sem, piece_sem, team_sem = refs[2 * count + 4:]
    barrier_with([flipped(*dim) for dim in CUBE])
    bits = [own_bit(*dim) for dim in CUBE]
    here = tuple(pl.ds(bit, 1) for bit in bits)
    own = [pltpu.make_async_copy(shards[i], fulls[i].at[here], own_sem.at[i]) for i in range(count)]
    own.append(pltpu.make_async_copy(routes_ref, team_ref.at[0:1, 0:1, 0:1], own_sem.at[count]))
    for copy in own:
        copy.start()
    for copy in own:
        copy.wait()

    def routes_step(step):
        index = [pl.ds(0, 2) if d < step else pl.ds(0, 1) for d in range(3)]
        src = team_ref.at[tuple(index)]
        index[step] = pl.ds(1, 1)
        return pltpu.make_async_remote_copy(
            src_ref=src, dst_ref=team_ref.at[tuple(index)], send_sem=team_sem.at[0, step],
            recv_sem=team_sem.at[1, step], device_id=flipped(*TEAM[step]), device_id_type=pl.DeviceIdType.MESH,
        )

    def spread(step, n, gathered, dim):
        source, start, width, _ = segments[n]
        at = tuple(pl.ds(0, 2) if d in gathered else pl.ds(bits[d], 1) for d in range(5))
        ref = fulls[source].at[at + (slice(None), pl.ds(start, width))]
        return pltpu.make_async_remote_copy(
            src_ref=ref, dst_ref=ref, send_sem=send_sem.at[step, n], recv_sem=recv_sem.at[step, n],
            device_id=flipped(*CUBE[dim]), device_id_type=pl.DeviceIdType.MESH,
        )

    def hand(k):
        return pltpu.make_async_remote_copy(
            src_ref=give_ref.at[k], dst_ref=take_ref.at[k], send_sem=piece_sem.at[0, k],
            recv_sem=piece_sem.at[1, k], device_id=flipped("dp", 2), device_id_type=pl.DeviceIdType.MESH,
        )

    copies, passed = [], []
    running = [None] * len(segments)
    for step in range(5):
        if 0 < step < 4:
            routes_step(step - 1).wait()
        if step < 3:
            routes_step(step).start()
        for n, segment in enumerate(segments):
            if running[n] is not None:
                running[n].wait_recv()
            order = ROTATIONS[segment[3]] + (4,)
            copy = spread(step, n, order[:step], order[step])
            copy.start()
            copies.append(copy)
            running[n] = copy
        for k in range(pieces) if step == 4 else range(step, min(step + 1, pieces)):
            if step == 4 and k < 4:
                continue
            passed.append(hand(k))
            passed[-1].start()
    for copy in running:
        copy.wait_recv()
    for copy in copies:
        copy.wait_send()
    for copy in passed:
        copy.wait()


def gather_all(shards, segments, give, routes):
    rows = shards[0].shape[0]
    count, pieces = len(shards), give.shape[0]
    anywhere, vmem = pl.BlockSpec(memory_space=pl.ANY), pl.BlockSpec(memory_space=pltpu.VMEM)
    outs = pl.pallas_call(
        functools.partial(gather_all_kernel, pieces, segments, count),
        in_specs=[vmem] * count + [anywhere, vmem],
        out_specs=[anywhere] * (count + 2),
        out_shape=[jax.ShapeDtypeStruct((2,) * 5 + shard.shape, BF) for shard in shards]
        + [jax.ShapeDtypeStruct(give.shape, BF), jax.ShapeDtypeStruct((2, 2, 2) + routes.shape, jnp.int32)],
        scratch_shapes=[
            pltpu.SemaphoreType.DMA((count + 1,)),
            pltpu.SemaphoreType.DMA((5, len(segments))),
            pltpu.SemaphoreType.DMA((5, len(segments))),
            pltpu.SemaphoreType.DMA((2, pieces)),
            pltpu.SemaphoreType.DMA((2, 3)),
        ],
        compiler_params=pltpu.CompilerParams(collective_id=1, has_side_effects=True),
        name="gather_all",
    )(*[shard.reshape((1,) * 5 + shard.shape) for shard in shards], give, routes.reshape((1, 1, 1) + routes.shape))
    fulls = [full.reshape(32 * rows, full.shape[-1]) for full in outs[:count]]
    return fulls, outs[count], outs[count + 1].reshape((8,) + routes.shape)


def job_copies(jobs, gives, takes, sems):
    return [
        pltpu.make_async_remote_copy(
            src_ref=gives[j], dst_ref=takes[j], send_sem=sems.at[0, j], recv_sem=sems.at[1, j],
            device_id=flipped(*jobs[j]), device_id_type=pl.DeviceIdType.MESH,
        )
        for j in range(len(jobs))
    ]


def partners_of(dims, jobs):
    return [flipped(*dim) for dim in dict.fromkeys(tuple(dims) + tuple(jobs))]


def inner_plane():
    return own_bit("dp", 2) != own_bit("dp", 4)


def across():
    at = lax.axis_index("dp")
    return {"dp": at + 2 * (1 - 2 * own_bit("dp", 2)) + 4 * (1 - 2 * own_bit("dp", 4))}


def team_rows_kernel(jobs, relays, layout, experts, rows_ref, gates_ref, pos_ref, *refs):
    count, lanes = len(jobs), len(relays)
    gives, pairs = refs[0:count], refs[count:count + lanes]
    refs = refs[count + lanes:]
    if lanes:
        other_ref, refs = refs[0], refs[1:]
    all_ref, table_ref = refs[0:2]
    takes, far = refs[2:2 + count], refs[2 + count:2 + count + lanes]
    picked_ref, pick, held, built = refs[2 + count + lanes:6 + count + lanes]
    own_sem, send_sem, recv_sem, job_sem, relay_sem, held_sem, built_sem = refs[6 + count + lanes:]
    partners = partners_of(TEAM, jobs)
    if lanes:
        partners += [flipped("dp", 4), across()]
    barrier_with(partners)
    own = [
        pltpu.make_async_copy(rows_ref, all_ref.at[0:1, 0:1, 0:1], own_sem.at[0]),
        pltpu.make_async_copy(gates_ref, table_ref.at[0:1, 0:1, 0:1], own_sem.at[1]),
    ]
    for copy in own:
        copy.start()

    def leg(j, n):
        src = (pairs[j].at[0], pairs[j].at[1], other_ref.at[relays[j]])[n]
        return pltpu.make_async_remote_copy(
            src_ref=src, dst_ref=far[j].at[min(n, 1)], send_sem=relay_sem.at[n, j],
            recv_sem=relay_sem.at[3 + min(n, 1), j], device_id=across() if n == 2 else flipped("dp", 4),
            device_id_type=pl.DeviceIdType.MESH,
        )

    for copy in own:
        copy.wait()
    parts = 4
    width = all_ref.shape[4] // parts
    flows = [(all_ref, (slice(None), pl.ds(c * width, width))) for c in range(parts)]
    flows.append((table_ref, (slice(None), slice(None))))

    def hop(step, f):
        ref, tail = flows[f]
        index = [pl.ds(0, 2) if d < step else pl.ds(0, 1) for d in range(3)]
        src = ref.at[tuple(index) + tail]
        index[step] = pl.ds(1, 1)
        return pltpu.make_async_remote_copy(
            src_ref=src, dst_ref=ref.at[tuple(index) + tail], send_sem=send_sem.at[step, f],
            recv_sem=recv_sem.at[step, f], device_id=flipped(*TEAM[step]), device_id_type=pl.DeviceIdType.MESH,
        )

    order = [parts] + list(range(parts))
    for f in order:
        hop(0, f).start()
    background = job_copies(jobs, gives, takes, job_sem)
    for copy in background:
        copy.start()
    if lanes:

        @pl.when(inner_plane())
        def _():
            for n in (2, 0, 1):
                for j in range(lanes):
                    leg(j, n).start()

        @pl.when(jnp.logical_not(inner_plane()))
        def _():
            for j in range(lanes):
                leg(j, 0).start()

    tokens = rows_ref.shape[3]
    slots = pick.shape[0] // experts
    middle = all_ref.shape[4] // 2
    slot_id = lax.broadcasted_iota(jnp.int32, (slots, tokens), 0)
    turns = [(core, source) for core in range(2) for source in range(4)]

    def fetches(turn):
        core, source = turns[turn]
        copies, at = [], 0
        for n, job in enumerate(layout[source]):
            ref = (takes if core else gives)[job]
            size = ref.shape[0]
            copies.append(pltpu.make_async_copy(ref, held.at[turn % 2, pl.ds(at, size), :], held_sem.at[turn % 2, n]))
            at += size
        return copies

    def store(turn):
        core, source = turns[turn]
        return pltpu.make_async_copy(built.at[turn % 2], picked_ref.at[2 * source + core], built_sem.at[turn % 2])

    def begin(turn):
        if turns[turn][0]:
            for job in layout[turns[turn][1]]:
                background[job].wait()
        for copy in fetches(turn):
            copy.start()

    def gather(turn):
        core, source = turns[turn]
        slot = turn % 2
        for copy in fetches(turn):
            copy.wait()
        if turn + 1 < len(turns):
            begin(turn + 1)
        for k in range(experts):
            hit = slot_id == pos_ref[2 * source + core, k:k + 1, :]
            pick[k * slots:(k + 1) * slots, :] = jnp.where(hit, 1.0, 0.0).astype(BF)
        if turn >= 2:
            store(turn - 2).wait()
        built[slot, :, 0:middle] = dot_nn(pick[...], held[slot, :, 0:middle]).astype(BF)
        built[slot, :, middle:] = dot_nn(pick[...], held[slot, :, middle:]).astype(BF)
        store(turn).start()

    begin(0)
    for step in range(1, 3):
        for n, f in enumerate(order):
            hop(step - 1, f).wait_recv()
            hop(step, f).start()
            if n:
                gather(4 * (step - 1) + n - 1)
    for f in order:
        hop(2, f).wait_recv()
    store(6).wait()
    store(7).wait()
    for step in range(3):
        for f in order:
            hop(step, f).wait_send()
    used = [job for jobs_of in layout for job in jobs_of]
    for job, copy in enumerate(background):
        if job not in used:
            copy.wait()
    for j in range(lanes):
        leg(j, 0).wait()
        leg(j, 1).wait_recv()
    if lanes:

        @pl.when(inner_plane())
        def _():
            for j in range(lanes):
                leg(j, 1).wait_send()
                leg(j, 2).wait_send()


def team_rows(rows, gates, positions, layout, experts, slots, jobs=(), gives=(), relays=(), pairs=(), other=None):
    tokens, width = rows.shape
    size = experts * slots
    table = gates.shape
    anywhere = pl.BlockSpec(memory_space=pl.ANY)
    extra = [] if other is None else [other]
    full, tables, *takes = pl.pallas_call(
        functools.partial(team_rows_kernel, tuple(jobs), tuple(relays), layout, experts),
        in_specs=[pl.BlockSpec(memory_space=pltpu.VMEM)] * 3 + [anywhere] * (len(jobs) + len(pairs) + len(extra)),
        out_specs=[anywhere] * (3 + len(jobs) + len(pairs)),
        out_shape=[
            jax.ShapeDtypeStruct((2, 2, 2, tokens, width), BF),
            jax.ShapeDtypeStruct((2, 2, 2) + table, F32),
        ] + [jax.ShapeDtypeStruct(give.shape, give.dtype) for give in list(gives) + list(pairs)]
        + [jax.ShapeDtypeStruct((8, size, width), BF)],
        scratch_shapes=[
            pltpu.VMEM((size, tokens), BF),
            pltpu.VMEM((2, tokens, width), BF),
            pltpu.VMEM((2, size, width), BF),
            pltpu.SemaphoreType.DMA((2,)),
            pltpu.SemaphoreType.DMA((3, 5)),
            pltpu.SemaphoreType.DMA((3, 5)),
            pltpu.SemaphoreType.DMA((2, max(1, len(jobs)))),
            pltpu.SemaphoreType.DMA((5, max(1, len(relays)))),
            pltpu.SemaphoreType.DMA((2, 2)),
            pltpu.SemaphoreType.DMA((2,)),
        ],
        compiler_params=pltpu.CompilerParams(collective_id=2, has_side_effects=True, vmem_limit_bytes=60 * 2**20),
        name="team_rows",
    )(rows.reshape(1, 1, 1, tokens, width), gates.reshape((1, 1, 1) + table), positions, *gives, *pairs, *extra)
    *takes, picked = takes
    return full.reshape(8, tokens, width), tables.reshape((8,) + table), takes, picked


def add_into(acc, at, other):
    acc[at] = (acc[at].astype(F32) + other.astype(F32)).astype(BF)


def return_kernel(count, slots, jobs, relays, pos_ref, *refs):
    x_refs, y_refs, dg_refs = refs[0:count], refs[count:2 * count], refs[2 * count:3 * count]
    refs = refs[3 * count:]
    gives, takes = refs[0:len(jobs)], refs[len(jobs) + 4:2 * len(jobs) + 4]
    out_ref, gate_ref, kept_ref, sent_ref = refs[len(jobs):len(jobs) + 4]
    (acc, core_in, even_out, row_in, pair_in, last_in, ys, pick, table, table_core, table_row, table_pair,
     load_sem, send_sem, recv_sem, job_sem, store_sem, free_sem) = refs[2 * len(jobs) + 4:]
    tokens, width = out_ref.shape
    half = width // 2
    barrier_with(partners_of(TEAM, jobs))
    background = job_copies(jobs, gives, takes, job_sem)
    for copy in background[relays:]:
        copy.start()
    if relays:

        @pl.when(jnp.logical_not(inner_plane()))
        def _():
            for copy in background[:relays]:
                copy.start()

    first = (lax.axis_index("expert") * 2 + own_bit("dp", 2)) * count
    slot_id = lax.broadcasted_iota(jnp.int32, (slots, tokens), 0)

    def remote(src, dst, n, dim):
        return pltpu.make_async_remote_copy(
            src_ref=src, dst_ref=dst, send_sem=send_sem.at[n], recv_sem=recv_sem.at[n],
            device_id=flipped(*TEAM[dim]), device_id_type=pl.DeviceIdType.MESH,
        )

    def loads(parts, r, slot):
        return [
            pltpu.make_async_copy(
                parts[k].at[pl.ds(pl.multiple_of(r * slots, 16), slots), :],
                ys.at[slot, pl.ds(k * slots, slots), :], load_sem.at[slot, k],
            )
            for k in range(count)
        ]

    table[...] = jnp.zeros_like(table)

    def build(parts, step, r, following, dst, at, with_gates):
        slot = lax.rem(step, 2)
        for copy in loads(parts, r, slot):
            copy.wait()

        @pl.when(step < 7)
        def _():
            for copy in loads(parts, following, 1 - slot):
                copy.start()

        for k in range(count):
            hit = slot_id == pos_ref[r, k:k + 1, :]
            pick[k * slots:(k + 1) * slots, :] = jnp.where(hit, 1.0, 0.0).astype(BF)
            if with_gates:
                pulled = dg_refs[k][pl.ds(pl.multiple_of(r * slots, 16), slots), 0:1]
                table[r, pl.ds(first + k, 1), :] = jnp.sum(jnp.where(hit, pulled, 0.0), 0, keepdims=True)
        dst[at, :, 0:half] = dot_tn(pick[...], ys[slot, :, 0:half]).astype(BF)
        dst[at, :, half:] = dot_tn(pick[...], ys[slot, :, half:]).astype(BF)

    def core_copy(i, base):
        return remote(acc.at[2 * i + 1], core_in.at[i], base + i, 2)

    def build_odd(parts, base, with_gates):
        def odd(i, carry):
            r = 2 * i + 1
            build(parts, i, r, jnp.where(i < 3, r + 2, 0), acc, r, with_gates)
            core_copy(i, base).start()
            return carry

        lax.fori_loop(0, 4, odd, 0)

    for copy in loads(x_refs, 1, 0):
        copy.start()
    build_odd(x_refs, 0, True)
    tables = [remote(table.at[2 * i + 1], table_core.at[i], 4 + i, 2) for i in range(4)]
    for copy in tables:
        copy.start()

    def even(i, carry):
        build(x_refs, i + 4, 2 * i, 2 * i + 2, acc, 2 * i, True)
        return carry

    lax.fori_loop(0, 4, even, 0)
    if relays:

        @pl.when(inner_plane())
        def _():
            for copy in background[:relays]:
                copy.start()

    for copy in loads(y_refs, 1, 0):
        copy.start()

    def settle(i):
        core_copy(i, 0).wait()
        add_into(acc, 2 * i, core_in[i])

    left, right = slice(0, half), slice(half, width)
    settle(3)
    a = [remote(acc.at[6, :, pl.ds(0, half)], row_in.at[1], 8, 1), remote(acc.at[6, :, pl.ds(half, half)], pair_in.at[1], 9, 0)]
    for copy in a:
        copy.start()
    settle(1)
    a.append(remote(acc.at[2, :, pl.ds(0, half)], row_in.at[0], 10, 1))
    a[-1].start()
    settle(2)
    a.append(remote(acc.at[4, :, pl.ds(half, half)], pair_in.at[0], 11, 0))
    a[-1].start()
    settle(0)
    pl.semaphore_signal(free_sem, inc=1, device_id=flipped(*TEAM[2]), device_id_type=pl.DeviceIdType.MESH)
    for i, copy in enumerate(tables):
        copy.wait()
        table[2 * i] = table[2 * i] + table_core[i]
    t = [remote(table.at[2], table_row.at[0], 12, 1), remote(table.at[6], table_row.at[1], 13, 1)]
    for copy in t:
        copy.start()
    pl.semaphore_wait(free_sem, 1)
    build_odd(y_refs, 17, False)
    a[0].wait()
    add_into(acc, (4, slice(None), left), row_in[1])
    b = [remote(acc.at[4, :, pl.ds(0, half)], last_in.at[0], 14, 0)]
    b[0].start()
    a[1].wait()
    add_into(acc, (2, slice(None), right), pair_in[1])
    b.append(remote(acc.at[2, :, pl.ds(half, half)], last_in.at[1], 15, 1))
    b[1].start()
    for i, copy in enumerate(t):
        copy.wait()
        table[4 * i] = table[4 * i] + table_row[i]
    t = remote(table.at[4], table_pair, 16, 0)
    t.start()

    def even_y(i, carry):
        build(y_refs, i + 4, 2 * i, 2 * i + 2, even_out, i, False)
        return carry

    lax.fori_loop(0, 4, even_y, 0)
    stores = []
    for i in range(4):
        core_copy(i, 17).wait()
        add_into(even_out, i, core_in[i])
        stores.append(
            pltpu.make_async_copy(even_out.at[i], (sent_ref if i % 2 else kept_ref).at[i // 2], store_sem.at[i])
        )
        stores[-1].start()
    a[2].wait()
    add_into(acc, (0, slice(None), left), row_in[0])
    a[3].wait()
    add_into(acc, (0, slice(None), right), pair_in[0])
    b[0].wait()
    out_ref[:, left] = (acc[0, :, left].astype(F32) + last_in[0].astype(F32)).astype(BF)
    b[1].wait()
    out_ref[:, right] = (acc[0, :, right].astype(F32) + last_in[1].astype(F32)).astype(BF)
    t.wait()
    gate_ref[...] = table[0] + table_pair[...]
    for copy in stores:
        copy.wait()
    for copy in background:
        copy.wait()


def return_rows(positions, backs, results, gate_rows, experts, slots, jobs=(), gives=(), relays=0):
    sources, _, tokens = positions.shape
    count = len(results)
    width = results[0].shape[1]
    half = width // 2
    vmem, anywhere = pl.BlockSpec(memory_space=pltpu.VMEM), pl.BlockSpec(memory_space=pl.ANY)
    rows, gates, kept, sent, *takes = pl.pallas_call(
        functools.partial(return_kernel, count, slots, tuple(jobs), relays),
        in_specs=[vmem] + [anywhere] * (2 * count) + [vmem] * count + [anywhere] * len(jobs),
        out_specs=[vmem, vmem] + [anywhere] * (2 + len(jobs)),
        out_shape=[jax.ShapeDtypeStruct((tokens, width), BF), jax.ShapeDtypeStruct((experts, tokens), F32)]
        + [jax.ShapeDtypeStruct((2, tokens, width), BF)] * 2
        + [jax.ShapeDtypeStruct(give.shape, give.dtype) for give in gives],
        scratch_shapes=[
            pltpu.VMEM((8, tokens, width), BF),
            pltpu.VMEM((4, tokens, width), BF),
            pltpu.VMEM((4, tokens, width), BF),
            pltpu.VMEM((2, tokens, half), BF),
            pltpu.VMEM((2, tokens, half), BF),
            pltpu.VMEM((2, tokens, half), BF),
            pltpu.VMEM((2, count * slots, width), BF),
            pltpu.VMEM((count * slots, tokens), BF),
            pltpu.VMEM((8, experts, tokens), F32),
            pltpu.VMEM((4, experts, tokens), F32),
            pltpu.VMEM((2, experts, tokens), F32),
            pltpu.VMEM((experts, tokens), F32),
            pltpu.SemaphoreType.DMA((2, count)),
            pltpu.SemaphoreType.DMA((21,)),
            pltpu.SemaphoreType.DMA((21,)),
            pltpu.SemaphoreType.DMA((2, max(1, len(jobs)))),
            pltpu.SemaphoreType.DMA((4,)),
            pltpu.SemaphoreType.REGULAR,
        ],
        compiler_params=pltpu.CompilerParams(collective_id=3, has_side_effects=True, vmem_limit_bytes=63 * 2**20),
        name="return_rows",
    )(positions, *backs, *results, *gate_rows, *gives)
    return rows, gates, kept, sent, takes


class Group:
    def __init__(self, copies):
        self.copies = copies

    def wait(self):
        for copy in self.copies:
            copy.wait()


def scatter_kernel(dims, rotations, chunks, segments, sources, relays, *refs):
    last = len(dims) - 1
    grads, refs = refs[0:sources], refs[sources:]
    gives, takes = refs[0:relays], refs[relays + 1:2 * relays + 1]
    out_ref, refs = refs[relays], refs[2 * relays + 1:]
    acc, core_in = refs[0:2]
    inboxes = refs[2:2 + last]
    load_sem, send_sem, recv_sem, job_sem = refs[2 + last:]
    barrier_with([flipped(*dim) for dim in dims])
    background = job_copies(((("dp", 4), ("dp", 2)) * relays)[:relays], gives, takes, job_sem)

    def relay(outer):
        if relays:

            @pl.when(jnp.logical_not(inner_plane()) if outer else inner_plane())
            def _():
                background[0].start()

    bits = [own_bit(*dim) for dim in dims]
    every = tuple(pl.ds(0, 2) for _ in range(last))
    number = iter(range(send_sem.shape[0]))

    def remote(src, dst, dim):
        n = next(number)
        return pltpu.make_async_remote_copy(
            src_ref=src, dst_ref=dst, send_sem=send_sem.at[n], recv_sem=recv_sem.at[n],
            device_id=flipped(*dims[dim]), device_id_type=pl.DeviceIdType.MESH,
        )

    firsts, loads = [[] for _ in chunks], []
    for source, start, at, width, chunk in segments:
        src, dst = (slice(None), pl.ds(start, width)), (slice(None), pl.ds(at, width))
        copy = remote(
            grads[source].at[every + (pl.ds(1 - bits[last], 1),) + src], core_in.at[every + (pl.ds(0, 1),) + dst], last
        )
        copy.start()
        firsts[chunk].append(copy)
        load = pltpu.make_async_copy(
            grads[source].at[every + (pl.ds(bits[last], 1),) + src], acc.at[every + (pl.ds(0, 1),) + dst],
            load_sem.at[len(loads)],
        )
        load.start()
        loads.append(load)
    for load in loads:
        load.wait()
    sends = [Group(copies) for copies in firsts]
    relay(True)
    for step in range(last + 1):
        for c, (start, width) in enumerate(chunks):
            cols = pl.ds(start, width)
            rest = rotations[c][:last - step]
            sends[c].wait()
            for n in range(2 ** len(rest)):
                spread = [(n >> (len(rest) - 1 - i)) & 1 for i in range(len(rest))]
                index = [bits[d] if d not in rest else spread[rest.index(d)] for d in range(last)]
                at = tuple(index) + (0, slice(None), cols)
                other = core_in[at] if step == 0 else inboxes[step - 1][n, :, cols]
                if step < last:
                    add_into(acc, at, other)
                else:
                    out_ref[:, cols] = (acc[at].astype(F32) + other.astype(F32)).astype(out_ref.dtype)
            if step < last:
                dim, spread_dims = rest[-1], rest[:-1]
                group = []
                for n in range(2 ** len(spread_dims)):
                    spread = [(n >> (len(spread_dims) - 1 - i)) & 1 for i in range(len(spread_dims))]
                    index = [
                        1 - bits[d] if d == dim else (spread[spread_dims.index(d)] if d in spread_dims else bits[d])
                        for d in range(last)
                    ]
                    copy = remote(acc.at[tuple(index) + (0, slice(None), cols)], inboxes[step].at[n, :, cols], dim)
                    copy.start()
                    group.append(copy)
                sends[c] = Group(group)
        if step == 0:
            relay(False)
        if step == last - 1:
            for copy in background[1:]:
                copy.start()
    for copy in background:
        copy.wait()


def cube_scatter(dims, rotations, chunks, segments, grads, dtype, collective, name, gives=()):
    last = len(dims) - 1
    rows = grads[0].shape[0] // 2 ** len(dims)
    width = sum(chunk[1] for chunk in chunks)
    copies = len(segments) + len(chunks) * (2 ** last - 1)
    out, *takes = pl.pallas_call(
        functools.partial(scatter_kernel, dims, rotations, chunks, segments, len(grads), len(gives)),
        in_specs=[pl.BlockSpec(memory_space=pl.ANY)] * (len(grads) + len(gives)),
        out_specs=[pl.BlockSpec(memory_space=pltpu.VMEM)] + [pl.BlockSpec(memory_space=pl.ANY)] * len(gives),
        out_shape=[jax.ShapeDtypeStruct((rows, width), dtype)]
        + [jax.ShapeDtypeStruct(give.shape, give.dtype) for give in gives],
        scratch_shapes=[pltpu.VMEM((2,) * last + (1, rows, width), BF)] * 2
        + [pltpu.VMEM((2 ** n, rows, width), BF) for n in reversed(range(last))]
        + [
            pltpu.SemaphoreType.DMA((len(segments),)),
            pltpu.SemaphoreType.DMA((copies,)),
            pltpu.SemaphoreType.DMA((copies,)),
            pltpu.SemaphoreType.DMA((2, max(1, len(gives)))),
        ],
        compiler_params=pltpu.CompilerParams(
            collective_id=collective, has_side_effects=True, vmem_limit_bytes=60 * 2**20
        ),
        name=name,
    )(*[g.reshape((2,) * len(dims) + (rows, g.shape[1])) for g in grads], *gives)
    return out, takes


def dense_segments(wide):
    cut = wide // 256 * 128 + 128
    return ((0, 0, cut, 0), (0, cut, wide - cut, 1), (1, 0, 128, 1), (2, 0, 1536, 2), (3, 0, 128, 2))


def scatter_all(grads, gives):
    segments, chunks, at = [], [0, 0, 0], 0
    for source, start, width, chunk in dense_segments(grads[0].shape[1]):
        segments.append((source, start, at, width, chunk))
        chunks[chunk] += width
        at += width
    starts = (0, chunks[0], chunks[0] + chunks[1])
    return cube_scatter(
        CUBE, ROTATIONS, tuple(zip(starts, chunks)), tuple(segments), grads, F32, 4, "scatter_all", gives
    )


def group_back(grad_key, grad_value):
    width = grad_key.shape[1]
    segments = ((0, 0, 0, width, 0), (1, 0, width, width, 1))
    return cube_scatter(
        GROUP, ((0, 1), (1, 0)), ((0, width), (width, width)), segments, [grad_key, grad_value], BF, 6, "group_back"
    )[0]


def group_rows_kernel(rows_ref, key_ref, value_ref, own_sem, send_sem, recv_sem):
    barrier_with([flipped(*dim) for dim in GROUP])
    bits = [own_bit(*dim) for dim in GROUP]
    width = key_ref.shape[4]
    here = tuple(pl.ds(bit, 1) for bit in bits)
    own = [
        pltpu.make_async_copy(rows_ref.at[:, :, :, :, pl.ds(i * width, width)], ref.at[here], own_sem.at[i])
        for i, ref in enumerate((key_ref, value_ref))
    ]
    for copy in own:
        copy.start()
    for copy in own:
        copy.wait()
    copies = []
    running = [None, None]
    for step in range(3):
        for f, (ref, order) in enumerate(((key_ref, (0, 1, 2)), (value_ref, (1, 0, 2)))):
            if running[f] is not None:
                running[f].wait_recv()
            at = tuple(pl.ds(0, 2) if d in order[:step] else pl.ds(bits[d], 1) for d in range(3))
            copy = pltpu.make_async_remote_copy(
                src_ref=ref.at[at], dst_ref=ref.at[at], send_sem=send_sem.at[step, f], recv_sem=recv_sem.at[step, f],
                device_id=flipped(*GROUP[order[step]]), device_id_type=pl.DeviceIdType.MESH,
            )
            copy.start()
            copies.append(copy)
            running[f] = copy
    for copy in running:
        copy.wait_recv()
    for copy in copies:
        copy.wait_send()


def group_rows(key_value):
    rows, width = key_value.shape
    anywhere = pl.BlockSpec(memory_space=pl.ANY)
    outs = pl.pallas_call(
        group_rows_kernel,
        in_specs=[pl.BlockSpec(memory_space=pltpu.VMEM)],
        out_specs=[anywhere] * 2,
        out_shape=[jax.ShapeDtypeStruct((2, 2, 2, rows, width // 2), BF)] * 2,
        scratch_shapes=[
            pltpu.SemaphoreType.DMA((2,)),
            pltpu.SemaphoreType.DMA((3, 2)),
            pltpu.SemaphoreType.DMA((3, 2)),
        ],
        compiler_params=pltpu.CompilerParams(collective_id=5, has_side_effects=True),
        name="group_rows",
    )(key_value.reshape(1, 1, 1, rows, width))
    return [out.reshape(8 * rows, width // 2) for out in outs]


D = 1536
EPSILON = 1e-06
EVERYWHERE = ("dp", "expert")


def exchange(value, axis, mask):
    return lax.ppermute(value, axis, [(i, i ^ mask) for i in range(lax.axis_size(axis))])


def tie(first, *others):
    return lax.optimization_barrier((first, *others))[0]


def rms_scale(values):
    return lax.rsqrt(jnp.mean(values * values, axis=-1, keepdims=True) + EPSILON)


def product(left, right):
    return jnp.dot(left, right, preferred_element_type=F32)


def contract_rows(left, right):
    return jnp.einsum("ta,tb->ab", left, right, preferred_element_type=F32)


def times_transposed(left, right):
    return jnp.einsum("ta,ba->tb", left, right, preferred_element_type=F32)


def added(left, right):
    return (left.astype(F32) + right.astype(F32)).astype(BF)


def team_gather(value, order):
    pieces = {0: value}
    for axis, mask, bit in order:
        pieces.update({r | bit: exchange(v, axis, mask) for r, v in list(pieces.items())})
    return jnp.stack([pieces[r] for r in sorted(pieces)])


TEAM_BITS = (("dp", 2, 4), ("expert", 2, 2), ("expert", 1, 1))


def local(tokens, attn_gain, w_query, w_key, w_value, w_out, w_router, ffn_gain, w_gate, w_up, w_down, routes, cotangent):
    dp, expert_at = lax.axis_index("dp"), lax.axis_index("expert")
    shards, owners = lax.axis_size("dp"), lax.axis_size("expert")
    cube = shards == 8 and owners == 4
    turn = (dp >> 1) & 1
    tok_rows = tokens.shape[0]
    per_owner, piece, hidden = w_gate.shape
    count = per_owner // 2
    expert_count = per_owner * owners
    top_count = routes.shape[1]
    kvw = w_key.shape[1]
    capacity = 8 * ((17 * top_count * tok_rows + 128 * expert_count - 1) // (128 * expert_count))
    slots = SLOTS_ALIGN * (-(-capacity // SLOTS_ALIGN))
    dp_index = dp.astype(jnp.int32).reshape(1)
    wide = D + 2 * kvw

    stacked = jnp.stack([w_gate, w_up, w_down.transpose(0, 2, 1)], 1)
    own = lax.dynamic_slice_in_dim(stacked, turn * count, count, 0)
    other = lax.dynamic_slice_in_dim(stacked, (1 - turn) * count, count, 0)
    gains = jnp.pad(jnp.stack([attn_gain, ffn_gain], 1), ((0, 0), (0, 126)))
    dense = [
        jnp.concatenate([w_query, w_key, w_value], 1), gains, w_out,
        jnp.pad(w_router, ((0, 0), (0, 128 - expert_count))),
    ]
    ahead = 2
    if cube:
        dense_full, taken, routes_t = gather_all(dense, dense_segments(wide), other[:ahead], routes.T)
    else:
        routes_t = team_gather(routes.T, TEAM_BITS)
        dense_full = [lax.all_gather(shard, EVERYWHERE, axis=0, tiled=True) for shard in dense]
        taken = exchange(other[:ahead], "dp", 2)
    qkv_full, gains_full, out_full, router_full = dense_full
    gains_full = gains_full.astype(F32).T
    gain_first, gain_second = gains_full[0], gains_full[1]

    relay_bits = [1 << b for b in range(2, shards.bit_length() - 1)]
    pairs = [jnp.stack([own[k], taken[k]]) for k in range(ahead)]

    def crossed(relayed):
        return [w for v in relayed for w in (v, exchange(v, "dp", 1))]

    def relays(pair):
        pieces = [pair]
        for bit in relay_bits:
            pieces += [exchange(v, "dp", bit) for v in pieces]
        return pieces

    first_expert = expert_at * per_owner + turn * count
    local_ids = first_expert + jnp.arange(count, dtype=jnp.int32)
    hits = jnp.any(routes_t[:, None] == local_ids[None, :, None, None], axis=2)
    row_id = lax.broadcasted_iota(jnp.int32, (tok_rows, tok_rows), 0)
    col_id = lax.broadcasted_iota(jnp.int32, (tok_rows, tok_rows), 1)
    before = jnp.where(row_id < col_id, 1.0, 0.0).astype(BF)
    ranks = product(hits.astype(BF).reshape(-1, tok_rows), before).reshape(hits.shape)
    positions = jnp.where(hits, ranks.astype(jnp.int32), -1)
    positions = jnp.pad(positions, ((0, 0), (0, 8 - count), (0, 0)), constant_values=-1)

    inputs = tokens.astype(F32)
    scale_one = rms_scale(inputs)
    normed_one = inputs * scale_one
    hidden_one = (normed_one * gain_first).astype(BF)
    qkv = product(hidden_one, qkv_full).astype(BF)
    query, key_value = qkv[:, :D], qkv[:, D:]
    place = ((dp & 1) * owners + expert_at).astype(jnp.int32).reshape(1)
    prompt_key, prompt_value = group_rows(key_value[:P_DEV])
    own_key, own_value = key_value[P_DEV:, :kvw], key_value[P_DEV:, kvw:]
    early = tie(cotangent, qkv_full)
    middle = tok_rows // 2
    paired = exchange(early, "dp", 2)
    upper = exchange(early[:middle], "expert", 2)
    query, early, paired, prompt_key, pairs[:2], late = lax.optimization_barrier(
        (query, early, paired, prompt_key, pairs[:2], other[ahead:])
    )
    parts = [early, paired, upper, None, exchange(paired, "expert", 2)]
    layout = ((0,), (2, 3), (1,), (4,))
    taken_late = exchange(late, "dp", 2)
    pairs += [jnp.stack([own[k], taken_late[k - ahead]]) for k in range(ahead, count)]
    crossings = [exchange(pairs[k], "dp", 1) for k in range(2)]
    mixed, levels = attend(place, query, prompt_key, prompt_value, own_key, own_value)
    mixed, parts[4] = lax.optimization_barrier((mixed, parts[4]))
    parts[3] = exchange(tie(early[middle:], parts[4]), "expert", 2)
    second = inputs + product(mixed, out_full)
    scale_two = rms_scale(second)
    normed_two = second * scale_two
    hidden_two = (normed_two * gain_second).astype(BF)
    logits = product(hidden_two, router_full)[:, :expert_count]
    expert_ids = jnp.arange(expert_count, dtype=jnp.int32)
    chosen = jnp.any(routes[:, :, None] == expert_ids, axis=1)
    peak = jnp.max(jnp.where(chosen, logits, NEGATIVE), axis=-1, keepdims=True)
    raised = jnp.where(chosen, jnp.exp(jnp.where(chosen, logits - peak, 0.0)), 0.0)
    gates = raised / jnp.sum(raised, axis=-1, keepdims=True)

    weights = [None] * count
    near = exchange(tie(pairs[0], taken_late), "dp", 4) if cube else None
    sent_rows, parts, crossings = lax.optimization_barrier((hidden_two, parts, crossings))
    core_jobs = (("expert", 1),) * 5
    if cube:
        rows, gates_t, takes, grad_slots = team_rows(
            sent_rows, gates.T, positions, layout, count, slots,
            core_jobs + (("dp", 1),) * 3, (*parts, *pairs[2:]), (1, 2), pairs[1:3], other,
        )
        crossings = crossings + takes[5:8]
        relayed_pairs = [near] + takes[8:10]
        for k in range(3, count):
            relayed_pairs.append(exchange(tie(pairs[k], rows), "dp", 4))
        for k in range(count):
            weights[k] = [pairs[k], crossings[k], relayed_pairs[k]]
    else:
        rows, gates_t, _, grad_slots = team_rows(
            sent_rows, gates.T, positions, layout, count, slots, core_jobs, parts
        )
        for k in range(count):
            weights[k] = crossed(relays(tie(pairs[k], rows)))
    gates_t = lax.dynamic_slice_in_dim(gates_t, first_expert, count, 1)
    gates_t = jnp.pad(gates_t, ((0, 0), (0, 8 - count), (0, 0)))
    row_slots, gate_slots = gather_rows(positions, gates_t, rows, count, slots)

    results, backs, gate_rows, sums = [], [], [], []
    expert_index = dp_index
    for k in range(count):
        if cube:
            relayed_pair = tie(weights[k][2], rows) if k < 3 else tie(weights[k][2], gate_rows[k - 2], weights[k - 1][3])
            weights[k].append(exchange(relayed_pair, "dp", 1))
        y, dx, dg, keep, send = run_expert(k, expert_index, row_slots, grad_slots, gate_slots, weights[k], slots)
        results.append(y)
        backs.append(dx)
        gate_rows.append(dg)
        sums.append((keep, send))
        expert_index = tie(dp_index, dg)

    before_return = added(sums[0][0], exchange(tie(sums[0][1], gate_rows[1], weights[4]), "dp", 1))
    jobs, gives, relays_in = (("dp", 1),) * 2, (sums[1][1], sums[2][1]), 0
    if cube:
        jobs, gives, relays_in = (("dp", 4),) + jobs, (before_return[2:],) + gives, 1
    routed_back, gate_grad, out_keep, out_sent, takes = return_rows(
        positions, backs, results, gate_rows, expert_count, slots, jobs, gives, relays_in
    )
    halved = [before_return, added(sums[1][0], takes[-2]), added(sums[2][0], takes[-1])]
    crossed_back = [exchange(tie(sums[k][1], routed_back), "dp", 1) for k in range(3, count)]
    relay_bits = relay_bits[::-1]

    def sent_on(keep):
        return exchange(keep[keep.shape[0] // 2:], "dp", relay_bits[0])

    def settled(keep, came):
        keep = added(keep[:keep.shape[0] // 2], came)
        for bit in relay_bits[1:]:
            middle = keep.shape[0] // 2
            keep = added(keep[:middle], exchange(keep[middle:], "dp", bit))
        return keep

    relay_came = [takes[0] if cube else sent_on(before_return)] + [sent_on(keep) for keep in halved[1:]]
    gate_grad = gate_grad.T
    routed_back = routed_back.astype(F32)

    grad_output = cotangent.astype(F32)
    picked = jnp.where(chosen, gate_grad, 0.0)
    grad_logits = (gates * (picked - jnp.sum(gates * picked, axis=-1, keepdims=True))).astype(BF)
    wide_logits = jnp.pad(grad_logits, ((0, 0), (0, 128 - expert_count)))
    grad_hidden_two = times_transposed(wide_logits, router_full) + routed_back
    grad_normed_two = grad_hidden_two * gain_second
    grad_second = grad_output + scale_two * (
        grad_normed_two - normed_two * jnp.mean(grad_normed_two * normed_two, axis=-1, keepdims=True)
    )
    grad_branch = grad_second.astype(BF)
    ones = jnp.ones((tok_rows, 128), BF)
    lane = lax.broadcasted_iota(jnp.int32, (tok_rows, 128), 1)
    small = contract_rows(hidden_two, wide_logits) + contract_rows(
        (grad_hidden_two * normed_two).astype(BF), jnp.where(lane == expert_count, ones, jnp.zeros_like(ones))
    )
    out_grad = contract_rows(mixed, grad_branch).astype(BF)
    grad_mixed = times_transposed(grad_branch, out_full).astype(BF)

    grad_mixed, halved = lax.optimization_barrier((grad_mixed, halved))
    row_came = exchange(out_sent, "expert", 2)
    grad_query, dkp, dvp, dko, dvo = attend_back(
        place, query, prompt_key, prompt_value, own_key, own_value, mixed, grad_mixed, levels
    )
    halved, relay_came, crossed_back, grad_query, row_came, dkp = lax.optimization_barrier(
        (halved, relay_came, crossed_back, grad_query, row_came, dkp)
    )
    halved += [added(sums[k][0], crossed_back[k - 3]) for k in range(3, count)]
    relay_came += [sent_on(halved[3])]
    total = tie(added(out_keep, row_came), halved[3])
    pair_came = exchange(total[1], "dp", 2)
    grad_prompt = group_back(dkp, dvp)
    grad_qkv = jnp.concatenate([
        grad_query, jnp.concatenate([grad_prompt, jnp.concatenate([dko, dvo], 1)], 0)
    ], 1)
    grad_hidden_one = times_transposed(grad_qkv, qkv_full)
    weight_rows, grad_hidden_one, relay_came[3], total = lax.optimization_barrier(
        (grad_qkv, grad_hidden_one, relay_came[3], total)
    )
    relayed = [settled(halved[k], relay_came[k]) for k in range(3)]
    passing = jnp.stack([keep[1] for keep in relayed])
    dense_grads = [
        contract_rows(hidden_one, weight_rows).astype(BF),
        contract_rows((grad_hidden_one * normed_one).astype(BF), ones).astype(BF),
        out_grad, small.astype(BF),
    ]
    if cube:
        share, takes = scatter_all(dense_grads, (halved[4][2:], passing))
        relay_came.append(takes[0])
        theirs = takes[1]
    else:
        share = lax.psum_scatter(
            jnp.concatenate(dense_grads, 1), EVERYWHERE, scatter_dimension=0, tiled=True
        ).astype(F32)
        relay_came.append(sent_on(halved[4]))
        theirs = exchange(passing, "dp", 2)
    grad_normed_one = grad_hidden_one * gain_first
    grad_input = grad_second + scale_one * (
        grad_normed_one - normed_one * jnp.mean(grad_normed_one * normed_one, axis=-1, keepdims=True)
    )

    share, halved, relay_came, total, pair_came = lax.optimization_barrier(
        (share, halved, relay_came, total, pair_came)
    )
    output = (second + added(total[0], pair_came).astype(F32)).astype(BF)
    first_share, second_share = share[:, :wide + 128], share[:, wide + 128:]
    relayed += [settled(halved[k], relay_came[k]) for k in range(3, count)]
    theirs = jnp.concatenate([theirs, exchange(jnp.stack([keep[1] for keep in relayed[3:]]), "dp", 2)])
    mine = jnp.stack([keep[0] for keep in relayed])
    lower = jnp.where(turn == 0, mine, theirs)
    upper = jnp.where(turn == 0, theirs, mine)
    expert_grads = jnp.concatenate([lower, upper]).astype(F32)
    return (
        output,
        grad_input.astype(BF),
        first_share[:, wide],
        first_share[:, :D],
        first_share[:, D:D + kvw],
        first_share[:, D + kvw:wide],
        second_share[:, :D].astype(F32),
        second_share[:, D:D + expert_count].astype(F32),
        second_share[:, D + expert_count].astype(F32),
        expert_grads[:, 0],
        expert_grads[:, 1],
        expert_grads[:, 2].transpose(0, 2, 1),
    )


def solution(mesh):
    rows, line = P(("dp", "expert"), None), P(("dp", "expert"))
    gate, down = P("expert", "dp", None), P("expert", None, "dp")
    return jax.shard_map(
        local,
        mesh=mesh,
        in_specs=(rows, line, rows, rows, rows, rows, rows, line, gate, gate, down, rows, rows),
        out_specs=(rows, rows, line, rows, rows, rows, rows, rows, line, gate, gate, down),
        check_vma=False,
    )
```

```python
import functools
import jax
import jax.numpy as jnp
from jax import lax
from jax.sharding import PartitionSpec as P
from jax.experimental import pallas as pl
from jax.experimental.pallas import tpu as pltpu

HD = 64
P_DEV = 128
NEGATIVE = -1e30
F32 = jnp.float32
BF = jnp.bfloat16


def dot_nt(a, b):
    return lax.dot_general(a, b, (((1,), (1,)), ((), ())), preferred_element_type=F32)


def dot_nn(a, b):
    return lax.dot_general(a, b, (((1,), (0,)), ((), ())), preferred_element_type=F32)


def dot_tn(a, b):
    return lax.dot_general(a, b, (((0,), (0,)), ((), ())), preferred_element_type=F32)


def halves(pair):
    lane = lax.broadcasted_iota(jnp.int32, pair.shape, 1)
    zero = jnp.zeros_like(pair)
    return jnp.where(lane < HD, pair, zero), jnp.where(lane < HD, zero, pair)


def placed_halves(pair_f32):
    low0, high1 = halves(pair_f32)
    high0 = pltpu.roll(low0, HD, 1)
    low1 = pltpu.roll(high1, HD, 1)
    return ((low0.astype(BF), high0.astype(BF)), (low1.astype(BF), high1.astype(BF)))


def attend_kernel(place_ref, q_ref, kp_ref, vp_ref, ko_ref, vo_ref, o_ref, lse_ref, kpad, vpad, s_scr, p_scr):
    rows = q_ref.shape[0]
    prompt = kp_ref.shape[0]
    cont = ko_ref.shape[0]
    place = place_ref[0]
    for src, dst in ((kp_ref, kpad), (vp_ref, vpad)):
        for head, pair in enumerate(placed_halves(src[...].astype(F32))):
            for half in range(2):
                dst[head, half, 0:prompt, :] = pair[half]
    for src, dst in ((ko_ref, kpad), (vo_ref, vpad)):
        for head, pair in enumerate(placed_halves(src[...].astype(F32))):
            for half in range(2):
                dst[head, half, prompt:prompt + cont, :] = pair[half]
    key_id = lax.broadcasted_iota(jnp.int32, (prompt, P_DEV), 0)
    row_id = lax.broadcasted_iota(jnp.int32, (prompt, P_DEV), 1)
    seen_prompt = key_id <= place * P_DEV + row_id
    diag = lax.broadcasted_iota(jnp.int32, (P_DEV, P_DEV), 0) <= lax.broadcasted_iota(jnp.int32, (P_DEV, P_DEV), 1)
    blocks = cont // P_DEV
    stats = []
    for chunk in range(3):
        queries = (q_ref[:, chunk * 128:(chunk + 1) * 128].astype(F32) * HD ** (-0.5)).astype(BF)
        total = None
        for half in range(2):
            position = chunk * 2 + half
            head = position // 3
            keys = kpad.at[head, half]
            scores = dot_nt(keys[0:prompt, :], queries)
            first = jnp.where(seen_prompt, scores[:, 0:P_DEV], NEGATIVE)
            rest = scores[:, P_DEV:]
            s_scr[0:prompt, 0:P_DEV] = first
            s_scr[0:prompt, P_DEV:] = rest
            top = jnp.concatenate([jnp.max(first, 0, keepdims=True), jnp.max(rest, 0, keepdims=True)], 1)
            tops = [top[:, i * P_DEV:(i + 1) * P_DEV] for i in range(1 + blocks)]
            for block in range(blocks):
                start = (1 + block) * P_DEV
                at = prompt + block * P_DEV
                own = dot_nt(keys[at:at + P_DEV, :], queries[start:, :])
                edge = jnp.where(diag, own[:, 0:P_DEV], NEGATIVE)
                s_scr[at:at + P_DEV, start:start + P_DEV] = edge
                tops[1 + block] = jnp.maximum(tops[1 + block], jnp.max(edge, 0, keepdims=True))
                if block + 1 < blocks:
                    later = own[:, P_DEV:]
                    s_scr[at:at + P_DEV, start + P_DEV:] = later
                    best = jnp.max(later, 0, keepdims=True)
                    for i in range(block + 1, blocks):
                        at_i = (i - block - 1) * P_DEV
                        tops[1 + i] = jnp.maximum(tops[1 + i], best[:, at_i:at_i + P_DEV])
            top = jnp.concatenate(tops, 1)
            weights = jnp.exp(s_scr[0:prompt, :] - top)
            mass = jnp.sum(weights, 0, keepdims=True)
            masses = [mass[:, i * P_DEV:(i + 1) * P_DEV] for i in range(1 + blocks)]
            values = vpad.at[head, half]
            mixed = dot_tn(values[0:prompt, :], weights.astype(BF))
            for block in range(blocks):
                start = (1 + block) * P_DEV
                at = prompt + block * P_DEV
                part = jnp.exp(s_scr[at:at + P_DEV, start:] - top[:, start:])
                p_scr[block * P_DEV:(block + 1) * P_DEV, start:] = part.astype(BF)
                if block:
                    p_scr[block * P_DEV:(block + 1) * P_DEV, P_DEV:start] = jnp.zeros((P_DEV, block * P_DEV), BF)
                part_mass = jnp.sum(part, 0, keepdims=True)
                for i in range(block, blocks):
                    at_i = (i - block) * P_DEV
                    masses[1 + i] = masses[1 + i] + part_mass[:, at_i:at_i + P_DEV]
            own_mixed = dot_tn(values[prompt:prompt + cont, :], p_scr[:, P_DEV:])
            mass = jnp.concatenate(masses, 1)
            scale = 1.0 / mass
            mixed = jnp.concatenate([mixed[:, 0:P_DEV], mixed[:, P_DEV:] + own_mixed], 1) * scale
            total = mixed if total is None else total + mixed
            stats.append(top + jnp.log(mass))
        o_ref[:, chunk * 128:(chunk + 1) * 128] = jnp.transpose(total).astype(BF)
    lse_ref[0] = jnp.concatenate(stats + [jnp.zeros((2, rows), F32)], 0)


def attend(place, query, prompt_key, prompt_value, own_key, own_value):
    rows = query.shape[0]
    prompt = prompt_key.shape[0]
    cont = own_key.shape[0]
    pairs = prompt_key.shape[1] // 128
    col = lambda i: (0, i)
    return pl.pallas_call(
        attend_kernel,
        grid=(pairs,),
        in_specs=[
            pl.BlockSpec(memory_space=pltpu.SMEM),
            pl.BlockSpec((rows, 384), col),
            pl.BlockSpec((prompt, 128), col),
            pl.BlockSpec((prompt, 128), col),
            pl.BlockSpec((cont, 128), col),
            pl.BlockSpec((cont, 128), col),
        ],
        out_specs=[pl.BlockSpec((rows, 384), col), pl.BlockSpec((1, 8, rows), lambda i: (i, 0, 0))],
        out_shape=[
            jax.ShapeDtypeStruct(query.shape, BF),
            jax.ShapeDtypeStruct((pairs, 8, rows), F32),
        ],
        scratch_shapes=[
            pltpu.VMEM((2, 2, prompt + cont, 128), BF),
            pltpu.VMEM((2, 2, prompt + cont, 128), BF),
            pltpu.VMEM((prompt + cont, rows), F32),
            pltpu.VMEM((cont, rows), BF),
        ],
        cost_estimate=pl.CostEstimate(flops=10**6, bytes_accessed=10**6, transcendentals=0),
        name="attend",
    )(place, query, prompt_key, prompt_value, own_key, own_value)


def attend_back_kernel(place_ref, q_ref, kp_ref, vp_ref, ko_ref, vo_ref, o_ref, do_ref, lse_ref,
                       dq_ref, dkp_ref, dvp_ref, dko_ref, dvo_ref, kpad, vpad, dk_acc, dv_acc):
    rows = q_ref.shape[0]
    prompt = kp_ref.shape[0]
    cont = ko_ref.shape[0]
    step = 2 * P_DEV
    place = place_ref[0]
    for src, dst, at, size in ((kp_ref, kpad, 0, prompt), (vp_ref, vpad, 0, prompt),
                               (ko_ref, kpad, prompt, cont), (vo_ref, vpad, prompt, cont)):
        for head, pair in enumerate(placed_halves(src[...].astype(F32))):
            for half in range(2):
                dst[head, half, at:at + size, :] = pair[half]
    dk_acc[...] = jnp.zeros_like(dk_acc)
    dv_acc[...] = jnp.zeros_like(dv_acc)
    for chunk in range(3):
        lanes = slice(chunk * 128, (chunk + 1) * 128)
        scaled = q_ref[:, lanes].astype(F32) * HD ** (-0.5)
        queries = scaled.astype(BF)
        query_halves = [part.astype(BF) for part in halves(scaled)]
        outs = o_ref[:, lanes].astype(F32)
        grads_f32 = do_ref[:, lanes].astype(F32)
        grads = do_ref[:, lanes]
        grad_halves = [part.astype(BF) for part in halves(grads_f32)]
        inner = jnp.transpose(outs * grads_f32)
        total = jnp.zeros((128, rows), F32)
        for half in range(2):
            position = chunk * 2 + half
            head = position // 3
            level = lse_ref[0, position:position + 1, :]
            delta = jnp.sum(inner[half * HD:(half + 1) * HD, :], 0, keepdims=True)

            def block(at, cols, mask, queries=queries, grads=grads, query_half=query_halves[half],
                      grad_half=grad_halves[half], level=level, delta=delta, head=head, half=half):
                keys = kpad[head, half, pl.ds(at, step), :]
                values = vpad[head, half, pl.ds(at, step), :]
                scores = dot_nt(keys, queries[cols, :])
                weights = jnp.exp(mask(scores) - level[:, cols])
                grad_weights = dot_nt(values, grads[cols, :])
                grad_scores = weights * (grad_weights - delta[:, cols])
                low_weights = weights.astype(BF)
                low_scores = grad_scores.astype(BF)
                dv_acc[head, pl.ds(at, step), :] += dot_nn(low_weights, grad_half[cols, :])
                dk_acc[head, pl.ds(at, step), :] += dot_nn(low_scores, query_half[cols, :])
                return dot_tn(keys, low_scores)

            def prompt_step(i, carry):
                at = pl.multiple_of(i * step, step)

                def mask(scores):
                    key_id = at + lax.broadcasted_iota(jnp.int32, (step, P_DEV), 0)
                    row_id = lax.broadcasted_iota(jnp.int32, (step, P_DEV), 1)
                    first = jnp.where(key_id <= place * P_DEV + row_id, scores[:, 0:P_DEV], NEGATIVE)
                    return jnp.concatenate([first, scores[:, P_DEV:]], 1)

                return carry + block(at, slice(0, rows), mask)

            total = lax.fori_loop(0, prompt // step, prompt_step, total)
            for own in range(cont // step):
                start = P_DEV + own * step

                def mask(scores):
                    key_id = lax.broadcasted_iota(jnp.int32, (step, step), 0)
                    row_id = lax.broadcasted_iota(jnp.int32, (step, step), 1)
                    edge = jnp.where(key_id <= row_id, scores[:, 0:step], NEGATIVE)
                    if scores.shape[1] == step:
                        return edge
                    return jnp.concatenate([edge, scores[:, step:]], 1)

                part = block(prompt + own * step, slice(start, rows), mask)
                total = jnp.concatenate([total[:, 0:start], total[:, start:] + part], 1)
        dq_ref[:, lanes] = (jnp.transpose(total) * HD ** (-0.5)).astype(BF)
    for acc, out_prompt, out_own in ((dk_acc, dkp_ref, dko_ref), (dv_acc, dvp_ref, dvo_ref)):
        low0, high0 = halves(acc[0])
        low1, high1 = halves(acc[1])
        merged = low0 + pltpu.roll(high0, HD, 1) + high1 + pltpu.roll(low1, HD, 1)
        out_prompt[...] = merged[0:prompt].astype(BF)
        out_own[...] = merged[prompt:].astype(BF)


def attend_back(place, query, prompt_key, prompt_value, own_key, own_value, mixed, grad, lse):
    rows = query.shape[0]
    prompt = prompt_key.shape[0]
    cont = own_key.shape[0]
    pairs = prompt_key.shape[1] // 128
    col = lambda i: (0, i)
    wide = pl.BlockSpec((rows, 384), col)
    keys_p = pl.BlockSpec((prompt, 128), col)
    keys_o = pl.BlockSpec((cont, 128), col)
    return pl.pallas_call(
        attend_back_kernel,
        grid=(pairs,),
        in_specs=[
            pl.BlockSpec(memory_space=pltpu.SMEM),
            wide, keys_p, keys_p, keys_o, keys_o, wide, wide,
            pl.BlockSpec((1, 8, rows), lambda i: (i, 0, 0)),
        ],
        out_specs=[wide, keys_p, keys_p, keys_o, keys_o],
        out_shape=[
            jax.ShapeDtypeStruct(query.shape, BF),
            jax.ShapeDtypeStruct(prompt_key.shape, BF),
            jax.ShapeDtypeStruct(prompt_key.shape, BF),
            jax.ShapeDtypeStruct(own_key.shape, BF),
            jax.ShapeDtypeStruct(own_key.shape, BF),
        ],
        scratch_shapes=[
            pltpu.VMEM((2, 2, prompt + cont, 128), BF),
            pltpu.VMEM((2, 2, prompt + cont, 128), BF),
            pltpu.VMEM((2, prompt + cont, 128), F32),
            pltpu.VMEM((2, prompt + cont, 128), F32),
        ],
        cost_estimate=pl.CostEstimate(flops=10**6, bytes_accessed=10**6, transcendentals=0),
        name="attend_back",
    )(place, query, prompt_key, prompt_value, own_key, own_value, mixed, grad, lse)


SLOTS_ALIGN = 16


def gather_kernel(count, with_gates, pos_ref, *refs):
    if with_gates:
        gate_ref, rows_ref, x_ref, g_ref, pick = refs
    else:
        rows_ref, x_ref, pick = refs
    tokens = rows_ref.shape[1]
    slots = x_ref.shape[1] // count
    half = rows_ref.shape[2] // 2
    slot_id = lax.broadcasted_iota(jnp.int32, (slots, tokens), 0)
    for k in range(count):
        hit = slot_id == pos_ref[0, k:k + 1, :]
        pick[k * slots:(k + 1) * slots, :] = jnp.where(hit, 1.0, 0.0).astype(BF)
        if with_gates:
            gate = jnp.sum(jnp.where(hit, gate_ref[0, k:k + 1, :], 0.0), 1, keepdims=True)
            g_ref[0, k * slots:(k + 1) * slots, :] = jnp.broadcast_to(gate, (slots, 128))
    x_ref[0, :, 0:half] = dot_nn(pick[...], rows_ref[0, :, 0:half]).astype(BF)
    x_ref[0, :, half:] = dot_nn(pick[...], rows_ref[0, :, half:]).astype(BF)


def gather_rows(positions, gates, rows, count, slots):
    sources, tokens, width = rows.shape
    size = count * slots
    table = pl.BlockSpec((1, 8, tokens), lambda s: (s, 0, 0))
    block = lambda shape: pl.BlockSpec((1,) + shape, lambda s: (s, 0, 0))
    tables = [positions] if gates is None else [positions, gates]
    outs = [((size, width), BF)] if gates is None else [((size, width), BF), ((size, 128), F32)]
    return pl.pallas_call(
        functools.partial(gather_kernel, count, gates is not None),
        grid=(sources,),
        in_specs=[table] * len(tables) + [block((tokens, width))],
        out_specs=[block(shape) for shape, _ in outs],
        out_shape=[jax.ShapeDtypeStruct((sources,) + shape, dtype) for shape, dtype in outs],
        scratch_shapes=[pltpu.VMEM((size, tokens), BF)],
        cost_estimate=pl.CostEstimate(flops=10**6, bytes_accessed=10**6, transcendentals=0),
        name="gather_rows",
    )(*tables, rows)


def expert_kernel(k, shards, slots, dp_ref, x_ref, g_ref, gate_ref, *refs):
    w_refs = refs[0:shards // 2]
    (y_out, dx_out, dg_out, keep_out, send_out,
     xs, gs, gates, ws, ys, dxs, dgs, dab, actg, stage,
     in_sem, w_sem, out_sem, grad_sem) = refs[shards // 2:]
    dp = dp_ref[0]
    sources = x_ref.shape[0]
    width = xs.shape[1]
    piece = width // shards
    hidden = ws.shape[2]
    mine = pl.ds(k * slots, slots)

    def row_copies(s):
        at = pl.ds(pl.multiple_of(s * slots, 16), slots)
        return (
            pltpu.make_async_copy(x_ref.at[s, mine, :], xs.at[at, :], in_sem.at[0, s]),
            pltpu.make_async_copy(g_ref.at[s, mine, :], gs.at[at, :], in_sem.at[1, s]),
            pltpu.make_async_copy(gate_ref.at[s, mine, :], gates.at[at, :], in_sem.at[2, s]),
        )

    weight_copies = [
        pltpu.make_async_copy(
            w_refs[(r & 1) + 2 * (r >> 2)].at[(r >> 1) & 1], ws.at[:, pl.ds(pl.multiple_of((dp ^ r) * piece, 16), piece), :], w_sem.at[r]
        )
        for r in range(shards)
    ]
    for s in range(sources):
        for copy in row_copies(s):
            copy.start()
        if s == 1:
            for copy in weight_copies:
                copy.start()
    for copy in weight_copies:
        copy.wait()
    chunk = 2 * slots

    def out_copies(c):
        at = pl.ds(pl.multiple_of(c * chunk, 32), chunk)
        return [
            pltpu.make_async_copy(src.at[at, :], dst.at[at, :], out_sem.at[i, c])
            for i, (src, dst) in enumerate(((ys, y_out), (dxs, dx_out), (dgs, dg_out)))
        ]

    def forward_chunk(c, carry):
        for copy in row_copies(2 * c) + row_copies(2 * c + 1):
            copy.wait()
        rows = pl.ds(pl.multiple_of(c * chunk, 32), chunk)
        x = xs[rows, :]
        a = dot_nn(x, ws[0])
        b = dot_nn(x, ws[1])
        pulled = dot_nn(gs[rows, :], ws[2])
        gate = gates[rows, 0:1]
        sig = jax.nn.sigmoid(a)
        silu = a * sig
        act = silu * b
        dgs[rows, :] = jnp.broadcast_to(jnp.sum(act * pulled, 1, keepdims=True), (chunk, 128))
        weighted = (gate * act).astype(BF)
        actg[rows, :] = weighted
        dact = gate * pulled
        da = (dact * b * sig * (1.0 + a * (1.0 - sig))).astype(BF)
        db = (dact * silu).astype(BF)
        dab[rows, 0:hidden] = da
        dab[rows, hidden:] = db
        ys[rows, :] = dot_nt(weighted, ws[2]).astype(BF)
        dxs[rows, :] = (dot_nt(da, ws[0]) + dot_nt(db, ws[1])).astype(BF)
        for copy in out_copies(c):
            copy.start()
        return carry

    lax.fori_loop(0, sources // 2, forward_chunk, 0)
    block = 384
    inner = block // piece
    high = dp // inner
    low = dp % inner

    def grad_copies(jr):
        slot = lax.rem(jr, 2)
        copies = []
        for ri in range(inner):
            dst = (send_out if ri % 2 else keep_out).at[jr * (inner // 2) + ri // 2]
            src = stage.at[slot, :, pl.ds(pl.multiple_of((low ^ ri) * piece, 16), piece), :]
            copies.append(pltpu.make_async_copy(src, dst, grad_sem.at[slot, ri]))
        return copies

    def grad_block(jr, carry):
        slot = lax.rem(jr, 2)

        @pl.when(jr >= 2)
        def _():
            for copy in grad_copies(jr - 2):
                copy.wait()

        cols = pl.ds(pl.multiple_of((high ^ jr) * block, 128), block)
        left = dot_tn(xs[:, cols], dab[...])
        stage[slot, 0] = left[:, 0:hidden].astype(BF)
        stage[slot, 1] = left[:, hidden:].astype(BF)
        stage[slot, 2] = dot_tn(gs[:, cols], actg[...]).astype(BF)
        for copy in grad_copies(jr):
            copy.start()
        return carry

    blocks = width // block
    lax.fori_loop(0, blocks, grad_block, 0)
    for jr in range(blocks - 2, blocks):
        for copy in grad_copies(jr):
            copy.wait()
    for c in range(sources // 2):
        for copy in out_copies(c):
            copy.wait()


def run_expert(k, dp_index, xs, gs, gates, weights, slots):
    sources, shards = xs.shape[0], 2 * len(weights)
    rows = sources * slots
    width = xs.shape[2]
    piece, hidden = weights[0].shape[2:]
    inner = 384 // piece
    anywhere = pl.BlockSpec(memory_space=pl.ANY)
    return pl.pallas_call(
        functools.partial(expert_kernel, k, shards, slots),
        in_specs=[pl.BlockSpec(memory_space=pltpu.SMEM)] + [anywhere] * (3 + shards // 2),
        out_specs=[anywhere] * 5,
        out_shape=[
            jax.ShapeDtypeStruct((rows, width), BF),
            jax.ShapeDtypeStruct((rows, width), BF),
            jax.ShapeDtypeStruct((rows, 128), F32),
            jax.ShapeDtypeStruct((shards // 2, 3, piece, hidden), BF),
            jax.ShapeDtypeStruct((shards // 2, 3, piece, hidden), BF),
        ],
        scratch_shapes=[
            pltpu.VMEM((rows, width), BF),
            pltpu.VMEM((rows, width), BF),
            pltpu.VMEM((rows, 128), F32),
            pltpu.VMEM((3, width, hidden), BF),
            pltpu.VMEM((rows, width), BF),
            pltpu.VMEM((rows, width), BF),
            pltpu.VMEM((rows, 128), F32),
            pltpu.VMEM((rows, 2 * hidden), BF),
            pltpu.VMEM((rows, hidden), BF),
            pltpu.VMEM((2, 3, 384, hidden), BF),
            pltpu.SemaphoreType.DMA((3, sources)),
            pltpu.SemaphoreType.DMA((shards,)),
            pltpu.SemaphoreType.DMA((3, sources // 2)),
            pltpu.SemaphoreType.DMA((2, inner)),
        ],
        compiler_params=pltpu.CompilerParams(vmem_limit_bytes=60 * 2**20),
        cost_estimate=pl.CostEstimate(flops=10**6, bytes_accessed=10**6, transcendentals=0),
        name="expert",
    )(dp_index, xs, gs, gates, *weights)


def barrier_with(partners):
    sem = pltpu.get_barrier_semaphore()
    for partner in partners:
        pl.semaphore_signal(sem, inc=1, device_id=partner, device_id_type=pl.DeviceIdType.MESH)
    pl.semaphore_wait(sem, len(partners))


def flipped(axis, mask):
    at = lax.axis_index(axis)
    bit = lax.rem(lax.div(at, mask), 2)
    return {axis: at + mask * (1 - 2 * bit)}


def own_bit(axis, mask):
    return lax.rem(lax.div(lax.axis_index(axis), mask), 2)


TEAM = (("dp", 2), ("expert", 2), ("expert", 1))
GROUP = (("dp", 1), ("expert", 2), ("expert", 1))
CUBE = (("dp", 4), ("dp", 2), ("dp", 1), ("expert", 2), ("expert", 1))
ROTATIONS = ((0, 1, 2, 3), (0, 2, 3, 1), (0, 3, 1, 2))


def gather_all_kernel(pieces, segments, count, *refs):
    shards, give_ref, routes_ref = refs[0:count], refs[count], refs[count + 1]
    fulls, take_ref, team_ref = refs[count + 2:2 * count + 2], refs[2 * count + 2], refs[2 * count + 3]
    own_sem, send_sem, recv_sem, piece_sem, team_sem = refs[2 * count + 4:]
    barrier_with([flipped(*dim) for dim in CUBE])
    bits = [own_bit(*dim) for dim in CUBE]
    here = tuple(pl.ds(bit, 1) for bit in bits)
    own = [pltpu.make_async_copy(shards[i], fulls[i].at[here], own_sem.at[i]) for i in range(count)]
    own.append(pltpu.make_async_copy(routes_ref, team_ref.at[0:1, 0:1, 0:1], own_sem.at[count]))
    for copy in own:
        copy.start()
    for copy in own:
        copy.wait()

    def routes_step(step):
        index = [pl.ds(0, 2) if d < step else pl.ds(0, 1) for d in range(3)]
        src = team_ref.at[tuple(index)]
        index[step] = pl.ds(1, 1)
        return pltpu.make_async_remote_copy(
            src_ref=src, dst_ref=team_ref.at[tuple(index)], send_sem=team_sem.at[0, step],
            recv_sem=team_sem.at[1, step], device_id=flipped(*TEAM[step]), device_id_type=pl.DeviceIdType.MESH,
        )

    def spread(step, n, gathered, dim):
        source, start, width, _ = segments[n]
        at = tuple(pl.ds(0, 2) if d in gathered else pl.ds(bits[d], 1) for d in range(5))
        ref = fulls[source].at[at + (slice(None), pl.ds(start, width))]
        return pltpu.make_async_remote_copy(
            src_ref=ref, dst_ref=ref, send_sem=send_sem.at[step, n], recv_sem=recv_sem.at[step, n],
            device_id=flipped(*CUBE[dim]), device_id_type=pl.DeviceIdType.MESH,
        )

    def hand(k):
        return pltpu.make_async_remote_copy(
            src_ref=give_ref.at[k], dst_ref=take_ref.at[k], send_sem=piece_sem.at[0, k],
            recv_sem=piece_sem.at[1, k], device_id=flipped("dp", 2), device_id_type=pl.DeviceIdType.MESH,
        )

    copies, passed = [], []
    running = [None] * len(segments)
    for step in range(5):
        if 0 < step < 4:
            routes_step(step - 1).wait()
        if step < 3:
            routes_step(step).start()
        for n, segment in enumerate(segments):
            if running[n] is not None:
                running[n].wait_recv()
            order = ROTATIONS[segment[3]] + (4,)
            copy = spread(step, n, order[:step], order[step])
            copy.start()
            copies.append(copy)
            running[n] = copy
        for k in range(pieces) if step == 4 else range(step, min(step + 1, pieces)):
            if step == 4 and k < 4:
                continue
            passed.append(hand(k))
            passed[-1].start()
    for copy in running:
        copy.wait_recv()
    for copy in copies:
        copy.wait_send()
    for copy in passed:
        copy.wait()


def gather_all(shards, segments, give, routes):
    rows = shards[0].shape[0]
    count, pieces = len(shards), give.shape[0]
    anywhere, vmem = pl.BlockSpec(memory_space=pl.ANY), pl.BlockSpec(memory_space=pltpu.VMEM)
    outs = pl.pallas_call(
        functools.partial(gather_all_kernel, pieces, segments, count),
        in_specs=[vmem] * count + [anywhere, vmem],
        out_specs=[anywhere] * (count + 2),
        out_shape=[jax.ShapeDtypeStruct((2,) * 5 + shard.shape, BF) for shard in shards]
        + [jax.ShapeDtypeStruct(give.shape, BF), jax.ShapeDtypeStruct((2, 2, 2) + routes.shape, jnp.int32)],
        scratch_shapes=[
            pltpu.SemaphoreType.DMA((count + 1,)),
            pltpu.SemaphoreType.DMA((5, len(segments))),
            pltpu.SemaphoreType.DMA((5, len(segments))),
            pltpu.SemaphoreType.DMA((2, pieces)),
            pltpu.SemaphoreType.DMA((2, 3)),
        ],
        compiler_params=pltpu.CompilerParams(collective_id=1, has_side_effects=True),
        name="gather_all",
    )(*[shard.reshape((1,) * 5 + shard.shape) for shard in shards], give, routes.reshape((1, 1, 1) + routes.shape))
    fulls = [full.reshape(32 * rows, full.shape[-1]) for full in outs[:count]]
    return fulls, outs[count], outs[count + 1].reshape((8,) + routes.shape)


def job_copies(jobs, gives, takes, sems):
    return [
        pltpu.make_async_remote_copy(
            src_ref=gives[j], dst_ref=takes[j], send_sem=sems.at[0, j], recv_sem=sems.at[1, j],
            device_id=flipped(*jobs[j]), device_id_type=pl.DeviceIdType.MESH,
        )
        for j in range(len(jobs))
    ]


def partners_of(dims, jobs):
    return [flipped(*dim) for dim in dict.fromkeys(tuple(dims) + tuple(jobs))]


def inner_plane():
    return own_bit("dp", 2) != own_bit("dp", 4)


def across():
    at = lax.axis_index("dp")
    return {"dp": at + 2 * (1 - 2 * own_bit("dp", 2)) + 4 * (1 - 2 * own_bit("dp", 4))}


def team_rows_kernel(jobs, relays, layout, experts, rows_ref, gates_ref, pos_ref, *refs):
    count, lanes = len(jobs), len(relays)
    gives, pairs = refs[0:count], refs[count:count + lanes]
    refs = refs[count + lanes:]
    if lanes:
        other_ref, refs = refs[0], refs[1:]
    all_ref, table_ref = refs[0:2]
    takes, far = refs[2:2 + count], refs[2 + count:2 + count + lanes]
    picked_ref, pick, held, built = refs[2 + count + lanes:6 + count + lanes]
    own_sem, send_sem, recv_sem, job_sem, relay_sem, held_sem, built_sem = refs[6 + count + lanes:]
    partners = partners_of(TEAM, jobs)
    if lanes:
        partners += [flipped("dp", 4), across()]
    barrier_with(partners)
    own = [
        pltpu.make_async_copy(rows_ref, all_ref.at[0:1, 0:1, 0:1], own_sem.at[0]),
        pltpu.make_async_copy(gates_ref, table_ref.at[0:1, 0:1, 0:1], own_sem.at[1]),
    ]
    for copy in own:
        copy.start()

    def leg(j, n):
        src = (pairs[j].at[0], pairs[j].at[1], other_ref.at[relays[j]])[n]
        return pltpu.make_async_remote_copy(
            src_ref=src, dst_ref=far[j].at[min(n, 1)], send_sem=relay_sem.at[n, j],
            recv_sem=relay_sem.at[3 + min(n, 1), j], device_id=across() if n == 2 else flipped("dp", 4),
            device_id_type=pl.DeviceIdType.MESH,
        )

    for copy in own:
        copy.wait()
    parts = 4
    width = all_ref.shape[4] // parts
    flows = [(all_ref, (slice(None), pl.ds(c * width, width))) for c in range(parts)]
    flows.append((table_ref, (slice(None), slice(None))))

    def hop(step, f):
        ref, tail = flows[f]
        index = [pl.ds(0, 2) if d < step else pl.ds(0, 1) for d in range(3)]
        src = ref.at[tuple(index) + tail]
        index[step] = pl.ds(1, 1)
        return pltpu.make_async_remote_copy(
            src_ref=src, dst_ref=ref.at[tuple(index) + tail], send_sem=send_sem.at[step, f],
            recv_sem=recv_sem.at[step, f], device_id=flipped(*TEAM[step]), device_id_type=pl.DeviceIdType.MESH,
        )

    order = [parts] + list(range(parts))
    for f in order:
        hop(0, f).start()
    background = job_copies(jobs, gives, takes, job_sem)
    for copy in background:
        copy.start()
    if lanes:

        @pl.when(inner_plane())
        def _():
            for n in (2, 0, 1):
                for j in range(lanes):
                    leg(j, n).start()

        @pl.when(jnp.logical_not(inner_plane()))
        def _():
            for j in range(lanes):
                leg(j, 0).start()

    tokens = rows_ref.shape[3]
    slots = pick.shape[0] // experts
    middle = all_ref.shape[4] // 2
    slot_id = lax.broadcasted_iota(jnp.int32, (slots, tokens), 0)
    turns = [(core, source) for core in range(2) for source in range(4)]

    def fetches(turn):
        core, source = turns[turn]
        copies, at = [], 0
        for n, job in enumerate(layout[source]):
            ref = (takes if core else gives)[job]
            size = ref.shape[0]
            copies.append(pltpu.make_async_copy(ref, held.at[turn % 2, pl.ds(at, size), :], held_sem.at[turn % 2, n]))
            at += size
        return copies

    def store(turn):
        core, source = turns[turn]
        return pltpu.make_async_copy(built.at[turn % 2], picked_ref.at[2 * source + core], built_sem.at[turn % 2])

    def begin(turn):
        if turns[turn][0]:
            for job in layout[turns[turn][1]]:
                background[job].wait()
        for copy in fetches(turn):
            copy.start()

    def gather(turn):
        core, source = turns[turn]
        slot = turn % 2
        for copy in fetches(turn):
            copy.wait()
        if turn + 1 < len(turns):
            begin(turn + 1)
        for k in range(experts):
            hit = slot_id == pos_ref[2 * source + core, k:k + 1, :]
            pick[k * slots:(k + 1) * slots, :] = jnp.where(hit, 1.0, 0.0).astype(BF)
        if turn >= 2:
            store(turn - 2).wait()
        built[slot, :, 0:middle] = dot_nn(pick[...], held[slot, :, 0:middle]).astype(BF)
        built[slot, :, middle:] = dot_nn(pick[...], held[slot, :, middle:]).astype(BF)
        store(turn).start()

    begin(0)
    for step in range(1, 3):
        for n, f in enumerate(order):
            hop(step - 1, f).wait_recv()
            hop(step, f).start()
            if n:
                gather(4 * (step - 1) + n - 1)
    for f in order:
        hop(2, f).wait_recv()
    store(6).wait()
    store(7).wait()
    for step in range(3):
        for f in order:
            hop(step, f).wait_send()
    used = [job for jobs_of in layout for job in jobs_of]
    for job, copy in enumerate(background):
        if job not in used:
            copy.wait()
    for j in range(lanes):
        leg(j, 0).wait()
        leg(j, 1).wait_recv()
    if lanes:

        @pl.when(inner_plane())
        def _():
            for j in range(lanes):
                leg(j, 1).wait_send()
                leg(j, 2).wait_send()


def team_rows(rows, gates, positions, layout, experts, slots, jobs=(), gives=(), relays=(), pairs=(), other=None):
    tokens, width = rows.shape
    size = experts * slots
    table = gates.shape
    anywhere = pl.BlockSpec(memory_space=pl.ANY)
    extra = [] if other is None else [other]
    full, tables, *takes = pl.pallas_call(
        functools.partial(team_rows_kernel, tuple(jobs), tuple(relays), layout, experts),
        in_specs=[pl.BlockSpec(memory_space=pltpu.VMEM)] * 3 + [anywhere] * (len(jobs) + len(pairs) + len(extra)),
        out_specs=[anywhere] * (3 + len(jobs) + len(pairs)),
        out_shape=[
            jax.ShapeDtypeStruct((2, 2, 2, tokens, width), BF),
            jax.ShapeDtypeStruct((2, 2, 2) + table, F32),
        ] + [jax.ShapeDtypeStruct(give.shape, give.dtype) for give in list(gives) + list(pairs)]
        + [jax.ShapeDtypeStruct((8, size, width), BF)],
        scratch_shapes=[
            pltpu.VMEM((size, tokens), BF),
            pltpu.VMEM((2, tokens, width), BF),
            pltpu.VMEM((2, size, width), BF),
            pltpu.SemaphoreType.DMA((2,)),
            pltpu.SemaphoreType.DMA((3, 5)),
            pltpu.SemaphoreType.DMA((3, 5)),
            pltpu.SemaphoreType.DMA((2, max(1, len(jobs)))),
            pltpu.SemaphoreType.DMA((5, max(1, len(relays)))),
            pltpu.SemaphoreType.DMA((2, 2)),
            pltpu.SemaphoreType.DMA((2,)),
        ],
        compiler_params=pltpu.CompilerParams(collective_id=2, has_side_effects=True, vmem_limit_bytes=60 * 2**20),
        name="team_rows",
    )(rows.reshape(1, 1, 1, tokens, width), gates.reshape((1, 1, 1) + table), positions, *gives, *pairs, *extra)
    *takes, picked = takes
    return full.reshape(8, tokens, width), tables.reshape((8,) + table), takes, picked


def add_into(acc, at, other):
    acc[at] = (acc[at].astype(F32) + other.astype(F32)).astype(BF)


def return_kernel(count, slots, jobs, relays, pos_ref, *refs):
    x_refs, y_refs, dg_refs = refs[0:count], refs[count:2 * count], refs[2 * count:3 * count]
    refs = refs[3 * count:]
    gives, takes = refs[0:len(jobs)], refs[len(jobs) + 4:2 * len(jobs) + 4]
    out_ref, gate_ref, kept_ref, sent_ref = refs[len(jobs):len(jobs) + 4]
    (acc, core_in, even_out, row_in, pair_in, last_in, ys, pick, table, table_core, table_row, table_pair,
     load_sem, send_sem, recv_sem, job_sem, store_sem, free_sem) = refs[2 * len(jobs) + 4:]
    tokens, width = out_ref.shape
    half = width // 2
    barrier_with(partners_of(TEAM, jobs))
    background = job_copies(jobs, gives, takes, job_sem)
    for copy in background[relays:]:
        copy.start()
    if relays:

        @pl.when(jnp.logical_not(inner_plane()))
        def _():
            for copy in background[:relays]:
                copy.start()

    first = (lax.axis_index("expert") * 2 + own_bit("dp", 2)) * count
    slot_id = lax.broadcasted_iota(jnp.int32, (slots, tokens), 0)

    def remote(src, dst, n, dim):
        return pltpu.make_async_remote_copy(
            src_ref=src, dst_ref=dst, send_sem=send_sem.at[n], recv_sem=recv_sem.at[n],
            device_id=flipped(*TEAM[dim]), device_id_type=pl.DeviceIdType.MESH,
        )

    def loads(parts, r, slot):
        return [
            pltpu.make_async_copy(
                parts[k].at[pl.ds(pl.multiple_of(r * slots, 16), slots), :],
                ys.at[slot, pl.ds(k * slots, slots), :], load_sem.at[slot, k],
            )
            for k in range(count)
        ]

    table[...] = jnp.zeros_like(table)

    def build(parts, step, r, following, dst, at, with_gates):
        slot = lax.rem(step, 2)
        for copy in loads(parts, r, slot):
            copy.wait()

        @pl.when(step < 7)
        def _():
            for copy in loads(parts, following, 1 - slot):
                copy.start()

        for k in range(count):
            hit = slot_id == pos_ref[r, k:k + 1, :]
            pick[k * slots:(k + 1) * slots, :] = jnp.where(hit, 1.0, 0.0).astype(BF)
            if with_gates:
                pulled = dg_refs[k][pl.ds(pl.multiple_of(r * slots, 16), slots), 0:1]
                table[r, pl.ds(first + k, 1), :] = jnp.sum(jnp.where(hit, pulled, 0.0), 0, keepdims=True)
        dst[at, :, 0:half] = dot_tn(pick[...], ys[slot, :, 0:half]).astype(BF)
        dst[at, :, half:] = dot_tn(pick[...], ys[slot, :, half:]).astype(BF)

    def core_copy(i, base):
        return remote(acc.at[2 * i + 1], core_in.at[i], base + i, 2)

    def build_odd(parts, base, with_gates):
        def odd(i, carry):
            r = 2 * i + 1
            build(parts, i, r, jnp.where(i < 3, r + 2, 0), acc, r, with_gates)
            core_copy(i, base).start()
            return carry

        lax.fori_loop(0, 4, odd, 0)

    for copy in loads(x_refs, 1, 0):
        copy.start()
    build_odd(x_refs, 0, True)
    tables = [remote(table.at[2 * i + 1], table_core.at[i], 4 + i, 2) for i in range(4)]
    for copy in tables:
        copy.start()

    def even(i, carry):
        build(x_refs, i + 4, 2 * i, 2 * i + 2, acc, 2 * i, True)
        return carry

    lax.fori_loop(0, 4, even, 0)
    if relays:

        @pl.when(inner_plane())
        def _():
            for copy in background[:relays]:
                copy.start()

    for copy in loads(y_refs, 1, 0):
        copy.start()

    def settle(i):
        core_copy(i, 0).wait()
        add_into(acc, 2 * i, core_in[i])

    left, right = slice(0, half), slice(half, width)
    settle(3)
    a = [remote(acc.at[6, :, pl.ds(0, half)], row_in.at[1], 8, 1), remote(acc.at[6, :, pl.ds(half, half)], pair_in.at[1], 9, 0)]
    for copy in a:
        copy.start()
    settle(1)
    a.append(remote(acc.at[2, :, pl.ds(0, half)], row_in.at[0], 10, 1))
    a[-1].start()
    settle(2)
    a.append(remote(acc.at[4, :, pl.ds(half, half)], pair_in.at[0], 11, 0))
    a[-1].start()
    settle(0)
    pl.semaphore_signal(free_sem, inc=1, device_id=flipped(*TEAM[2]), device_id_type=pl.DeviceIdType.MESH)
    for i, copy in enumerate(tables):
        copy.wait()
        table[2 * i] = table[2 * i] + table_core[i]
    t = [remote(table.at[2], table_row.at[0], 12, 1), remote(table.at[6], table_row.at[1], 13, 1)]
    for copy in t:
        copy.start()
    pl.semaphore_wait(free_sem, 1)
    build_odd(y_refs, 17, False)
    a[0].wait()
    add_into(acc, (4, slice(None), left), row_in[1])
    b = [remote(acc.at[4, :, pl.ds(0, half)], last_in.at[0], 14, 0)]
    b[0].start()
    a[1].wait()
    add_into(acc, (2, slice(None), right), pair_in[1])
    b.append(remote(acc.at[2, :, pl.ds(half, half)], last_in.at[1], 15, 1))
    b[1].start()
    for i, copy in enumerate(t):
        copy.wait()
        table[4 * i] = table[4 * i] + table_row[i]
    t = remote(table.at[4], table_pair, 16, 0)
    t.start()

    def even_y(i, carry):
        build(y_refs, i + 4, 2 * i, 2 * i + 2, even_out, i, False)
        return carry

    lax.fori_loop(0, 4, even_y, 0)
    stores = []
    for i in range(4):
        core_copy(i, 17).wait()
        add_into(even_out, i, core_in[i])
        stores.append(
            pltpu.make_async_copy(even_out.at[i], (sent_ref if i % 2 else kept_ref).at[i // 2], store_sem.at[i])
        )
        stores[-1].start()
    a[2].wait()
    add_into(acc, (0, slice(None), left), row_in[0])
    a[3].wait()
    add_into(acc, (0, slice(None), right), pair_in[0])
    b[0].wait()
    out_ref[:, left] = (acc[0, :, left].astype(F32) + last_in[0].astype(F32)).astype(BF)
    b[1].wait()
    out_ref[:, right] = (acc[0, :, right].astype(F32) + last_in[1].astype(F32)).astype(BF)
    t.wait()
    gate_ref[...] = table[0] + table_pair[...]
    for copy in stores:
        copy.wait()
    for copy in background:
        copy.wait()


def return_rows(positions, backs, results, gate_rows, experts, slots, jobs=(), gives=(), relays=0):
    sources, _, tokens = positions.shape
    count = len(results)
    width = results[0].shape[1]
    half = width // 2
    vmem, anywhere = pl.BlockSpec(memory_space=pltpu.VMEM), pl.BlockSpec(memory_space=pl.ANY)
    rows, gates, kept, sent, *takes = pl.pallas_call(
        functools.partial(return_kernel, count, slots, tuple(jobs), relays),
        in_specs=[vmem] + [anywhere] * (2 * count) + [vmem] * count + [anywhere] * len(jobs),
        out_specs=[vmem, vmem] + [anywhere] * (2 + len(jobs)),
        out_shape=[jax.ShapeDtypeStruct((tokens, width), BF), jax.ShapeDtypeStruct((experts, tokens), F32)]
        + [jax.ShapeDtypeStruct((2, tokens, width), BF)] * 2
        + [jax.ShapeDtypeStruct(give.shape, give.dtype) for give in gives],
        scratch_shapes=[
            pltpu.VMEM((8, tokens, width), BF),
            pltpu.VMEM((4, tokens, width), BF),
            pltpu.VMEM((4, tokens, width), BF),
            pltpu.VMEM((2, tokens, half), BF),
            pltpu.VMEM((2, tokens, half), BF),
            pltpu.VMEM((2, tokens, half), BF),
            pltpu.VMEM((2, count * slots, width), BF),
            pltpu.VMEM((count * slots, tokens), BF),
            pltpu.VMEM((8, experts, tokens), F32),
            pltpu.VMEM((4, experts, tokens), F32),
            pltpu.VMEM((2, experts, tokens), F32),
            pltpu.VMEM((experts, tokens), F32),
            pltpu.SemaphoreType.DMA((2, count)),
            pltpu.SemaphoreType.DMA((21,)),
            pltpu.SemaphoreType.DMA((21,)),
            pltpu.SemaphoreType.DMA((2, max(1, len(jobs)))),
            pltpu.SemaphoreType.DMA((4,)),
            pltpu.SemaphoreType.REGULAR,
        ],
        compiler_params=pltpu.CompilerParams(collective_id=3, has_side_effects=True, vmem_limit_bytes=63 * 2**20),
        name="return_rows",
    )(positions, *backs, *results, *gate_rows, *gives)
    return rows, gates, kept, sent, takes


class Group:
    def __init__(self, copies):
        self.copies = copies

    def wait(self):
        for copy in self.copies:
            copy.wait()


def scatter_kernel(dims, rotations, chunks, segments, sources, relays, *refs):
    last = len(dims) - 1
    grads, refs = refs[0:sources], refs[sources:]
    gives, takes = refs[0:relays], refs[relays + 1:2 * relays + 1]
    out_ref, refs = refs[relays], refs[2 * relays + 1:]
    acc, core_in = refs[0:2]
    inboxes = refs[2:2 + last]
    load_sem, send_sem, recv_sem, job_sem = refs[2 + last:]
    barrier_with([flipped(*dim) for dim in dims])
    background = job_copies(((("dp", 4), ("dp", 2)) * relays)[:relays], gives, takes, job_sem)

    def relay(outer):
        if relays:

            @pl.when(jnp.logical_not(inner_plane()) if outer else inner_plane())
            def _():
                background[0].start()

    bits = [own_bit(*dim) for dim in dims]
    every = tuple(pl.ds(0, 2) for _ in range(last))
    number = iter(range(send_sem.shape[0]))

    def remote(src, dst, dim):
        n = next(number)
        return pltpu.make_async_remote_copy(
            src_ref=src, dst_ref=dst, send_sem=send_sem.at[n], recv_sem=recv_sem.at[n],
            device_id=flipped(*dims[dim]), device_id_type=pl.DeviceIdType.MESH,
        )

    firsts, loads = [[] for _ in chunks], []
    for source, start, at, width, chunk in segments:
        src, dst = (slice(None), pl.ds(start, width)), (slice(None), pl.ds(at, width))
        copy = remote(
            grads[source].at[every + (pl.ds(1 - bits[last], 1),) + src], core_in.at[every + (pl.ds(0, 1),) + dst], last
        )
        copy.start()
        firsts[chunk].append(copy)
        load = pltpu.make_async_copy(
            grads[source].at[every + (pl.ds(bits[last], 1),) + src], acc.at[every + (pl.ds(0, 1),) + dst],
            load_sem.at[len(loads)],
        )
        load.start()
        loads.append(load)
    for load in loads:
        load.wait()
    sends = [Group(copies) for copies in firsts]
    relay(True)
    for step in range(last + 1):
        for c, (start, width) in enumerate(chunks):
            cols = pl.ds(start, width)
            rest = rotations[c][:last - step]
            sends[c].wait()
            for n in range(2 ** len(rest)):
                spread = [(n >> (len(rest) - 1 - i)) & 1 for i in range(len(rest))]
                index = [bits[d] if d not in rest else spread[rest.index(d)] for d in range(last)]
                at = tuple(index) + (0, slice(None), cols)
                other = core_in[at] if step == 0 else inboxes[step - 1][n, :, cols]
                if step < last:
                    add_into(acc, at, other)
                else:
                    out_ref[:, cols] = (acc[at].astype(F32) + other.astype(F32)).astype(out_ref.dtype)
            if step < last:
                dim, spread_dims = rest[-1], rest[:-1]
                group = []
                for n in range(2 ** len(spread_dims)):
                    spread = [(n >> (len(spread_dims) - 1 - i)) & 1 for i in range(len(spread_dims))]
                    index = [
                        1 - bits[d] if d == dim else (spread[spread_dims.index(d)] if d in spread_dims else bits[d])
                        for d in range(last)
                    ]
                    copy = remote(acc.at[tuple(index) + (0, slice(None), cols)], inboxes[step].at[n, :, cols], dim)
                    copy.start()
                    group.append(copy)
                sends[c] = Group(group)
        if step == 0:
            relay(False)
        if step == last - 1:
            for copy in background[1:]:
                copy.start()
    for copy in background:
        copy.wait()


def cube_scatter(dims, rotations, chunks, segments, grads, dtype, collective, name, gives=()):
    last = len(dims) - 1
    rows = grads[0].shape[0] // 2 ** len(dims)
    width = sum(chunk[1] for chunk in chunks)
    copies = len(segments) + len(chunks) * (2 ** last - 1)
    out, *takes = pl.pallas_call(
        functools.partial(scatter_kernel, dims, rotations, chunks, segments, len(grads), len(gives)),
        in_specs=[pl.BlockSpec(memory_space=pl.ANY)] * (len(grads) + len(gives)),
        out_specs=[pl.BlockSpec(memory_space=pltpu.VMEM)] + [pl.BlockSpec(memory_space=pl.ANY)] * len(gives),
        out_shape=[jax.ShapeDtypeStruct((rows, width), dtype)]
        + [jax.ShapeDtypeStruct(give.shape, give.dtype) for give in gives],
        scratch_shapes=[pltpu.VMEM((2,) * last + (1, rows, width), BF)] * 2
        + [pltpu.VMEM((2 ** n, rows, width), BF) for n in reversed(range(last))]
        + [
            pltpu.SemaphoreType.DMA((len(segments),)),
            pltpu.SemaphoreType.DMA((copies,)),
            pltpu.SemaphoreType.DMA((copies,)),
            pltpu.SemaphoreType.DMA((2, max(1, len(gives)))),
        ],
        compiler_params=pltpu.CompilerParams(
            collective_id=collective, has_side_effects=True, vmem_limit_bytes=60 * 2**20
        ),
        name=name,
    )(*[g.reshape((2,) * len(dims) + (rows, g.shape[1])) for g in grads], *gives)
    return out, takes


def dense_segments(wide):
    cut = wide // 256 * 128 + 128
    return ((0, 0, cut, 0), (0, cut, wide - cut, 1), (1, 0, 128, 1), (2, 0, 1536, 2), (3, 0, 128, 2))


def scatter_all(grads, gives):
    segments, chunks, at = [], [0, 0, 0], 0
    for source, start, width, chunk in dense_segments(grads[0].shape[1]):
        segments.append((source, start, at, width, chunk))
        chunks[chunk] += width
        at += width
    starts = (0, chunks[0], chunks[0] + chunks[1])
    return cube_scatter(
        CUBE, ROTATIONS, tuple(zip(starts, chunks)), tuple(segments), grads, F32, 4, "scatter_all", gives
    )


def group_back(grad_key, grad_value):
    width = grad_key.shape[1]
    segments = ((0, 0, 0, width, 0), (1, 0, width, width, 1))
    return cube_scatter(
        GROUP, ((0, 1), (1, 0)), ((0, width), (width, width)), segments, [grad_key, grad_value], BF, 6, "group_back"
    )[0]


def group_rows_kernel(rows_ref, key_ref, value_ref, own_sem, send_sem, recv_sem):
    barrier_with([flipped(*dim) for dim in GROUP])
    bits = [own_bit(*dim) for dim in GROUP]
    width = key_ref.shape[4]
    here = tuple(pl.ds(bit, 1) for bit in bits)
    own = [
        pltpu.make_async_copy(rows_ref.at[:, :, :, :, pl.ds(i * width, width)], ref.at[here], own_sem.at[i])
        for i, ref in enumerate((key_ref, value_ref))
    ]
    for copy in own:
        copy.start()
    for copy in own:
        copy.wait()
    copies = []
    running = [None, None]
    for step in range(3):
        for f, (ref, order) in enumerate(((key_ref, (0, 1, 2)), (value_ref, (1, 0, 2)))):
            if running[f] is not None:
                running[f].wait_recv()
            at = tuple(pl.ds(0, 2) if d in order[:step] else pl.ds(bits[d], 1) for d in range(3))
            copy = pltpu.make_async_remote_copy(
                src_ref=ref.at[at], dst_ref=ref.at[at], send_sem=send_sem.at[step, f], recv_sem=recv_sem.at[step, f],
                device_id=flipped(*GROUP[order[step]]), device_id_type=pl.DeviceIdType.MESH,
            )
            copy.start()
            copies.append(copy)
            running[f] = copy
    for copy in running:
        copy.wait_recv()
    for copy in copies:
        copy.wait_send()


def group_rows(key_value):
    rows, width = key_value.shape
    anywhere = pl.BlockSpec(memory_space=pl.ANY)
    outs = pl.pallas_call(
        group_rows_kernel,
        in_specs=[pl.BlockSpec(memory_space=pltpu.VMEM)],
        out_specs=[anywhere] * 2,
        out_shape=[jax.ShapeDtypeStruct((2, 2, 2, rows, width // 2), BF)] * 2,
        scratch_shapes=[
            pltpu.SemaphoreType.DMA((2,)),
            pltpu.SemaphoreType.DMA((3, 2)),
            pltpu.SemaphoreType.DMA((3, 2)),
        ],
        compiler_params=pltpu.CompilerParams(collective_id=5, has_side_effects=True),
        name="group_rows",
    )(key_value.reshape(1, 1, 1, rows, width))
    return [out.reshape(8 * rows, width // 2) for out in outs]


D = 1536
EPSILON = 1e-06
EVERYWHERE = ("dp", "expert")


def exchange(value, axis, mask):
    return lax.ppermute(value, axis, [(i, i ^ mask) for i in range(lax.axis_size(axis))])


def tie(first, *others):
    return lax.optimization_barrier((first, *others))[0]


def rms_scale(values):
    return lax.rsqrt(jnp.mean(values * values, axis=-1, keepdims=True) + EPSILON)


def product(left, right):
    return jnp.dot(left, right, preferred_element_type=F32)


def contract_rows(left, right):
    return jnp.einsum("ta,tb->ab", left, right, preferred_element_type=F32)


def times_transposed(left, right):
    return jnp.einsum("ta,ba->tb", left, right, preferred_element_type=F32)


def added(left, right):
    return (left.astype(F32) + right.astype(F32)).astype(BF)


def team_gather(value, order):
    pieces = {0: value}
    for axis, mask, bit in order:
        pieces.update({r | bit: exchange(v, axis, mask) for r, v in list(pieces.items())})
    return jnp.stack([pieces[r] for r in sorted(pieces)])


TEAM_BITS = (("dp", 2, 4), ("expert", 2, 2), ("expert", 1, 1))


def local(tokens, attn_gain, w_query, w_key, w_value, w_out, w_router, ffn_gain, w_gate, w_up, w_down, routes, cotangent):
    dp, expert_at = lax.axis_index("dp"), lax.axis_index("expert")
    shards, owners = lax.axis_size("dp"), lax.axis_size("expert")
    cube = shards == 8 and owners == 4
    turn = (dp >> 1) & 1
    tok_rows = tokens.shape[0]
    per_owner, piece, hidden = w_gate.shape
    count = per_owner // 2
    expert_count = per_owner * owners
    top_count = routes.shape[1]
    kvw = w_key.shape[1]
    capacity = 8 * ((17 * top_count * tok_rows + 128 * expert_count - 1) // (128 * expert_count))
    slots = SLOTS_ALIGN * (-(-capacity // SLOTS_ALIGN))
    dp_index = dp.astype(jnp.int32).reshape(1)
    wide = D + 2 * kvw

    stacked = jnp.stack([w_gate, w_up, w_down.transpose(0, 2, 1)], 1)
    own = lax.dynamic_slice_in_dim(stacked, turn * count, count, 0)
    other = lax.dynamic_slice_in_dim(stacked, (1 - turn) * count, count, 0)
    gains = jnp.pad(jnp.stack([attn_gain, ffn_gain], 1), ((0, 0), (0, 126)))
    dense = [
        jnp.concatenate([w_query, w_key, w_value], 1), gains, w_out,
        jnp.pad(w_router, ((0, 0), (0, 128 - expert_count))),
    ]
    ahead = 2
    if cube:
        dense_full, taken, routes_t = gather_all(dense, dense_segments(wide), other[:ahead], routes.T)
    else:
        routes_t = team_gather(routes.T, TEAM_BITS)
        dense_full = [lax.all_gather(shard, EVERYWHERE, axis=0, tiled=True) for shard in dense]
        taken = exchange(other[:ahead], "dp", 2)
    qkv_full, gains_full, out_full, router_full = dense_full
    gains_full = gains_full.astype(F32).T
    gain_first, gain_second = gains_full[0], gains_full[1]

    relay_bits = [1 << b for b in range(2, shards.bit_length() - 1)]
    pairs = [jnp.stack([own[k], taken[k]]) for k in range(ahead)]

    def crossed(relayed):
        return [w for v in relayed for w in (v, exchange(v, "dp", 1))]

    def relays(pair):
        pieces = [pair]
        for bit in relay_bits:
            pieces += [exchange(v, "dp", bit) for v in pieces]
        return pieces

    first_expert = expert_at * per_owner + turn * count
    local_ids = first_expert + jnp.arange(count, dtype=jnp.int32)
    hits = jnp.any(routes_t[:, None] == local_ids[None, :, None, None], axis=2)
    row_id = lax.broadcasted_iota(jnp.int32, (tok_rows, tok_rows), 0)
    col_id = lax.broadcasted_iota(jnp.int32, (tok_rows, tok_rows), 1)
    before = jnp.where(row_id < col_id, 1.0, 0.0).astype(BF)
    ranks = product(hits.astype(BF).reshape(-1, tok_rows), before).reshape(hits.shape)
    positions = jnp.where(hits, ranks.astype(jnp.int32), -1)
    positions = jnp.pad(positions, ((0, 0), (0, 8 - count), (0, 0)), constant_values=-1)

    inputs = tokens.astype(F32)
    scale_one = rms_scale(inputs)
    normed_one = inputs * scale_one
    hidden_one = (normed_one * gain_first).astype(BF)
    qkv = product(hidden_one, qkv_full).astype(BF)
    query, key_value = qkv[:, :D], qkv[:, D:]
    place = ((dp & 1) * owners + expert_at).astype(jnp.int32).reshape(1)
    prompt_key, prompt_value = group_rows(key_value[:P_DEV])
    own_key, own_value = key_value[P_DEV:, :kvw], key_value[P_DEV:, kvw:]
    early = tie(cotangent, qkv_full)
    middle = tok_rows // 2
    paired = exchange(early, "dp", 2)
    upper = exchange(early[:middle], "expert", 2)
    query, early, paired, upper, prompt_key, pairs[:2], late = lax.optimization_barrier(
        (query, early, paired, upper, prompt_key, pairs[:2], other[ahead:])
    )
    parts = [early, paired, upper, None, exchange(paired, "expert", 2)]
    layout = ((0,), (2, 3), (1,), (4,))
    taken_late = exchange(late, "dp", 2)
    pairs += [jnp.stack([own[k], taken_late[k - ahead]]) for k in range(ahead, count)]
    crossings = [exchange(pairs[k], "dp", 1) for k in range(2)]
    mixed, levels = attend(place, query, prompt_key, prompt_value, own_key, own_value)
    mixed, parts[4] = lax.optimization_barrier((mixed, parts[4]))
    parts[3] = exchange(tie(early[middle:], parts[4]), "expert", 2)
    second = inputs + product(mixed, out_full)
    scale_two = rms_scale(second)
    normed_two = second * scale_two
    hidden_two = (normed_two * gain_second).astype(BF)
    logits = product(hidden_two, router_full)[:, :expert_count]
    expert_ids = jnp.arange(expert_count, dtype=jnp.int32)
    chosen = jnp.any(routes[:, :, None] == expert_ids, axis=1)
    peak = jnp.max(jnp.where(chosen, logits, NEGATIVE), axis=-1, keepdims=True)
    raised = jnp.where(chosen, jnp.exp(jnp.where(chosen, logits - peak, 0.0)), 0.0)
    gates = raised / jnp.sum(raised, axis=-1, keepdims=True)

    weights = [None] * count
    near = exchange(tie(pairs[0], taken_late), "dp", 4) if cube else None
    sent_rows, parts, crossings = lax.optimization_barrier((hidden_two, parts, crossings))
    core_jobs = (("expert", 1),) * 5
    if cube:
        rows, gates_t, takes, grad_slots = team_rows(
            sent_rows, gates.T, positions, layout, count, slots,
            core_jobs + (("dp", 1),) * 3, (*parts, *pairs[2:]), (1, 2), pairs[1:3], other,
        )
        crossings = crossings + takes[5:8]
        relayed_pairs = [near] + takes[8:10]
        for k in range(3, count):
            relayed_pairs.append(exchange(tie(pairs[k], rows), "dp", 4))
        for k in range(count):
            weights[k] = [pairs[k], crossings[k], relayed_pairs[k]]
    else:
        rows, gates_t, _, grad_slots = team_rows(
            sent_rows, gates.T, positions, layout, count, slots, core_jobs, parts
        )
        for k in range(count):
            weights[k] = crossed(relays(tie(pairs[k], rows)))
    gates_t = lax.dynamic_slice_in_dim(gates_t, first_expert, count, 1)
    gates_t = jnp.pad(gates_t, ((0, 0), (0, 8 - count), (0, 0)))
    row_slots, gate_slots = gather_rows(positions, gates_t, rows, count, slots)

    results, backs, gate_rows, sums = [], [], [], []
    expert_index = dp_index
    for k in range(count):
        if cube:
            relayed_pair = tie(weights[k][2], rows) if k < 3 else tie(weights[k][2], gate_rows[k - 2], weights[k - 1][3])
            weights[k].append(exchange(relayed_pair, "dp", 1))
        y, dx, dg, keep, send = run_expert(k, expert_index, row_slots, grad_slots, gate_slots, weights[k], slots)
        results.append(y)
        backs.append(dx)
        gate_rows.append(dg)
        sums.append((keep, send))
        expert_index = tie(dp_index, dg)

    before_return = added(sums[0][0], exchange(tie(sums[0][1], gate_rows[1], weights[4]), "dp", 1))
    jobs, gives, relays_in = (("dp", 1),) * 2, (sums[1][1], sums[2][1]), 0
    if cube:
        jobs, gives, relays_in = (("dp", 4),) + jobs, (before_return[2:],) + gives, 1
    routed_back, gate_grad, out_keep, out_sent, takes = return_rows(
        positions, backs, results, gate_rows, expert_count, slots, jobs, gives, relays_in
    )
    halved = [before_return, added(sums[1][0], takes[-2]), added(sums[2][0], takes[-1])]
    crossed_back = [exchange(tie(sums[k][1], routed_back), "dp", 1) for k in range(3, count)]
    relay_bits = relay_bits[::-1]

    def sent_on(keep):
        return exchange(keep[keep.shape[0] // 2:], "dp", relay_bits[0])

    def settled(keep, came):
        keep = added(keep[:keep.shape[0] // 2], came)
        for bit in relay_bits[1:]:
            middle = keep.shape[0] // 2
            keep = added(keep[:middle], exchange(keep[middle:], "dp", bit))
        return keep

    relay_came = [takes[0] if cube else sent_on(before_return)] + [sent_on(keep) for keep in halved[1:]]
    gate_grad = gate_grad.T
    routed_back = routed_back.astype(F32)

    grad_output = cotangent.astype(F32)
    picked = jnp.where(chosen, gate_grad, 0.0)
    grad_logits = (gates * (picked - jnp.sum(gates * picked, axis=-1, keepdims=True))).astype(BF)
    wide_logits = jnp.pad(grad_logits, ((0, 0), (0, 128 - expert_count)))
    grad_hidden_two = times_transposed(wide_logits, router_full) + routed_back
    grad_normed_two = grad_hidden_two * gain_second
    grad_second = grad_output + scale_two * (
        grad_normed_two - normed_two * jnp.mean(grad_normed_two * normed_two, axis=-1, keepdims=True)
    )
    grad_branch = grad_second.astype(BF)
    ones = jnp.ones((tok_rows, 128), BF)
    lane = lax.broadcasted_iota(jnp.int32, (tok_rows, 128), 1)
    small = contract_rows(hidden_two, wide_logits) + contract_rows(
        (grad_hidden_two * normed_two).astype(BF), jnp.where(lane == expert_count, ones, jnp.zeros_like(ones))
    )
    grad_mixed = times_transposed(grad_branch, out_full).astype(BF)

    grad_mixed, halved = lax.optimization_barrier((grad_mixed, halved))
    row_came = exchange(out_sent, "expert", 2)
    grad_query, dkp, dvp, dko, dvo = attend_back(
        place, query, prompt_key, prompt_value, own_key, own_value, mixed, grad_mixed, levels
    )
    halved, relay_came, crossed_back, grad_query, row_came, dkp = lax.optimization_barrier(
        (halved, relay_came, crossed_back, grad_query, row_came, dkp)
    )
    halved += [added(sums[k][0], crossed_back[k - 3]) for k in range(3, count)]
    relay_came += [sent_on(halved[3])]
    total = tie(added(out_keep, row_came), halved[3])
    pair_came = exchange(total[1], "dp", 2)
    grad_prompt = group_back(dkp, dvp)
    out_grad = contract_rows(mixed, tie(grad_branch, grad_prompt, relay_came[3])).astype(BF)
    grad_qkv = jnp.concatenate([
        grad_query, jnp.concatenate([grad_prompt, jnp.concatenate([dko, dvo], 1)], 0)
    ], 1)
    grad_hidden_one = times_transposed(grad_qkv, qkv_full)
    weight_rows, grad_hidden_one, relay_came[3], total = lax.optimization_barrier(
        (grad_qkv, grad_hidden_one, relay_came[3], total)
    )
    relayed = [settled(halved[k], relay_came[k]) for k in range(3)]
    passing = jnp.stack([keep[1] for keep in relayed])
    dense_grads = [
        contract_rows(hidden_one, weight_rows).astype(BF),
        contract_rows((grad_hidden_one * normed_one).astype(BF), ones).astype(BF),
        out_grad, small.astype(BF),
    ]
    if cube:
        share, takes = scatter_all(dense_grads, (halved[4][2:], passing))
        relay_came.append(takes[0])
        theirs = takes[1]
    else:
        share = lax.psum_scatter(
            jnp.concatenate(dense_grads, 1), EVERYWHERE, scatter_dimension=0, tiled=True
        ).astype(F32)
        relay_came.append(sent_on(halved[4]))
        theirs = exchange(passing, "dp", 2)
    grad_normed_one = grad_hidden_one * gain_first
    grad_input = grad_second + scale_one * (
        grad_normed_one - normed_one * jnp.mean(grad_normed_one * normed_one, axis=-1, keepdims=True)
    )

    share, halved, relay_came, total, pair_came = lax.optimization_barrier(
        (share, halved, relay_came, total, pair_came)
    )
    output = (second + added(total[0], pair_came).astype(F32)).astype(BF)
    first_share, second_share = share[:, :wide + 128], share[:, wide + 128:]
    relayed += [settled(halved[k], relay_came[k]) for k in range(3, count)]
    theirs = jnp.concatenate([theirs, exchange(jnp.stack([keep[1] for keep in relayed[3:]]), "dp", 2)])
    mine = jnp.stack([keep[0] for keep in relayed])
    lower = jnp.where(turn == 0, mine, theirs)
    upper = jnp.where(turn == 0, theirs, mine)
    expert_grads = jnp.concatenate([lower, upper]).astype(F32)
    return (
        output,
        grad_input.astype(BF),
        first_share[:, wide],
        first_share[:, :D],
        first_share[:, D:D + kvw],
        first_share[:, D + kvw:wide],
        second_share[:, :D].astype(F32),
        second_share[:, D:D + expert_count].astype(F32),
        second_share[:, D + expert_count].astype(F32),
        expert_grads[:, 0],
        expert_grads[:, 1],
        expert_grads[:, 2].transpose(0, 2, 1),
    )


def solution(mesh):
    rows, line = P(("dp", "expert"), None), P(("dp", "expert"))
    gate, down = P("expert", "dp", None), P("expert", None, "dp")
    return jax.shard_map(
        local,
        mesh=mesh,
        in_specs=(rows, line, rows, rows, rows, rows, rows, line, gate, gate, down, rows, rows),
        out_specs=(rows, rows, line, rows, rows, rows, rows, rows, line, gate, gate, down),
        check_vma=False,
    )
```

```python
import functools
import jax
import jax.numpy as jnp
from jax import lax
from jax.sharding import PartitionSpec as P
from jax.experimental import pallas as pl
from jax.experimental.pallas import tpu as pltpu

HD = 64
P_DEV = 128
NEGATIVE = -1e30
F32 = jnp.float32
BF = jnp.bfloat16


def dot_nt(a, b):
    return lax.dot_general(a, b, (((1,), (1,)), ((), ())), preferred_element_type=F32)


def dot_nn(a, b):
    return lax.dot_general(a, b, (((1,), (0,)), ((), ())), preferred_element_type=F32)


def dot_tn(a, b):
    return lax.dot_general(a, b, (((0,), (0,)), ((), ())), preferred_element_type=F32)


def halves(pair):
    lane = lax.broadcasted_iota(jnp.int32, pair.shape, 1)
    zero = jnp.zeros_like(pair)
    return jnp.where(lane < HD, pair, zero), jnp.where(lane < HD, zero, pair)


def placed_halves(pair_f32):
    low0, high1 = halves(pair_f32)
    high0 = pltpu.roll(low0, HD, 1)
    low1 = pltpu.roll(high1, HD, 1)
    return ((low0.astype(BF), high0.astype(BF)), (low1.astype(BF), high1.astype(BF)))


def attend_kernel(place_ref, q_ref, kp_ref, vp_ref, ko_ref, vo_ref, o_ref, lse_ref, kpad, vpad, s_scr, p_scr):
    rows = q_ref.shape[0]
    prompt = kp_ref.shape[0]
    cont = ko_ref.shape[0]
    place = place_ref[0]
    for src, dst in ((kp_ref, kpad), (vp_ref, vpad)):
        for head, pair in enumerate(placed_halves(src[...].astype(F32))):
            for half in range(2):
                dst[head, half, 0:prompt, :] = pair[half]
    for src, dst in ((ko_ref, kpad), (vo_ref, vpad)):
        for head, pair in enumerate(placed_halves(src[...].astype(F32))):
            for half in range(2):
                dst[head, half, prompt:prompt + cont, :] = pair[half]
    key_id = lax.broadcasted_iota(jnp.int32, (prompt, P_DEV), 0)
    row_id = lax.broadcasted_iota(jnp.int32, (prompt, P_DEV), 1)
    seen_prompt = key_id <= place * P_DEV + row_id
    diag = lax.broadcasted_iota(jnp.int32, (P_DEV, P_DEV), 0) <= lax.broadcasted_iota(jnp.int32, (P_DEV, P_DEV), 1)
    blocks = cont // P_DEV
    stats = []
    for chunk in range(3):
        queries = (q_ref[:, chunk * 128:(chunk + 1) * 128].astype(F32) * HD ** (-0.5)).astype(BF)
        total = None
        for half in range(2):
            position = chunk * 2 + half
            head = position // 3
            keys = kpad.at[head, half]
            scores = dot_nt(keys[0:prompt, :], queries)
            first = jnp.where(seen_prompt, scores[:, 0:P_DEV], NEGATIVE)
            rest = scores[:, P_DEV:]
            s_scr[0:prompt, 0:P_DEV] = first
            s_scr[0:prompt, P_DEV:] = rest
            top = jnp.concatenate([jnp.max(first, 0, keepdims=True), jnp.max(rest, 0, keepdims=True)], 1)
            tops = [top[:, i * P_DEV:(i + 1) * P_DEV] for i in range(1 + blocks)]
            for block in range(blocks):
                start = (1 + block) * P_DEV
                at = prompt + block * P_DEV
                own = dot_nt(keys[at:at + P_DEV, :], queries[start:, :])
                edge = jnp.where(diag, own[:, 0:P_DEV], NEGATIVE)
                s_scr[at:at + P_DEV, start:start + P_DEV] = edge
                tops[1 + block] = jnp.maximum(tops[1 + block], jnp.max(edge, 0, keepdims=True))
                if block + 1 < blocks:
                    later = own[:, P_DEV:]
                    s_scr[at:at + P_DEV, start + P_DEV:] = later
                    best = jnp.max(later, 0, keepdims=True)
                    for i in range(block + 1, blocks):
                        at_i = (i - block - 1) * P_DEV
                        tops[1 + i] = jnp.maximum(tops[1 + i], best[:, at_i:at_i + P_DEV])
            top = jnp.concatenate(tops, 1)
            weights = jnp.exp(s_scr[0:prompt, :] - top)
            mass = jnp.sum(weights, 0, keepdims=True)
            masses = [mass[:, i * P_DEV:(i + 1) * P_DEV] for i in range(1 + blocks)]
            values = vpad.at[head, half]
            mixed = dot_tn(values[0:prompt, :], weights.astype(BF))
            for block in range(blocks):
                start = (1 + block) * P_DEV
                at = prompt + block * P_DEV
                part = jnp.exp(s_scr[at:at + P_DEV, start:] - top[:, start:])
                p_scr[block * P_DEV:(block + 1) * P_DEV, start:] = part.astype(BF)
                if block:
                    p_scr[block * P_DEV:(block + 1) * P_DEV, P_DEV:start] = jnp.zeros((P_DEV, block * P_DEV), BF)
                part_mass = jnp.sum(part, 0, keepdims=True)
                for i in range(block, blocks):
                    at_i = (i - block) * P_DEV
                    masses[1 + i] = masses[1 + i] + part_mass[:, at_i:at_i + P_DEV]
            own_mixed = dot_tn(values[prompt:prompt + cont, :], p_scr[:, P_DEV:])
            mass = jnp.concatenate(masses, 1)
            scale = 1.0 / mass
            mixed = jnp.concatenate([mixed[:, 0:P_DEV], mixed[:, P_DEV:] + own_mixed], 1) * scale
            total = mixed if total is None else total + mixed
            stats.append(top + jnp.log(mass))
        o_ref[:, chunk * 128:(chunk + 1) * 128] = jnp.transpose(total).astype(BF)
    lse_ref[0] = jnp.concatenate(stats + [jnp.zeros((2, rows), F32)], 0)


def attend(place, query, prompt_key, prompt_value, own_key, own_value):
    rows = query.shape[0]
    prompt = prompt_key.shape[0]
    cont = own_key.shape[0]
    pairs = prompt_key.shape[1] // 128
    col = lambda i: (0, i)
    return pl.pallas_call(
        attend_kernel,
        grid=(pairs,),
        in_specs=[
            pl.BlockSpec(memory_space=pltpu.SMEM),
            pl.BlockSpec((rows, 384), col),
            pl.BlockSpec((prompt, 128), col),
            pl.BlockSpec((prompt, 128), col),
            pl.BlockSpec((cont, 128), col),
            pl.BlockSpec((cont, 128), col),
        ],
        out_specs=[pl.BlockSpec((rows, 384), col), pl.BlockSpec((1, 8, rows), lambda i: (i, 0, 0))],
        out_shape=[
            jax.ShapeDtypeStruct(query.shape, BF),
            jax.ShapeDtypeStruct((pairs, 8, rows), F32),
        ],
        scratch_shapes=[
            pltpu.VMEM((2, 2, prompt + cont, 128), BF),
            pltpu.VMEM((2, 2, prompt + cont, 128), BF),
            pltpu.VMEM((prompt + cont, rows), F32),
            pltpu.VMEM((cont, rows), BF),
        ],
        cost_estimate=pl.CostEstimate(flops=10**6, bytes_accessed=10**6, transcendentals=0),
        name="attend",
    )(place, query, prompt_key, prompt_value, own_key, own_value)


def attend_back_kernel(place_ref, q_ref, kp_ref, vp_ref, ko_ref, vo_ref, o_ref, do_ref, lse_ref,
                       dq_ref, dkp_ref, dvp_ref, dko_ref, dvo_ref, kpad, vpad, dk_acc, dv_acc):
    rows = q_ref.shape[0]
    prompt = kp_ref.shape[0]
    cont = ko_ref.shape[0]
    step = 2 * P_DEV
    place = place_ref[0]
    for src, dst, at, size in ((kp_ref, kpad, 0, prompt), (vp_ref, vpad, 0, prompt),
                               (ko_ref, kpad, prompt, cont), (vo_ref, vpad, prompt, cont)):
        for head, pair in enumerate(placed_halves(src[...].astype(F32))):
            for half in range(2):
                dst[head, half, at:at + size, :] = pair[half]
    dk_acc[...] = jnp.zeros_like(dk_acc)
    dv_acc[...] = jnp.zeros_like(dv_acc)
    for chunk in range(3):
        lanes = slice(chunk * 128, (chunk + 1) * 128)
        scaled = q_ref[:, lanes].astype(F32) * HD ** (-0.5)
        queries = scaled.astype(BF)
        query_halves = [part.astype(BF) for part in halves(scaled)]
        outs = o_ref[:, lanes].astype(F32)
        grads_f32 = do_ref[:, lanes].astype(F32)
        grads = do_ref[:, lanes]
        grad_halves = [part.astype(BF) for part in halves(grads_f32)]
        inner = jnp.transpose(outs * grads_f32)
        total = jnp.zeros((128, rows), F32)
        for half in range(2):
            position = chunk * 2 + half
            head = position // 3
            level = lse_ref[0, position:position + 1, :]
            delta = jnp.sum(inner[half * HD:(half + 1) * HD, :], 0, keepdims=True)

            def block(at, cols, mask, queries=queries, grads=grads, query_half=query_halves[half],
                      grad_half=grad_halves[half], level=level, delta=delta, head=head, half=half):
                keys = kpad[head, half, pl.ds(at, step), :]
                values = vpad[head, half, pl.ds(at, step), :]
                scores = dot_nt(keys, queries[cols, :])
                weights = jnp.exp(mask(scores) - level[:, cols])
                grad_weights = dot_nt(values, grads[cols, :])
                grad_scores = weights * (grad_weights - delta[:, cols])
                low_weights = weights.astype(BF)
                low_scores = grad_scores.astype(BF)
                dv_acc[head, pl.ds(at, step), :] += dot_nn(low_weights, grad_half[cols, :])
                dk_acc[head, pl.ds(at, step), :] += dot_nn(low_scores, query_half[cols, :])
                return dot_tn(keys, low_scores)

            def prompt_step(i, carry):
                at = pl.multiple_of(i * step, step)

                def mask(scores):
                    key_id = at + lax.broadcasted_iota(jnp.int32, (step, P_DEV), 0)
                    row_id = lax.broadcasted_iota(jnp.int32, (step, P_DEV), 1)
                    first = jnp.where(key_id <= place * P_DEV + row_id, scores[:, 0:P_DEV], NEGATIVE)
                    return jnp.concatenate([first, scores[:, P_DEV:]], 1)

                return carry + block(at, slice(0, rows), mask)

            total = lax.fori_loop(0, prompt // step, prompt_step, total)
            for own in range(cont // step):
                start = P_DEV + own * step

                def mask(scores):
                    key_id = lax.broadcasted_iota(jnp.int32, (step, step), 0)
                    row_id = lax.broadcasted_iota(jnp.int32, (step, step), 1)
                    edge = jnp.where(key_id <= row_id, scores[:, 0:step], NEGATIVE)
                    if scores.shape[1] == step:
                        return edge
                    return jnp.concatenate([edge, scores[:, step:]], 1)

                part = block(prompt + own * step, slice(start, rows), mask)
                total = jnp.concatenate([total[:, 0:start], total[:, start:] + part], 1)
        dq_ref[:, lanes] = (jnp.transpose(total) * HD ** (-0.5)).astype(BF)
    for acc, out_prompt, out_own in ((dk_acc, dkp_ref, dko_ref), (dv_acc, dvp_ref, dvo_ref)):
        low0, high0 = halves(acc[0])
        low1, high1 = halves(acc[1])
        merged = low0 + pltpu.roll(high0, HD, 1) + high1 + pltpu.roll(low1, HD, 1)
        out_prompt[...] = merged[0:prompt].astype(BF)
        out_own[...] = merged[prompt:].astype(BF)


def attend_back(place, query, prompt_key, prompt_value, own_key, own_value, mixed, grad, lse):
    rows = query.shape[0]
    prompt = prompt_key.shape[0]
    cont = own_key.shape[0]
    pairs = prompt_key.shape[1] // 128
    col = lambda i: (0, i)
    wide = pl.BlockSpec((rows, 384), col)
    keys_p = pl.BlockSpec((prompt, 128), col)
    keys_o = pl.BlockSpec((cont, 128), col)
    return pl.pallas_call(
        attend_back_kernel,
        grid=(pairs,),
        in_specs=[
            pl.BlockSpec(memory_space=pltpu.SMEM),
            wide, keys_p, keys_p, keys_o, keys_o, wide, wide,
            pl.BlockSpec((1, 8, rows), lambda i: (i, 0, 0)),
        ],
        out_specs=[wide, keys_p, keys_p, keys_o, keys_o],
        out_shape=[
            jax.ShapeDtypeStruct(query.shape, BF),
            jax.ShapeDtypeStruct(prompt_key.shape, BF),
            jax.ShapeDtypeStruct(prompt_key.shape, BF),
            jax.ShapeDtypeStruct(own_key.shape, BF),
            jax.ShapeDtypeStruct(own_key.shape, BF),
        ],
        scratch_shapes=[
            pltpu.VMEM((2, 2, prompt + cont, 128), BF),
            pltpu.VMEM((2, 2, prompt + cont, 128), BF),
            pltpu.VMEM((2, prompt + cont, 128), F32),
            pltpu.VMEM((2, prompt + cont, 128), F32),
        ],
        cost_estimate=pl.CostEstimate(flops=10**6, bytes_accessed=10**6, transcendentals=0),
        name="attend_back",
    )(place, query, prompt_key, prompt_value, own_key, own_value, mixed, grad, lse)


SLOTS_ALIGN = 16


def gather_kernel(count, with_gates, pos_ref, *refs):
    if with_gates:
        gate_ref, rows_ref, x_ref, g_ref, pick = refs
    else:
        rows_ref, x_ref, pick = refs
    tokens = rows_ref.shape[1]
    slots = x_ref.shape[1] // count
    half = rows_ref.shape[2] // 2
    slot_id = lax.broadcasted_iota(jnp.int32, (slots, tokens), 0)
    for k in range(count):
        hit = slot_id == pos_ref[0, k:k + 1, :]
        pick[k * slots:(k + 1) * slots, :] = jnp.where(hit, 1.0, 0.0).astype(BF)
        if with_gates:
            gate = jnp.sum(jnp.where(hit, gate_ref[0, k:k + 1, :], 0.0), 1, keepdims=True)
            g_ref[0, k * slots:(k + 1) * slots, :] = jnp.broadcast_to(gate, (slots, 128))
    x_ref[0, :, 0:half] = dot_nn(pick[...], rows_ref[0, :, 0:half]).astype(BF)
    x_ref[0, :, half:] = dot_nn(pick[...], rows_ref[0, :, half:]).astype(BF)


def gather_rows(positions, gates, rows, count, slots):
    sources, tokens, width = rows.shape
    size = count * slots
    table = pl.BlockSpec((1, 8, tokens), lambda s: (s, 0, 0))
    block = lambda shape: pl.BlockSpec((1,) + shape, lambda s: (s, 0, 0))
    tables = [positions] if gates is None else [positions, gates]
    outs = [((size, width), BF)] if gates is None else [((size, width), BF), ((size, 128), F32)]
    return pl.pallas_call(
        functools.partial(gather_kernel, count, gates is not None),
        grid=(sources,),
        in_specs=[table] * len(tables) + [block((tokens, width))],
        out_specs=[block(shape) for shape, _ in outs],
        out_shape=[jax.ShapeDtypeStruct((sources,) + shape, dtype) for shape, dtype in outs],
        scratch_shapes=[pltpu.VMEM((size, tokens), BF)],
        cost_estimate=pl.CostEstimate(flops=10**6, bytes_accessed=10**6, transcendentals=0),
        name="gather_rows",
    )(*tables, rows)


def expert_kernel(k, shards, slots, dp_ref, x_ref, g_ref, gate_ref, *refs):
    w_refs = refs[0:shards // 2]
    (y_out, dx_out, dg_out, keep_out, send_out,
     xs, gs, gates, ws, ys, dxs, dgs, dab, actg, stage,
     in_sem, w_sem, out_sem, grad_sem) = refs[shards // 2:]
    dp = dp_ref[0]
    sources = x_ref.shape[0]
    width = xs.shape[1]
    piece = width // shards
    hidden = ws.shape[2]
    mine = pl.ds(k * slots, slots)

    def row_copies(s):
        at = pl.ds(pl.multiple_of(s * slots, 16), slots)
        return (
            pltpu.make_async_copy(x_ref.at[s, mine, :], xs.at[at, :], in_sem.at[0, s]),
            pltpu.make_async_copy(g_ref.at[s, mine, :], gs.at[at, :], in_sem.at[1, s]),
            pltpu.make_async_copy(gate_ref.at[s, mine, :], gates.at[at, :], in_sem.at[2, s]),
        )

    weight_copies = [
        pltpu.make_async_copy(
            w_refs[(r & 1) + 2 * (r >> 2)].at[(r >> 1) & 1], ws.at[:, pl.ds(pl.multiple_of((dp ^ r) * piece, 16), piece), :], w_sem.at[r]
        )
        for r in range(shards)
    ]
    for s in range(sources):
        for copy in row_copies(s):
            copy.start()
        if s == 1:
            for copy in weight_copies:
                copy.start()
    for copy in weight_copies:
        copy.wait()
    chunk = 2 * slots

    def out_copies(c):
        at = pl.ds(pl.multiple_of(c * chunk, 32), chunk)
        return [
            pltpu.make_async_copy(src.at[at, :], dst.at[at, :], out_sem.at[i, c])
            for i, (src, dst) in enumerate(((ys, y_out), (dxs, dx_out), (dgs, dg_out)))
        ]

    def forward_chunk(c, carry):
        for copy in row_copies(2 * c) + row_copies(2 * c + 1):
            copy.wait()
        rows = pl.ds(pl.multiple_of(c * chunk, 32), chunk)
        x = xs[rows, :]
        a = dot_nn(x, ws[0])
        b = dot_nn(x, ws[1])
        pulled = dot_nn(gs[rows, :], ws[2])
        gate = gates[rows, 0:1]
        sig = jax.nn.sigmoid(a)
        silu = a * sig
        act = silu * b
        dgs[rows, :] = jnp.broadcast_to(jnp.sum(act * pulled, 1, keepdims=True), (chunk, 128))
        weighted = (gate * act).astype(BF)
        actg[rows, :] = weighted
        dact = gate * pulled
        da = (dact * b * sig * (1.0 + a * (1.0 - sig))).astype(BF)
        db = (dact * silu).astype(BF)
        dab[rows, 0:hidden] = da
        dab[rows, hidden:] = db
        ys[rows, :] = dot_nt(weighted, ws[2]).astype(BF)
        dxs[rows, :] = (dot_nt(da, ws[0]) + dot_nt(db, ws[1])).astype(BF)
        for copy in out_copies(c):
            copy.start()
        return carry

    lax.fori_loop(0, sources // 2, forward_chunk, 0)
    block = 384
    inner = block // piece
    high = dp // inner
    low = dp % inner

    def grad_copies(jr):
        slot = lax.rem(jr, 2)
        copies = []
        for ri in range(inner):
            dst = (send_out if ri % 2 else keep_out).at[jr * (inner // 2) + ri // 2]
            src = stage.at[slot, :, pl.ds(pl.multiple_of((low ^ ri) * piece, 16), piece), :]
            copies.append(pltpu.make_async_copy(src, dst, grad_sem.at[slot, ri]))
        return copies

    def grad_block(jr, carry):
        slot = lax.rem(jr, 2)

        @pl.when(jr >= 2)
        def _():
            for copy in grad_copies(jr - 2):
                copy.wait()

        cols = pl.ds(pl.multiple_of((high ^ jr) * block, 128), block)
        left = dot_tn(xs[:, cols], dab[...])
        stage[slot, 0] = left[:, 0:hidden].astype(BF)
        stage[slot, 1] = left[:, hidden:].astype(BF)
        stage[slot, 2] = dot_tn(gs[:, cols], actg[...]).astype(BF)
        for copy in grad_copies(jr):
            copy.start()
        return carry

    blocks = width // block
    lax.fori_loop(0, blocks, grad_block, 0)
    for jr in range(blocks - 2, blocks):
        for copy in grad_copies(jr):
            copy.wait()
    for c in range(sources // 2):
        for copy in out_copies(c):
            copy.wait()


def run_expert(k, dp_index, xs, gs, gates, weights, slots):
    sources, shards = xs.shape[0], 2 * len(weights)
    rows = sources * slots
    width = xs.shape[2]
    piece, hidden = weights[0].shape[2:]
    inner = 384 // piece
    anywhere = pl.BlockSpec(memory_space=pl.ANY)
    return pl.pallas_call(
        functools.partial(expert_kernel, k, shards, slots),
        in_specs=[pl.BlockSpec(memory_space=pltpu.SMEM)] + [anywhere] * (3 + shards // 2),
        out_specs=[anywhere] * 5,
        out_shape=[
            jax.ShapeDtypeStruct((rows, width), BF),
            jax.ShapeDtypeStruct((rows, width), BF),
            jax.ShapeDtypeStruct((rows, 128), F32),
            jax.ShapeDtypeStruct((shards // 2, 3, piece, hidden), BF),
            jax.ShapeDtypeStruct((shards // 2, 3, piece, hidden), BF),
        ],
        scratch_shapes=[
            pltpu.VMEM((rows, width), BF),
            pltpu.VMEM((rows, width), BF),
            pltpu.VMEM((rows, 128), F32),
            pltpu.VMEM((3, width, hidden), BF),
            pltpu.VMEM((rows, width), BF),
            pltpu.VMEM((rows, width), BF),
            pltpu.VMEM((rows, 128), F32),
            pltpu.VMEM((rows, 2 * hidden), BF),
            pltpu.VMEM((rows, hidden), BF),
            pltpu.VMEM((2, 3, 384, hidden), BF),
            pltpu.SemaphoreType.DMA((3, sources)),
            pltpu.SemaphoreType.DMA((shards,)),
            pltpu.SemaphoreType.DMA((3, sources // 2)),
            pltpu.SemaphoreType.DMA((2, inner)),
        ],
        compiler_params=pltpu.CompilerParams(vmem_limit_bytes=60 * 2**20),
        cost_estimate=pl.CostEstimate(flops=10**6, bytes_accessed=10**6, transcendentals=0),
        name="expert",
    )(dp_index, xs, gs, gates, *weights)


def barrier_with(partners):
    sem = pltpu.get_barrier_semaphore()
    for partner in partners:
        pl.semaphore_signal(sem, inc=1, device_id=partner, device_id_type=pl.DeviceIdType.MESH)
    pl.semaphore_wait(sem, len(partners))


def flipped(axis, mask):
    at = lax.axis_index(axis)
    bit = lax.rem(lax.div(at, mask), 2)
    return {axis: at + mask * (1 - 2 * bit)}


def own_bit(axis, mask):
    return lax.rem(lax.div(lax.axis_index(axis), mask), 2)


TEAM = (("dp", 2), ("expert", 2), ("expert", 1))
GROUP = (("dp", 1), ("expert", 2), ("expert", 1))
CUBE = (("dp", 4), ("dp", 2), ("dp", 1), ("expert", 2), ("expert", 1))
ROTATIONS = ((0, 1, 2, 3), (0, 2, 3, 1), (0, 3, 1, 2))


def gather_all_kernel(pieces, segments, count, *refs):
    shards, give_ref, routes_ref = refs[0:count], refs[count], refs[count + 1]
    fulls, take_ref, team_ref = refs[count + 2:2 * count + 2], refs[2 * count + 2], refs[2 * count + 3]
    own_sem, send_sem, recv_sem, piece_sem, team_sem = refs[2 * count + 4:]
    barrier_with([flipped(*dim) for dim in CUBE])
    bits = [own_bit(*dim) for dim in CUBE]
    here = tuple(pl.ds(bit, 1) for bit in bits)
    own = [pltpu.make_async_copy(shards[i], fulls[i].at[here], own_sem.at[i]) for i in range(count)]
    own.append(pltpu.make_async_copy(routes_ref, team_ref.at[0:1, 0:1, 0:1], own_sem.at[count]))
    for copy in own:
        copy.start()
    for copy in own:
        copy.wait()

    def routes_step(step):
        index = [pl.ds(0, 2) if d < step else pl.ds(0, 1) for d in range(3)]
        src = team_ref.at[tuple(index)]
        index[step] = pl.ds(1, 1)
        return pltpu.make_async_remote_copy(
            src_ref=src, dst_ref=team_ref.at[tuple(index)], send_sem=team_sem.at[0, step],
            recv_sem=team_sem.at[1, step], device_id=flipped(*TEAM[step]), device_id_type=pl.DeviceIdType.MESH,
        )

    def spread(step, n, gathered, dim):
        source, start, width, _ = segments[n]
        at = tuple(pl.ds(0, 2) if d in gathered else pl.ds(bits[d], 1) for d in range(5))
        ref = fulls[source].at[at + (slice(None), pl.ds(start, width))]
        return pltpu.make_async_remote_copy(
            src_ref=ref, dst_ref=ref, send_sem=send_sem.at[step, n], recv_sem=recv_sem.at[step, n],
            device_id=flipped(*CUBE[dim]), device_id_type=pl.DeviceIdType.MESH,
        )

    def hand(k):
        return pltpu.make_async_remote_copy(
            src_ref=give_ref.at[k], dst_ref=take_ref.at[k], send_sem=piece_sem.at[0, k],
            recv_sem=piece_sem.at[1, k], device_id=flipped("dp", 2), device_id_type=pl.DeviceIdType.MESH,
        )

    copies, passed = [], []
    running = [None] * len(segments)
    for step in range(5):
        if 0 < step < 4:
            routes_step(step - 1).wait()
        if step < 3:
            routes_step(step).start()
        for n, segment in enumerate(segments):
            if running[n] is not None:
                running[n].wait_recv()
            order = ROTATIONS[segment[3]] + (4,)
            copy = spread(step, n, order[:step], order[step])
            copy.start()
            copies.append(copy)
            running[n] = copy
        for k in range(pieces) if step == 4 else range(step, min(step + 1, pieces)):
            if step == 4 and k < 4:
                continue
            passed.append(hand(k))
            passed[-1].start()
    for copy in running:
        copy.wait_recv()
    for copy in copies:
        copy.wait_send()
    for copy in passed:
        copy.wait()


def gather_all(shards, segments, give, routes):
    rows = shards[0].shape[0]
    count, pieces = len(shards), give.shape[0]
    anywhere, vmem = pl.BlockSpec(memory_space=pl.ANY), pl.BlockSpec(memory_space=pltpu.VMEM)
    outs = pl.pallas_call(
        functools.partial(gather_all_kernel, pieces, segments, count),
        in_specs=[vmem] * count + [anywhere, vmem],
        out_specs=[anywhere] * (count + 2),
        out_shape=[jax.ShapeDtypeStruct((2,) * 5 + shard.shape, BF) for shard in shards]
        + [jax.ShapeDtypeStruct(give.shape, BF), jax.ShapeDtypeStruct((2, 2, 2) + routes.shape, jnp.int32)],
        scratch_shapes=[
            pltpu.SemaphoreType.DMA((count + 1,)),
            pltpu.SemaphoreType.DMA((5, len(segments))),
            pltpu.SemaphoreType.DMA((5, len(segments))),
            pltpu.SemaphoreType.DMA((2, pieces)),
            pltpu.SemaphoreType.DMA((2, 3)),
        ],
        compiler_params=pltpu.CompilerParams(collective_id=1, has_side_effects=True),
        name="gather_all",
    )(*[shard.reshape((1,) * 5 + shard.shape) for shard in shards], give, routes.reshape((1, 1, 1) + routes.shape))
    fulls = [full.reshape(32 * rows, full.shape[-1]) for full in outs[:count]]
    return fulls, outs[count], outs[count + 1].reshape((8,) + routes.shape)


def job_copies(jobs, gives, takes, sems):
    return [
        pltpu.make_async_remote_copy(
            src_ref=gives[j], dst_ref=takes[j], send_sem=sems.at[0, j], recv_sem=sems.at[1, j],
            device_id=flipped(*jobs[j]), device_id_type=pl.DeviceIdType.MESH,
        )
        for j in range(len(jobs))
    ]


def partners_of(dims, jobs):
    return [flipped(*dim) for dim in dict.fromkeys(tuple(dims) + tuple(jobs))]


def inner_plane():
    return own_bit("dp", 2) != own_bit("dp", 4)


def across():
    at = lax.axis_index("dp")
    return {"dp": at + 2 * (1 - 2 * own_bit("dp", 2)) + 4 * (1 - 2 * own_bit("dp", 4))}


def team_rows_kernel(jobs, relays, layout, experts, rows_ref, gates_ref, pos_ref, *refs):
    count, lanes = len(jobs), len(relays)
    gives, pairs = refs[0:count], refs[count:count + lanes]
    refs = refs[count + lanes:]
    if lanes:
        other_ref, refs = refs[0], refs[1:]
    all_ref, table_ref = refs[0:2]
    takes, far = refs[2:2 + count], refs[2 + count:2 + count + lanes]
    picked_ref, pick, held, built = refs[2 + count + lanes:6 + count + lanes]
    own_sem, send_sem, recv_sem, job_sem, relay_sem, held_sem, built_sem = refs[6 + count + lanes:]
    partners = partners_of(TEAM, jobs)
    if lanes:
        partners += [flipped("dp", 4), across()]
    barrier_with(partners)
    own = [
        pltpu.make_async_copy(rows_ref, all_ref.at[0:1, 0:1, 0:1], own_sem.at[0]),
        pltpu.make_async_copy(gates_ref, table_ref.at[0:1, 0:1, 0:1], own_sem.at[1]),
    ]
    for copy in own:
        copy.start()

    def leg(j, n):
        src = (pairs[j].at[0], pairs[j].at[1], other_ref.at[relays[j]])[n]
        return pltpu.make_async_remote_copy(
            src_ref=src, dst_ref=far[j].at[min(n, 1)], send_sem=relay_sem.at[n, j],
            recv_sem=relay_sem.at[3 + min(n, 1), j], device_id=across() if n == 2 else flipped("dp", 4),
            device_id_type=pl.DeviceIdType.MESH,
        )

    for copy in own:
        copy.wait()
    parts = 4
    width = all_ref.shape[4] // parts
    flows = [(all_ref, (slice(None), pl.ds(c * width, width))) for c in range(parts)]
    flows.append((table_ref, (slice(None), slice(None))))

    def hop(step, f):
        ref, tail = flows[f]
        index = [pl.ds(0, 2) if d < step else pl.ds(0, 1) for d in range(3)]
        src = ref.at[tuple(index) + tail]
        index[step] = pl.ds(1, 1)
        return pltpu.make_async_remote_copy(
            src_ref=src, dst_ref=ref.at[tuple(index) + tail], send_sem=send_sem.at[step, f],
            recv_sem=recv_sem.at[step, f], device_id=flipped(*TEAM[step]), device_id_type=pl.DeviceIdType.MESH,
        )

    order = [parts] + list(range(parts))
    for f in order:
        hop(0, f).start()
    background = job_copies(jobs, gives, takes, job_sem)
    for copy in background:
        copy.start()
    if lanes:

        @pl.when(inner_plane())
        def _():
            for n in (2, 0, 1):
                for j in range(lanes):
                    leg(j, n).start()

        @pl.when(jnp.logical_not(inner_plane()))
        def _():
            for j in range(lanes):
                leg(j, 0).start()

    tokens = rows_ref.shape[3]
    slots = pick.shape[0] // experts
    middle = all_ref.shape[4] // 2
    slot_id = lax.broadcasted_iota(jnp.int32, (slots, tokens), 0)
    turns = [(core, source) for core in range(2) for source in range(4)]

    def fetches(turn):
        core, source = turns[turn]
        copies, at = [], 0
        for n, job in enumerate(layout[source]):
            ref = (takes if core else gives)[job]
            size = ref.shape[0]
            copies.append(pltpu.make_async_copy(ref, held.at[turn % 2, pl.ds(at, size), :], held_sem.at[turn % 2, n]))
            at += size
        return copies

    def store(turn):
        core, source = turns[turn]
        return pltpu.make_async_copy(built.at[turn % 2], picked_ref.at[2 * source + core], built_sem.at[turn % 2])

    def begin(turn):
        if turns[turn][0]:
            for job in layout[turns[turn][1]]:
                background[job].wait()
        for copy in fetches(turn):
            copy.start()

    def gather(turn):
        core, source = turns[turn]
        slot = turn % 2
        for copy in fetches(turn):
            copy.wait()
        if turn + 1 < len(turns):
            begin(turn + 1)
        for k in range(experts):
            hit = slot_id == pos_ref[2 * source + core, k:k + 1, :]
            pick[k * slots:(k + 1) * slots, :] = jnp.where(hit, 1.0, 0.0).astype(BF)
        if turn >= 2:
            store(turn - 2).wait()
        built[slot, :, 0:middle] = dot_nn(pick[...], held[slot, :, 0:middle]).astype(BF)
        built[slot, :, middle:] = dot_nn(pick[...], held[slot, :, middle:]).astype(BF)
        store(turn).start()

    begin(0)
    for step in range(1, 3):
        for n, f in enumerate(order):
            hop(step - 1, f).wait_recv()
            hop(step, f).start()
            if n:
                gather(4 * (step - 1) + n - 1)
    for f in order:
        hop(2, f).wait_recv()
    store(6).wait()
    store(7).wait()
    for step in range(3):
        for f in order:
            hop(step, f).wait_send()
    used = [job for jobs_of in layout for job in jobs_of]
    for job, copy in enumerate(background):
        if job not in used:
            copy.wait()
    for j in range(lanes):
        leg(j, 0).wait()
        leg(j, 1).wait_recv()
    if lanes:

        @pl.when(inner_plane())
        def _():
            for j in range(lanes):
                leg(j, 1).wait_send()
                leg(j, 2).wait_send()


def team_rows(rows, gates, positions, layout, experts, slots, jobs=(), gives=(), relays=(), pairs=(), other=None):
    tokens, width = rows.shape
    size = experts * slots
    table = gates.shape
    anywhere = pl.BlockSpec(memory_space=pl.ANY)
    extra = [] if other is None else [other]
    full, tables, *takes = pl.pallas_call(
        functools.partial(team_rows_kernel, tuple(jobs), tuple(relays), layout, experts),
        in_specs=[pl.BlockSpec(memory_space=pltpu.VMEM)] * 3 + [anywhere] * (len(jobs) + len(pairs) + len(extra)),
        out_specs=[anywhere] * (3 + len(jobs) + len(pairs)),
        out_shape=[
            jax.ShapeDtypeStruct((2, 2, 2, tokens, width), BF),
            jax.ShapeDtypeStruct((2, 2, 2) + table, F32),
        ] + [jax.ShapeDtypeStruct(give.shape, give.dtype) for give in list(gives) + list(pairs)]
        + [jax.ShapeDtypeStruct((8, size, width), BF)],
        scratch_shapes=[
            pltpu.VMEM((size, tokens), BF),
            pltpu.VMEM((2, tokens, width), BF),
            pltpu.VMEM((2, size, width), BF),
            pltpu.SemaphoreType.DMA((2,)),
            pltpu.SemaphoreType.DMA((3, 5)),
            pltpu.SemaphoreType.DMA((3, 5)),
            pltpu.SemaphoreType.DMA((2, max(1, len(jobs)))),
            pltpu.SemaphoreType.DMA((5, max(1, len(relays)))),
            pltpu.SemaphoreType.DMA((2, 2)),
            pltpu.SemaphoreType.DMA((2,)),
        ],
        compiler_params=pltpu.CompilerParams(collective_id=2, has_side_effects=True, vmem_limit_bytes=60 * 2**20),
        name="team_rows",
    )(rows.reshape(1, 1, 1, tokens, width), gates.reshape((1, 1, 1) + table), positions, *gives, *pairs, *extra)
    *takes, picked = takes
    return full.reshape(8, tokens, width), tables.reshape((8,) + table), takes, picked


def add_into(acc, at, other):
    acc[at] = (acc[at].astype(F32) + other.astype(F32)).astype(BF)


def return_kernel(count, slots, jobs, relays, pos_ref, *refs):
    x_refs, y_refs, dg_refs = refs[0:count], refs[count:2 * count], refs[2 * count:3 * count]
    refs = refs[3 * count:]
    gives, takes = refs[0:len(jobs)], refs[len(jobs) + 4:2 * len(jobs) + 4]
    out_ref, gate_ref, kept_ref, sent_ref = refs[len(jobs):len(jobs) + 4]
    (acc, core_in, even_out, row_in, pair_in, last_in, ys, pick, table, table_core, table_row, table_pair,
     load_sem, send_sem, recv_sem, job_sem, store_sem, free_sem) = refs[2 * len(jobs) + 4:]
    tokens, width = out_ref.shape
    half = width // 2
    barrier_with(partners_of(TEAM, jobs))
    background = job_copies(jobs, gives, takes, job_sem)
    for copy in background[relays:]:
        copy.start()
    if relays:

        @pl.when(jnp.logical_not(inner_plane()))
        def _():
            for copy in background[:relays]:
                copy.start()

    first = (lax.axis_index("expert") * 2 + own_bit("dp", 2)) * count
    slot_id = lax.broadcasted_iota(jnp.int32, (slots, tokens), 0)

    def remote(src, dst, n, dim):
        return pltpu.make_async_remote_copy(
            src_ref=src, dst_ref=dst, send_sem=send_sem.at[n], recv_sem=recv_sem.at[n],
            device_id=flipped(*TEAM[dim]), device_id_type=pl.DeviceIdType.MESH,
        )

    def loads(parts, r, slot):
        return [
            pltpu.make_async_copy(
                parts[k].at[pl.ds(pl.multiple_of(r * slots, 16), slots), :],
                ys.at[slot, pl.ds(k * slots, slots), :], load_sem.at[slot, k],
            )
            for k in range(count)
        ]

    table[...] = jnp.zeros_like(table)

    def build(parts, step, r, following, dst, at, with_gates):
        slot = lax.rem(step, 2)
        for copy in loads(parts, r, slot):
            copy.wait()

        @pl.when(step < 7)
        def _():
            for copy in loads(parts, following, 1 - slot):
                copy.start()

        for k in range(count):
            hit = slot_id == pos_ref[r, k:k + 1, :]
            pick[k * slots:(k + 1) * slots, :] = jnp.where(hit, 1.0, 0.0).astype(BF)
            if with_gates:
                pulled = dg_refs[k][pl.ds(pl.multiple_of(r * slots, 16), slots), 0:1]
                table[r, pl.ds(first + k, 1), :] = jnp.sum(jnp.where(hit, pulled, 0.0), 0, keepdims=True)
        dst[at, :, 0:half] = dot_tn(pick[...], ys[slot, :, 0:half]).astype(BF)
        dst[at, :, half:] = dot_tn(pick[...], ys[slot, :, half:]).astype(BF)

    def core_copy(i, base):
        return remote(acc.at[2 * i + 1], core_in.at[i], base + i, 2)

    def build_odd(parts, base, with_gates):
        def odd(i, carry):
            r = 2 * i + 1
            build(parts, i, r, jnp.where(i < 3, r + 2, 0), acc, r, with_gates)
            core_copy(i, base).start()
            return carry

        lax.fori_loop(0, 4, odd, 0)

    for copy in loads(x_refs, 1, 0):
        copy.start()
    build_odd(x_refs, 0, True)
    tables = [remote(table.at[2 * i + 1], table_core.at[i], 4 + i, 2) for i in range(4)]
    for copy in tables:
        copy.start()

    def even(i, carry):
        build(x_refs, i + 4, 2 * i, 2 * i + 2, acc, 2 * i, True)
        return carry

    lax.fori_loop(0, 4, even, 0)
    if relays:

        @pl.when(inner_plane())
        def _():
            for copy in background[:relays]:
                copy.start()

    for copy in loads(y_refs, 1, 0):
        copy.start()

    def settle(i):
        core_copy(i, 0).wait()
        add_into(acc, 2 * i, core_in[i])

    left, right = slice(0, half), slice(half, width)
    settle(3)
    a = [remote(acc.at[6, :, pl.ds(0, half)], row_in.at[1], 8, 1), remote(acc.at[6, :, pl.ds(half, half)], pair_in.at[1], 9, 0)]
    for copy in a:
        copy.start()
    settle(1)
    a.append(remote(acc.at[2, :, pl.ds(0, half)], row_in.at[0], 10, 1))
    a[-1].start()
    settle(2)
    a.append(remote(acc.at[4, :, pl.ds(half, half)], pair_in.at[0], 11, 0))
    a[-1].start()
    settle(0)
    pl.semaphore_signal(free_sem, inc=1, device_id=flipped(*TEAM[2]), device_id_type=pl.DeviceIdType.MESH)
    for i, copy in enumerate(tables):
        copy.wait()
        table[2 * i] = table[2 * i] + table_core[i]
    t = [remote(table.at[2], table_row.at[0], 12, 1), remote(table.at[6], table_row.at[1], 13, 1)]
    for copy in t:
        copy.start()
    pl.semaphore_wait(free_sem, 1)
    build_odd(y_refs, 17, False)
    a[0].wait()
    add_into(acc, (4, slice(None), left), row_in[1])
    b = [remote(acc.at[4, :, pl.ds(0, half)], last_in.at[0], 14, 0)]
    b[0].start()
    a[1].wait()
    add_into(acc, (2, slice(None), right), pair_in[1])
    b.append(remote(acc.at[2, :, pl.ds(half, half)], last_in.at[1], 15, 1))
    b[1].start()
    for i, copy in enumerate(t):
        copy.wait()
        table[4 * i] = table[4 * i] + table_row[i]
    t = remote(table.at[4], table_pair, 16, 0)
    t.start()

    def even_y(i, carry):
        build(y_refs, i + 4, 2 * i, 2 * i + 2, even_out, i, False)
        return carry

    lax.fori_loop(0, 4, even_y, 0)
    stores = []
    for i in range(4):
        core_copy(i, 17).wait()
        add_into(even_out, i, core_in[i])
        stores.append(
            pltpu.make_async_copy(even_out.at[i], (sent_ref if i % 2 else kept_ref).at[i // 2], store_sem.at[i])
        )
        stores[-1].start()
    a[2].wait()
    add_into(acc, (0, slice(None), left), row_in[0])
    a[3].wait()
    add_into(acc, (0, slice(None), right), pair_in[0])
    b[0].wait()
    out_ref[:, left] = (acc[0, :, left].astype(F32) + last_in[0].astype(F32)).astype(BF)
    b[1].wait()
    out_ref[:, right] = (acc[0, :, right].astype(F32) + last_in[1].astype(F32)).astype(BF)
    t.wait()
    gate_ref[...] = table[0] + table_pair[...]
    for copy in stores:
        copy.wait()
    for copy in background:
        copy.wait()


def return_rows(positions, backs, results, gate_rows, experts, slots, jobs=(), gives=(), relays=0):
    sources, _, tokens = positions.shape
    count = len(results)
    width = results[0].shape[1]
    half = width // 2
    vmem, anywhere = pl.BlockSpec(memory_space=pltpu.VMEM), pl.BlockSpec(memory_space=pl.ANY)
    rows, gates, kept, sent, *takes = pl.pallas_call(
        functools.partial(return_kernel, count, slots, tuple(jobs), relays),
        in_specs=[vmem] + [anywhere] * (2 * count) + [vmem] * count + [anywhere] * len(jobs),
        out_specs=[vmem, vmem] + [anywhere] * (2 + len(jobs)),
        out_shape=[jax.ShapeDtypeStruct((tokens, width), BF), jax.ShapeDtypeStruct((experts, tokens), F32)]
        + [jax.ShapeDtypeStruct((2, tokens, width), BF)] * 2
        + [jax.ShapeDtypeStruct(give.shape, give.dtype) for give in gives],
        scratch_shapes=[
            pltpu.VMEM((8, tokens, width), BF),
            pltpu.VMEM((4, tokens, width), BF),
            pltpu.VMEM((4, tokens, width), BF),
            pltpu.VMEM((2, tokens, half), BF),
            pltpu.VMEM((2, tokens, half), BF),
            pltpu.VMEM((2, tokens, half), BF),
            pltpu.VMEM((2, count * slots, width), BF),
            pltpu.VMEM((count * slots, tokens), BF),
            pltpu.VMEM((8, experts, tokens), F32),
            pltpu.VMEM((4, experts, tokens), F32),
            pltpu.VMEM((2, experts, tokens), F32),
            pltpu.VMEM((experts, tokens), F32),
            pltpu.SemaphoreType.DMA((2, count)),
            pltpu.SemaphoreType.DMA((21,)),
            pltpu.SemaphoreType.DMA((21,)),
            pltpu.SemaphoreType.DMA((2, max(1, len(jobs)))),
            pltpu.SemaphoreType.DMA((4,)),
            pltpu.SemaphoreType.REGULAR,
        ],
        compiler_params=pltpu.CompilerParams(collective_id=3, has_side_effects=True, vmem_limit_bytes=63 * 2**20),
        name="return_rows",
    )(positions, *backs, *results, *gate_rows, *gives)
    return rows, gates, kept, sent, takes


class Group:
    def __init__(self, copies):
        self.copies = copies

    def wait(self):
        for copy in self.copies:
            copy.wait()


def scatter_kernel(dims, rotations, chunks, segments, sources, relays, *refs):
    last = len(dims) - 1
    grads, refs = refs[0:sources], refs[sources:]
    gives, takes = refs[0:relays], refs[relays + 1:2 * relays + 1]
    out_ref, refs = refs[relays], refs[2 * relays + 1:]
    acc, core_in = refs[0:2]
    inboxes = refs[2:2 + last]
    load_sem, send_sem, recv_sem, job_sem = refs[2 + last:]
    barrier_with([flipped(*dim) for dim in dims])
    background = job_copies(((("dp", 4), ("dp", 2)) * relays)[:relays], gives, takes, job_sem)

    def relay(outer):
        if relays:

            @pl.when(jnp.logical_not(inner_plane()) if outer else inner_plane())
            def _():
                background[0].start()

    bits = [own_bit(*dim) for dim in dims]
    every = tuple(pl.ds(0, 2) for _ in range(last))
    number = iter(range(send_sem.shape[0]))

    def remote(src, dst, dim):
        n = next(number)
        return pltpu.make_async_remote_copy(
            src_ref=src, dst_ref=dst, send_sem=send_sem.at[n], recv_sem=recv_sem.at[n],
            device_id=flipped(*dims[dim]), device_id_type=pl.DeviceIdType.MESH,
        )

    firsts, loads = [[] for _ in chunks], []
    for source, start, at, width, chunk in segments:
        src, dst = (slice(None), pl.ds(start, width)), (slice(None), pl.ds(at, width))
        copy = remote(
            grads[source].at[every + (pl.ds(1 - bits[last], 1),) + src], core_in.at[every + (pl.ds(0, 1),) + dst], last
        )
        copy.start()
        firsts[chunk].append(copy)
        load = pltpu.make_async_copy(
            grads[source].at[every + (pl.ds(bits[last], 1),) + src], acc.at[every + (pl.ds(0, 1),) + dst],
            load_sem.at[len(loads)],
        )
        load.start()
        loads.append(load)
    for load in loads:
        load.wait()
    sends = [Group(copies) for copies in firsts]
    relay(True)
    for step in range(last + 1):
        for c, (start, width) in enumerate(chunks):
            cols = pl.ds(start, width)
            rest = rotations[c][:last - step]
            sends[c].wait()
            for n in range(2 ** len(rest)):
                spread = [(n >> (len(rest) - 1 - i)) & 1 for i in range(len(rest))]
                index = [bits[d] if d not in rest else spread[rest.index(d)] for d in range(last)]
                at = tuple(index) + (0, slice(None), cols)
                other = core_in[at] if step == 0 else inboxes[step - 1][n, :, cols]
                if step < last:
                    add_into(acc, at, other)
                else:
                    out_ref[:, cols] = (acc[at].astype(F32) + other.astype(F32)).astype(out_ref.dtype)
            if step < last:
                dim, spread_dims = rest[-1], rest[:-1]
                group = []
                for n in range(2 ** len(spread_dims)):
                    spread = [(n >> (len(spread_dims) - 1 - i)) & 1 for i in range(len(spread_dims))]
                    index = [
                        1 - bits[d] if d == dim else (spread[spread_dims.index(d)] if d in spread_dims else bits[d])
                        for d in range(last)
                    ]
                    copy = remote(acc.at[tuple(index) + (0, slice(None), cols)], inboxes[step].at[n, :, cols], dim)
                    copy.start()
                    group.append(copy)
                sends[c] = Group(group)
        if step == 0:
            relay(False)
        if step == last - 1:
            for copy in background[1:]:
                copy.start()
    for copy in background:
        copy.wait()


def cube_scatter(dims, rotations, chunks, segments, grads, dtype, collective, name, gives=()):
    last = len(dims) - 1
    rows = grads[0].shape[0] // 2 ** len(dims)
    width = sum(chunk[1] for chunk in chunks)
    copies = len(segments) + len(chunks) * (2 ** last - 1)
    out, *takes = pl.pallas_call(
        functools.partial(scatter_kernel, dims, rotations, chunks, segments, len(grads), len(gives)),
        in_specs=[pl.BlockSpec(memory_space=pl.ANY)] * (len(grads) + len(gives)),
        out_specs=[pl.BlockSpec(memory_space=pltpu.VMEM)] + [pl.BlockSpec(memory_space=pl.ANY)] * len(gives),
        out_shape=[jax.ShapeDtypeStruct((rows, width), dtype)]
        + [jax.ShapeDtypeStruct(give.shape, give.dtype) for give in gives],
        scratch_shapes=[pltpu.VMEM((2,) * last + (1, rows, width), BF)] * 2
        + [pltpu.VMEM((2 ** n, rows, width), BF) for n in reversed(range(last))]
        + [
            pltpu.SemaphoreType.DMA((len(segments),)),
            pltpu.SemaphoreType.DMA((copies,)),
            pltpu.SemaphoreType.DMA((copies,)),
            pltpu.SemaphoreType.DMA((2, max(1, len(gives)))),
        ],
        compiler_params=pltpu.CompilerParams(
            collective_id=collective, has_side_effects=True, vmem_limit_bytes=60 * 2**20
        ),
        name=name,
    )(*[g.reshape((2,) * len(dims) + (rows, g.shape[1])) for g in grads], *gives)
    return out, takes


def dense_segments(wide):
    cut = wide // 256 * 128 + 128
    return ((0, 0, cut, 0), (0, cut, wide - cut, 1), (1, 0, 128, 1), (2, 0, 1536, 2), (3, 0, 128, 2))


def scatter_all(grads, gives):
    segments, chunks, at = [], [0, 0, 0], 0
    for source, start, width, chunk in dense_segments(grads[0].shape[1]):
        segments.append((source, start, at, width, chunk))
        chunks[chunk] += width
        at += width
    starts = (0, chunks[0], chunks[0] + chunks[1])
    return cube_scatter(
        CUBE, ROTATIONS, tuple(zip(starts, chunks)), tuple(segments), grads, F32, 4, "scatter_all", gives
    )


def group_back(grad_key, grad_value):
    width = grad_key.shape[1]
    segments = ((0, 0, 0, width, 0), (1, 0, width, width, 1))
    return cube_scatter(
        GROUP, ((0, 1), (1, 0)), ((0, width), (width, width)), segments, [grad_key, grad_value], BF, 6, "group_back"
    )[0]


def group_rows_kernel(rows_ref, key_ref, value_ref, own_sem, send_sem, recv_sem):
    barrier_with([flipped(*dim) for dim in GROUP])
    bits = [own_bit(*dim) for dim in GROUP]
    width = key_ref.shape[4]
    here = tuple(pl.ds(bit, 1) for bit in bits)
    own = [
        pltpu.make_async_copy(rows_ref.at[:, :, :, :, pl.ds(i * width, width)], ref.at[here], own_sem.at[i])
        for i, ref in enumerate((key_ref, value_ref))
    ]
    for copy in own:
        copy.start()
    for copy in own:
        copy.wait()
    copies = []
    running = [None, None]
    for step in range(3):
        for f, (ref, order) in enumerate(((key_ref, (0, 1, 2)), (value_ref, (1, 0, 2)))):
            if running[f] is not None:
                running[f].wait_recv()
            at = tuple(pl.ds(0, 2) if d in order[:step] else pl.ds(bits[d], 1) for d in range(3))
            copy = pltpu.make_async_remote_copy(
                src_ref=ref.at[at], dst_ref=ref.at[at], send_sem=send_sem.at[step, f], recv_sem=recv_sem.at[step, f],
                device_id=flipped(*GROUP[order[step]]), device_id_type=pl.DeviceIdType.MESH,
            )
            copy.start()
            copies.append(copy)
            running[f] = copy
    for copy in running:
        copy.wait_recv()
    for copy in copies:
        copy.wait_send()


def group_rows(key_value):
    rows, width = key_value.shape
    anywhere = pl.BlockSpec(memory_space=pl.ANY)
    outs = pl.pallas_call(
        group_rows_kernel,
        in_specs=[pl.BlockSpec(memory_space=pltpu.VMEM)],
        out_specs=[anywhere] * 2,
        out_shape=[jax.ShapeDtypeStruct((2, 2, 2, rows, width // 2), BF)] * 2,
        scratch_shapes=[
            pltpu.SemaphoreType.DMA((2,)),
            pltpu.SemaphoreType.DMA((3, 2)),
            pltpu.SemaphoreType.DMA((3, 2)),
        ],
        compiler_params=pltpu.CompilerParams(collective_id=5, has_side_effects=True),
        name="group_rows",
    )(key_value.reshape(1, 1, 1, rows, width))
    return [out.reshape(8 * rows, width // 2) for out in outs]


D = 1536
EPSILON = 1e-06
EVERYWHERE = ("dp", "expert")


def exchange(value, axis, mask):
    return lax.ppermute(value, axis, [(i, i ^ mask) for i in range(lax.axis_size(axis))])


def tie(first, *others):
    return lax.optimization_barrier((first, *others))[0]


def rms_scale(values):
    return lax.rsqrt(jnp.mean(values * values, axis=-1, keepdims=True) + EPSILON)


def product(left, right):
    return jnp.dot(left, right, preferred_element_type=F32)


def contract_rows(left, right):
    return jnp.einsum("ta,tb->ab", left, right, preferred_element_type=F32)


def times_transposed(left, right):
    return jnp.einsum("ta,ba->tb", left, right, preferred_element_type=F32)


def added(left, right):
    return (left.astype(F32) + right.astype(F32)).astype(BF)


def team_gather(value, order):
    pieces = {0: value}
    for axis, mask, bit in order:
        pieces.update({r | bit: exchange(v, axis, mask) for r, v in list(pieces.items())})
    return jnp.stack([pieces[r] for r in sorted(pieces)])


TEAM_BITS = (("dp", 2, 4), ("expert", 2, 2), ("expert", 1, 1))


def local(tokens, attn_gain, w_query, w_key, w_value, w_out, w_router, ffn_gain, w_gate, w_up, w_down, routes, cotangent):
    dp, expert_at = lax.axis_index("dp"), lax.axis_index("expert")
    shards, owners = lax.axis_size("dp"), lax.axis_size("expert")
    cube = shards == 8 and owners == 4
    turn = (dp >> 1) & 1
    tok_rows = tokens.shape[0]
    per_owner, piece, hidden = w_gate.shape
    count = per_owner // 2
    expert_count = per_owner * owners
    top_count = routes.shape[1]
    kvw = w_key.shape[1]
    capacity = 8 * ((17 * top_count * tok_rows + 128 * expert_count - 1) // (128 * expert_count))
    slots = SLOTS_ALIGN * (-(-capacity // SLOTS_ALIGN))
    dp_index = dp.astype(jnp.int32).reshape(1)
    wide = D + 2 * kvw

    stacked = jnp.stack([w_gate, w_up, w_down.transpose(0, 2, 1)], 1)
    own = lax.dynamic_slice_in_dim(stacked, turn * count, count, 0)
    other = lax.dynamic_slice_in_dim(stacked, (1 - turn) * count, count, 0)
    gains = jnp.pad(jnp.stack([attn_gain, ffn_gain], 1), ((0, 0), (0, 126)))
    dense = [
        jnp.concatenate([w_query, w_key, w_value], 1), gains, w_out,
        jnp.pad(w_router, ((0, 0), (0, 128 - expert_count))),
    ]
    ahead = 2
    if cube:
        dense_full, taken, routes_t = gather_all(dense, dense_segments(wide), other[:ahead], routes.T)
    else:
        routes_t = team_gather(routes.T, TEAM_BITS)
        dense_full = [lax.all_gather(shard, EVERYWHERE, axis=0, tiled=True) for shard in dense]
        taken = exchange(other[:ahead], "dp", 2)
    qkv_full, gains_full, out_full, router_full = dense_full
    gains_full = gains_full.astype(F32).T
    gain_first, gain_second = gains_full[0], gains_full[1]

    relay_bits = [1 << b for b in range(2, shards.bit_length() - 1)]
    pairs = [jnp.stack([own[k], taken[k]]) for k in range(ahead)]

    def crossed(relayed):
        return [w for v in relayed for w in (v, exchange(v, "dp", 1))]

    def relays(pair):
        pieces = [pair]
        for bit in relay_bits:
            pieces += [exchange(v, "dp", bit) for v in pieces]
        return pieces

    first_expert = expert_at * per_owner + turn * count
    local_ids = first_expert + jnp.arange(count, dtype=jnp.int32)
    hits = jnp.any(routes_t[:, None] == local_ids[None, :, None, None], axis=2)
    row_id = lax.broadcasted_iota(jnp.int32, (tok_rows, tok_rows), 0)
    col_id = lax.broadcasted_iota(jnp.int32, (tok_rows, tok_rows), 1)
    before = jnp.where(row_id < col_id, 1.0, 0.0).astype(BF)
    ranks = product(hits.astype(BF).reshape(-1, tok_rows), before).reshape(hits.shape)
    positions = jnp.where(hits, ranks.astype(jnp.int32), -1)
    positions = jnp.pad(positions, ((0, 0), (0, 8 - count), (0, 0)), constant_values=-1)

    inputs = tokens.astype(F32)
    scale_one = rms_scale(inputs)
    normed_one = inputs * scale_one
    hidden_one = (normed_one * gain_first).astype(BF)
    qkv = product(hidden_one, qkv_full).astype(BF)
    query, key_value = qkv[:, :D], qkv[:, D:]
    place = ((dp & 1) * owners + expert_at).astype(jnp.int32).reshape(1)
    prompt_key, prompt_value = group_rows(key_value[:P_DEV])
    own_key, own_value = key_value[P_DEV:, :kvw], key_value[P_DEV:, kvw:]
    early = tie(cotangent, qkv_full)
    middle = tok_rows // 2
    paired = exchange(early, "dp", 2)
    upper = exchange(early[:middle], "expert", 2)
    query, early, paired, upper, prompt_key, pairs[:2], late = lax.optimization_barrier(
        (query, early, paired, upper, prompt_key, pairs[:2], other[ahead:])
    )
    parts = [early, paired, upper, None, exchange(paired, "expert", 2)]
    layout = ((0,), (2, 3), (1,), (4,))
    taken_late = exchange(late, "dp", 2)
    pairs += [jnp.stack([own[k], taken_late[k - ahead]]) for k in range(ahead, count)]
    crossings = [exchange(pairs[k], "dp", 1) for k in range(2)]
    mixed, levels = attend(place, query, prompt_key, prompt_value, own_key, own_value)
    parts[3] = exchange(early[middle:], "expert", 2)
    second = inputs + product(mixed, out_full)
    second, parts[3:5] = lax.optimization_barrier((second, parts[3:5]))
    scale_two = rms_scale(second)
    normed_two = second * scale_two
    hidden_two = (normed_two * gain_second).astype(BF)
    logits = product(hidden_two, router_full)[:, :expert_count]
    expert_ids = jnp.arange(expert_count, dtype=jnp.int32)
    chosen = jnp.any(routes[:, :, None] == expert_ids, axis=1)
    peak = jnp.max(jnp.where(chosen, logits, NEGATIVE), axis=-1, keepdims=True)
    raised = jnp.where(chosen, jnp.exp(jnp.where(chosen, logits - peak, 0.0)), 0.0)
    gates = raised / jnp.sum(raised, axis=-1, keepdims=True)

    weights = [None] * count
    near = exchange(tie(pairs[0], taken_late), "dp", 4) if cube else None
    sent_rows, parts, crossings = lax.optimization_barrier((hidden_two, parts, crossings))
    core_jobs = (("expert", 1),) * 5
    if cube:
        rows, gates_t, takes, grad_slots = team_rows(
            sent_rows, gates.T, positions, layout, count, slots,
            core_jobs + (("dp", 1),) * 3, (*parts, *pairs[2:]), (1, 2), pairs[1:3], other,
        )
        crossings = crossings + takes[5:8]
        relayed_pairs = [near] + takes[8:10]
        for k in range(3, count):
            relayed_pairs.append(exchange(tie(pairs[k], rows), "dp", 4))
        for k in range(count):
            weights[k] = [pairs[k], crossings[k], relayed_pairs[k]]
    else:
        rows, gates_t, _, grad_slots = team_rows(
            sent_rows, gates.T, positions, layout, count, slots, core_jobs, parts
        )
        for k in range(count):
            weights[k] = crossed(relays(tie(pairs[k], rows)))
    gates_t = lax.dynamic_slice_in_dim(gates_t, first_expert, count, 1)
    gates_t = jnp.pad(gates_t, ((0, 0), (0, 8 - count), (0, 0)))
    row_slots, gate_slots = gather_rows(positions, gates_t, rows, count, slots)

    results, backs, gate_rows, sums = [], [], [], []
    expert_index = dp_index
    for k in range(count):
        if cube:
            relayed_pair = tie(weights[k][2], rows) if k < 3 else tie(weights[k][2], gate_rows[k - 2], weights[k - 1][3])
            weights[k].append(exchange(relayed_pair, "dp", 1))
        y, dx, dg, keep, send = run_expert(k, expert_index, row_slots, grad_slots, gate_slots, weights[k], slots)
        results.append(y)
        backs.append(dx)
        gate_rows.append(dg)
        sums.append((keep, send))
        expert_index = tie(dp_index, dg)

    before_return = added(sums[0][0], exchange(tie(sums[0][1], gate_rows[1], weights[4]), "dp", 1))
    jobs, gives, relays_in = (("dp", 1),) * 2, (sums[1][1], sums[2][1]), 0
    if cube:
        jobs, gives, relays_in = (("dp", 4),) + jobs, (before_return[2:],) + gives, 1
    routed_back, gate_grad, out_keep, out_sent, takes = return_rows(
        positions, backs, results, gate_rows, expert_count, slots, jobs, gives, relays_in
    )
    halved = [before_return, added(sums[1][0], takes[-2]), added(sums[2][0], takes[-1])]
    crossed_back = [exchange(tie(sums[k][1], routed_back), "dp", 1) for k in range(3, count)]
    relay_bits = relay_bits[::-1]

    def sent_on(keep):
        return exchange(keep[keep.shape[0] // 2:], "dp", relay_bits[0])

    def settled(keep, came):
        keep = added(keep[:keep.shape[0] // 2], came)
        for bit in relay_bits[1:]:
            middle = keep.shape[0] // 2
            keep = added(keep[:middle], exchange(keep[middle:], "dp", bit))
        return keep

    relay_came = [takes[0] if cube else sent_on(before_return)] + [sent_on(keep) for keep in halved[1:]]
    gate_grad = gate_grad.T
    routed_back = routed_back.astype(F32)

    grad_output = cotangent.astype(F32)
    picked = jnp.where(chosen, gate_grad, 0.0)
    grad_logits = (gates * (picked - jnp.sum(gates * picked, axis=-1, keepdims=True))).astype(BF)
    wide_logits = jnp.pad(grad_logits, ((0, 0), (0, 128 - expert_count)))
    grad_hidden_two = times_transposed(wide_logits, router_full) + routed_back
    grad_normed_two = grad_hidden_two * gain_second
    grad_second = grad_output + scale_two * (
        grad_normed_two - normed_two * jnp.mean(grad_normed_two * normed_two, axis=-1, keepdims=True)
    )
    grad_branch = grad_second.astype(BF)
    ones = jnp.ones((tok_rows, 128), BF)
    lane = lax.broadcasted_iota(jnp.int32, (tok_rows, 128), 1)
    small = contract_rows(hidden_two, wide_logits) + contract_rows(
        (grad_hidden_two * normed_two).astype(BF), jnp.where(lane == expert_count, ones, jnp.zeros_like(ones))
    )
    grad_mixed = times_transposed(grad_branch, out_full).astype(BF)

    grad_mixed, halved = lax.optimization_barrier((grad_mixed, halved))
    row_came = exchange(out_sent, "expert", 2)
    grad_query, dkp, dvp, dko, dvo = attend_back(
        place, query, prompt_key, prompt_value, own_key, own_value, mixed, grad_mixed, levels
    )
    halved, relay_came, crossed_back, grad_query, row_came, dkp = lax.optimization_barrier(
        (halved, relay_came, crossed_back, grad_query, row_came, dkp)
    )
    halved += [added(sums[k][0], crossed_back[k - 3]) for k in range(3, count)]
    relay_came += [sent_on(halved[3])]
    total = tie(added(out_keep, row_came), halved[3])
    pair_came = exchange(total[1], "dp", 2)
    grad_prompt = group_back(dkp, dvp)
    out_grad = contract_rows(mixed, tie(grad_branch, grad_prompt, relay_came[3])).astype(BF)
    grad_qkv = jnp.concatenate([
        grad_query, jnp.concatenate([grad_prompt, jnp.concatenate([dko, dvo], 1)], 0)
    ], 1)
    grad_hidden_one = times_transposed(grad_qkv, qkv_full)
    weight_rows, grad_hidden_one, relay_came[3], total = lax.optimization_barrier(
        (grad_qkv, grad_hidden_one, relay_came[3], total)
    )
    relayed = [settled(halved[k], relay_came[k]) for k in range(3)]
    passing = jnp.stack([keep[1] for keep in relayed])
    dense_grads = [
        contract_rows(hidden_one, weight_rows).astype(BF),
        contract_rows((grad_hidden_one * normed_one).astype(BF), ones).astype(BF),
        out_grad, small.astype(BF),
    ]
    if cube:
        share, takes = scatter_all(dense_grads, (halved[4][2:], passing))
        relay_came.append(takes[0])
        theirs = takes[1]
    else:
        share = lax.psum_scatter(
            jnp.concatenate(dense_grads, 1), EVERYWHERE, scatter_dimension=0, tiled=True
        ).astype(F32)
        relay_came.append(sent_on(halved[4]))
        theirs = exchange(passing, "dp", 2)
    grad_normed_one = grad_hidden_one * gain_first
    grad_input = grad_second + scale_one * (
        grad_normed_one - normed_one * jnp.mean(grad_normed_one * normed_one, axis=-1, keepdims=True)
    )

    share, halved, relay_came, total, pair_came = lax.optimization_barrier(
        (share, halved, relay_came, total, pair_came)
    )
    output = (second + added(total[0], pair_came).astype(F32)).astype(BF)
    first_share, second_share = share[:, :wide + 128], share[:, wide + 128:]
    relayed += [settled(halved[k], relay_came[k]) for k in range(3, count)]
    theirs = jnp.concatenate([theirs, exchange(jnp.stack([keep[1] for keep in relayed[3:]]), "dp", 2)])
    mine = jnp.stack([keep[0] for keep in relayed])
    lower = jnp.where(turn == 0, mine, theirs)
    upper = jnp.where(turn == 0, theirs, mine)
    expert_grads = jnp.concatenate([lower, upper]).astype(F32)
    return (
        output,
        grad_input.astype(BF),
        first_share[:, wide],
        first_share[:, :D],
        first_share[:, D:D + kvw],
        first_share[:, D + kvw:wide],
        second_share[:, :D].astype(F32),
        second_share[:, D:D + expert_count].astype(F32),
        second_share[:, D + expert_count].astype(F32),
        expert_grads[:, 0],
        expert_grads[:, 1],
        expert_grads[:, 2].transpose(0, 2, 1),
    )


def solution(mesh):
    rows, line = P(("dp", "expert"), None), P(("dp", "expert"))
    gate, down = P("expert", "dp", None), P("expert", None, "dp")
    return jax.shard_map(
        local,
        mesh=mesh,
        in_specs=(rows, line, rows, rows, rows, rows, rows, line, gate, gate, down, rows, rows),
        out_specs=(rows, rows, line, rows, rows, rows, rows, rows, line, gate, gate, down),
        check_vma=False,
    )
```
